32 devices in a mesh: batch: 4 (over y, core), rows: 8 (over z, x).
Axes of the slice: x: 2, y: 2, z: 4, core: 2. Of those that a mesh axis runs over, the one named last changes fastest.
Arguments:
- features: float32 [4, 16384, 100], P('batch', 'rows'), may hold values from -6 to 6
- edge_rows: int32 [4, 8, 2, 16384], P('batch', 'rows'), may hold values from 0 to 3071, as said below
- edge_weight: float32 [4, 8, 16384], P('batch', 'rows'), may hold values from 0.02 to 0.2
- halo_counts: int32 [4, 8, 2], P('batch', 'rows'), may hold values from 1 to 512
- labels: int32 [4, 16384], P('batch', 'rows'), may hold values from 0 to 46
- pair_rows: int32 [4, 8, 8, 4], P('batch', 'rows'), may hold values from 0 to 2047
- step: int32 [1], replicated, may hold values from 2 to 20
- w_in: float32 [100, 256], P(None, 'batch'), may hold values from -0.625 to 0.625
- w_conv: float32 [3, 512, 256], P(None, 'batch'), may hold values from -0.25 to 0.25
- w_head: float32 [256, 47], P('batch'), may hold values from -0.375 to 0.375
- biases: float32 [4, 256], replicated, may hold values from -1 to 1
- norm_params: float32 [3, 2, 256], replicated, may hold values from 0.5 to 1.5
- head_bias: float32 [47], replicated, may hold values from -2 to 2
- mom_in: float32 [100, 256], P(None, 'batch'), may hold values from -0.0234375 to 0.0234375
- mom_conv: float32 [3, 512, 256], P(None, 'batch'), may hold values from -0.0234375 to 0.0234375
- mom_head: float32 [256, 47], P('batch'), may hold values from -0.0234375 to 0.0234375
- first_bias: float32 [4, 256], replicated, may hold values from -0.0024414062 to 0.0024414062
- first_norm: float32 [3, 2, 256], replicated, may hold values from -0.0024414062 to 0.0024414062
- first_head: float32 [47], replicated, may hold values from -0.0024414062 to 0.0024414062
- second_bias: float32 [4, 256], replicated, as said below
- second_norm: float32 [3, 2, 256], replicated, as said below
- second_head: float32 [47], replicated, as said below
Outputs:
- loss: float32 [], replicated
- new_w_in: float32 [100, 256], P(None, 'batch')
- new_w_conv: float32 [3, 512, 256], P(None, 'batch')
- new_w_head: float32 [256, 47], P('batch')
- new_mom_in: float32 [100, 256], P(None, 'batch')
- new_mom_conv: float32 [3, 512, 256], P(None, 'batch')
- new_mom_head: float32 [256, 47], P('batch')
- new_biases: float32 [4, 256], replicated
- new_norm_params: float32 [3, 2, 256], replicated
- new_head_bias: float32 [47], replicated
- new_first_bias: float32 [4, 256], replicated
- new_first_norm: float32 [3, 2, 256], replicated
- new_first_head: float32 [47], replicated
- new_second_bias: float32 [4, 256], replicated
- new_second_norm: float32 [3, 2, 256], replicated
- new_second_head: float32 [47], replicated
The draws below stay inside these ranges and needn't reach their ends.
Inputs may be any that keep to these rules, and one draw needn't show every extreme that they name: edge_rows[b,r,0] are rows of block r; edge_rows[b,r,1] index the extended block and lie between 512 - halo_counts[b,r,0] and 2560 + halo_counts[b,r,1] - 1. `second_bias`: positive. `second_norm`: positive. `second_head`: positive.
All inputs are finite; a program needn't handle non-finite values.
Results may differ from the reference program's by a relative error of at most 0.002.
Values sent between devices are 32-bit elements; how exact they have to be, the bound alone decides.
A program may use at most 128 MiB of HBM per device.

```python
import math
from functools import partial
import jax
import jax.numpy as jnp
from jax import lax

FEAT = 100
HID = 256
CLASSES = 47
LAYERS = 3
NS_STEPS = 5
PAIRS = 4
ROWS_DEV = 2048
HALO = 512
EDGES = 16384
NODES = 16384
TOTAL_NODES = 65536
N_BATCH = 4
N_ROWS = 8


def graph_draw(key):
    base = jax.random.fold_in(key, 101)
    count_key, target_key, offset_key = jax.random.split(base, 3)
    counts = jax.random.randint(count_key, (N_BATCH, N_ROWS, 2), 1, HALO + 1)
    counts = counts.at[:, 1, 0].set(HALO).at[:, 0, 1].set(HALO).at[:, 2, 1].set(1)
    target = jax.random.randint(target_key, (N_BATCH, N_ROWS, EDGES), 0, ROWS_DEV)
    offset = jax.random.randint(offset_key, (N_BATCH, N_ROWS, EDGES), -HALO, HALO + 1)
    lowest = HALO - counts[:, :, 0:1]
    highest_row = ROWS_DEV + HALO + counts[:, :, 1:2] - 1
    source = jnp.clip(target + HALO + offset, lowest, highest_row)
    source = source.at[:, :, 0].set(highest_row[:, :, 0]).at[:, :, 1].set(lowest[:, :, 0])
    return (counts, jnp.stack([target, source], 2))


def draw_edge_rows(key, part):
    return graph_draw(key)[1]


def draw_halo_counts(key, part):
    return graph_draw(key)[0]


def second_moment(key, shape):
    factor = jnp.exp(jax.random.uniform(key, shape, jnp.float32, math.log(0.5), math.log(8.0)))
    return factor * (0.001 / TOTAL_NODES)


def draw_second_bias(key, part):
    return second_moment(jax.random.fold_in(key, 11), (LAYERS + 1, HID))


def draw_second_norm(key, part):
    return second_moment(jax.random.fold_in(key, 12), (LAYERS, 2, HID))


def draw_second_head(key, part):
    return second_moment(jax.random.fold_in(key, 13), (CLASSES,))


def set_ends(drawn, rng, smallest, high):
    spot = [jax.random.randint(jax.random.fold_in(rng, axis), (), 0, length) for axis, length in enumerate(drawn.shape)]
    widest = drawn.shape.index(max(drawn.shape))
    next_to = spot[:widest] + [(spot[widest] + 1) % drawn.shape[widest]] + spot[widest + 1:]
    return drawn.at[tuple(spot)].set(smallest).at[tuple(next_to)].set(high)


def steps_of(own_key, extent, shards, low, largest):
    loudness = 1.0
    for dim, parts in shards:
        steps = jax.random.uniform(jax.random.fold_in(jax.random.fold_in(own_key, 6), dim), (parts,), jnp.float32, low / len(shards), largest / len(shards))
        loudness = loudness * jnp.repeat(jnp.exp(steps), extent[dim] // parts).reshape((-1,) + (1,) * (len(extent) - 1 - dim))
    return loudness


def normal_values(rng, shape, scale, bound, pieces=(), kind=jnp.bfloat16):
    level = steps_of(rng, shape, pieces, -0.22, 0.18) if pieces else 1.0
    entries = jax.random.normal(rng, shape, jnp.float32) * scale * level
    return jnp.minimum(jnp.maximum(entries, -bound), bound).astype(kind)


def setup_inputs(seed: int = 0) -> dict:
    keys = jax.random.split(jax.random.key(seed), 23)
    features = normal_values(keys[0], (N_BATCH, NODES, FEAT), 1.0, 6.0, ((0, 4), (1, 8)), jnp.float32)
    edge_rows = draw_edge_rows(jax.random.fold_in(keys[22], 71), 0)
    edge_weight = jnp.clip(0.02 + 0.18 * jax.random.uniform(keys[2], (N_BATCH, N_ROWS, EDGES), jnp.float32) ** steps_of(keys[2], (N_BATCH, N_ROWS, EDGES), ((0, 4), (1, 8)), -0.2, 0.2), 0.02, 0.2)
    halo_counts = draw_halo_counts(jax.random.fold_in(keys[22], 71), 0)
    labels = set_ends(jax.random.randint(keys[4], (N_BATCH, NODES), 0, CLASSES), jax.random.fold_in(keys[4], 1), 0, CLASSES - 1).astype(jnp.int32)
    pair_rows = set_ends(jax.random.randint(keys[5], (N_BATCH, N_ROWS, N_ROWS, PAIRS), 0, ROWS_DEV), jax.random.fold_in(keys[5], 1), 0, ROWS_DEV - 1).astype(jnp.int32)
    step = jax.random.randint(keys[6], (1,), 2, 21).astype(jnp.int32)
    w_in = normal_values(keys[7], (FEAT, HID), FEAT ** -0.5, 0.625, ((1, 4),), jnp.float32)
    w_conv = normal_values(keys[8], (LAYERS, 2 * HID, HID), (2 * HID) ** -0.5, 0.25, ((1, 4),), jnp.float32)
    w_head = normal_values(keys[9], (HID, CLASSES), HID ** -0.5, 0.375, ((0, 4),), jnp.float32)
    biases = normal_values(keys[10], (LAYERS + 1, HID), 0.2, 1.0, (), jnp.float32)
    norm_params = jnp.clip(jax.random.uniform(keys[11], (LAYERS, 2, HID), jnp.float32, 0.5, 1.5), 0.5, 1.5)
    head_bias = normal_values(keys[12], (CLASSES,), 0.5, 2.0, (), jnp.float32)
    mom_in = normal_values(keys[13], (FEAT, HID), TOTAL_NODES ** -0.5, 0.0234375, ((1, 4),), jnp.float32)
    mom_conv = normal_values(keys[14], (LAYERS, 2 * HID, HID), TOTAL_NODES ** -0.5, 0.0234375, ((1, 4),), jnp.float32)
    mom_head = normal_values(keys[15], (HID, CLASSES), TOTAL_NODES ** -0.5, 0.0234375, ((0, 4),), jnp.float32)
    first_bias = normal_values(keys[16], (LAYERS + 1, HID), (81 * TOTAL_NODES) ** -0.5, 0.0024414062, (), jnp.float32)
    first_norm = normal_values(keys[17], (LAYERS, 2, HID), (81 * TOTAL_NODES) ** -0.5, 0.0024414062, (), jnp.float32)
    first_head = normal_values(keys[18], (CLASSES,), (81 * TOTAL_NODES) ** -0.5, 0.0024414062, (), jnp.float32)
    second_bias = draw_second_bias(jax.random.fold_in(keys[22], 71), 0)
    second_norm = draw_second_norm(jax.random.fold_in(keys[22], 71), 0)
    second_head = draw_second_head(jax.random.fold_in(keys[22], 71), 0)
    return dict(features=features, edge_rows=edge_rows, edge_weight=edge_weight, halo_counts=halo_counts, labels=labels, pair_rows=pair_rows, step=step, w_in=w_in, w_conv=w_conv, w_head=w_head, biases=biases, norm_params=norm_params, head_bias=head_bias, mom_in=mom_in, mom_conv=mom_conv, mom_head=mom_head, first_bias=first_bias, first_norm=first_norm, first_head=first_head, second_bias=second_bias, second_norm=second_norm, second_head=second_head)


highest = lax.Precision.HIGHEST
norm_epsilon = 1e-05
pair_weight = 0.05
newton_a = 3.4445
newton_b = -4.775
newton_c = 2.0315
muon_decay = 0.9
muon_rate = 0.5
muon_shrink = 0.01
adam_first_decay = 0.9
adam_second_decay = 0.999
adam_epsilon = 1e-08
adam_rate = 0.1
adam_shrink = 0.01

def product(left, right):
    return jnp.dot(left, right, precision=highest, preferred_element_type=jnp.float32)

def extend_blocks(blocks, counts):
    width = blocks.shape[2]
    empty = jnp.zeros((1, HALO, width), jnp.float32)
    below = jnp.concatenate([empty, blocks[:-1, ROWS_DEV - HALO:]], 0)
    above = jnp.concatenate([blocks[1:, :HALO], empty], 0)
    place = jnp.arange(HALO, dtype=jnp.int32)
    keep_below = (place[None, :] >= HALO - counts[:, 0:1]).astype(jnp.float32)
    keep_above = (place[None, :] < counts[:, 1:2]).astype(jnp.float32)
    return jnp.concatenate([below * keep_below[:, :, None], blocks, above * keep_above[:, :, None]], 1)

def one_block(extended_block, edges, weights):
    picked = extended_block[edges[1]] * weights[:, None]
    return jax.ops.segment_sum(picked, edges[0], num_segments=ROWS_DEV)

def conv_layer(hidden, matrix, bias, gain, shift, edge_rows, edge_weight, counts):
    blocks = hidden.reshape(N_ROWS, ROWS_DEV, HID)
    extended = extend_blocks(blocks, counts)
    gathered = jax.vmap(one_block)(extended, edge_rows, edge_weight).reshape(NODES, HID)
    pre = product(jnp.concatenate([hidden, gathered], 1), matrix) + bias
    active = jnp.maximum(pre, 0.0)
    mean = lax.optimization_barrier(jnp.mean(active, 0))
    spread = lax.optimization_barrier(jnp.mean(active * active, 0)) - mean * mean
    return gain * ((active - mean) * lax.rsqrt(spread + norm_epsilon)) + shift

def pick_rows(block_logits, picked):
    return block_logits[picked]

def batch_total(params, batch):
    w_in, w_conv, w_head, biases, norm_params, head_bias = params
    features, edge_rows, edge_weight, counts, labels, pair_rows = batch
    hidden = product(features, w_in) + biases[0]
    for layer in range(LAYERS):
        hidden = conv_layer(hidden, w_conv[layer], biases[layer + 1], norm_params[layer, 0], norm_params[layer, 1], edge_rows, edge_weight, counts)
    logits = product(hidden, w_head) + head_bias
    log_total = jax.nn.logsumexp(logits, axis=1)
    target = jnp.take_along_axis(logits, labels[:, None], axis=1)[:, 0]
    sent = jax.vmap(pick_rows)(logits.reshape(N_ROWS, ROWS_DEV, CLASSES), pair_rows)
    gap = sent - jnp.swapaxes(sent, 0, 1)
    return jnp.sum(log_total - target) + pair_weight * jnp.sum(gap * gap)

def orthogonal(moment):
    scaled = moment / (jnp.sqrt(jnp.sum(moment * moment)) + 1e-07)
    for repeat in range(NS_STEPS):
        gram = product(scaled, scaled.T)
        scaled = newton_a * scaled + product(newton_b * gram + newton_c * product(gram, gram), scaled)
    return scaled

def muon(weight, moment, grad, flipped):
    new_moment = muon_decay * moment + grad
    fan_in, fan_out = weight.shape
    scale = math.sqrt(max(1.0, fan_out / fan_in))
    if flipped:
        direction = orthogonal(new_moment.T).T
    else:
        direction = orthogonal(new_moment)
    return (weight - muon_rate * (scale * direction + muon_shrink * weight), new_moment)

def adamw(param, grad, first, second, count):
    first = adam_first_decay * first + (1.0 - adam_first_decay) * grad
    second = adam_second_decay * second + (1.0 - adam_second_decay) * grad * grad
    first_hat = first / (1.0 - jnp.power(adam_first_decay, count))
    second_hat = second / (1.0 - jnp.power(adam_second_decay, count))
    param = param - adam_rate * (first_hat / (jnp.sqrt(second_hat) + adam_epsilon) + adam_shrink * param)
    return (param, first, second)

def reference(features, edge_rows, edge_weight, halo_counts, labels, pair_rows, step, w_in, w_conv, w_head, biases, norm_params, head_bias, mom_in, mom_conv, mom_head, first_bias, first_norm, first_head, second_bias, second_norm, second_head):
    data = (features, edge_rows, edge_weight, halo_counts, labels, pair_rows)

    def forward(*params):
        totals = lax.map(partial(batch_total, params), data)
        return jnp.sum(totals) / (N_BATCH * NODES)
    loss, pullback = jax.vjp(forward, w_in, w_conv, w_head, biases, norm_params, head_bias)
    grads = pullback(jnp.ones_like(loss))
    new_in, new_mom_in = muon(w_in, mom_in, grads[0], False)
    conv_weights = []
    conv_moments = []
    for layer in range(LAYERS):
        weight, moment = muon(w_conv[layer], mom_conv[layer], grads[1][layer], True)
        conv_weights.append(weight)
        conv_moments.append(moment)
    new_head, new_mom_head = muon(w_head, mom_head, grads[2], True)
    count = step[0].astype(jnp.float32)
    new_bias, bias_first, bias_second = adamw(biases, grads[3], first_bias, second_bias, count)
    new_norm, norm_first, norm_second = adamw(norm_params, grads[4], first_norm, second_norm, count)
    new_hb, head_first, head_second = adamw(head_bias, grads[5], first_head, second_head, count)
    return (loss, new_in, jnp.stack(conv_weights), new_head, new_mom_in, jnp.stack(conv_moments), new_mom_head, new_bias, new_norm, new_hb, bias_first, norm_first, head_first, bias_second, norm_second, head_second)
```

```python
import functools
import math

import jax
import jax.numpy as jnp
from jax import lax
from jax.experimental import pallas as pl
from jax.experimental.pallas import tpu as pltpu
from jax.sharding import PartitionSpec as P

NS_STEPS = 5

f32 = jnp.float32
highest = lax.Precision.HIGHEST
three_pass = lax.Precision.HIGH
norm_epsilon = 1e-05
pair_weight = 0.05
newton_a = 3.4445
newton_b = -4.775
newton_c = 2.0315
muon_decay = 0.9
muon_rate = 0.5
muon_shrink = 0.01
adam_first_decay = 0.9
adam_second_decay = 0.999
adam_epsilon = 1e-08
adam_rate = 0.1
adam_shrink = 0.01


def product(left, right):
    return jnp.matmul(left, right, precision=highest, preferred_element_type=f32)


def product3(left, right):
    return jnp.matmul(left, right, precision=three_pass, preferred_element_type=f32)


def swap(b, r):
    return 2 * (b // 2) + r % 2, 2 * (r // 2) + b % 2


def flat_pairs(n_batch, n_rows, move):
    pairs = []
    for b in range(n_batch):
        for r in range(n_rows):
            to = move(b, r)
            if to is not None:
                pairs.append((b * n_rows + r, to[0] * n_rows + to[1]))
    return pairs


def redeal(array, n_batch, n_rows):
    return lax.ppermute(array, ("batch", "rows"), flat_pairs(n_batch, n_rows, swap))


def pass_rows(array, n_batch, n_rows, by):
    def move(b, r):
        batch, block = swap(b, r)
        block = block + by
        return swap(batch, block) if 0 <= block < n_rows else None

    return lax.ppermute(array, ("batch", "rows"), flat_pairs(n_batch, n_rows, move))


def peer_place(batch, block):
    two = jnp.int32(2)
    return (
        two * lax.div(batch, two) + lax.rem(block, two),
        two * lax.div(block, two) + lax.rem(batch, two),
    )


def my_place():
    return peer_place(lax.axis_index("batch"), lax.axis_index("rows"))


def greet(n, batch, block):
    barrier = pltpu.get_barrier_semaphore()
    for k in range(1, n):
        pl.semaphore_signal(
            barrier,
            inc=1,
            device_id=peer_place(batch, lax.rem(block + k, n)),
            device_id_type=pl.DeviceIdType.MESH,
        )
    pl.semaphore_wait(barrier, n - 1)


def group_sum_kernel(n, x_ref, o_ref, held, send_sem, recv_sem):
    batch, block = my_place()
    greet(n, batch, block)
    held[0] = x_ref[...]
    copies = []
    for k in range(1, n):
        copy = pltpu.make_async_remote_copy(
            src_ref=x_ref,
            dst_ref=held.at[k],
            send_sem=send_sem.at[k],
            recv_sem=recv_sem.at[k],
            device_id=peer_place(batch, lax.rem(block + k, n)),
            device_id_type=pl.DeviceIdType.MESH,
        )
        copy.start()
        copies.append(copy)
    for copy in copies:
        copy.wait()
    total = held[lax.rem(block, n)]
    for q in range(1, n):
        total = total + held[lax.rem(block + n - q, n)]
    o_ref[...] = total


def group_sum(x, n):
    return pl.pallas_call(
        functools.partial(group_sum_kernel, n),
        out_shape=jax.ShapeDtypeStruct(x.shape, f32),
        in_specs=[pl.BlockSpec(memory_space=pltpu.VMEM)],
        out_specs=pl.BlockSpec(memory_space=pltpu.VMEM),
        scratch_shapes=[
            pltpu.VMEM((n,) + x.shape, f32),
            pltpu.SemaphoreType.DMA((n,)),
            pltpu.SemaphoreType.DMA((n,)),
        ],
        compiler_params=pltpu.CompilerParams(collective_id=1, has_side_effects=True),
        name="group_sum",
    )(x)


def group_gather_kernel(n, x_ref, o_ref, send_sem, recv_sem):
    batch, block = my_place()
    greet(n, batch, block)
    copies = []
    for k in range(1, n):
        peer = lax.rem(block + k, n)
        copy = pltpu.make_async_remote_copy(
            src_ref=x_ref.at[peer],
            dst_ref=o_ref.at[k],
            send_sem=send_sem.at[k],
            recv_sem=recv_sem.at[k],
            device_id=peer_place(batch, peer),
            device_id_type=pl.DeviceIdType.MESH,
        )
        copy.start()
        copies.append(copy)
    o_ref[0] = x_ref[block]
    for copy in copies:
        copy.wait()


def group_gather(x, n):
    return pl.pallas_call(
        functools.partial(group_gather_kernel, n),
        out_shape=jax.ShapeDtypeStruct(x.shape, f32),
        in_specs=[pl.BlockSpec(memory_space=pltpu.VMEM)],
        out_specs=pl.BlockSpec(memory_space=pltpu.VMEM),
        scratch_shapes=[pltpu.SemaphoreType.DMA((n,)), pltpu.SemaphoreType.DMA((n,))],
        compiler_params=pltpu.CompilerParams(collective_id=2, has_side_effects=True),
        name="pair_exchange",
    )(x)


def kdot(left, right, dims=((1,), (0,))):
    return lax.dot_general(left, right, (dims, ((), ())), precision=highest, preferred_element_type=f32)


def muon_kernel(scale_in, scale_head, conv_mom, in_mom, head_mom, conv_q, in_q, head_q, gram_c, poly_c, gram_s, poly_s):
    layers = conv_mom.shape[0]
    for which in range(layers):
        m = conv_mom[which]
        size = jnp.sqrt(jnp.sum(m * m)) + 1e-07
        gram_c[which] = kdot(m, m, ((0,), (0,))) / (size * size)
    m = in_mom[...]
    size = jnp.sqrt(jnp.sum(m * m)) + 1e-07
    gram_s[0] = kdot(m, m, ((1,), (1,))) / (size * size)
    in_size = size
    m = head_mom[...]
    head_size = jnp.sqrt(jnp.sum(m * m)) + 1e-07
    gram_s[1] = kdot(m, m, ((1,), (1,))) / (head_size * head_size)

    def eye(n):
        return (lax.broadcasted_iota(jnp.int32, (n, n), 0) == lax.broadcasted_iota(jnp.int32, (n, n), 1)).astype(f32)

    for which in range(layers):
        poly_c[which] = eye(poly_c.shape[1])
    for which in range(2):
        poly_s[which] = eye(poly_s.shape[1])

    def step(grams, polys):
        n = grams.shape[1]
        count = grams.shape[0]
        a1 = [grams[i] for i in range(count)]
        a2 = [kdot(a, a) for a in a1]
        p = [newton_a * eye(n) + newton_b * x + newton_c * y for x, y in zip(a1, a2)]
        pa = [kdot(x, y) for x, y in zip(p, a1)]
        q = [kdot(x, polys[i]) for i, x in enumerate(p)]
        nxt = [kdot(x, y) for x, y in zip(pa, p)]
        for i in range(count):
            polys[i] = q[i]
            grams[i] = nxt[i]

    def body(_, carry):
        step(gram_c, poly_c)
        step(gram_s, poly_s)
        return carry

    lax.fori_loop(0, NS_STEPS, body, 0)
    for which in range(layers):
        m = conv_mom[which]
        size = jnp.sqrt(jnp.sum(m * m)) + 1e-07
        conv_q[which] = poly_c[which] / size
    in_q[...] = poly_s[0] / in_size * scale_in
    head_q[...] = poly_s[1] / head_size * scale_head


def muon_factors(conv_mom, in_mom, head_mom, scale_in, scale_head):
    layers, _, hid = conv_mom.shape
    small = 128
    in_pad = jnp.pad(in_mom, ((0, small - in_mom.shape[0]), (0, 0)))
    head_t = jnp.pad(head_mom.T, ((0, small - head_mom.shape[1]), (0, 0)))
    return pl.pallas_call(
        functools.partial(muon_kernel, scale_in, scale_head),
        out_shape=(
            jax.ShapeDtypeStruct((layers, hid, hid), f32),
            jax.ShapeDtypeStruct((small, small), f32),
            jax.ShapeDtypeStruct((small, small), f32),
        ),
        in_specs=[pl.BlockSpec(memory_space=pltpu.VMEM)] * 3,
        out_specs=(pl.BlockSpec(memory_space=pltpu.VMEM),) * 3,
        scratch_shapes=[
            pltpu.VMEM((layers, hid, hid), f32),
            pltpu.VMEM((layers, hid, hid), f32),
            pltpu.VMEM((2, small, small), f32),
            pltpu.VMEM((2, small, small), f32),
        ],
        compiler_params=pltpu.CompilerParams(vmem_limit_bytes=40 << 20),
        name="muon",
    )(conv_mom, in_pad, head_t)


def layer_forward(hidden, matrix, bias, gain, shift, adjacency, rim_below, rim_above, node_count, dims):
    halo_rows = rim_below.shape[0]
    rows_dev = hidden.shape[0]
    below = pass_rows(hidden[rows_dev - halo_rows :], *dims, 1)
    above = pass_rows(hidden[:halo_rows], *dims, -1)
    padded = jnp.concatenate([below * rim_below, hidden, above * rim_above], 0)
    joined = jnp.concatenate([hidden, product(adjacency, padded)], 1)
    pre = product(joined, matrix) + bias
    active = jnp.maximum(pre, 0.0)
    totals = group_sum(jnp.stack([jnp.sum(active, 0), jnp.sum(active * active, 0)]), dims[1])
    mean = totals[0] / node_count
    inverse = lax.rsqrt(totals[1] / node_count - mean * mean + norm_epsilon)
    normed = (active - mean) * inverse
    return (gain * normed + shift, (joined, pre, normed, inverse))


def layer_backward(grad_out, kept, matrix, gain, adjacency, rim_below, rim_above, node_count, dims):
    joined, pre, normed, inverse = kept
    halo_rows = rim_below.shape[0]
    rows_dev = joined.shape[0]
    width = matrix.shape[1]
    grad_gain = jnp.sum(grad_out * normed, 0)
    grad_shift = jnp.sum(grad_out, 0)
    totals = group_sum(jnp.stack([grad_shift, grad_gain]), dims[1]) * gain
    grad_normed = grad_out * gain
    grad_active = inverse * (
        grad_normed - totals[0] / node_count - normed * (totals[1] / node_count)
    )
    grad_pre = jnp.where(pre > 0.0, grad_active, 0.0)
    grad_matrix = product3(joined.T, grad_pre)
    grad_bias = jnp.sum(grad_pre, 0)
    grad_joined = product3(grad_pre, matrix.T)
    grad_padded = product3(adjacency.T, grad_joined[:, width:])
    from_above = pass_rows(grad_padded[:halo_rows] * rim_below, *dims, -1)
    from_below = pass_rows(grad_padded[halo_rows + rows_dev :] * rim_above, *dims, 1)
    grad_hidden = grad_joined[:, :width] + grad_padded[halo_rows : halo_rows + rows_dev]
    grad_hidden = grad_hidden + jnp.pad(from_above, ((rows_dev - halo_rows, 0), (0, 0)))
    grad_hidden = grad_hidden + jnp.pad(from_below, ((0, rows_dev - halo_rows), (0, 0)))
    return (grad_hidden, grad_matrix, grad_bias, grad_gain, grad_shift)


def adamw(param, grad, first, second, count):
    first = adam_first_decay * first + (1.0 - adam_first_decay) * grad
    second = adam_second_decay * second + (1.0 - adam_second_decay) * grad * grad
    first_hat = first / (1.0 - jnp.power(adam_first_decay, count))
    second_hat = second / (1.0 - jnp.power(adam_second_decay, count))
    param = param - adam_rate * (
        first_hat / (jnp.sqrt(second_hat) + adam_epsilon) + adam_shrink * param
    )
    return (param, first, second)


def per_device(
    n_batch,
    n_rows,
    features,
    edge_rows,
    edge_weight,
    halo_counts,
    labels,
    pair_rows,
    step,
    w_in,
    w_conv,
    w_head,
    biases,
    norm_params,
    head_bias,
    mom_in,
    mom_conv,
    mom_head,
    first_bias,
    first_norm,
    first_head,
    second_bias,
    second_norm,
    second_head,
):
    dims = (n_batch, n_rows)
    edge_rows, edge_weight, features, halo_counts, labels, pair_rows = (
        redeal(x, *dims) for x in (edge_rows, edge_weight, features, halo_counts, labels, pair_rows)
    )
    full_in, full_conv, full_head, full_mom_in, full_mom_conv, full_mom_head = (
        lax.all_gather(w_in, "batch", axis=1, tiled=True),
        lax.all_gather(w_conv, "batch", axis=1, tiled=True),
        lax.all_gather(w_head, "batch", axis=0, tiled=True),
        lax.all_gather(mom_in, "batch", axis=1, tiled=True),
        lax.all_gather(mom_conv, "batch", axis=1, tiled=True),
        lax.all_gather(mom_head, "batch", axis=0, tiled=True),
    )
    inputs = features[0]
    rows_dev = inputs.shape[0]
    halo_rows = rows_dev // 4
    layers = full_conv.shape[0]
    node_count = rows_dev * n_rows
    all_nodes = node_count * n_batch
    edges = edge_rows[0, 0]
    counts = halo_counts[0, 0]
    adjacency = (
        jnp.zeros((rows_dev, rows_dev + 2 * halo_rows), f32)
        .at[edges[0], edges[1]]
        .add(edge_weight[0, 0])
    )
    place = jnp.arange(halo_rows, dtype=jnp.int32)
    rim_below = (place >= halo_rows - counts[0]).astype(f32)[:, None]
    rim_above = (place < counts[1]).astype(f32)[:, None]
    hidden = product(inputs, full_in) + biases[0]
    kept_all = []
    for layer in range(layers):
        hidden, kept = layer_forward(
            hidden,
            full_conv[layer],
            biases[layer + 1],
            norm_params[layer, 0],
            norm_params[layer, 1],
            adjacency,
            rim_below,
            rim_above,
            node_count,
            dims,
        )
        kept_all.append(kept)
    logits = product(hidden, full_head) + head_bias
    log_total = jax.nn.logsumexp(logits, axis=1)
    classes = logits.shape[1]
    onehot = (labels[0][:, None] == jnp.arange(classes, dtype=jnp.int32)[None, :]).astype(f32)
    cross = jnp.sum(log_total) - jnp.sum(onehot * logits)
    picks = pair_rows[0, 0]
    sent = logits[picks]
    block = my_place()[1]
    got = group_gather(sent, n_rows)
    received = got[lax.rem(block + n_rows - jnp.arange(n_rows, dtype=jnp.int32), n_rows)]
    gap = sent - received
    local_total = cross + pair_weight * jnp.sum(gap * gap)
    grad_logits = jnp.exp(logits - log_total[:, None]) - onehot
    grad_logits = grad_logits.at[picks].add(4.0 * pair_weight * gap)
    grad_logits = grad_logits / all_nodes
    grad_head = product3(hidden.T, grad_logits)
    grad_head_bias = jnp.sum(grad_logits, 0)
    grad_hidden = product3(grad_logits, full_head.T)
    conv_grads = [None] * layers
    bias_grads = [None] * layers
    norm_grads = [None] * layers
    for layer in reversed(range(layers)):
        grad_hidden, grad_matrix, grad_bias, grad_gain, grad_shift = layer_backward(
            grad_hidden,
            kept_all[layer],
            full_conv[layer],
            norm_params[layer, 0],
            adjacency,
            rim_below,
            rim_above,
            node_count,
            dims,
        )
        conv_grads[layer] = grad_matrix
        bias_grads[layer] = grad_bias
        norm_grads[layer] = jnp.stack([grad_gain, grad_shift])
    grad_in = product3(inputs.T, grad_hidden)
    grad_biases = jnp.stack([jnp.sum(grad_hidden, 0)] + bias_grads)
    grad_norms = jnp.stack(norm_grads)
    grad_conv = jnp.stack(conv_grads)
    summed = lax.psum(
        (grad_in, grad_conv, grad_head, grad_biases, grad_norms, grad_head_bias, local_total),
        ("batch", "rows"),
    )
    small = (summed[3], summed[4], summed[5], summed[6])
    moment_in = muon_decay * full_mom_in + summed[0]
    moment_conv = muon_decay * full_mom_conv + summed[1]
    moment_head = muon_decay * full_mom_head + summed[2]
    scale_in = math.sqrt(max(1.0, full_in.shape[1] / full_in.shape[0]))
    scale_conv = math.sqrt(max(1.0, full_conv.shape[2] / full_conv.shape[1]))
    scale_head = math.sqrt(max(1.0, full_head.shape[1] / full_head.shape[0]))
    conv_q, in_q, head_q = muon_factors(moment_conv, moment_in, moment_head, scale_in, scale_head)
    at = lax.axis_index("batch")
    moment_in = lax.dynamic_slice_in_dim(moment_in, at * w_in.shape[1], w_in.shape[1], 1)
    moment_conv = lax.dynamic_slice_in_dim(moment_conv, at * w_conv.shape[1], w_conv.shape[1], 1)
    moment_head = lax.dynamic_slice_in_dim(moment_head, at * w_head.shape[0], w_head.shape[0], 0)
    feat, classes = w_in.shape[0], w_head.shape[1]
    turn_in = product(in_q[:feat, :feat], moment_in)
    turn_conv = jnp.einsum("lij,ljk->lik", moment_conv, conv_q, precision=highest)
    turn_head = product(moment_head, head_q[:classes, :classes])
    new_in = w_in - muon_rate * (turn_in + muon_shrink * w_in)
    new_conv = w_conv - muon_rate * (scale_conv * turn_conv + muon_shrink * w_conv)
    new_head = w_head - muon_rate * (turn_head + muon_shrink * w_head)
    count = step[0].astype(f32)
    new_bias, bias_first, bias_second = adamw(biases, small[0], first_bias, second_bias, count)
    new_norm, norm_first, norm_second = adamw(norm_params, small[1], first_norm, second_norm, count)
    new_hb, head_first, head_second = adamw(head_bias, small[2], first_head, second_head, count)
    loss = small[3] / all_nodes
    return (
        loss,
        new_in,
        new_conv,
        new_head,
        moment_in,
        moment_conv,
        moment_head,
        new_bias,
        new_norm,
        new_hb,
        bias_first,
        norm_first,
        head_first,
        bias_second,
        norm_second,
        head_second,
    )


def solution(mesh):
    in_specs = (
        P("batch", "rows", None),
        P("batch", "rows", None, None),
        P("batch", "rows", None),
        P("batch", "rows", None),
        P("batch", "rows"),
        P("batch", "rows", None, None),
        P(),
        P(None, "batch"),
        P(None, "batch", None),
        P("batch", None),
        P(),
        P(),
        P(),
        P(None, "batch"),
        P(None, "batch", None),
        P("batch", None),
        P(),
        P(),
        P(),
        P(),
        P(),
        P(),
    )
    out_specs = (
        P(),
        P(None, "batch"),
        P(None, "batch", None),
        P("batch", None),
        P(None, "batch"),
        P(None, "batch", None),
        P("batch", None),
        P(),
        P(),
        P(),
        P(),
        P(),
        P(),
        P(),
        P(),
        P(),
    )
    body = functools.partial(per_device, mesh.shape["batch"], mesh.shape["rows"])
    return jax.shard_map(body, mesh=mesh, in_specs=in_specs, out_specs=out_specs, check_vma=False)
```

```python
import functools
import math

import jax
import jax.numpy as jnp
from jax import lax
from jax.experimental import pallas as pl
from jax.experimental.pallas import tpu as pltpu
from jax.sharding import PartitionSpec as P

NS_STEPS = 5
FORWARD_PARTS = (2, 2, 2)

f32 = jnp.float32
bf16 = jnp.bfloat16
LANES = 128
TILE = 256
highest = lax.Precision.HIGHEST
three_pass = lax.Precision.HIGH
norm_epsilon = 1e-05
pair_weight = 0.05
newton_a = 3.4445
newton_b = -4.775
newton_c = 2.0315
muon_decay = 0.9
muon_rate = 0.5
muon_shrink = 0.01
adam_first_decay = 0.9
adam_second_decay = 0.999
adam_epsilon = 1e-08
adam_rate = 0.1
adam_shrink = 0.01


def product(left, right):
    return jnp.matmul(left, right, precision=highest, preferred_element_type=f32)


def product3(left, right):
    return jnp.matmul(left, right, precision=three_pass, preferred_element_type=f32)


def swap(b, r):
    return 2 * (b // 2) + r % 2, 2 * (r // 2) + b % 2


def flat_pairs(n_batch, n_rows, move):
    pairs = []
    for b in range(n_batch):
        for r in range(n_rows):
            to = move(b, r)
            if to is not None:
                pairs.append((b * n_rows + r, to[0] * n_rows + to[1]))
    return pairs


def redeal(array, n_batch, n_rows):
    return lax.ppermute(array, ("batch", "rows"), flat_pairs(n_batch, n_rows, swap))


def pass_rows(array, n_batch, n_rows, by):
    def move(b, r):
        batch, block = swap(b, r)
        block = block + by
        return swap(batch, block) if 0 <= block < n_rows else None

    return lax.ppermute(array, ("batch", "rows"), flat_pairs(n_batch, n_rows, move))


def peer_place(batch, block):
    two = jnp.int32(2)
    return (
        two * lax.div(batch, two) + lax.rem(block, two),
        two * lax.div(block, two) + lax.rem(batch, two),
    )


def my_place():
    return peer_place(lax.axis_index("batch"), lax.axis_index("rows"))


def greet(n, batch, block):
    barrier = pltpu.get_barrier_semaphore()
    for k in range(1, n):
        pl.semaphore_signal(
            barrier,
            inc=1,
            device_id=peer_place(batch, lax.rem(block + k, n)),
            device_id_type=pl.DeviceIdType.MESH,
        )
    pl.semaphore_wait(barrier, n - 1)


def group_sum_kernel(n, x_ref, o_ref, held, send_sem, recv_sem):
    batch, block = my_place()
    greet(n, batch, block)
    held[0] = x_ref[...]
    copies = []
    for k in range(1, n):
        copy = pltpu.make_async_remote_copy(
            src_ref=x_ref,
            dst_ref=held.at[k],
            send_sem=send_sem.at[k],
            recv_sem=recv_sem.at[k],
            device_id=peer_place(batch, lax.rem(block + k, n)),
            device_id_type=pl.DeviceIdType.MESH,
        )
        copy.start()
        copies.append(copy)
    for copy in copies:
        copy.wait()
    total = held[lax.rem(block, n)]
    for q in range(1, n):
        total = total + held[lax.rem(block + n - q, n)]
    o_ref[...] = total


def group_sum(x, n):
    return pl.pallas_call(
        functools.partial(group_sum_kernel, n),
        out_shape=jax.ShapeDtypeStruct(x.shape, f32),
        in_specs=[pl.BlockSpec(memory_space=pltpu.VMEM)],
        out_specs=pl.BlockSpec(memory_space=pltpu.VMEM),
        scratch_shapes=[
            pltpu.VMEM((n,) + x.shape, f32),
            pltpu.SemaphoreType.DMA((n,)),
            pltpu.SemaphoreType.DMA((n,)),
        ],
        compiler_params=pltpu.CompilerParams(collective_id=1, has_side_effects=True),
        name="group_sum",
    )(x)


def group_gather_kernel(n, x_ref, o_ref, send_sem, recv_sem):
    batch, block = my_place()
    greet(n, batch, block)
    copies = []
    for k in range(1, n):
        peer = lax.rem(block + k, n)
        copy = pltpu.make_async_remote_copy(
            src_ref=x_ref.at[peer],
            dst_ref=o_ref.at[k],
            send_sem=send_sem.at[k],
            recv_sem=recv_sem.at[k],
            device_id=peer_place(batch, peer),
            device_id_type=pl.DeviceIdType.MESH,
        )
        copy.start()
        copies.append(copy)
    o_ref[0] = x_ref[block]
    for copy in copies:
        copy.wait()


def group_gather(x, n):
    return pl.pallas_call(
        functools.partial(group_gather_kernel, n),
        out_shape=jax.ShapeDtypeStruct(x.shape, f32),
        in_specs=[pl.BlockSpec(memory_space=pltpu.VMEM)],
        out_specs=pl.BlockSpec(memory_space=pltpu.VMEM),
        scratch_shapes=[pltpu.SemaphoreType.DMA((n,)), pltpu.SemaphoreType.DMA((n,))],
        compiler_params=pltpu.CompilerParams(collective_id=2, has_side_effects=True),
        name="pair_exchange",
    )(x)


def kdot(left, right, dims=((1,), (0,))):
    return lax.dot_general(left, right, (dims, ((), ())), precision=highest, preferred_element_type=f32)


def muon_kernel(scale_in, scale_head, conv_mom, in_mom, head_mom, conv_q, in_q, head_q, gram_c, poly_c, gram_s, poly_s):
    layers = conv_mom.shape[0]
    for which in range(layers):
        m = conv_mom[which]
        size = jnp.sqrt(jnp.sum(m * m)) + 1e-07
        gram_c[which] = kdot(m, m, ((0,), (0,))) / (size * size)
    m = in_mom[...]
    size = jnp.sqrt(jnp.sum(m * m)) + 1e-07
    gram_s[0] = kdot(m, m, ((1,), (1,))) / (size * size)
    in_size = size
    m = head_mom[...]
    head_size = jnp.sqrt(jnp.sum(m * m)) + 1e-07
    gram_s[1] = kdot(m, m, ((1,), (1,))) / (head_size * head_size)

    def eye(n):
        return (lax.broadcasted_iota(jnp.int32, (n, n), 0) == lax.broadcasted_iota(jnp.int32, (n, n), 1)).astype(f32)

    for which in range(layers):
        poly_c[which] = eye(poly_c.shape[1])
    for which in range(2):
        poly_s[which] = eye(poly_s.shape[1])

    def step(grams, polys):
        n = grams.shape[1]
        count = grams.shape[0]
        a1 = [grams[i] for i in range(count)]
        a2 = [kdot(a, a) for a in a1]
        p = [newton_a * eye(n) + newton_b * x + newton_c * y for x, y in zip(a1, a2)]
        pa = [kdot(x, y) for x, y in zip(p, a1)]
        q = [kdot(x, polys[i]) for i, x in enumerate(p)]
        nxt = [kdot(x, y) for x, y in zip(pa, p)]
        for i in range(count):
            polys[i] = q[i]
            grams[i] = nxt[i]

    def body(_, carry):
        step(gram_c, poly_c)
        step(gram_s, poly_s)
        return carry

    lax.fori_loop(0, NS_STEPS, body, 0)
    for which in range(layers):
        m = conv_mom[which]
        size = jnp.sqrt(jnp.sum(m * m)) + 1e-07
        conv_q[which] = poly_c[which] / size
    in_q[...] = poly_s[0] / in_size * scale_in
    head_q[...] = poly_s[1] / head_size * scale_head


def muon_factors(conv_mom, in_mom, head_mom, scale_in, scale_head):
    layers, _, hid = conv_mom.shape
    small = 128
    in_pad = jnp.pad(in_mom, ((0, small - in_mom.shape[0]), (0, 0)))
    head_t = jnp.pad(head_mom.T, ((0, small - head_mom.shape[1]), (0, 0)))
    return pl.pallas_call(
        functools.partial(muon_kernel, scale_in, scale_head),
        out_shape=(
            jax.ShapeDtypeStruct((layers, hid, hid), f32),
            jax.ShapeDtypeStruct((small, small), f32),
            jax.ShapeDtypeStruct((small, small), f32),
        ),
        in_specs=[pl.BlockSpec(memory_space=pltpu.VMEM)] * 3,
        out_specs=(pl.BlockSpec(memory_space=pltpu.VMEM),) * 3,
        scratch_shapes=[
            pltpu.VMEM((layers, hid, hid), f32),
            pltpu.VMEM((layers, hid, hid), f32),
            pltpu.VMEM((2, small, small), f32),
            pltpu.VMEM((2, small, small), f32),
        ],
        compiler_params=pltpu.CompilerParams(vmem_limit_bytes=40 << 20),
        name="muon",
    )(conv_mom, in_pad, head_t)


def order_kernel(wide, to_ref, from_ref, w_ref, key_out, w_out, col_out, lo_out, hi_out):
    to, frm = to_ref[...], from_ref[...]
    key = (((to >> 8) * wide + (frm >> 8)) << 16) | ((to & 255) << 8) | (frm & 255)
    shape3 = (16, 8, LANES)
    key = key.astype(f32).reshape(shape3)
    w = w_ref[...].reshape(shape3)
    sub = lax.broadcasted_iota(jnp.int32, shape3, 1)
    lane = lax.broadcasted_iota(jnp.int32, shape3, 2)
    vreg = lax.broadcasted_iota(jnp.int32, shape3, 0)
    place = vreg + 16 * sub + 128 * lane
    for phase in range(14):
        for bit in range(phase, -1, -1):
            down = ((place >> (phase + 1)) & 1) == 1
            if bit < 4:
                view = (16 >> (bit + 1), 2, 1 << bit, 8, LANES)
                kv, wv = key.reshape(view), w.reshape(view)
                dv = down.astype(jnp.int32).reshape(view)[:, 0] == 1
                a, b, wa, wb = kv[:, 0], kv[:, 1], wv[:, 0], wv[:, 1]
                turn = jnp.logical_xor(a > b, dv)
                key = jnp.stack([jnp.where(turn, b, a), jnp.where(turn, a, b)], 1).reshape(shape3)
                w = jnp.stack([jnp.where(turn, wb, wa), jnp.where(turn, wa, wb)], 1).reshape(shape3)
            else:
                if bit < 7:
                    axis, gap, size, pos = 1, 1 << (bit - 4), 8, sub
                else:
                    axis, gap, size, pos = 2, 1 << (bit - 7), LANES, lane
                low = (pos & gap) == 0
                kp = jnp.where(low, pltpu.roll(key, size - gap, axis), pltpu.roll(key, gap, axis))
                wp = jnp.where(low, pltpu.roll(w, size - gap, axis), pltpu.roll(w, gap, axis))
                smaller = jnp.logical_xor(low, down)
                take = jnp.where(smaller, kp, key) < jnp.where(smaller, key, kp)
                key = jnp.where(take, kp, key)
                w = jnp.where(take, wp, w)
    flat = key.reshape(LANES, LANES)
    key_out[...] = flat.T.astype(jnp.int32)
    w_out[...] = w.reshape(LANES, LANES).T
    start = (lax.broadcasted_iota(jnp.int32, (8, LANES), 1).astype(f32) * 65536.0)[None]
    below = jnp.zeros(shape3, f32)
    upto = jnp.zeros(shape3, f32)
    for c in range(LANES):
        wide_key = jnp.broadcast_to(flat[:, c : c + 1], (LANES, LANES))
        col_out[c] = (wide_key - jnp.floor(wide_key * (1.0 / 256.0)) * 256.0).astype(bf16)
        wide_key = wide_key.reshape(shape3)
        below = below + jnp.where(wide_key < start, 1.0, 0.0)
        upto = upto + jnp.where(wide_key < start + 65536.0, 1.0, 0.0)
    n_below = jnp.sum(below.reshape(LANES, LANES), axis=0, keepdims=True)
    n_upto = jnp.sum(upto.reshape(LANES, LANES), axis=0, keepdims=True)
    first = jnp.floor(n_below * (1.0 / 128.0))
    end = jnp.floor((n_upto + 127.0) * (1.0 / 128.0))
    lo_out[...] = first.astype(jnp.int32)
    hi_out[...] = jnp.where(n_upto > n_below, end, first).astype(jnp.int32)


def order_edges(to, frm, w, wide):
    vmem = pl.BlockSpec(memory_space=pltpu.VMEM)
    return pl.pallas_call(
        functools.partial(order_kernel, wide),
        out_shape=(
            jax.ShapeDtypeStruct((LANES, LANES), jnp.int32),
            jax.ShapeDtypeStruct((LANES, LANES), f32),
            jax.ShapeDtypeStruct((LANES, LANES, LANES), bf16),
            jax.ShapeDtypeStruct((1, LANES), jnp.int32),
            jax.ShapeDtypeStruct((1, LANES), jnp.int32),
        ),
        in_specs=[vmem] * 3,
        out_specs=(vmem,) * 5,
        compiler_params=pltpu.CompilerParams(vmem_limit_bytes=40 << 20),
        name="order_edges",
    )(to.reshape(LANES, LANES), frm.reshape(LANES, LANES), w.reshape(LANES, LANES))


def fill_kernel(wide, rim, chunk, parts, lo, hi, rims, key_ref, w_ref, col_ref, *refs):
    outs, sums, acc, rowacc = refs[:parts], refs[parts], refs[parts + 1], refs[parts + 2]
    i = pl.program_id(0)
    pack = 16
    shape = (TILE // pack, pack, LANES)
    rows = lax.broadcasted_iota(jnp.int32, shape, 0) * pack + lax.broadcasted_iota(jnp.int32, shape, 1)
    rows = rows.astype(f32).astype(bf16)
    lanes = lax.broadcasted_iota(jnp.int32, (LANES, LANES), 1).astype(f32)
    lanes0, lanes1 = lanes.astype(bf16), (lanes + 128.0).astype(bf16)
    one, zero = jnp.ones((), bf16), jnp.zeros((), bf16)

    def spread(row):
        return jnp.broadcast_to(row, (pack, LANES)).astype(bf16)[None]

    rowacc[...] = jnp.zeros_like(rowacc)

    def tile(j, _):
        b = i * wide + j
        first, end = lo[0, b], hi[0, b]
        end = jnp.where(jnp.logical_and(j < rim, rims[0] == 0), first, end)
        end = jnp.where(jnp.logical_and(j >= wide - rim, rims[1] == 0), first, end)
        cols = pl.ds(pl.multiple_of(j * TILE, TILE), TILE)

        @pl.when(end <= first)
        def _():
            for out in outs:
                out[:, cols] = jnp.zeros((TILE, TILE), bf16)

        @pl.when(end > first)
        def _():
            def part(base, c):
                row = jnp.minimum(base + c, LANES - 1)
                here = key_ref[pl.ds(row, 1), :] - (b << 16)
                if c:
                    here = jnp.where(base + c < end, here, -1)
                at = rows == spread((here >> 8).astype(f32))
                rest = w_ref[pl.ds(row, 1), :]
                left = []
                for q in range(parts):
                    piece = rest.astype(bf16).astype(f32)
                    rest = rest - piece
                    left.append(jnp.where(at, spread(piece), zero).reshape(TILE, LANES))
                col = col_ref[row]
                right = jnp.concatenate(
                    [jnp.where(col == lanes0, one, zero), jnp.where(col == lanes1, one, zero)], 1
                )
                return left, right

            def get(base):
                made = [part(base, c) for c in range(chunk)]
                lhs = jnp.concatenate([m[0][q] for q in range(parts) for m in made], 1)
                rhs = jnp.concatenate([m[1] for m in made] * parts, 0)
                return jnp.dot(lhs, rhs, preferred_element_type=f32)

            acc[...] = get(first)

            def more(t, _):
                acc[...] += get(first + t * chunk)
                return 0

            lax.fori_loop(1, lax.div(end - first + chunk - 1, chunk), more, 0)
            rest = acc[...]
            rowacc[...] += rest[:, :LANES] + rest[:, LANES:]
            for out in outs:
                piece = rest.astype(bf16)
                out[:, cols] = piece
                rest = rest - piece.astype(f32)

        return 0

    lax.fori_loop(0, wide, tile, 0)
    sums[...] = jnp.broadcast_to(jnp.sum(rowacc[...], axis=1, keepdims=True), sums.shape)


def fill(order, rims, tiles, wide, rim, parts, chunk=4):
    key, w, col, lo, hi = order
    cols = wide * TILE
    return pl.pallas_call(
        functools.partial(fill_kernel, wide, rim, chunk, parts),
        out_shape=tuple(jax.ShapeDtypeStruct((tiles * TILE, cols), bf16) for _ in range(parts))
        + (jax.ShapeDtypeStruct((tiles * TILE, LANES), f32),),
        grid_spec=pltpu.PrefetchScalarGridSpec(
            num_scalar_prefetch=3,
            grid=(tiles,),
            in_specs=[pl.BlockSpec((LANES, LANES), lambda i, *_: (0, 0))] * 2
            + [pl.BlockSpec((LANES, LANES, LANES), lambda i, *_: (0, 0, 0))],
            out_specs=tuple(pl.BlockSpec((TILE, cols), lambda i, *_: (i, 0)) for _ in range(parts))
            + (pl.BlockSpec((TILE, LANES), lambda i, *_: (i, 0)),),
            scratch_shapes=[pltpu.VMEM((TILE, TILE), f32), pltpu.VMEM((TILE, LANES), f32)],
        ),
        compiler_params=pltpu.CompilerParams(vmem_limit_bytes=50 << 20),
        name="fill_tiles",
    )(lo, hi, rims, key, w, col)


def parts_of(x, count):
    found = []
    for q in range(count):
        piece = x.astype(bf16)
        found.append(piece)
        if q + 1 < count:
            x = x - piece.astype(f32)
    return found


def pair_list(count):
    return [(p, q) for p in range(count) for q in range(count) if p + q < count]


def dots(left, right, dims=((1,), (0,))):
    total = None
    for p, q in pair_list(len(left)):
        piece = lax.dot_general(left[p], right[q], (dims, ((), ())), preferred_element_type=f32)
        total = piece if total is None else total + piece
    return total


def start_stats(n, batch, block, src, held, send_sem, recv_sem):
    copies = []
    for k in range(1, n):
        copy = pltpu.make_async_remote_copy(
            src_ref=src,
            dst_ref=held.at[k],
            send_sem=send_sem.at[k],
            recv_sem=recv_sem.at[k],
            device_id=peer_place(batch, lax.rem(block + k, n)),
            device_id_type=pl.DeviceIdType.MESH,
        )
        copy.start()
        copies.append(copy)
    held[0] = src[...]
    return copies


def finish_stats(n, block, copies, held):
    for copy in copies:
        copy.wait()
    total = held[lax.rem(block, n)]
    for q in range(1, n):
        total = total + held[lax.rem(block + n - q, n)]
    return total


def rim_copy(batch, to, src, dst, sems, which):
    return pltpu.make_async_remote_copy(
        src_ref=src,
        dst_ref=dst,
        send_sem=sems[0].at[which],
        recv_sem=sems[1].at[which],
        device_id=peer_place(batch, to),
        device_id_type=pl.DeviceIdType.MESH,
    )


def load_adjacency(hbm, vmem, sem, height):
    copies = []
    steps = vmem[0].shape[0] // height
    for s in range(steps):
        here = pl.ds(s * height, height)
        copies.append(
            [
                pltpu.make_async_copy(src.at[here], dst.at[here], sem.at[s * len(hbm) + q])
                for q, (src, dst) in enumerate(zip(hbm, vmem))
            ]
        )
    for group in copies[:2]:
        for copy in group:
            copy.start()
    return copies


def next_rows(copies, s):
    for copy in copies[s]:
        copy.wait()
    if s + 2 < len(copies):
        for copy in copies[s + 2]:
            copy.start()


def column_sums(x):
    return jnp.sum(x, axis=0, keepdims=True)


def forward_kernel(n, normed, parts, nodes, height, x_ref, stat_ref, param_ref, w_ref, bias_ref, sums_ref, *refs):
    a_hbm, refs = refs[:parts], refs[parts:]
    out_ref, agg_ref, stat_out, affine_out = refs[:4]
    refs = refs[4:]
    a, refs = refs[:parts], refs[parts:]
    xs, refs = refs[:parts], refs[parts:]
    rim, held, a_sem, send_sem, recv_sem, rim_send, rim_recv = refs
    batch, block = my_place()
    rows, width = x_ref.shape
    halo = rim.shape[1]
    greet(n, batch, block)
    sems = (rim_send, rim_recv)
    up = rim_copy(batch, lax.rem(block + 1, n), x_ref.at[pl.ds(rows - halo, halo)], rim.at[0], sems, 0)
    down = rim_copy(batch, lax.rem(block + n - 1, n), x_ref.at[pl.ds(0, halo)], rim.at[1], sems, 1)
    first, last = block == 0, block == n - 1

    @pl.when(jnp.logical_not(last))
    def _():
        up.start()

    @pl.when(jnp.logical_not(first))
    def _():
        down.start()

    if normed:
        copies = start_stats(n, batch, block, stat_ref, held, send_sem, recv_sem)
    loads = load_adjacency(a_hbm, a, a_sem, height)

    @pl.when(first)
    def _():
        rim[0] = jnp.zeros((halo, width), f32)

    @pl.when(last)
    def _():
        rim[1] = jnp.zeros((halo, width), f32)

    step = 256
    for s in range(rows // step):
        here = pl.ds(s * step, step)
        for dst, piece in zip(xs, parts_of(x_ref[here, :], parts)):
            dst[pl.ds(halo + s * step, step), :] = piece
    own = pl.ds(halo, rows)
    for s in range(len(loads)):
        next_rows(loads, s)
        here = pl.ds(s * height, height)
        agg_ref[here, :] = dots([q[here, own] for q in a], [q[own, :] for q in xs])
    if normed:
        totals = finish_stats(n, block, copies, held) * (1.0 / nodes)
        mean = totals[0:1]
        inverse = lax.rsqrt(totals[1:2] - mean * mean + norm_epsilon)
        scale = param_ref[0:1] * inverse
        offset = param_ref[1:2] - mean * scale
        affine_out[0:1] = mean
        affine_out[1:2] = inverse
        affine_out[2:3] = scale
        affine_out[3:4] = offset
    else:
        affine_out[...] = jnp.zeros_like(affine_out)

    @pl.when(jnp.logical_not(first))
    def _():
        rim_copy(batch, block, rim.at[0], rim.at[0], sems, 0).wait_recv()

    @pl.when(jnp.logical_not(last))
    def _():
        rim_copy(batch, block, rim.at[1], rim.at[1], sems, 1).wait_recv()

    for dst, low, high in zip(xs, parts_of(rim[0], parts), parts_of(rim[1], parts)):
        dst[pl.ds(0, halo), :] = low
        dst[pl.ds(halo + rows, halo), :] = high
    stat_out[...] = jnp.zeros_like(stat_out)
    weights = parts_of(w_ref[...], 3)
    lower, upper = pl.ds(0, halo), pl.ds(halo + rows, halo)

    def finish(s, _):
        here = pl.ds(pl.multiple_of(s * step, step), step)
        agg = agg_ref[here, :]
        agg = agg + dots([q[here, lower] for q in a], [q[lower, :] for q in xs])
        agg = agg + dots([q[here, upper] for q in a], [q[upper, :] for q in xs])
        h = x_ref[here, :]
        if normed:
            row_sum = sums_ref[here, :]
            agg = agg * scale + jnp.concatenate([row_sum, row_sum], 1) * offset
            h = h * scale + offset
        agg_ref[here, :] = agg
        joined = jnp.concatenate([h, agg], 1)
        pre = dots(parts_of(joined, 3), weights) + bias_ref[...]
        active = jnp.maximum(pre, 0.0)
        out_ref[here, :] = active
        stat_out[0:1] += column_sums(active)
        stat_out[1:2] += column_sums(active * active)
        return 0

    lax.fori_loop(0, rows // step, finish, 0)

    @pl.when(jnp.logical_not(last))
    def _():
        up.wait_send()

    @pl.when(jnp.logical_not(first))
    def _():
        down.wait_send()


def forward_layer(n, normed, nodes, x, stats, params, w_parts, bias, sums, a, collective_id):
    rows, width = x.shape
    parts = len(a)
    cols = a[0].shape[1]
    halo = (cols - rows) // 2
    height = 256
    vmem = pl.BlockSpec(memory_space=pltpu.VMEM)
    steps = rows // height
    return pl.pallas_call(
        functools.partial(forward_kernel, n, normed, parts, nodes, height),
        out_shape=(
            jax.ShapeDtypeStruct((rows, width), f32),
            jax.ShapeDtypeStruct((rows, width), f32),
            jax.ShapeDtypeStruct((2, width), f32),
            jax.ShapeDtypeStruct((4, width), f32),
        ),
        in_specs=[vmem] * 6 + [pl.BlockSpec(memory_space=pl.ANY)] * parts,
        out_specs=(vmem,) * 4,
        scratch_shapes=[pltpu.VMEM((rows, cols), bf16) for _ in range(parts)]
        + [pltpu.VMEM((cols, width), bf16) for _ in range(parts)]
        + [
            pltpu.VMEM((2, halo, width), f32),
            pltpu.VMEM((n, 2, width), f32),
            pltpu.SemaphoreType.DMA((steps * parts,)),
            pltpu.SemaphoreType.DMA((n,)),
            pltpu.SemaphoreType.DMA((n,)),
            pltpu.SemaphoreType.DMA((2,)),
            pltpu.SemaphoreType.DMA((2,)),
        ],
        compiler_params=pltpu.CompilerParams(
            collective_id=collective_id, has_side_effects=True, vmem_limit_bytes=62 << 20
        ),
        name="forward_layer",
    )(x, stats, params, w_parts, bias, sums, *a)


def backward_kernel(n, below_normed, nodes, height, g_ref, stat_ref, affine_ref, gain_ref, act_ref, agg_ref, x_ref,
                    below_ref, wt_ref, a1_hbm, a2_hbm, out_ref, gw_ref, gb_ref, stat_out, a1, a2, g1, g2, b1, b2,
                    out_rim, rim, held, a_sem, send_sem, recv_sem, rim_send, rim_recv):
    batch, block = my_place()
    rows, width = g_ref.shape
    halo = rim.shape[1]
    a = (a1, a2)
    greet(n, batch, block)
    copies = start_stats(n, batch, block, stat_ref, held, send_sem, recv_sem)
    loads = load_adjacency((a1_hbm, a2_hbm), a, a_sem, height)
    first, last = block == 0, block == n - 1
    sems = (rim_send, rim_recv)
    mean, inverse = affine_ref[0:1], affine_ref[1:2]
    gain = gain_ref[...]
    totals = finish_stats(n, block, copies, held) * gain * (1.0 / nodes)
    gb_ref[...] = jnp.zeros_like(gb_ref)
    w_t = parts_of(wt_ref[...], 2)
    step = 256

    def enter(s, _):
        here = pl.ds(pl.multiple_of(s * step, step), step)
        act = act_ref[here, :]
        normed = (act - mean) * inverse
        grad = inverse * (g_ref[here, :] * gain - totals[0:1] - normed * totals[1:2])
        grad = jnp.where(act > 0.0, grad, 0.0)
        gb_ref[...] += column_sums(grad)
        pieces = parts_of(grad, 2)
        g1[here, :] = pieces[0]
        g2[here, :] = pieces[1]
        joined = dots(pieces, w_t)
        out_ref[here, :] = joined[:, :width]
        pieces = parts_of(joined[:, width:], 2)
        b1[here, :] = pieces[0]
        b2[here, :] = pieces[1]
        return 0

    lax.fori_loop(0, rows // step, enter, 0)
    for s in range(len(loads)):
        next_rows(loads, s)
    turned = ((0,), (0,))
    b = [b1[...], b2[...]]
    out_rim[0] = dots([q[:, pl.ds(0, halo)] for q in a], b, turned)
    down = rim_copy(batch, lax.rem(block + n - 1, n), out_rim.at[0], rim.at[0], sems, 0)
    up = rim_copy(batch, lax.rem(block + 1, n), out_rim.at[1], rim.at[1], sems, 1)

    @pl.when(jnp.logical_not(first))
    def _():
        down.start()

    out_rim[1] = dots([q[:, pl.ds(halo + rows, halo)] for q in a], b, turned)

    @pl.when(jnp.logical_not(last))
    def _():
        up.start()

    wide = 512

    def own(s, _):
        here = pl.ds(pl.multiple_of(s * wide, wide), wide)
        cols = pl.ds(pl.multiple_of(halo + s * wide, 128), wide)
        out_ref[here, :] += dots([q[:, cols] for q in a], b, turned)
        return 0

    lax.fori_loop(0, rows // wide, own, 0)
    gw_ref[...] = jnp.zeros_like(gw_ref)

    def weights(s, _):
        here = pl.ds(pl.multiple_of(s * wide, wide), wide)
        h = x_ref[here, :]
        if below_normed:
            h = h * below_ref[2:3] + below_ref[3:4]
        g = [g1[here, :], g2[here, :]]
        gw_ref[pl.ds(0, width), :] += dots(parts_of(h, 2), g, turned)
        gw_ref[pl.ds(width, width), :] += dots(parts_of(agg_ref[here, :], 2), g, turned)
        return 0

    lax.fori_loop(0, rows // wide, weights, 0)

    @pl.when(jnp.logical_not(last))
    def _():
        rim_copy(batch, block, rim.at[0], rim.at[0], sems, 0).wait_recv()
        out_ref[pl.ds(rows - halo, halo), :] += rim[0]

    @pl.when(jnp.logical_not(first))
    def _():
        rim_copy(batch, block, rim.at[1], rim.at[1], sems, 1).wait_recv()
        out_ref[pl.ds(0, halo), :] += rim[1]

    stat_out[...] = jnp.zeros_like(stat_out)

    def tail(s, _):
        here = pl.ds(pl.multiple_of(s * step, step), step)
        grad = out_ref[here, :]
        stat_out[0:1] += column_sums(grad)
        if below_normed:
            stat_out[1:2] += column_sums(grad * ((x_ref[here, :] - below_ref[0:1]) * below_ref[1:2]))
        return 0

    lax.fori_loop(0, rows // step, tail, 0)

    @pl.when(jnp.logical_not(first))
    def _():
        down.wait_send()

    @pl.when(jnp.logical_not(last))
    def _():
        up.wait_send()


def backward_layer(n, below_normed, nodes, g, stats, affine, gain, act, agg, x, below, w_t, a, collective_id):
    rows, width = x.shape
    cols = a[0].shape[1]
    halo = (cols - rows) // 2
    height = 512
    vmem = pl.BlockSpec(memory_space=pltpu.VMEM)
    steps = rows // height
    return pl.pallas_call(
        functools.partial(backward_kernel, n, below_normed, nodes, height),
        out_shape=(
            jax.ShapeDtypeStruct((rows, width), f32),
            jax.ShapeDtypeStruct((2 * width, width), f32),
            jax.ShapeDtypeStruct((1, width), f32),
            jax.ShapeDtypeStruct((2, width), f32),
        ),
        in_specs=[vmem] * 9 + [pl.BlockSpec(memory_space=pl.ANY)] * 2,
        out_specs=(vmem,) * 4,
        scratch_shapes=[pltpu.VMEM((rows, cols), bf16)] * 2
        + [pltpu.VMEM((rows, width), bf16)] * 4
        + [
            pltpu.VMEM((2, halo, width), f32),
            pltpu.VMEM((2, halo, width), f32),
            pltpu.VMEM((n, 2, width), f32),
            pltpu.SemaphoreType.DMA((steps * 2,)),
            pltpu.SemaphoreType.DMA((n,)),
            pltpu.SemaphoreType.DMA((n,)),
            pltpu.SemaphoreType.DMA((2,)),
            pltpu.SemaphoreType.DMA((2,)),
        ],
        compiler_params=pltpu.CompilerParams(
            collective_id=collective_id, has_side_effects=True, vmem_limit_bytes=62 << 20
        ),
        name="backward_layer",
    )(g, stats, affine, gain, act, agg, x, below, w_t, *a)


def adamw(param, grad, first, second, count):
    first = adam_first_decay * first + (1.0 - adam_first_decay) * grad
    second = adam_second_decay * second + (1.0 - adam_second_decay) * grad * grad
    first_hat = first / (1.0 - jnp.power(adam_first_decay, count))
    second_hat = second / (1.0 - jnp.power(adam_second_decay, count))
    param = param - adam_rate * (
        first_hat / (jnp.sqrt(second_hat) + adam_epsilon) + adam_shrink * param
    )
    return (param, first, second)


def per_device(
    n_batch,
    n_rows,
    features,
    edge_rows,
    edge_weight,
    halo_counts,
    labels,
    pair_rows,
    step,
    w_in,
    w_conv,
    w_head,
    biases,
    norm_params,
    head_bias,
    mom_in,
    mom_conv,
    mom_head,
    first_bias,
    first_norm,
    first_head,
    second_bias,
    second_norm,
    second_head,
):
    dims = (n_batch, n_rows)
    edge_rows, edge_weight, features, halo_counts, labels, pair_rows = (
        redeal(x, *dims) for x in (edge_rows, edge_weight, features, halo_counts, labels, pair_rows)
    )
    full_in, full_conv, full_head, full_mom_in, full_mom_conv, full_mom_head = (
        lax.all_gather(w_in, "batch", axis=1, tiled=True),
        lax.all_gather(w_conv, "batch", axis=1, tiled=True),
        lax.all_gather(w_head, "batch", axis=0, tiled=True),
        lax.all_gather(mom_in, "batch", axis=1, tiled=True),
        lax.all_gather(mom_conv, "batch", axis=1, tiled=True),
        lax.all_gather(mom_head, "batch", axis=0, tiled=True),
    )
    inputs = features[0]
    rows_dev = inputs.shape[0]
    halo_rows = rows_dev // 4
    layers = full_conv.shape[0]
    node_count = rows_dev * n_rows
    all_nodes = node_count * n_batch
    edges = edge_rows[0, 0]
    block = my_place()[1]
    wide = (rows_dev + 2 * halo_rows) // TILE
    rims = jnp.stack([(block > 0).astype(jnp.int32), (block < n_rows - 1).astype(jnp.int32)])
    order = order_edges(edges[0], edges[1], edge_weight[0, 0], wide)
    *adjacency, row_sums = fill(order, rims, rows_dev // TILE, wide, halo_rows // TILE, 3)
    w_turned = jnp.swapaxes(full_conv, 1, 2)
    x = product(inputs, full_in) + biases[0]
    xs, aggs, affines = [x], [], []
    stats = jnp.zeros((2, x.shape[1]), f32)
    for layer in range(layers):
        used = FORWARD_PARTS[min(layer, len(FORWARD_PARTS) - 1)]
        x, agg, stats, affine = forward_layer(
            n_rows,
            layer > 0,
            node_count,
            x,
            stats,
            norm_params[max(layer - 1, 0)],
            full_conv[layer],
            biases[layer + 1][None],
            row_sums,
            adjacency[:used],
            10 + (layer > 0) + 2 * used,
        )
        xs.append(x)
        aggs.append(agg)
        affines.append(affine)
    totals = group_sum(stats, n_rows) / node_count
    mean = totals[0]
    inverse = lax.rsqrt(totals[1] - mean * mean + norm_epsilon)
    normed = (x - mean) * inverse
    hidden = norm_params[layers - 1, 0] * normed + norm_params[layers - 1, 1]
    affines.append(jnp.stack([mean, inverse, mean, inverse]))
    logits = product(hidden, full_head) + head_bias
    log_total = jax.nn.logsumexp(logits, axis=1)
    classes = logits.shape[1]
    onehot = (labels[0][:, None] == jnp.arange(classes, dtype=jnp.int32)[None, :]).astype(f32)
    cross = jnp.sum(log_total) - jnp.sum(onehot * logits)
    picks = pair_rows[0, 0]
    sent = logits[picks]
    got = group_gather(sent, n_rows)
    received = got[lax.rem(block + n_rows - jnp.arange(n_rows, dtype=jnp.int32), n_rows)]
    gap = sent - received
    local_total = cross + pair_weight * jnp.sum(gap * gap)
    grad_logits = jnp.exp(logits - log_total[:, None]) - onehot
    grad_logits = grad_logits.at[picks].add(4.0 * pair_weight * gap)
    grad_logits = grad_logits / all_nodes
    grad_head = product3(hidden.T, grad_logits)
    grad_head_bias = jnp.sum(grad_logits, 0)
    grad_hidden = product3(grad_logits, full_head.T)
    conv_grads = [None] * layers
    bias_grads = [None] * layers
    norm_grads = [None] * layers
    stats = jnp.stack([jnp.sum(grad_hidden, 0), jnp.sum(grad_hidden * normed, 0)])
    for layer in reversed(range(layers)):
        norm_grads[layer] = stats[::-1]
        grad_hidden, conv_grads[layer], grad_bias, stats = backward_layer(
            n_rows,
            layer > 0,
            node_count,
            grad_hidden,
            stats,
            affines[layer + 1],
            norm_params[layer, 0][None],
            xs[layer + 1],
            aggs[layer],
            xs[layer],
            affines[layer],
            w_turned[layer],
            adjacency[:2],
            20 + (layer > 0),
        )
        bias_grads[layer] = grad_bias[0]
    grad_in = product3(inputs.T, grad_hidden)
    grad_biases = jnp.stack([stats[0]] + bias_grads)
    grad_norms = jnp.stack(norm_grads)
    grad_conv = jnp.stack(conv_grads)
    summed = lax.psum(
        (grad_in, grad_conv, grad_head, grad_biases, grad_norms, grad_head_bias, local_total),
        ("batch", "rows"),
    )
    small = (summed[3], summed[4], summed[5], summed[6])
    moment_in = muon_decay * full_mom_in + summed[0]
    moment_conv = muon_decay * full_mom_conv + summed[1]
    moment_head = muon_decay * full_mom_head + summed[2]
    scale_in = math.sqrt(max(1.0, full_in.shape[1] / full_in.shape[0]))
    scale_conv = math.sqrt(max(1.0, full_conv.shape[2] / full_conv.shape[1]))
    scale_head = math.sqrt(max(1.0, full_head.shape[1] / full_head.shape[0]))
    conv_q, in_q, head_q = muon_factors(moment_conv, moment_in, moment_head, scale_in, scale_head)
    at = lax.axis_index("batch")
    moment_in = lax.dynamic_slice_in_dim(moment_in, at * w_in.shape[1], w_in.shape[1], 1)
    moment_conv = lax.dynamic_slice_in_dim(moment_conv, at * w_conv.shape[1], w_conv.shape[1], 1)
    moment_head = lax.dynamic_slice_in_dim(moment_head, at * w_head.shape[0], w_head.shape[0], 0)
    feat, classes = w_in.shape[0], w_head.shape[1]
    turn_in = product(in_q[:feat, :feat], moment_in)
    turn_conv = jnp.einsum("lij,ljk->lik", moment_conv, conv_q, precision=highest)
    turn_head = product(moment_head, head_q[:classes, :classes])
    new_in = w_in - muon_rate * (turn_in + muon_shrink * w_in)
    new_conv = w_conv - muon_rate * (scale_conv * turn_conv + muon_shrink * w_conv)
    new_head = w_head - muon_rate * (turn_head + muon_shrink * w_head)
    count = step[0].astype(f32)
    new_bias, bias_first, bias_second = adamw(biases, small[0], first_bias, second_bias, count)
    new_norm, norm_first, norm_second = adamw(norm_params, small[1], first_norm, second_norm, count)
    new_hb, head_first, head_second = adamw(head_bias, small[2], first_head, second_head, count)
    loss = small[3] / all_nodes
    return (
        loss,
        new_in,
        new_conv,
        new_head,
        moment_in,
        moment_conv,
        moment_head,
        new_bias,
        new_norm,
        new_hb,
        bias_first,
        norm_first,
        head_first,
        bias_second,
        norm_second,
        head_second,
    )


def solution(mesh):
    in_specs = (
        P("batch", "rows", None),
        P("batch", "rows", None, None),
        P("batch", "rows", None),
        P("batch", "rows", None),
        P("batch", "rows"),
        P("batch", "rows", None, None),
        P(),
        P(None, "batch"),
        P(None, "batch", None),
        P("batch", None),
        P(),
        P(),
        P(),
        P(None, "batch"),
        P(None, "batch", None),
        P("batch", None),
        P(),
        P(),
        P(),
        P(),
        P(),
        P(),
    )
    out_specs = (
        P(),
        P(None, "batch"),
        P(None, "batch", None),
        P("batch", None),
        P(None, "batch"),
        P(None, "batch", None),
        P("batch", None),
        P(),
        P(),
        P(),
        P(),
        P(),
        P(),
        P(),
        P(),
        P(),
    )
    body = functools.partial(per_device, mesh.shape["batch"], mesh.shape["rows"])
    return jax.shard_map(body, mesh=mesh, in_specs=in_specs, out_specs=out_specs, check_vma=False)
```

```python
import functools
import math

import jax
import jax.numpy as jnp
from jax import lax
from jax.experimental import pallas as pl
from jax.experimental.pallas import tpu as pltpu
from jax.sharding import PartitionSpec as P

NS_STEPS = 5

f32 = jnp.float32
bf16 = jnp.bfloat16
LANES = 128
TILE = 256
highest = lax.Precision.HIGHEST
norm_epsilon = 1e-05
pair_weight = 0.05
newton_a = 3.4445
newton_b = -4.775
newton_c = 2.0315
muon_decay = 0.9
muon_rate = 0.5
muon_shrink = 0.01
adam_first_decay = 0.9
adam_second_decay = 0.999
adam_epsilon = 1e-08
adam_rate = 0.1
adam_shrink = 0.01


def swap(b, r):
    return 2 * (b // 2) + r % 2, 2 * (r // 2) + b % 2


def flat_pairs(n_batch, n_rows, move):
    pairs = []
    for b in range(n_batch):
        for r in range(n_rows):
            to = move(b, r)
            if to is not None:
                pairs.append((b * n_rows + r, to[0] * n_rows + to[1]))
    return pairs


def redeal(array, n_batch, n_rows):
    return lax.ppermute(array, ("batch", "rows"), flat_pairs(n_batch, n_rows, swap))


def peer_place(batch, block):
    two = jnp.int32(2)
    return (
        two * lax.div(batch, two) + lax.rem(block, two),
        two * lax.div(block, two) + lax.rem(batch, two),
    )


def my_place():
    return peer_place(lax.axis_index("batch"), lax.axis_index("rows"))


def order_kernel(wide, to_ref, from_ref, w_ref, key_out, w_out, col_out, lo_out, hi_out):
    to, frm = to_ref[...].astype(jnp.int32), from_ref[...].astype(jnp.int32)
    key = (((to >> 8) * wide + (frm >> 8)) << 16) | ((to & 255) << 8) | (frm & 255)
    shape3 = (16, 8, LANES)
    key = key.astype(f32).reshape(shape3)
    w = w_ref[...].reshape(shape3)
    sub = lax.broadcasted_iota(jnp.int32, shape3, 1)
    lane = lax.broadcasted_iota(jnp.int32, shape3, 2)
    vreg = lax.broadcasted_iota(jnp.int32, shape3, 0)
    place = vreg + 16 * sub + 128 * lane
    for phase in range(14):
        for bit in range(phase, -1, -1):
            down = ((place >> (phase + 1)) & 1) == 1
            if bit < 4:
                view = (16 >> (bit + 1), 2, 1 << bit, 8, LANES)
                kv, wv = key.reshape(view), w.reshape(view)
                dv = down.astype(jnp.int32).reshape(view)[:, 0] == 1
                a, b, wa, wb = kv[:, 0], kv[:, 1], wv[:, 0], wv[:, 1]
                turn = jnp.logical_xor(a > b, dv)
                key = jnp.stack([jnp.where(turn, b, a), jnp.where(turn, a, b)], 1).reshape(shape3)
                w = jnp.stack([jnp.where(turn, wb, wa), jnp.where(turn, wa, wb)], 1).reshape(shape3)
            else:
                if bit < 7:
                    axis, gap, size, pos = 1, 1 << (bit - 4), 8, sub
                else:
                    axis, gap, size, pos = 2, 1 << (bit - 7), LANES, lane
                low = (pos & gap) == 0
                kp = jnp.where(low, pltpu.roll(key, size - gap, axis), pltpu.roll(key, gap, axis))
                wp = jnp.where(low, pltpu.roll(w, size - gap, axis), pltpu.roll(w, gap, axis))
                smaller = jnp.logical_xor(low, down)
                take = jnp.where(smaller, kp, key) < jnp.where(smaller, key, kp)
                key = jnp.where(take, kp, key)
                w = jnp.where(take, wp, w)
    flat = key.reshape(LANES, LANES)
    key_out[...] = flat.T.astype(jnp.int32)
    w_out[...] = w.reshape(LANES, LANES).T
    start = (lax.broadcasted_iota(jnp.int32, (8, LANES), 1).astype(f32) * 65536.0)[None]
    below = jnp.zeros(shape3, f32)
    upto = jnp.zeros(shape3, f32)
    for c in range(LANES):
        wide_key = jnp.broadcast_to(flat[:, c : c + 1], (LANES, LANES))
        col_out[c] = (wide_key - jnp.floor(wide_key * (1.0 / 256.0)) * 256.0).astype(bf16)
        wide_key = wide_key.reshape(shape3)
        below = below + jnp.where(wide_key < start, 1.0, 0.0)
        upto = upto + jnp.where(wide_key < start + 65536.0, 1.0, 0.0)
    n_below = jnp.sum(below.reshape(LANES, LANES), axis=0, keepdims=True)
    n_upto = jnp.sum(upto.reshape(LANES, LANES), axis=0, keepdims=True)
    first = jnp.floor(n_below * (1.0 / 128.0))
    end = jnp.floor((n_upto + 127.0) * (1.0 / 128.0))
    lo_out[...] = first.astype(jnp.int32)
    hi_out[...] = jnp.where(n_upto > n_below, end, first).astype(jnp.int32)


def order_edges(to, frm, w, wide):
    vmem = pl.BlockSpec(memory_space=pltpu.VMEM)
    return pl.pallas_call(
        functools.partial(order_kernel, wide),
        out_shape=(
            jax.ShapeDtypeStruct((LANES, LANES), jnp.int32),
            jax.ShapeDtypeStruct((LANES, LANES), f32),
            jax.ShapeDtypeStruct((LANES, LANES, LANES), bf16),
            jax.ShapeDtypeStruct((1, LANES), jnp.int32),
            jax.ShapeDtypeStruct((1, LANES), jnp.int32),
        ),
        in_specs=[vmem] * 3,
        out_specs=(vmem,) * 5,
        compiler_params=pltpu.CompilerParams(vmem_limit_bytes=40 << 20),
        name="order_edges",
    )(to, frm, w)


def fill_kernel(wide, rim, chunk, parts, lo, hi, rims, key_ref, w_ref, col_ref, *refs):
    outs, sums, acc, rowacc = refs[:parts], refs[parts], refs[parts + 1], refs[parts + 2]
    i = pl.program_id(0)
    pack = 16
    shape = (TILE // pack, pack, LANES)
    rows = lax.broadcasted_iota(jnp.int32, shape, 0) * pack + lax.broadcasted_iota(jnp.int32, shape, 1)
    rows = rows.astype(f32).astype(bf16)
    lanes = lax.broadcasted_iota(jnp.int32, (LANES, LANES), 1).astype(f32)
    lanes0, lanes1 = lanes.astype(bf16), (lanes + 128.0).astype(bf16)
    one, zero = jnp.ones((), bf16), jnp.zeros((), bf16)

    def spread(row):
        return jnp.broadcast_to(row, (pack, LANES)).astype(bf16)[None]

    rowacc[...] = jnp.zeros_like(rowacc)

    def tile(j, _):
        b = i * wide + j
        first, end = lo[0, b], hi[0, b]
        end = jnp.where(jnp.logical_and(j < rim, rims[0] == 0), first, end)
        end = jnp.where(jnp.logical_and(j >= wide - rim, rims[1] == 0), first, end)
        slot = jnp.where(j < rim, wide - 2 * rim + j, jnp.where(j < wide - rim, j - rim, j))
        cols = pl.ds(pl.multiple_of(slot * TILE, TILE), TILE)

        @pl.when(end <= first)
        def _():
            for out in outs:
                out[:, cols] = jnp.zeros((TILE, TILE), bf16)

        @pl.when(end > first)
        def _():
            def part(base, c):
                row = jnp.minimum(base + c, LANES - 1)
                here = key_ref[pl.ds(row, 1), :] - (b << 16)
                if c:
                    here = jnp.where(base + c < end, here, -1)
                at = rows == spread((here >> 8).astype(f32))
                rest = w_ref[pl.ds(row, 1), :]
                left = []
                for q in range(parts):
                    piece = rest.astype(bf16).astype(f32)
                    rest = rest - piece
                    left.append(jnp.where(at, spread(piece), zero).reshape(TILE, LANES))
                col = col_ref[row]
                right = jnp.concatenate(
                    [jnp.where(col == lanes0, one, zero), jnp.where(col == lanes1, one, zero)], 1
                )
                return left, right

            def get(base):
                made = [part(base, c) for c in range(chunk)]
                lhs = jnp.concatenate([m[0][q] for q in range(parts) for m in made], 1)
                rhs = jnp.concatenate([m[1] for m in made] * parts, 0)
                return jnp.dot(lhs, rhs, preferred_element_type=f32)

            acc[...] = get(first)

            def more(t, _):
                acc[...] += get(first + t * chunk)
                return 0

            lax.fori_loop(1, lax.div(end - first + chunk - 1, chunk), more, 0)
            rest = acc[...]
            rowacc[...] += rest[:, :LANES] + rest[:, LANES:]
            for out in outs:
                piece = rest.astype(bf16)
                out[:, cols] = piece
                rest = rest - piece.astype(f32)

        return 0

    lax.fori_loop(0, wide, tile, 0)
    sums[...] = jnp.broadcast_to(jnp.sum(rowacc[...], axis=1, keepdims=True), sums.shape)


def fill(order, rims, tiles, wide, rim, parts, chunk=4):
    key, w, col, lo, hi = order
    cols = wide * TILE
    return pl.pallas_call(
        functools.partial(fill_kernel, wide, rim, chunk, parts),
        out_shape=tuple(jax.ShapeDtypeStruct((tiles * TILE, cols), bf16) for _ in range(parts))
        + (jax.ShapeDtypeStruct((tiles * TILE, LANES), f32),),
        grid_spec=pltpu.PrefetchScalarGridSpec(
            num_scalar_prefetch=3,
            grid=(tiles,),
            in_specs=[pl.BlockSpec((LANES, LANES), lambda i, *_: (0, 0))] * 2
            + [pl.BlockSpec((LANES, LANES, LANES), lambda i, *_: (0, 0, 0))],
            out_specs=tuple(pl.BlockSpec((TILE, cols), lambda i, *_: (i, 0)) for _ in range(parts))
            + (pl.BlockSpec((TILE, LANES), lambda i, *_: (i, 0)),),
            scratch_shapes=[pltpu.VMEM((TILE, TILE), f32), pltpu.VMEM((TILE, LANES), f32)],
        ),
        compiler_params=pltpu.CompilerParams(vmem_limit_bytes=50 << 20),
        name="fill_tiles",
    )(lo, hi, rims, key, w, col)


def parts_of(x, count):
    found = []
    for q in range(count):
        piece = x.astype(bf16)
        found.append(piece)
        if q + 1 < count:
            x = x - piece.astype(f32)
    return found


def pair_list(count):
    return [(p, q) for p in range(count) for q in range(count) if p + q < count]


def dots(left, right, dims=((1,), (0,))):
    total = None
    for p, q in pair_list(len(left)):
        piece = lax.dot_general(left[p], right[q], (dims, ((), ())), preferred_element_type=f32)
        total = piece if total is None else total + piece
    return total


def remote(src, dst, send, recv, to):
    return pltpu.make_async_remote_copy(
        src_ref=src,
        dst_ref=dst,
        send_sem=send,
        recv_sem=recv,
        device_id=to,
        device_id_type=pl.DeviceIdType.MESH,
    )


def column_sums(x):
    return jnp.sum(x, axis=0, keepdims=True)


def folded(x):
    return jnp.sum(x.reshape(x.shape[0] // 8, 8, x.shape[1]), axis=0)


TURNED = ((0,), (0,))
GATHERED = 3


def step_kernel(n, nb, layers, nodes, all_nodes, classes, rows_at, *refs):
    (x_ref, label_ref, sums_ref, bias_ref, norm_ref, head_bias_ref, pick_smem, pick_row, a1_hbm, a2_hbm) = refs[:10]
    own_in, own_conv, own_head, own_min, own_mconv, own_mhead = refs[10:16]
    pay, full_min, full_mconv, full_mhead = refs[16:20]
    (act, agg, a1, a2, p1, p2, g1, g2, gh, rim, out_rim, logit, sent, got, stat, held, w_in, w_conv, w_head,
     wt, a_sem, stat_send, stat_recv, rim_send, rim_recv, pair_send, pair_recv, w_send, w_recv, w_own) = refs[20:]
    rows, width = act.shape[1], act.shape[2]
    halo = rim.shape[2]
    a, ps, gs = (a1, a2), (p1, p2), (g1, g2)
    here_b, here_r = lax.axis_index("batch"), lax.axis_index("rows")
    batch, block = my_place()
    first, last = block == 0, block == n - 1
    not_first, not_last = jnp.logical_not(first), jnp.logical_not(last)

    barrier = pltpu.get_barrier_semaphore()
    for k in range(1, n):
        pl.semaphore_signal(
            barrier, inc=1, device_id=peer_place(batch, lax.rem(block + k, n)), device_id_type=pl.DeviceIdType.MESH
        )
    for k in range(1, nb):
        pl.semaphore_signal(
            barrier, inc=1, device_id=(lax.rem(here_b + k, nb), here_r), device_id_type=pl.DeviceIdType.MESH
        )
    height = 512
    loads = []
    for s in range(rows // height):
        span = pl.ds(s * height, height)
        loads.append(
            [pltpu.make_async_copy(src.at[span], dst.at[span], a_sem.at[2 * s + q]) for q, (src, dst) in enumerate(zip((a1_hbm, a2_hbm), a))]
        )
        for copy in loads[-1]:
            copy.start()
    pl.semaphore_wait(barrier, n - 1 + nb - 1)

    def gather(item, src, dst):
        span = src.shape[-2]
        lead = (slice(None),) * (len(src.shape) - 2)
        mine = dst.at[lead + (pl.ds(pl.multiple_of(here_b * span, 8), span),)]
        copies = [pltpu.make_async_copy(src, mine, w_own.at[item])]
        for k in range(1, nb):
            copies.append(remote(src, mine, w_send.at[item, k], w_recv.at[item, k], (lax.rem(here_b + k, nb), here_r)))
        for copy in copies:
            copy.start()
        return copies

    def arrived(copies):
        for copy in copies:
            copy.wait()

    in_copies = gather(0, own_in, w_in)
    conv_copies = [gather(2, own_conv.at[0], w_conv.at[0])]

    def stats_start(e):
        held[e, 0] = stat[e]
        copies = []
        for k in range(1, n):
            copy = remote(stat.at[e], held.at[e, k], stat_send.at[e, k], stat_recv.at[e, k], peer_place(batch, lax.rem(block + k, n)))
            copy.start()
            copies.append(copy)
        return copies

    def stats_finish(e, copies):
        arrived(copies)
        total = held[e, lax.rem(block, n)]
        for q in range(1, n):
            total = total + held[e, lax.rem(block + n - q, n)]
        return total

    def rims_of(e, low_src, high_src):
        slot = e % 2
        return (
            remote(low_src, rim.at[slot, 1], rim_send.at[e, 1], rim_recv.at[e, 1], peer_place(batch, lax.rem(block + n - 1, n))),
            remote(high_src, rim.at[slot, 0], rim_send.at[e, 0], rim_recv.at[e, 0], peer_place(batch, lax.rem(block + 1, n))),
        )

    def start_if(condition, copy):
        @pl.when(condition)
        def _():
            copy.start()

    def rims_sent(copies):
        @pl.when(not_first)
        def _():
            copies[0].wait_send()

        @pl.when(not_last)
        def _():
            copies[1].wait_send()

    tile = 256
    tiles = rows // tile

    def rows_of(s, size):
        return pl.ds(pl.multiple_of(s * size, size), size)

    arrived(in_copies)
    turned_in = parts_of(w_in[...].T, 3)

    def project(s, _):
        span = rows_of(s, tile)
        act[0, span] = dots(parts_of(x_ref[span, :], 3), turned_in) + bias_ref[0:1]
        return 0

    lax.fori_loop(0, tiles, project, 0)

    own_cols, rim_cols = pl.ds(0, rows), pl.ds(rows, 2 * halo)
    scales = []
    late = None
    for l in range(layers):
        copies = rims_of(l, act.at[l, pl.ds(0, halo)], act.at[l, pl.ds(rows - halo, halo)])
        start_if(not_first, copies[0])
        start_if(not_last, copies[1])
        if l:
            counted = stats_start(l - 1)

        def split(s, _):
            span = rows_of(s, tile)
            for dst, piece in zip(ps, parts_of(act[l, span], 2)):
                dst[span, :] = piece
            return 0

        lax.fori_loop(0, tiles, split, 0)

        def own(span):
            agg[l, span] = dots([q[span, own_cols] for q in a], [q[own_cols, :] for q in ps])

        if l == 0:
            for s in range(rows // height):
                for copy in loads[s]:
                    copy.wait()
                own(pl.ds(s * height, height))
            for q in range(1, layers):
                conv_copies.append(gather(1 + 1 + q, own_conv.at[q], w_conv.at[q]))
            head_copies = gather(1, own_head, w_head)
        else:
            lax.fori_loop(0, rows // height, lambda s, _: (own(rows_of(s, height)), 0)[1], 0)
        if l == 1:
            base = 2 + layers
            late = [gather(base, own_min, full_min), gather(base + 1, own_mhead, full_mhead), gather(base + 2, own_mconv, full_mconv)]
        if l:
            totals = stats_finish(l - 1, counted) * (1.0 / nodes)
            mean = totals[0:1]
            inverse = lax.rsqrt(totals[1:2] - mean * mean + norm_epsilon)
            scale = norm_ref[l - 1, 0:1] * inverse
            scales.append((mean, inverse, scale, norm_ref[l - 1, 1:2] - mean * scale))
        else:
            scales.append(None)

        for which, gone, copy_index in ((0, first, 0), (1, last, 1)):
            @pl.when(gone)
            def _():
                rim[l % 2, which] = jnp.zeros((halo, width), f32)

            @pl.when(jnp.logical_not(gone))
            def _():
                remote(rim.at[l % 2, which], rim.at[l % 2, which], rim_send.at[l, which], rim_recv.at[l, which],
                       peer_place(batch, lax.rem(block + 1, n))).wait_recv()

            for dst, piece in zip(ps, parts_of(rim[l % 2, which], 2)):
                dst[pl.ds(rows + which * halo, halo), :] = piece
        arrived(conv_copies[l])
        weights = parts_of(w_conv[l], 3)
        stat8 = (jnp.zeros((8, width), f32), jnp.zeros((8, width), f32))

        def finish(s, sums):
            span = rows_of(s, tile)
            found = agg[l, span] + dots([q[span, rim_cols] for q in a], [q[rim_cols, :] for q in ps])
            h = act[l, span]
            if l:
                _, _, scale, offset = scales[l]
                row_sum = sums_ref[span, :]
                found = found * scale + jnp.concatenate([row_sum] * (width // LANES), 1) * offset
                h = h * scale + offset
            agg[l, span] = found
            pre = dots(parts_of(jnp.concatenate([h, found], 1), 3), weights) + bias_ref[l + 1 : l + 2]
            active = jnp.maximum(pre, 0.0)
            act[l + 1, span] = active
            return sums[0] + folded(active), sums[1] + folded(active * active)

        sums = lax.fori_loop(0, tiles, finish, stat8)
        stat[l, 0:1] = column_sums(sums[0])
        stat[l, 1:2] = column_sums(sums[1])
        rims_sent(copies)

    counted = stats_start(layers - 1)
    arrived(head_copies)
    head_parts = parts_of(w_head[...], 3)
    head_turned = parts_of(w_head[...].T, 2)
    totals = stats_finish(layers - 1, counted) * (1.0 / nodes)
    mean = totals[0:1]
    inverse = lax.rsqrt(totals[1:2] - mean * mean + norm_epsilon)
    scale = norm_ref[layers - 1, 0:1] * inverse
    scales.append((mean, inverse, scale, norm_ref[layers - 1, 1:2] - mean * scale))

    def top(span):
        return act[layers, span] * scales[layers][2] + scales[layers][3]

    def classify(s, _):
        span = rows_of(s, tile)
        logit[span, :] = dots(parts_of(top(span), 3), head_parts) + head_bias_ref[...]
        return 0

    lax.fori_loop(0, tiles, classify, 0)
    per = pick_smem.shape[0] // n
    sent[...] = jnp.zeros_like(sent)
    for d in range(n):
        for k in range(per):
            sent[d, k : k + 1] = logit[pl.ds(pick_smem[d * per + k], 1), :]
    pair_copies = []
    for k in range(1, n):
        peer = lax.rem(block + k, n)
        copy = remote(sent.at[peer], got.at[k], pair_send.at[k], pair_recv.at[k], peer_place(batch, peer))
        copy.start()
        pair_copies.append(copy)
    got[0] = sent[block]
    lane = lax.broadcasted_iota(jnp.int32, (tile, LANES), 1)
    real = lane < classes

    def soften(s, loss):
        span = rows_of(s, tile)
        z = logit[span, :]
        top_z = jnp.max(jnp.where(real, z, -jnp.inf), axis=1, keepdims=True)
        e = jnp.where(real, jnp.exp(z - top_z), 0.0)
        total = jnp.sum(e, axis=1, keepdims=True)
        named = [
            jnp.broadcast_to(label_ref[pl.ds(s * (tile // LANES) + i, 1), :], (LANES, LANES)).T for i in range(tile // LANES)
        ]
        hot = jnp.logical_and(real, lane.astype(f32) == jnp.concatenate(named, 0))
        logit[span, :] = e / total - jnp.where(hot, 1.0, 0.0)
        part = jnp.where(lane == 0, top_z + jnp.log(total), 0.0) - jnp.where(hot, z, 0.0)
        return loss + folded(part)

    loss = lax.fori_loop(0, tiles, soften, jnp.zeros((8, LANES), f32))
    arrived(pair_copies)
    gaps = []
    for d in range(n):
        gaps.append(sent[d] - got[lax.rem(block + n - d, n)])
    gap = jnp.concatenate(gaps, 0)
    loss = loss + pair_weight * folded(gap * gap)
    spare = pick_row.shape[1] - gap.shape[0]
    if spare:
        gap = jnp.concatenate([gap, jnp.zeros((spare, LANES), f32)], 0)
    gap_parts = parts_of(gap * (4.0 * pair_weight), 3)
    at_head, at_small = rows_at[1], rows_at[2]
    small = layers + 1

    def finish_head(s, sums):
        span = rows_of(s, tile)
        spot = lax.broadcasted_iota(jnp.int32, (tile, pick_row.shape[1]), 0) + s * tile
        chosen = jnp.where(spot == pick_row[...], 1.0, 0.0).astype(bf16)
        add = None
        for piece in gap_parts:
            v = jnp.dot(chosen, piece, preferred_element_type=f32)
            add = v if add is None else add + v
        grad = (logit[span, :] + add) * (1.0 / all_nodes)
        grad_parts = parts_of(grad, 2)
        h = top(span)
        back = dots(grad_parts, head_turned)
        gh[span, :] = back
        normed = (act[layers, span] - scales[layers][0]) * scales[layers][1]
        return (
            sums[0] + dots(parts_of(h, 2), grad_parts, TURNED),
            sums[1] + folded(grad),
            sums[2] + folded(back),
            sums[3] + folded(back * normed),
        )

    begin = (
        jnp.zeros((width, LANES), f32),
        jnp.zeros((8, LANES), f32),
        jnp.zeros((8, width), f32),
        jnp.zeros((8, width), f32),
    )
    sums = lax.fori_loop(0, tiles, finish_head, begin)
    half = width // 2
    pay[pl.ds(at_head, half), :] = jnp.concatenate([sums[0][:half], sums[0][half:]], 1)
    tail = pl.ds(at_small, pay.shape[0] - at_small)
    pay[tail, :] = jnp.zeros((pay.shape[0] - at_small, width), f32)
    at_norm = at_small + small
    at_last = at_norm + 2 * layers
    pay[at_last : at_last + 1, 0:LANES] = column_sums(sums[1])
    pay[at_last + 1 : at_last + 2, 0:LANES] = column_sums(loss)
    e = layers
    stat[e, 0:1] = column_sums(sums[2])
    stat[e, 1:2] = column_sums(sums[3])
    counted = stats_start(e)

    def weight_grad(l):
        where = pl.ds(l * 2 * width, width)
        under = pl.ds(l * 2 * width + width, width)

        def weigh(s, sums):
            span = rows_of(s, height)
            h = act[l, span]
            if l:
                h = h * scales[l][2] + scales[l][3]
            grad = [q[span, :] for q in gs]
            pay[where, :] += dots(parts_of(h, 2), grad, TURNED)
            pay[under, :] += dots(parts_of(agg[l, span], 2), grad, TURNED)
            return sums

        pay[pl.ds(l * 2 * width, 2 * width), :] = jnp.zeros((2 * width, width), f32)
        lax.fori_loop(0, rows // height, weigh, 0)

    for l in range(layers - 1, -1, -1):
        e = layers + (layers - 1 - l)
        pay[at_norm + 2 * l : at_norm + 2 * l + 1, :] = stat[e, 1:2]
        pay[at_norm + 2 * l + 1 : at_norm + 2 * l + 2, :] = stat[e, 0:1]
        if l < layers - 1:
            weight_grad(l + 1)
        turned = w_conv[l].T
        for q, piece in enumerate(parts_of(turned, 2)):
            wt[q] = piece
        totals = stats_finish(e, counted) * norm_ref[l, 0:1] * (1.0 / nodes)
        mean, inverse, _, _ = scales[l + 1]
        gain = norm_ref[l, 0:1]

        def enter(s, total):
            span = rows_of(s, tile)
            active = act[l + 1, span]
            normed = (active - mean) * inverse
            grad = inverse * (gh[span, :] * gain - totals[0:1] - normed * totals[1:2])
            grad = jnp.where(active > 0.0, grad, 0.0)
            pieces = parts_of(grad, 2)
            for dst, piece in zip(gs, pieces):
                dst[span, :] = piece
            joined = dots(pieces, [wt[0], wt[1]])
            gh[span, :] = joined[:, :width]
            for dst, piece in zip(ps, parts_of(joined[:, width:], 2)):
                dst[span, :] = piece
            return total + folded(grad)

        total = lax.fori_loop(0, tiles, enter, jnp.zeros((8, width), f32))
        pay[at_small + 1 + l : at_small + 2 + l, :] = column_sums(total)
        right = [q[own_cols, :] for q in ps]
        copies = rims_of(e, out_rim.at[0], out_rim.at[1])
        for which, go in ((0, not_first), (1, not_last)):
            out_rim[which] = dots([q[:, pl.ds(rows + which * halo, halo)] for q in a], right, TURNED)
            start_if(go, copies[which])

        def spread_back(s, _):
            span = rows_of(s, height)
            gh[span, :] += dots([q[:, span] for q in a], right, TURNED)
            return 0

        lax.fori_loop(0, rows // height, spread_back, 0)
        slot = e % 2
        for which, go, start in ((1, not_last, rows - halo), (0, not_first, 0)):
            @pl.when(go)
            def _():
                remote(rim.at[slot, which], rim.at[slot, which], rim_send.at[e, which], rim_recv.at[e, which],
                       peer_place(batch, lax.rem(block + 1, n))).wait_recv()
                gh[pl.ds(start, halo), :] += rim[slot, which]

        def tail_sums(s, sums):
            span = rows_of(s, tile)
            grad = gh[span, :]
            second = sums[1]
            if l:
                second = second + folded(grad * ((act[l, span] - scales[l][0]) * scales[l][1]))
            return sums[0] + folded(grad), second

        sums = lax.fori_loop(0, tiles, tail_sums, (jnp.zeros((8, width), f32), jnp.zeros((8, width), f32)))
        if l:
            stat[e + 1, 0:1] = column_sums(sums[0])
            stat[e + 1, 1:2] = column_sums(sums[1])
            counted = stats_start(e + 1)
        else:
            pay[at_small : at_small + 1, :] = column_sums(sums[0])
        rims_sent(copies)
    weight_grad(0)
    feat = x_ref.shape[1]
    pay[pl.ds(rows_at[0], rows_at[1] - rows_at[0]), :] = jnp.zeros((rows_at[1] - rows_at[0], width), f32)

    def weigh_in(s, total):
        span = rows_of(s, height)
        return total + dots(parts_of(x_ref[span, :], 2), parts_of(gh[span, :], 2), TURNED)

    pay[pl.ds(rows_at[0], feat), :] = lax.fori_loop(0, rows // height, weigh_in, jnp.zeros((feat, width), f32))
    for copies in late:
        arrived(copies)


def step_call(n, nb, layers, nodes, all_nodes, classes, rows_at, pay_rows, x, labels, sums, biases, norms, head_bias,
              picks, pick_row, adjacency, shards):
    rows = x.shape[0]
    width = biases.shape[1]
    cols = adjacency[0].shape[1]
    halo = (cols - rows) // 2
    feat = x.shape[1]
    vmem = pl.BlockSpec(memory_space=pltpu.VMEM)
    smem = pl.BlockSpec(memory_space=pltpu.SMEM)
    hbm = pl.BlockSpec(memory_space=pl.ANY)
    dma = pltpu.SemaphoreType.DMA
    items = 2 + layers + 3
    exchanges = 2 * layers
    return pl.pallas_call(
        functools.partial(step_kernel, n, nb, layers, nodes, all_nodes, classes, rows_at),
        out_shape=(
            jax.ShapeDtypeStruct((pay_rows, width), f32),
            jax.ShapeDtypeStruct((width, feat), f32),
            jax.ShapeDtypeStruct((layers, 2 * width, width), f32),
            jax.ShapeDtypeStruct((width, LANES), f32),
        ),
        in_specs=[vmem] * 6 + [smem, vmem] + [hbm] * 8,
        out_specs=(vmem, hbm, hbm, hbm),
        scratch_shapes=[
            pltpu.VMEM((layers + 1, rows, width), f32),
            pltpu.VMEM((layers, rows, width), f32),
            pltpu.VMEM((rows, cols), bf16),
            pltpu.VMEM((rows, cols), bf16),
            pltpu.VMEM((cols, width), bf16),
            pltpu.VMEM((cols, width), bf16),
            pltpu.VMEM((rows, width), bf16),
            pltpu.VMEM((rows, width), bf16),
            pltpu.VMEM((rows, width), f32),
            pltpu.VMEM((2, 2, halo, width), f32),
            pltpu.VMEM((2, halo, width), f32),
            pltpu.VMEM((rows, LANES), f32),
            pltpu.VMEM((n, 8, LANES), f32),
            pltpu.VMEM((n, 8, LANES), f32),
            pltpu.VMEM((exchanges, 2, width), f32),
            pltpu.VMEM((exchanges, n, 2, width), f32),
            pltpu.VMEM((width, feat), f32),
            pltpu.VMEM((layers, 2 * width, width), f32),
            pltpu.VMEM((width, LANES), f32),
            pltpu.VMEM((2, width, 2 * width), bf16),
            dma((2 * rows // 512,)),
            dma((exchanges, n)),
            dma((exchanges, n)),
            dma((exchanges, 2)),
            dma((exchanges, 2)),
            dma((n,)),
            dma((n,)),
            dma((items, nb)),
            dma((items, nb)),
            dma((items,)),
        ],
        compiler_params=pltpu.CompilerParams(collective_id=1, has_side_effects=True, vmem_limit_bytes=63 << 20),
        name="forward_backward",
    )(x, labels, sums, biases, norms, head_bias, picks, pick_row, *adjacency, *shards)


def plane_split(nb, n):
    cores = 2 if nb % 2 == 0 else 1
    across = 1
    while across * across * 4 <= n and n % (across * 2) == 0:
        across *= 2
    return cores, nb // cores, across, n // across


def update_kernel(n, nb, layers, all_nodes, rows_at, classes, ns_parts, scales, pay, mom_in, mom_conv, mom_head, w_in, w_conv, w_head,
                  biases, norms, head_bias, fb, fn, fh, sb, sn, sh, power, *refs):
    (loss_o, in_o, conv_o, head_o, min_o, mconv_o, mhead_o, b_o, n_o, h_o, fb_o, fn_o, fh_o, sb_o, sn_o, sh_o) = refs[:16]
    (got1, sum1, got2, sum2, got3, full, gram, poly, small_gram, small_poly, mconv, send, recv) = refs[16:]
    cores, ys, xs, zs = plane_split(nb, n)
    planes = ys * xs
    here_b, here_r = lax.axis_index("batch"), lax.axis_index("rows")
    core, y = lax.rem(here_b, cores), lax.div(here_b, cores)
    x, z = lax.rem(here_r, xs), lax.div(here_r, xs)
    spot = y * xs + x
    width = w_conv.shape[2]

    def plane_peer(k):
        p = lax.rem(spot + k, planes)
        return p, (lax.div(p, xs) * cores + core, z * xs + lax.rem(p, xs))

    def column_peer(k):
        q = lax.rem(z + k, zs)
        return q, (here_b, q * xs + x)

    core_peer = (y * cores + lax.rem(core + 1, cores), here_r)
    barrier = pltpu.get_barrier_semaphore()
    peers = [plane_peer(k)[1] for k in range(1, planes)] + [column_peer(k)[1] for k in range(1, zs)]
    if cores == 2:
        peers.append(core_peer)
    for peer in peers:
        pl.semaphore_signal(barrier, inc=1, device_id=peer, device_id_type=pl.DeviceIdType.MESH)
    pl.semaphore_wait(barrier, len(peers))
    used = [0]

    def go(src, dst, to):
        i = used[0]
        used[0] += 1
        copy = remote(src, dst, send.at[i], recv.at[i], to)
        copy.start()
        return copy

    def settle(copies):
        for copy in copies:
            copy.wait()

    every = slice(None)
    if cores == 2:
        settle([go(pay.at[every, every, 1 - core], got1, core_peer)])
        sum1[...] = pay[every, every, core] + got1[...]
    else:
        sum1[...] = pay[every, every, 0]
    copies = []
    for k in range(1, planes):
        p, to = plane_peer(k)
        copies.append(go(sum1.at[every, p], got2.at[k], to))
    settle(copies)
    total = sum1[every, spot]
    for k in range(1, planes):
        total = total + got2[k]
    sum2[...] = total
    copies = []
    for k in range(1, zs):
        q, to = column_peer(k)
        copies.append(go(sum2.at[q], got3.at[k], to))
    settle(copies)
    total = sum2[z]
    for k in range(1, zs):
        total = total + got3[k]
    mine = full.at[z, spot, core]
    mine[...] = total
    settle([go(mine, mine, column_peer(k)[1]) for k in range(1, zs)])
    mine = full.at[every, spot, core]
    settle([go(mine, mine, plane_peer(k)[1]) for k in range(1, planes)])
    if cores == 2:
        mine = full.at[every, every, core]
        settle([go(mine, mine, core_peer)])
    summed = full[...].reshape(-1, width)

    def kdot(left, right, dims=((1,), (0,))):
        return dots(parts_of(left, ns_parts), parts_of(right, ns_parts), dims)

    def eye(k):
        return (lax.broadcasted_iota(jnp.int32, (k, k), 0) == lax.broadcasted_iota(jnp.int32, (k, k), 1)).astype(f32)

    sizes = []

    def begin(moment, grams, i):
        size = jnp.sqrt(jnp.sum(moment * moment)) + 1e-07
        g = kdot(moment, moment, TURNED) / (size * size)
        grams[i] = g
        sizes.append(size)

    for l in range(layers):
        mconv[l] = muon_decay * mom_conv[l] + summed[l * 2 * width : (l + 1) * 2 * width]
        begin(mconv[l], gram, l)
    feat = w_in.shape[1]
    half = width // 2
    grad_in = summed[rows_at[0] : rows_at[0] + LANES].T
    grad_head = summed[rows_at[1] : rows_at[1] + half]
    moment_in = muon_decay * mom_in[...] + jnp.where(lax.broadcasted_iota(jnp.int32, (width, LANES), 1) < feat, grad_in, 0.0)
    moment_head = muon_decay * mom_head[...] + jnp.concatenate([grad_head[:, :LANES], grad_head[:, LANES:]], 0)
    begin(moment_in, small_gram, 0)
    begin(moment_head, small_gram, 1)

    def step(grams, polys, which, early, late):
        k = grams.shape[1]
        count = len(which)
        a1 = [grams[i] for i in which]
        a2 = [kdot(v, v) for v in a1]
        p = [newton_a * eye(k) + newton_b * v + newton_c * u for v, u in zip(a1, a2)]
        if early:
            q = p
        else:
            q = [kdot(v, polys[i]) for i, v in zip(which, p)]
        if not late:
            pa = [kdot(v, u) for v, u in zip(p, a1)]
            nxt = [kdot(v, u) for v, u in zip(pa, p)]
        for j in range(count):
            polys[which[j]] = q[j]
            if not late:
                grams[which[j]] = nxt[j]

    convs = tuple(range(layers))

    def both(early, late):
        step(gram, poly, convs, early, late)
        step(small_gram, small_poly, (0, 1), early, late)

    both(True, False)
    lax.fori_loop(1, NS_STEPS - 1, lambda _, c: (both(False, False), c)[1], 0)
    both(False, True)
    scale_in, scale_conv, scale_head = scales
    span = w_conv.shape[1]
    for l in range(layers):
        part = mconv[l, pl.ds(pl.multiple_of(here_b * span, 8), span)]
        mconv_o[l] = part
        w = w_conv[l]
        turn = kdot(part, poly[l]) * (scale_conv / sizes[l])
        conv_o[l] = w - muon_rate * (turn + muon_shrink * w)
    span = w_in.shape[0]
    mconv[0, pl.ds(0, width), 0:LANES] = moment_in
    mconv[0, pl.ds(0, width), LANES : 2 * LANES] = moment_head
    part = mconv[0, pl.ds(pl.multiple_of(here_b * span, 8), span), 0:LANES]
    min_o[...] = part[:, :feat]
    w = w_in[...]
    turn = kdot(part, small_poly[0]) * (scale_in / sizes[layers])
    in_o[...] = w - muon_rate * (turn[:, :feat] + muon_shrink * w)
    span = w_head.shape[0]
    part = mconv[0, pl.ds(pl.multiple_of(here_b * span, 8), span), LANES : 2 * LANES]
    mhead_o[...] = part[:, :classes]
    w = w_head[...]
    turn = kdot(part, small_poly[1]) * (scale_head / sizes[layers + 1])
    head_o[...] = w - muon_rate * (turn[:, :classes] + muon_shrink * w)

    def adamw(param, grad, first, second, outs):
        first = adam_first_decay * first + (1.0 - adam_first_decay) * grad
        second = adam_second_decay * second + (1.0 - adam_second_decay) * grad * grad
        first_hat = first / power[0]
        second_hat = second / power[1]
        outs[0][...] = param - adam_rate * (first_hat / (jnp.sqrt(second_hat) + adam_epsilon) + adam_shrink * param)
        outs[1][...] = first
        outs[2][...] = second

    at = rows_at[2]
    adamw(biases[...], summed[at : at + layers + 1], fb[...], sb[...], (b_o, fb_o, sb_o))
    at = at + layers + 1
    adamw(norms[...], summed[at : at + 2 * layers], fn[...], sn[...], (n_o, fn_o, sn_o))
    at = at + 2 * layers
    adamw(head_bias[...], summed[at : at + 1, :classes], fh[...], sh[...], (h_o, fh_o, sh_o))
    loss_o[...] = jnp.sum(summed[at + 1 : at + 2], axis=1, keepdims=True) / all_nodes


def update_call(n, nb, layers, all_nodes, rows_at, classes, ns_parts, scales, pay, moments, shards, smalls, power):
    cores, ys, xs, zs = plane_split(nb, n)
    planes = ys * xs
    width = pay.shape[1]
    m = pay.shape[0] // (n * nb)
    pay = pay.reshape(zs, planes, cores, m, width)
    w_in, w_conv, w_head = shards
    vmem = pl.BlockSpec(memory_space=pltpu.VMEM)
    smem = pl.BlockSpec(memory_space=pltpu.SMEM)
    like = [jax.ShapeDtypeStruct(v.shape, f32) for v in (w_in, w_conv, w_head)]
    like_small = [jax.ShapeDtypeStruct(v.shape, f32) for v in smalls[:3]]
    copies = 2 * (planes + zs)
    return pl.pallas_call(
        functools.partial(update_kernel, n, nb, layers, all_nodes, rows_at, classes, ns_parts, scales),
        out_shape=tuple([jax.ShapeDtypeStruct((1, 1), f32)] + like + like + like_small * 3),
        in_specs=[vmem] * 16 + [smem],
        out_specs=(vmem,) * 16,
        scratch_shapes=[
            pltpu.VMEM((zs, planes, m, width), f32),
            pltpu.VMEM((zs, planes, m, width), f32),
            pltpu.VMEM((planes, zs, m, width), f32),
            pltpu.VMEM((zs, m, width), f32),
            pltpu.VMEM((zs, m, width), f32),
            pltpu.VMEM((zs, planes, cores, m, width), f32),
            pltpu.VMEM((layers, width, width), f32),
            pltpu.VMEM((layers, width, width), f32),
            pltpu.VMEM((2, LANES, LANES), f32),
            pltpu.VMEM((2, LANES, LANES), f32),
            pltpu.VMEM((layers, 2 * width, width), f32),
            pltpu.SemaphoreType.DMA((copies,)),
            pltpu.SemaphoreType.DMA((copies,)),
        ],
        compiler_params=pltpu.CompilerParams(collective_id=2, has_side_effects=True, vmem_limit_bytes=48 << 20),
        name="sum_and_update",
    )(pay, *moments, *shards, *smalls, power)


NS_PARTS = 3


def per_device(
    n_batch,
    n_rows,
    features,
    edge_rows,
    edge_weight,
    halo_counts,
    labels,
    pair_rows,
    step,
    w_in,
    w_conv,
    w_head,
    biases,
    norm_params,
    head_bias,
    mom_in,
    mom_conv,
    mom_head,
    first_bias,
    first_norm,
    first_head,
    second_bias,
    second_norm,
    second_head,
):
    rows_dev = features.shape[1]
    halo_rows = rows_dev // 4
    edge_count = edge_rows.shape[3]
    layers, hid = w_conv.shape[0], w_conv.shape[2]
    feat, classes = w_in.shape[0], w_head.shape[1]
    pairs = pair_rows.shape[3]
    node_count = rows_dev * n_rows
    all_nodes = node_count * n_batch
    flat = [
        edge_rows.reshape(2 * edge_count).astype(f32),
        edge_weight.reshape(edge_count),
        labels.reshape(rows_dev).astype(f32),
        pair_rows.reshape(n_rows * pairs).astype(f32),
    ]
    flat = jnp.concatenate(flat)
    flat = jnp.pad(flat, (0, -flat.shape[0] % (8 * LANES))).reshape(-1, LANES)
    flat = redeal(flat, n_batch, n_rows)
    inputs = redeal(features, n_batch, n_rows)[0]
    e = edge_count // LANES
    block = my_place()[1]
    wide = (rows_dev + 2 * halo_rows) // TILE
    rims = jnp.stack([(block > 0).astype(jnp.int32), (block < n_rows - 1).astype(jnp.int32)])
    order = order_edges(flat[:e], flat[e : 2 * e], flat[2 * e : 3 * e], wide)
    *adjacency, row_sums = fill(order, rims, rows_dev // TILE, wide, halo_rows // TILE, 2)
    label_rows = rows_dev // LANES
    node_labels = flat[3 * e : 3 * e + label_rows]
    picks = flat[3 * e + label_rows :].reshape(-1)[: n_rows * pairs].astype(jnp.int32)
    spread = jnp.pad(picks.reshape(n_rows, pairs), ((0, 0), (0, 8 - pairs)), constant_values=-1).reshape(1, n_rows * 8)
    spread = jnp.pad(spread, ((0, 0), (0, -spread.shape[1] % LANES)), constant_values=-1)
    at_in = layers * 2 * hid
    at_head = at_in + -(-feat // 8) * 8
    at_small = at_head + hid // 2
    used = at_small + layers + 1 + 2 * layers + 2
    unit = 8 * n_rows * n_batch
    pay_rows = -(-used // unit) * unit
    rows_at = (at_in, at_head, at_small)
    turned = [
        w_in.T,
        w_conv,
        jnp.pad(w_head, ((0, 0), (0, LANES - classes))),
        mom_in.T,
        mom_conv,
        jnp.pad(mom_head, ((0, 0), (0, LANES - classes))),
    ]
    pay, full_min, full_mconv, full_mhead = step_call(
        n_rows,
        n_batch,
        layers,
        node_count,
        all_nodes,
        classes,
        rows_at,
        pay_rows,
        inputs,
        node_labels,
        row_sums,
        biases,
        norm_params,
        jnp.pad(head_bias, (0, LANES - classes))[None],
        picks,
        spread,
        adjacency,
        turned,
    )
    count = step[0].astype(f32)
    power = jnp.stack([1.0 - jnp.power(adam_first_decay, count), 1.0 - jnp.power(adam_second_decay, count)])
    scales = (
        math.sqrt(max(1.0, hid / feat)),
        math.sqrt(max(1.0, hid / (2 * hid))),
        math.sqrt(max(1.0, classes / hid)),
    )
    norm_rows = (2 * layers, hid)
    smalls = (
        biases,
        norm_params.reshape(norm_rows),
        head_bias[None],
        first_bias,
        first_norm.reshape(norm_rows),
        first_head[None],
        second_bias,
        second_norm.reshape(norm_rows),
        second_head[None],
    )
    outs = update_call(
        n_rows,
        n_batch,
        layers,
        all_nodes,
        rows_at,
        classes,
        NS_PARTS,
        scales,
        pay,
        (jnp.pad(full_min, ((0, 0), (0, LANES - feat))), full_mconv, full_mhead),
        (turned[0], w_conv, w_head),
        smalls,
        power,
    )
    loss, new_in, new_conv, new_head, moment_in, moment_conv, moment_head = outs[:7]
    rest = []
    for i in range(0, 9, 3):
        rest += [outs[7 + i], outs[8 + i].reshape(layers, 2, hid), outs[9 + i][0]]
    return (loss[0, 0], new_in.T, new_conv, new_head, moment_in.T, moment_conv, moment_head, *rest)


def solution(mesh):
    in_specs = (
        P("batch", "rows", None),
        P("batch", "rows", None, None),
        P("batch", "rows", None),
        P("batch", "rows", None),
        P("batch", "rows"),
        P("batch", "rows", None, None),
        P(),
        P(None, "batch"),
        P(None, "batch", None),
        P("batch", None),
        P(),
        P(),
        P(),
        P(None, "batch"),
        P(None, "batch", None),
        P("batch", None),
        P(),
        P(),
        P(),
        P(),
        P(),
        P(),
    )
    out_specs = (
        P(),
        P(None, "batch"),
        P(None, "batch", None),
        P("batch", None),
        P(None, "batch"),
        P(None, "batch", None),
        P("batch", None),
        P(),
        P(),
        P(),
        P(),
        P(),
        P(),
        P(),
        P(),
        P(),
    )
    body = functools.partial(per_device, mesh.shape["batch"], mesh.shape["rows"])
    return jax.shard_map(body, mesh=mesh, in_specs=in_specs, out_specs=out_specs, check_vma=False)
```

```python
import functools
import math

import jax
import jax.numpy as jnp
from jax import lax
from jax.experimental import pallas as pl
from jax.experimental.pallas import tpu as pltpu
from jax.sharding import PartitionSpec as P

NS_STEPS = 5

f32 = jnp.float32
bf16 = jnp.bfloat16
LANES = 128
TILE = 256
highest = lax.Precision.HIGHEST
norm_epsilon = 1e-05
pair_weight = 0.05
newton_a = 3.4445
newton_b = -4.775
newton_c = 2.0315
muon_decay = 0.9
muon_rate = 0.5
muon_shrink = 0.01
adam_first_decay = 0.9
adam_second_decay = 0.999
adam_epsilon = 1e-08
adam_rate = 0.1
adam_shrink = 0.01


def swap(b, r):
    return 2 * (b // 2) + r % 2, 2 * (r // 2) + b % 2


def flat_pairs(n_batch, n_rows, move):
    pairs = []
    for b in range(n_batch):
        for r in range(n_rows):
            to = move(b, r)
            if to is not None:
                pairs.append((b * n_rows + r, to[0] * n_rows + to[1]))
    return pairs


def redeal(array, n_batch, n_rows):
    return lax.ppermute(array, ("batch", "rows"), flat_pairs(n_batch, n_rows, swap))


def peer_place(batch, block):
    two = jnp.int32(2)
    return (
        two * lax.div(batch, two) + lax.rem(block, two),
        two * lax.div(block, two) + lax.rem(batch, two),
    )


def my_place():
    return peer_place(lax.axis_index("batch"), lax.axis_index("rows"))


def order_kernel(wide, to_ref, from_ref, w_ref, key_out, w_out, col_out, lo_out, hi_out):
    to, frm = to_ref[...].astype(jnp.int32), from_ref[...].astype(jnp.int32)
    key = (((to >> 8) * wide + (frm >> 8)) << 16) | ((to & 255) << 8) | (frm & 255)
    shape3 = (16, 8, LANES)
    key = key.astype(f32).reshape(shape3)
    w = w_ref[...].reshape(shape3)
    sub = lax.broadcasted_iota(jnp.int32, shape3, 1)
    lane = lax.broadcasted_iota(jnp.int32, shape3, 2)
    vreg = lax.broadcasted_iota(jnp.int32, shape3, 0)
    place = vreg + 16 * sub + 128 * lane
    for phase in range(14):
        for bit in range(phase, -1, -1):
            down = ((place >> (phase + 1)) & 1) == 1
            if bit < 4:
                view = (16 >> (bit + 1), 2, 1 << bit, 8, LANES)
                kv, wv = key.reshape(view), w.reshape(view)
                dv = down.astype(jnp.int32).reshape(view)[:, 0] == 1
                a, b, wa, wb = kv[:, 0], kv[:, 1], wv[:, 0], wv[:, 1]
                turn = jnp.logical_xor(a > b, dv)
                key = jnp.stack([jnp.where(turn, b, a), jnp.where(turn, a, b)], 1).reshape(shape3)
                w = jnp.stack([jnp.where(turn, wb, wa), jnp.where(turn, wa, wb)], 1).reshape(shape3)
            else:
                if bit < 7:
                    axis, gap, size, pos = 1, 1 << (bit - 4), 8, sub
                else:
                    axis, gap, size, pos = 2, 1 << (bit - 7), LANES, lane
                low = (pos & gap) == 0
                kp = jnp.where(low, pltpu.roll(key, size - gap, axis), pltpu.roll(key, gap, axis))
                wp = jnp.where(low, pltpu.roll(w, size - gap, axis), pltpu.roll(w, gap, axis))
                smaller = jnp.logical_xor(low, down)
                take = jnp.where(smaller, kp, key) < jnp.where(smaller, key, kp)
                key = jnp.where(take, kp, key)
                w = jnp.where(take, wp, w)
    flat = key.reshape(LANES, LANES)
    key_out[...] = flat.T.astype(jnp.int32)
    w_out[...] = w.reshape(LANES, LANES).T
    start = (lax.broadcasted_iota(jnp.int32, (8, LANES), 1).astype(f32) * 65536.0)[None]
    below = jnp.zeros(shape3, f32)
    upto = jnp.zeros(shape3, f32)
    for c in range(LANES):
        wide_key = jnp.broadcast_to(flat[:, c : c + 1], (LANES, LANES))
        col_out[c] = (wide_key - jnp.floor(wide_key * (1.0 / 256.0)) * 256.0).astype(bf16)
        wide_key = wide_key.reshape(shape3)
        below = below + jnp.where(wide_key < start, 1.0, 0.0)
        upto = upto + jnp.where(wide_key < start + 65536.0, 1.0, 0.0)
    n_below = jnp.sum(below.reshape(LANES, LANES), axis=0, keepdims=True)
    n_upto = jnp.sum(upto.reshape(LANES, LANES), axis=0, keepdims=True)
    first = jnp.floor(n_below * (1.0 / 128.0))
    end = jnp.floor((n_upto + 127.0) * (1.0 / 128.0))
    lo_out[...] = first.astype(jnp.int32)
    hi_out[...] = jnp.where(n_upto > n_below, end, first).astype(jnp.int32)


def order_edges(to, frm, w, wide):
    vmem = pl.BlockSpec(memory_space=pltpu.VMEM)
    return pl.pallas_call(
        functools.partial(order_kernel, wide),
        out_shape=(
            jax.ShapeDtypeStruct((LANES, LANES), jnp.int32),
            jax.ShapeDtypeStruct((LANES, LANES), f32),
            jax.ShapeDtypeStruct((LANES, LANES, LANES), bf16),
            jax.ShapeDtypeStruct((1, LANES), jnp.int32),
            jax.ShapeDtypeStruct((1, LANES), jnp.int32),
        ),
        in_specs=[vmem] * 3,
        out_specs=(vmem,) * 5,
        compiler_params=pltpu.CompilerParams(vmem_limit_bytes=40 << 20),
        name="order_edges",
    )(to, frm, w)


def fill_kernel(wide, rim, chunk, parts, lo, hi, rims, key_ref, w_ref, col_ref, *refs):
    outs, sums, acc, rowacc = refs[:parts], refs[parts], refs[parts + 1], refs[parts + 2]
    i = pl.program_id(0)
    pack = 16
    shape = (TILE // pack, pack, LANES)
    rows = lax.broadcasted_iota(jnp.int32, shape, 0) * pack + lax.broadcasted_iota(jnp.int32, shape, 1)
    rows = rows.astype(f32).astype(bf16)
    lanes = lax.broadcasted_iota(jnp.int32, (LANES, LANES), 1).astype(f32)
    lanes0, lanes1 = lanes.astype(bf16), (lanes + 128.0).astype(bf16)
    one, zero = jnp.ones((), bf16), jnp.zeros((), bf16)

    def spread(row):
        return jnp.broadcast_to(row, (pack, LANES)).astype(bf16)[None]

    rowacc[...] = jnp.zeros_like(rowacc)

    def tile(j, _):
        b = i * wide + j
        first, end = lo[0, b], hi[0, b]
        end = jnp.where(jnp.logical_and(j < rim, rims[0] == 0), first, end)
        end = jnp.where(jnp.logical_and(j >= wide - rim, rims[1] == 0), first, end)
        slot = jnp.where(j < rim, wide - 2 * rim + j, jnp.where(j < wide - rim, j - rim, j))
        cols = pl.ds(pl.multiple_of(slot * TILE, TILE), TILE)

        @pl.when(end <= first)
        def _():
            for out in outs:
                out[:, cols] = jnp.zeros((TILE, TILE), bf16)

        @pl.when(end > first)
        def _():
            def part(base, c):
                row = jnp.minimum(base + c, LANES - 1)
                here = key_ref[pl.ds(row, 1), :] - (b << 16)
                if c:
                    here = jnp.where(base + c < end, here, -1)
                at = rows == spread((here >> 8).astype(f32))
                rest = w_ref[pl.ds(row, 1), :]
                left = []
                for q in range(parts):
                    piece = rest.astype(bf16).astype(f32)
                    rest = rest - piece
                    left.append(jnp.where(at, spread(piece), zero).reshape(TILE, LANES))
                col = col_ref[row]
                right = jnp.concatenate(
                    [jnp.where(col == lanes0, one, zero), jnp.where(col == lanes1, one, zero)], 1
                )
                return left, right

            def get(base):
                made = [part(base, c) for c in range(chunk)]
                lhs = jnp.concatenate([m[0][q] for q in range(parts) for m in made], 1)
                rhs = jnp.concatenate([m[1] for m in made] * parts, 0)
                return jnp.dot(lhs, rhs, preferred_element_type=f32)

            acc[...] = get(first)

            def more(t, _):
                acc[...] += get(first + t * chunk)
                return 0

            lax.fori_loop(1, lax.div(end - first + chunk - 1, chunk), more, 0)
            rest = acc[...]
            rowacc[...] += rest[:, :LANES] + rest[:, LANES:]
            for out in outs:
                piece = rest.astype(bf16)
                out[:, cols] = piece
                rest = rest - piece.astype(f32)

        return 0

    lax.fori_loop(0, wide, tile, 0)
    total = jnp.sum(rowacc[...], axis=1, keepdims=True)
    for half in range(TILE // LANES):
        column = jnp.broadcast_to(total[half * LANES : (half + 1) * LANES], (LANES, LANES))
        sums[0, half : half + 1] = column.T[0:1]


def fill(order, rims, tiles, wide, rim, parts, chunk=4):
    key, w, col, lo, hi = order
    cols = wide * TILE
    return pl.pallas_call(
        functools.partial(fill_kernel, wide, rim, chunk, parts),
        out_shape=tuple(jax.ShapeDtypeStruct((tiles * TILE, cols), bf16) for _ in range(parts))
        + (jax.ShapeDtypeStruct((tiles, TILE // LANES, LANES), f32),),
        grid_spec=pltpu.PrefetchScalarGridSpec(
            num_scalar_prefetch=3,
            grid=(tiles,),
            in_specs=[pl.BlockSpec((LANES, LANES), lambda i, *_: (0, 0))] * 2
            + [pl.BlockSpec((LANES, LANES, LANES), lambda i, *_: (0, 0, 0))],
            out_specs=tuple(pl.BlockSpec((TILE, cols), lambda i, *_: (i, 0)) for _ in range(parts))
            + (pl.BlockSpec((1, TILE // LANES, LANES), lambda i, *_: (i, 0, 0)),),
            scratch_shapes=[pltpu.VMEM((TILE, TILE), f32), pltpu.VMEM((TILE, LANES), f32)],
        ),
        compiler_params=pltpu.CompilerParams(vmem_limit_bytes=50 << 20),
        name="fill_tiles",
    )(lo, hi, rims, key, w, col)


def parts_of(x, count):
    found = []
    for q in range(count):
        piece = x.astype(bf16)
        found.append(piece)
        if q + 1 < count:
            x = x - piece.astype(f32)
    return found


def pair_list(count):
    return [(p, q) for p in range(count) for q in range(count) if p + q < count]


def dots(left, right, dims=((1,), (0,))):
    total = None
    for p, q in pair_list(len(left)):
        piece = lax.dot_general(left[p], right[q], (dims, ((), ())), preferred_element_type=f32)
        total = piece if total is None else total + piece
    return total


def remote(src, dst, send, recv, to):
    return pltpu.make_async_remote_copy(
        src_ref=src,
        dst_ref=dst,
        send_sem=send,
        recv_sem=recv,
        device_id=to,
        device_id_type=pl.DeviceIdType.MESH,
    )


def column_sums(x):
    return jnp.sum(x, axis=0, keepdims=True)


def folded(x):
    return jnp.sum(x.reshape(x.shape[0] // 8, 8, x.shape[1]), axis=0)


def plane_split(nb, n):
    cores = 2 if nb % 2 == 0 else 1
    across = 1
    while across * across * 4 <= n and n % (across * 2) == 0:
        across *= 2
    return cores, nb // cores, across, n // across


class Places:
    def __init__(self, n, nb):
        self.cores, ys, self.xs, self.zs = plane_split(nb, n)
        self.planes = ys * self.xs
        self.b, self.r = lax.axis_index("batch"), lax.axis_index("rows")
        self.core, y = lax.rem(self.b, self.cores), lax.div(self.b, self.cores)
        self.x, self.z = lax.rem(self.r, self.xs), lax.div(self.r, self.xs)
        self.spot = y * self.xs + self.x
        self.core_peer = (y * self.cores + lax.rem(self.core + 1, self.cores), self.r)
        self.peers = [self.plane_peer(k)[1] for k in range(1, self.planes)]
        self.peers += [self.column_peer(k)[1] for k in range(1, self.zs)]
        if self.cores == 2:
            self.peers.append(self.core_peer)

    def plane_peer(self, k):
        p = lax.rem(self.spot + k, self.planes)
        return p, (lax.div(p, self.xs) * self.cores + self.core, self.z * self.xs + lax.rem(p, self.xs))

    def column_peer(self, k):
        q = lax.rem(self.z + k, self.zs)
        return q, (self.b, q * self.xs + self.x)


TURNED = ((0,), (0,))
GATHERED = 3


def step_kernel(n, nb, layers, nodes, all_nodes, classes, rows_at, *refs):
    (x_ref, label_ref, sums_ref, bias_ref, norm_ref, head_bias_ref, pick_smem, pick_row, a1_hbm, a2_hbm) = refs[:10]
    own_in, own_conv, own_head, own_min, own_mconv, own_mhead = refs[10:16]
    pay, done, full_min, full_mconv, full_mhead = refs[16:21]
    (act, agg, a1, a2, p1, p2, g1, g2, gh, rim, out_rim, logit, sent, got, stat, held, w_in, w_conv, w_head,
     wt, a_sem, stat_send, stat_recv, rim_send, rim_recv, pair_send, pair_recv, w_send, w_recv, w_own, sum_send, sum_recv,
     ready) = refs[21:]
    rows, width = act.shape[1], act.shape[2]
    halo = rim.shape[2]
    a, ps, gs = (a1, a2), (p1, p2), (g1, g2)
    here_b, here_r = lax.axis_index("batch"), lax.axis_index("rows")
    batch, block = my_place()
    first, last = block == 0, block == n - 1
    not_first, not_last = jnp.logical_not(first), jnp.logical_not(last)

    barrier = pltpu.get_barrier_semaphore()
    for k in range(1, n):
        pl.semaphore_signal(
            barrier, inc=1, device_id=peer_place(batch, lax.rem(block + k, n)), device_id_type=pl.DeviceIdType.MESH
        )
    for k in range(1, nb):
        pl.semaphore_signal(
            barrier, inc=1, device_id=(lax.rem(here_b + k, nb), here_r), device_id_type=pl.DeviceIdType.MESH
        )
    places = Places(n, nb)
    for peer in places.peers:
        pl.semaphore_signal(barrier, inc=1, device_id=peer, device_id_type=pl.DeviceIdType.MESH)
    height = 512
    loads = []
    for s in range(rows // height):
        span = pl.ds(s * height, height)
        loads.append(
            [pltpu.make_async_copy(src.at[span], dst.at[span], a_sem.at[2 * s + q]) for q, (src, dst) in enumerate(zip((a1_hbm, a2_hbm), a))]
        )
        for copy in loads[-1]:
            copy.start()
    pl.semaphore_wait(barrier, n - 1 + nb - 1 + len(places.peers))

    def gather(item, src, dst):
        span = src.shape[-2]
        lead = (slice(None),) * (len(src.shape) - 2)
        mine = dst.at[lead + (pl.ds(pl.multiple_of(here_b * span, 8), span),)]
        copies = [pltpu.make_async_copy(src, mine, w_own.at[item])]
        for k in range(1, nb):
            copies.append(remote(src, mine, w_send.at[item, k], w_recv.at[item, k], (lax.rem(here_b + k, nb), here_r)))
        for copy in copies:
            copy.start()
        return copies

    def arrived(copies):
        for copy in copies:
            copy.wait()

    in_copies = gather(0, own_in, w_in)
    conv_copies = [gather(2, own_conv.at[0], w_conv.at[0])]

    def stats_start(e):
        held[e, 0] = stat[e]
        copies = []
        for k in range(1, n):
            copy = remote(stat.at[e], held.at[e, k], stat_send.at[e, k], stat_recv.at[e, k], peer_place(batch, lax.rem(block + k, n)))
            copy.start()
            copies.append(copy)
        return copies

    def stats_finish(e, copies):
        arrived(copies)
        total = held[e, lax.rem(block, n)]
        for q in range(1, n):
            total = total + held[e, lax.rem(block + n - q, n)]
        return total

    def rims_of(e, low_src, high_src):
        slot = e % 2
        return (
            remote(low_src, rim.at[slot, 1], rim_send.at[e, 1], rim_recv.at[e, 1], peer_place(batch, lax.rem(block + n - 1, n))),
            remote(high_src, rim.at[slot, 0], rim_send.at[e, 0], rim_recv.at[e, 0], peer_place(batch, lax.rem(block + 1, n))),
        )

    def start_if(condition, copy):
        @pl.when(condition)
        def _():
            copy.start()

    def rims_sent(copies):
        @pl.when(not_first)
        def _():
            copies[0].wait_send()

        @pl.when(not_last)
        def _():
            copies[1].wait_send()

    tile = 256
    tiles = rows // tile

    def rows_of(s, size):
        return pl.ds(pl.multiple_of(s * size, size), size)

    arrived(in_copies)
    turned_in = parts_of(w_in[...].T, 3)

    def project(s, _):
        span = rows_of(s, tile)
        act[0, span] = dots(parts_of(x_ref[span, :], 3), turned_in) + bias_ref[0:1]
        return 0

    lax.fori_loop(0, tiles, project, 0)

    own_cols, rim_cols = pl.ds(0, rows), pl.ds(rows, 2 * halo)
    scales = []
    late = None
    for l in range(layers):
        copies = rims_of(l, act.at[l, pl.ds(0, halo)], act.at[l, pl.ds(rows - halo, halo)])
        start_if(not_first, copies[0])
        start_if(not_last, copies[1])
        if l:
            counted = stats_start(l - 1)

        def split(s, _):
            span = rows_of(s, tile)
            for dst, piece in zip(ps, parts_of(act[l, span], 2)):
                dst[span, :] = piece
            return 0

        lax.fori_loop(0, tiles, split, 0)

        def own(span):
            agg[l, span] = dots([q[span, own_cols] for q in a], [q[own_cols, :] for q in ps])

        if l == 0:
            for s in range(rows // height):
                for copy in loads[s]:
                    copy.wait()
                own(pl.ds(s * height, height))
            for q in range(1, layers):
                conv_copies.append(gather(1 + 1 + q, own_conv.at[q], w_conv.at[q]))
            head_copies = gather(1, own_head, w_head)
        else:
            lax.fori_loop(0, rows // height, lambda s, _: (own(rows_of(s, height)), 0)[1], 0)
        if l == 1:
            base = 2 + layers
            late = [gather(base, own_min, full_min), gather(base + 1, own_mhead, full_mhead), gather(base + 2, own_mconv, full_mconv)]
        if l:
            totals = stats_finish(l - 1, counted) * (1.0 / nodes)
            mean = totals[0:1]
            inverse = lax.rsqrt(totals[1:2] - mean * mean + norm_epsilon)
            scale = norm_ref[l - 1, 0:1] * inverse
            scales.append((mean, inverse, scale, norm_ref[l - 1, 1:2] - mean * scale))
        else:
            scales.append(None)

        for which, gone, copy_index in ((0, first, 0), (1, last, 1)):
            @pl.when(gone)
            def _():
                rim[l % 2, which] = jnp.zeros((halo, width), f32)

            @pl.when(jnp.logical_not(gone))
            def _():
                remote(rim.at[l % 2, which], rim.at[l % 2, which], rim_send.at[l, which], rim_recv.at[l, which],
                       peer_place(batch, lax.rem(block + 1, n))).wait_recv()

            for dst, piece in zip(ps, parts_of(rim[l % 2, which], 2)):
                dst[pl.ds(rows + which * halo, halo), :] = piece
        arrived(conv_copies[l])
        weights = parts_of(w_conv[l], 3)
        stat8 = (jnp.zeros((8, width), f32), jnp.zeros((8, width), f32))

        def rims_in(s, _):
            span = rows_of(s, height)
            agg[l, span] += dots([q[span, rim_cols] for q in a], [q[rim_cols, :] for q in ps])
            return 0

        lax.fori_loop(0, rows // height, rims_in, 0)

        def finish(s, sums):
            span = rows_of(s, tile)
            found = agg[l, span]
            h = act[l, span]
            if l:
                _, _, scale, offset = scales[l]
                row_sum = jnp.concatenate(
                    [jnp.broadcast_to(sums_ref[s, i : i + 1], (LANES, LANES)).T for i in range(tile // LANES)], 0
                )
                found = found * scale + jnp.concatenate([row_sum] * (width // LANES), 1) * offset
                h = h * scale + offset
                agg[l, span] = found
            pre = dots(parts_of(jnp.concatenate([h, found], 1), 3), weights) + bias_ref[l + 1 : l + 2]
            active = jnp.maximum(pre, 0.0)
            act[l + 1, span] = active
            return sums[0] + folded(active), sums[1] + folded(active * active)

        sums = lax.fori_loop(0, tiles, finish, stat8)
        stat[l, 0:1] = column_sums(sums[0])
        stat[l, 1:2] = column_sums(sums[1])
        rims_sent(copies)

    counted = stats_start(layers - 1)
    arrived(head_copies)
    head_parts = parts_of(w_head[...], 3)
    head_turned = parts_of(w_head[...].T, 2)
    totals = stats_finish(layers - 1, counted) * (1.0 / nodes)
    mean = totals[0:1]
    inverse = lax.rsqrt(totals[1:2] - mean * mean + norm_epsilon)
    scale = norm_ref[layers - 1, 0:1] * inverse
    scales.append((mean, inverse, scale, norm_ref[layers - 1, 1:2] - mean * scale))

    def top(span):
        return act[layers, span] * scales[layers][2] + scales[layers][3]

    def classify(s, _):
        span = rows_of(s, tile)
        logit[span, :] = dots(parts_of(top(span), 3), head_parts) + head_bias_ref[...]
        return 0

    lax.fori_loop(0, tiles, classify, 0)
    per = pick_smem.shape[0] // n
    sent[...] = jnp.zeros_like(sent)
    for d in range(n):
        for k in range(per):
            sent[d, k : k + 1] = logit[pl.ds(pick_smem[d * per + k], 1), :]
    pair_copies = []
    for k in range(1, n):
        peer = lax.rem(block + k, n)
        copy = remote(sent.at[peer], got.at[k], pair_send.at[k], pair_recv.at[k], peer_place(batch, peer))
        copy.start()
        pair_copies.append(copy)
    got[0] = sent[block]
    lane = lax.broadcasted_iota(jnp.int32, (tile, LANES), 1)
    real = lane < classes

    def soften(s, loss):
        span = rows_of(s, tile)
        z = logit[span, :]
        top_z = jnp.max(jnp.where(real, z, -jnp.inf), axis=1, keepdims=True)
        e = jnp.where(real, jnp.exp(z - top_z), 0.0)
        total = jnp.sum(e, axis=1, keepdims=True)
        named = [
            jnp.broadcast_to(label_ref[pl.ds(s * (tile // LANES) + i, 1), :], (LANES, LANES)).T for i in range(tile // LANES)
        ]
        hot = jnp.logical_and(real, lane.astype(f32) == jnp.concatenate(named, 0))
        logit[span, :] = e / total - jnp.where(hot, 1.0, 0.0)
        part = jnp.where(lane == 0, top_z + jnp.log(total), 0.0) - jnp.where(hot, z, 0.0)
        return loss + folded(part)

    loss = lax.fori_loop(0, tiles, soften, jnp.zeros((8, LANES), f32))
    arrived(pair_copies)
    gaps = []
    for d in range(n):
        gaps.append(sent[d] - got[lax.rem(block + n - d, n)])
    gap = jnp.concatenate(gaps, 0)
    loss = loss + pair_weight * folded(gap * gap)
    spare = pick_row.shape[1] - gap.shape[0]
    if spare:
        gap = jnp.concatenate([gap, jnp.zeros((spare, LANES), f32)], 0)
    gap_parts = parts_of(gap * (4.0 * pair_weight), 3)
    at_head, at_small = rows_at[1], rows_at[2]
    small = layers + 1

    def finish_head(s, sums):
        span = rows_of(s, tile)
        spot = lax.broadcasted_iota(jnp.int32, (tile, pick_row.shape[1]), 0) + s * tile
        chosen = jnp.where(spot == pick_row[...], 1.0, 0.0).astype(bf16)
        add = None
        for piece in gap_parts:
            v = jnp.dot(chosen, piece, preferred_element_type=f32)
            add = v if add is None else add + v
        grad = (logit[span, :] + add) * (1.0 / all_nodes)
        grad_parts = parts_of(grad, 2)
        h = top(span)
        back = dots(grad_parts, head_turned)
        gh[span, :] = back
        normed = (act[layers, span] - scales[layers][0]) * scales[layers][1]
        return (
            sums[0] + dots(parts_of(h, 2), grad_parts, TURNED),
            sums[1] + folded(grad),
            sums[2] + folded(back),
            sums[3] + folded(back * normed),
        )

    begin = (
        jnp.zeros((width, LANES), f32),
        jnp.zeros((8, LANES), f32),
        jnp.zeros((8, width), f32),
        jnp.zeros((8, width), f32),
    )
    sums = lax.fori_loop(0, tiles, finish_head, begin)
    half = width // 2
    pay[pl.ds(at_head, half), :] = jnp.concatenate([sums[0][:half], sums[0][half:]], 1)
    tail = pl.ds(at_small, pay.shape[0] - at_small)
    pay[tail, :] = jnp.zeros((pay.shape[0] - at_small, width), f32)
    at_norm = at_small + small
    at_last = at_norm + 2 * layers
    pay[at_last : at_last + 1, 0:LANES] = column_sums(sums[1])
    pay[at_last + 1 : at_last + 2, 0:LANES] = column_sums(loss)
    e = layers
    stat[e, 0:1] = column_sums(sums[2])
    stat[e, 1:2] = column_sums(sums[3])
    counted = stats_start(e)

    def weight_grad(l):
        into = done if l else pay
        base = (l - 1) * 2 * width if l else 0
        where = pl.ds(base, width)
        under = pl.ds(base + width, width)

        def weigh(s, sums):
            span = rows_of(s, height)
            h = act[l, span]
            if l:
                h = h * scales[l][2] + scales[l][3]
            grad = [q[span, :] for q in gs]
            into[where, :] += dots(parts_of(h, 2), grad, TURNED)
            into[under, :] += dots(parts_of(agg[l, span], 2), grad, TURNED)
            return sums

        into[pl.ds(base, 2 * width), :] = jnp.zeros((2 * width, width), f32)
        lax.fori_loop(0, rows // height, weigh, 0)

    big = 2 * width

    def told(which):
        for peer in places.peers:
            pl.semaphore_signal(ready.at[which], inc=1, device_id=peer, device_id_type=pl.DeviceIdType.MESH)

    def summing(which, l, room):
        cores, planes, zs = places.cores, places.planes, places.zs
        piece = big // cores
        block_rows = piece // planes
        local = done.at[pl.ds((l - 1) * big, big)]
        offset = [0]

        def take(count):
            view = room.at[pl.ds(offset[0], count)]
            offset[0] += count
            return view

        whole = take(big)
        got1, sum1, got2 = take(piece), take(piece), take(piece)
        sum2, got3 = take(block_rows), take(block_rows * zs)
        number = [0]

        def go(src, dst, to):
            i = number[0]
            number[0] += 1
            copy = remote(src, dst, sum_send.at[which, i], sum_recv.at[which, i], to)
            copy.start()
            return copy

        def part(ref, index, count):
            return ref.at[pl.ds(pl.multiple_of(index * count, 8), count)]

        core, spot = places.core, places.spot
        pl.semaphore_wait(ready.at[which], len(places.peers))
        copies = []
        if cores == 2:
            copies = [go(part(local, 1 - core, piece), got1, places.core_peer)]
        yield
        arrived(copies)
        total = part(local, core, piece)[...]
        if cores == 2:
            total = total + got1[...]
        sum1[...] = total
        copies = []
        for k in range(1, planes):
            p, to = places.plane_peer(k)
            copies.append(go(part(sum1, p, block_rows), part(got2, k, block_rows), to))
        yield
        arrived(copies)
        total = part(sum1, spot, block_rows)[...]
        for k in range(1, planes):
            total = total + part(got2, k, block_rows)[...]
        sum2[...] = total
        got3[pl.ds(0, block_rows), :] = total
        copies = [go(sum2, part(got3, k, block_rows), places.column_peer(k)[1]) for k in range(1, zs)]
        yield
        arrived(copies)
        total = part(got3, lax.rem(places.z, zs), block_rows)[...]
        for q in range(1, zs):
            total = total + part(got3, lax.rem(places.z + zs - q, zs), block_rows)[...]
        mine = part(whole, core * planes + spot, block_rows)
        mine[...] = total
        copies = [go(mine, mine, places.plane_peer(k)[1]) for k in range(1, planes)]
        yield
        arrived(copies)
        copies = []
        if cores == 2:
            mine = part(whole, core, piece)
            copies = [go(mine, mine, places.core_peer)]
        yield
        arrived(copies)
        local[...] = whole[...]
        yield

    running = []

    def advance():
        for job in list(running):
            next(job, None)

    for l in range(layers - 1, -1, -1):
        e = layers + (layers - 1 - l)
        pay[at_norm + 2 * l : at_norm + 2 * l + 1, :] = stat[e, 1:2]
        pay[at_norm + 2 * l + 1 : at_norm + 2 * l + 2, :] = stat[e, 0:1]
        if l < layers - 1:
            weight_grad(l + 1)
            room = act.at[layers] if l == layers - 2 else agg.at[l + 2]
            if l < layers - 2:
                advance()
            job = summing(layers - 2 - l, l + 1, room)
            next(job)
            running.append(job)
            if l:
                told(layers - 1 - l)
        turned = w_conv[l].T
        for q, piece in enumerate(parts_of(turned, 2)):
            wt[q] = piece
        totals = stats_finish(e, counted) * norm_ref[l, 0:1] * (1.0 / nodes)
        mean, inverse, _, _ = scales[l + 1]
        gain = norm_ref[l, 0:1]

        def enter(s, total):
            span = rows_of(s, tile)
            active = act[l + 1, span]
            normed = (active - mean) * inverse
            grad = inverse * (gh[span, :] * gain - totals[0:1] - normed * totals[1:2])
            grad = jnp.where(active > 0.0, grad, 0.0)
            pieces = parts_of(grad, 2)
            for dst, piece in zip(gs, pieces):
                dst[span, :] = piece
            joined = dots(pieces, [wt[0], wt[1]])
            gh[span, :] = joined[:, :width]
            for dst, piece in zip(ps, parts_of(joined[:, width:], 2)):
                dst[span, :] = piece
            return total + folded(grad)

        total = lax.fori_loop(0, tiles, enter, jnp.zeros((8, width), f32))
        if l == layers - 1 and l:
            told(0)
        advance()
        pay[at_small + 1 + l : at_small + 2 + l, :] = column_sums(total)
        right = [q[own_cols, :] for q in ps]
        copies = rims_of(e, out_rim.at[0], out_rim.at[1])
        for which, go in ((0, not_first), (1, not_last)):
            out_rim[which] = dots([q[:, pl.ds(rows + which * halo, halo)] for q in a], right, TURNED)
            start_if(go, copies[which])

        if not l:
            advance()

        def spread_back(s, _):
            span = rows_of(s, height)
            gh[span, :] += dots([q[:, span] for q in a], right, TURNED)
            return 0

        lax.fori_loop(0, rows // height, spread_back, 0)
        advance()
        slot = e % 2
        for which, go, start in ((1, not_last, rows - halo), (0, not_first, 0)):
            @pl.when(go)
            def _():
                remote(rim.at[slot, which], rim.at[slot, which], rim_send.at[e, which], rim_recv.at[e, which],
                       peer_place(batch, lax.rem(block + 1, n))).wait_recv()
                gh[pl.ds(start, halo), :] += rim[slot, which]

        def tail_sums(s, sums):
            span = rows_of(s, tile)
            grad = gh[span, :]
            second = sums[1]
            if l:
                second = second + folded(grad * ((act[l, span] - scales[l][0]) * scales[l][1]))
            return sums[0] + folded(grad), second

        sums = lax.fori_loop(0, tiles, tail_sums, (jnp.zeros((8, width), f32), jnp.zeros((8, width), f32)))
        if l:
            stat[e + 1, 0:1] = column_sums(sums[0])
            stat[e + 1, 1:2] = column_sums(sums[1])
            counted = stats_start(e + 1)
        else:
            pay[at_small : at_small + 1, :] = column_sums(sums[0])
        rims_sent(copies)
    advance()
    weight_grad(0)
    advance()
    feat = x_ref.shape[1]
    pay[pl.ds(rows_at[0], rows_at[1] - rows_at[0]), :] = jnp.zeros((rows_at[1] - rows_at[0], width), f32)

    def weigh_in(s, total):
        span = rows_of(s, height)
        return total + dots(parts_of(x_ref[span, :], 2), parts_of(gh[span, :], 2), TURNED)

    pay[pl.ds(rows_at[0], feat), :] = lax.fori_loop(0, rows // height, weigh_in, jnp.zeros((feat, width), f32))
    advance()
    for copies in late:
        arrived(copies)


def step_call(n, nb, layers, nodes, all_nodes, classes, rows_at, pay_rows, x, labels, sums, biases, norms, head_bias,
              picks, pick_row, adjacency, shards):
    rows = x.shape[0]
    width = biases.shape[1]
    cols = adjacency[0].shape[1]
    halo = (cols - rows) // 2
    feat = x.shape[1]
    vmem = pl.BlockSpec(memory_space=pltpu.VMEM)
    smem = pl.BlockSpec(memory_space=pltpu.SMEM)
    hbm = pl.BlockSpec(memory_space=pl.ANY)
    dma = pltpu.SemaphoreType.DMA
    items = 2 + layers + 3
    exchanges = 2 * layers
    _, ys, across, zs = plane_split(nb, n)
    hops = 2 * ys * across + zs
    return pl.pallas_call(
        functools.partial(step_kernel, n, nb, layers, nodes, all_nodes, classes, rows_at),
        out_shape=(
            jax.ShapeDtypeStruct((pay_rows, width), f32),
            jax.ShapeDtypeStruct(((layers - 1) * 2 * width, width), f32),
            jax.ShapeDtypeStruct((width, feat), f32),
            jax.ShapeDtypeStruct((layers, 2 * width, width), f32),
            jax.ShapeDtypeStruct((width, LANES), f32),
        ),
        in_specs=[vmem] * 6 + [smem, vmem] + [hbm] * 8,
        out_specs=(vmem, vmem, hbm, hbm, hbm),
        scratch_shapes=[
            pltpu.VMEM((layers + 1, rows, width), f32),
            pltpu.VMEM((layers, rows, width), f32),
            pltpu.VMEM((rows, cols), bf16),
            pltpu.VMEM((rows, cols), bf16),
            pltpu.VMEM((cols, width), bf16),
            pltpu.VMEM((cols, width), bf16),
            pltpu.VMEM((rows, width), bf16),
            pltpu.VMEM((rows, width), bf16),
            pltpu.VMEM((rows, width), f32),
            pltpu.VMEM((2, 2, halo, width), f32),
            pltpu.VMEM((2, halo, width), f32),
            pltpu.VMEM((rows, LANES), f32),
            pltpu.VMEM((n, 8, LANES), f32),
            pltpu.VMEM((n, 8, LANES), f32),
            pltpu.VMEM((exchanges, 2, width), f32),
            pltpu.VMEM((exchanges, n, 2, width), f32),
            pltpu.VMEM((width, feat), f32),
            pltpu.VMEM((layers, 2 * width, width), f32),
            pltpu.VMEM((width, LANES), f32),
            pltpu.VMEM((2, width, 2 * width), bf16),
            dma((2 * rows // 512,)),
            dma((exchanges, n)),
            dma((exchanges, n)),
            dma((exchanges, 2)),
            dma((exchanges, 2)),
            dma((n,)),
            dma((n,)),
            dma((items, nb)),
            dma((items, nb)),
            dma((items,)),
            dma((layers - 1, hops)),
            dma((layers - 1, hops)),
            pltpu.SemaphoreType.REGULAR((layers - 1,)),
        ],
        compiler_params=pltpu.CompilerParams(collective_id=1, has_side_effects=True, vmem_limit_bytes=63 << 20),
        name="forward_backward",
    )(x, labels, sums, biases, norms, head_bias, picks, pick_row, *adjacency, *shards)


def update_kernel(n, nb, layers, all_nodes, rows_at, classes, ns_parts, scales, pay, done, mom_in, mom_conv, mom_head, w_in,
                  w_conv, w_head, biases, norms, head_bias, fb, fn, fh, sb, sn, sh, power, *refs):
    (loss_o, in_o, conv_o, head_o, min_o, mconv_o, mhead_o, b_o, n_o, h_o, fb_o, fn_o, fh_o, sb_o, sn_o, sh_o) = refs[:16]
    (got1, sum1, got2, sum2, got3, full, gram, poly, small_gram, small_poly, mconv, send, recv) = refs[16:]
    places = Places(n, nb)
    cores, planes, zs = places.cores, places.planes, places.zs
    core, spot, z = places.core, places.spot, places.z
    plane_peer, column_peer, core_peer = places.plane_peer, places.column_peer, places.core_peer
    here_b = places.b
    width = w_conv.shape[2]
    barrier = pltpu.get_barrier_semaphore()
    for peer in places.peers:
        pl.semaphore_signal(barrier, inc=1, device_id=peer, device_id_type=pl.DeviceIdType.MESH)

    def kdot(left, right, dims=((1,), (0,))):
        return dots(parts_of(left, ns_parts), parts_of(right, ns_parts), dims)

    def eye(k):
        return (lax.broadcasted_iota(jnp.int32, (k, k), 0) == lax.broadcasted_iota(jnp.int32, (k, k), 1)).astype(f32)

    def begin(moment, grams, i):
        size = jnp.sqrt(jnp.sum(moment * moment)) + 1e-07
        g = kdot(moment, moment, TURNED) / (size * size)
        grams[i] = g
        return size

    def step(grams, polys, which, early, late):
        k = grams.shape[1]
        count = len(which)
        a1 = [grams[i] for i in which]
        a2 = [kdot(v, v) for v in a1]
        p = [newton_a * eye(k) + newton_b * v + newton_c * u for v, u in zip(a1, a2)]
        if early:
            q = p
        else:
            q = [kdot(v, polys[i]) for i, v in zip(which, p)]
        if not late:
            pa = [kdot(v, u) for v, u in zip(p, a1)]
            nxt = [kdot(v, u) for v, u in zip(pa, p)]
        for j in range(count):
            polys[which[j]] = q[j]
            if not late:
                grams[which[j]] = nxt[j]

    sizes = {}
    ready = tuple(range(1, layers))

    def start_ready():
        for l in ready:
            mconv[l] = muon_decay * mom_conv[l] + done[(l - 1) * 2 * width : l * 2 * width]
            sizes[l] = begin(mconv[l], gram, l)

    def middle(count, grams, polys, which):
        lax.fori_loop(0, count, lambda _, c: (step(grams, polys, which, False, False), c)[1], 0)

    pl.semaphore_wait(barrier, len(places.peers))
    used = [0]

    def go(src, dst, to):
        i = used[0]
        used[0] += 1
        copy = remote(src, dst, send.at[i], recv.at[i], to)
        copy.start()
        return copy

    def settle(copies):
        for copy in copies:
            copy.wait()

    every = slice(None)
    if cores == 2:
        copies = [go(pay.at[every, every, 1 - core], got1, core_peer)]
        start_ready()
        settle(copies)
        sum1[...] = pay[every, every, core] + got1[...]
    else:
        start_ready()
        sum1[...] = pay[every, every, 0]
    copies = []
    for k in range(1, planes):
        p, to = plane_peer(k)
        copies.append(go(sum1.at[every, p], got2.at[k], to))
    step(gram, poly, ready, True, False)
    middle(1, gram, poly, ready)
    settle(copies)
    total = sum1[every, spot]
    for k in range(1, planes):
        total = total + got2[k]
    sum2[...] = total
    copies = []
    for k in range(1, zs):
        q, to = column_peer(k)
        copies.append(go(sum2.at[q], got3.at[k], to))
    middle(1, gram, poly, ready)
    settle(copies)
    total = sum2[z]
    for k in range(1, zs):
        total = total + got3[k]
    mine = full.at[z, spot, core]
    mine[...] = total
    copies = [go(mine, mine, column_peer(k)[1]) for k in range(1, zs)]
    middle(1, gram, poly, ready)
    settle(copies)
    mine = full.at[every, spot, core]
    copies = [go(mine, mine, plane_peer(k)[1]) for k in range(1, planes)]
    step(gram, poly, ready, False, True)
    scale_in, scale_conv, scale_head = scales
    span = w_conv.shape[1]

    def turn_conv(l):
        part = mconv[l, pl.ds(pl.multiple_of(here_b * span, 8), span)]
        mconv_o[l] = part
        w = w_conv[l]
        turn = kdot(part, poly[l]) * (scale_conv / sizes[l])
        conv_o[l] = w - muon_rate * (turn + muon_shrink * w)

    for l in ready:
        turn_conv(l)
    settle(copies)
    if cores == 2:
        mine = full.at[every, every, core]
        settle([go(mine, mine, core_peer)])
    summed = full[...].reshape(-1, width)
    mconv[0] = muon_decay * mom_conv[0] + summed[: 2 * width]
    sizes[0] = begin(mconv[0], gram, 0)
    feat = w_in.shape[1]
    half = width // 2
    grad_in = summed[rows_at[0] : rows_at[0] + LANES].T
    grad_head = summed[rows_at[1] : rows_at[1] + half]
    moment_in = muon_decay * mom_in[...] + jnp.where(lax.broadcasted_iota(jnp.int32, (width, LANES), 1) < feat, grad_in, 0.0)
    moment_head = muon_decay * mom_head[...] + jnp.concatenate([grad_head[:, :LANES], grad_head[:, LANES:]], 0)
    sizes[layers] = begin(moment_in, small_gram, 0)
    sizes[layers + 1] = begin(moment_head, small_gram, 1)

    def both(early, late):
        step(gram, poly, (0,), early, late)
        step(small_gram, small_poly, (0, 1), early, late)

    both(True, False)
    lax.fori_loop(1, NS_STEPS - 1, lambda _, c: (both(False, False), c)[1], 0)
    both(False, True)
    turn_conv(0)
    span = w_in.shape[0]
    mconv[0, pl.ds(0, width), 0:LANES] = moment_in
    mconv[0, pl.ds(0, width), LANES : 2 * LANES] = moment_head
    part = mconv[0, pl.ds(pl.multiple_of(here_b * span, 8), span), 0:LANES]
    min_o[...] = part[:, :feat]
    w = w_in[...]
    turn = kdot(part, small_poly[0]) * (scale_in / sizes[layers])
    in_o[...] = w - muon_rate * (turn[:, :feat] + muon_shrink * w)
    span = w_head.shape[0]
    part = mconv[0, pl.ds(pl.multiple_of(here_b * span, 8), span), LANES : 2 * LANES]
    mhead_o[...] = part[:, :classes]
    w = w_head[...]
    turn = kdot(part, small_poly[1]) * (scale_head / sizes[layers + 1])
    head_o[...] = w - muon_rate * (turn[:, :classes] + muon_shrink * w)

    def adamw(param, grad, first, second, outs):
        first = adam_first_decay * first + (1.0 - adam_first_decay) * grad
        second = adam_second_decay * second + (1.0 - adam_second_decay) * grad * grad
        first_hat = first / power[0]
        second_hat = second / power[1]
        outs[0][...] = param - adam_rate * (first_hat / (jnp.sqrt(second_hat) + adam_epsilon) + adam_shrink * param)
        outs[1][...] = first
        outs[2][...] = second

    at = rows_at[2]
    adamw(biases[...], summed[at : at + layers + 1], fb[...], sb[...], (b_o, fb_o, sb_o))
    at = at + layers + 1
    adamw(norms[...], summed[at : at + 2 * layers], fn[...], sn[...], (n_o, fn_o, sn_o))
    at = at + 2 * layers
    adamw(head_bias[...], summed[at : at + 1, :classes], fh[...], sh[...], (h_o, fh_o, sh_o))
    loss_o[...] = jnp.sum(summed[at + 1 : at + 2], axis=1, keepdims=True) / all_nodes


def update_call(n, nb, layers, all_nodes, rows_at, classes, ns_parts, scales, pay, done, moments, shards, smalls, power):
    cores, ys, xs, zs = plane_split(nb, n)
    planes = ys * xs
    width = pay.shape[1]
    m = pay.shape[0] // (n * nb)
    pay = pay.reshape(zs, planes, cores, m, width)
    w_in, w_conv, w_head = shards
    vmem = pl.BlockSpec(memory_space=pltpu.VMEM)
    smem = pl.BlockSpec(memory_space=pltpu.SMEM)
    like = [jax.ShapeDtypeStruct(v.shape, f32) for v in (w_in, w_conv, w_head)]
    like_small = [jax.ShapeDtypeStruct(v.shape, f32) for v in smalls[:3]]
    copies = 2 * (planes + zs)
    return pl.pallas_call(
        functools.partial(update_kernel, n, nb, layers, all_nodes, rows_at, classes, ns_parts, scales),
        out_shape=tuple([jax.ShapeDtypeStruct((1, 1), f32)] + like + like + like_small * 3),
        in_specs=[vmem] * 17 + [smem],
        out_specs=(vmem,) * 16,
        scratch_shapes=[
            pltpu.VMEM((zs, planes, m, width), f32),
            pltpu.VMEM((zs, planes, m, width), f32),
            pltpu.VMEM((planes, zs, m, width), f32),
            pltpu.VMEM((zs, m, width), f32),
            pltpu.VMEM((zs, m, width), f32),
            pltpu.VMEM((zs, planes, cores, m, width), f32),
            pltpu.VMEM((layers, width, width), f32),
            pltpu.VMEM((layers, width, width), f32),
            pltpu.VMEM((2, LANES, LANES), f32),
            pltpu.VMEM((2, LANES, LANES), f32),
            pltpu.VMEM((layers, 2 * width, width), f32),
            pltpu.SemaphoreType.DMA((copies,)),
            pltpu.SemaphoreType.DMA((copies,)),
        ],
        compiler_params=pltpu.CompilerParams(collective_id=2, has_side_effects=True, vmem_limit_bytes=48 << 20),
        name="sum_and_update",
    )(pay, done, *moments, *shards, *smalls, power)


NS_PARTS = 3


def per_device(
    n_batch,
    n_rows,
    features,
    edge_rows,
    edge_weight,
    halo_counts,
    labels,
    pair_rows,
    step,
    w_in,
    w_conv,
    w_head,
    biases,
    norm_params,
    head_bias,
    mom_in,
    mom_conv,
    mom_head,
    first_bias,
    first_norm,
    first_head,
    second_bias,
    second_norm,
    second_head,
):
    rows_dev = features.shape[1]
    halo_rows = rows_dev // 4
    edge_count = edge_rows.shape[3]
    layers, hid = w_conv.shape[0], w_conv.shape[2]
    feat, classes = w_in.shape[0], w_head.shape[1]
    pairs = pair_rows.shape[3]
    node_count = rows_dev * n_rows
    all_nodes = node_count * n_batch
    flat = [
        edge_rows.reshape(2 * edge_count).astype(f32),
        edge_weight.reshape(edge_count),
        labels.reshape(rows_dev).astype(f32),
        pair_rows.reshape(n_rows * pairs).astype(f32),
    ]
    flat = jnp.concatenate(flat)
    flat = jnp.pad(flat, (0, -flat.shape[0] % (8 * LANES))).reshape(-1, LANES)
    flat = redeal(flat, n_batch, n_rows)
    inputs = redeal(features, n_batch, n_rows)[0]
    e = edge_count // LANES
    block = my_place()[1]
    wide = (rows_dev + 2 * halo_rows) // TILE
    rims = jnp.stack([(block > 0).astype(jnp.int32), (block < n_rows - 1).astype(jnp.int32)])
    order = order_edges(flat[:e], flat[e : 2 * e], flat[2 * e : 3 * e], wide)
    *adjacency, row_sums = fill(order, rims, rows_dev // TILE, wide, halo_rows // TILE, 2)
    label_rows = rows_dev // LANES
    node_labels = flat[3 * e : 3 * e + label_rows]
    picks = flat[3 * e + label_rows :].reshape(-1)[: n_rows * pairs].astype(jnp.int32)
    spread = jnp.pad(picks.reshape(n_rows, pairs), ((0, 0), (0, 8 - pairs)), constant_values=-1).reshape(1, n_rows * 8)
    spread = jnp.pad(spread, ((0, 0), (0, -spread.shape[1] % LANES)), constant_values=-1)
    at_in = 2 * hid
    at_head = at_in + -(-feat // 8) * 8
    at_small = at_head + hid // 2
    used = at_small + layers + 1 + 2 * layers + 2
    unit = 8 * n_rows * n_batch
    pay_rows = -(-used // unit) * unit
    rows_at = (at_in, at_head, at_small)
    turned = [
        w_in.T,
        w_conv,
        jnp.pad(w_head, ((0, 0), (0, LANES - classes))),
        mom_in.T,
        mom_conv,
        jnp.pad(mom_head, ((0, 0), (0, LANES - classes))),
    ]
    pay, done, full_min, full_mconv, full_mhead = step_call(
        n_rows,
        n_batch,
        layers,
        node_count,
        all_nodes,
        classes,
        rows_at,
        pay_rows,
        inputs,
        node_labels,
        row_sums,
        biases,
        norm_params,
        jnp.pad(head_bias, (0, LANES - classes))[None],
        picks,
        spread,
        adjacency,
        turned,
    )
    count = step[0].astype(f32)
    power = jnp.stack([1.0 - jnp.power(adam_first_decay, count), 1.0 - jnp.power(adam_second_decay, count)])
    scales = (
        math.sqrt(max(1.0, hid / feat)),
        math.sqrt(max(1.0, hid / (2 * hid))),
        math.sqrt(max(1.0, classes / hid)),
    )
    norm_rows = (2 * layers, hid)
    smalls = (
        biases,
        norm_params.reshape(norm_rows),
        head_bias[None],
        first_bias,
        first_norm.reshape(norm_rows),
        first_head[None],
        second_bias,
        second_norm.reshape(norm_rows),
        second_head[None],
    )
    outs = update_call(
        n_rows,
        n_batch,
        layers,
        all_nodes,
        rows_at,
        classes,
        NS_PARTS,
        scales,
        pay,
        done,
        (jnp.pad(full_min, ((0, 0), (0, LANES - feat))), full_mconv, full_mhead),
        (turned[0], w_conv, w_head),
        smalls,
        power,
    )
    loss, new_in, new_conv, new_head, moment_in, moment_conv, moment_head = outs[:7]
    rest = []
    for i in range(0, 9, 3):
        rest += [outs[7 + i], outs[8 + i].reshape(layers, 2, hid), outs[9 + i][0]]
    return (loss[0, 0], new_in.T, new_conv, new_head, moment_in.T, moment_conv, moment_head, *rest)


def solution(mesh):
    in_specs = (
        P("batch", "rows", None),
        P("batch", "rows", None, None),
        P("batch", "rows", None),
        P("batch", "rows", None),
        P("batch", "rows"),
        P("batch", "rows", None, None),
        P(),
        P(None, "batch"),
        P(None, "batch", None),
        P("batch", None),
        P(),
        P(),
        P(),
        P(None, "batch"),
        P(None, "batch", None),
        P("batch", None),
        P(),
        P(),
        P(),
        P(),
        P(),
        P(),
    )
    out_specs = (
        P(),
        P(None, "batch"),
        P(None, "batch", None),
        P("batch", None),
        P(None, "batch"),
        P(None, "batch", None),
        P("batch", None),
        P(),
        P(),
        P(),
        P(),
        P(),
        P(),
        P(),
        P(),
        P(),
    )
    body = functools.partial(per_device, mesh.shape["batch"], mesh.shape["rows"])
    return jax.shard_map(body, mesh=mesh, in_specs=in_specs, out_specs=out_specs, check_vma=False)
```

```python
import functools
import math

import jax
import jax.numpy as jnp
from jax import lax
from jax.experimental import pallas as pl
from jax.experimental.pallas import tpu as pltpu
from jax.sharding import PartitionSpec as P

NS_STEPS = 5

f32 = jnp.float32
bf16 = jnp.bfloat16
LANES = 128
TILE = 256
highest = lax.Precision.HIGHEST
norm_epsilon = 1e-05
pair_weight = 0.05
newton_a = 3.4445
newton_b = -4.775
newton_c = 2.0315
muon_decay = 0.9
muon_rate = 0.5
muon_shrink = 0.01
adam_first_decay = 0.9
adam_second_decay = 0.999
adam_epsilon = 1e-08
adam_rate = 0.1
adam_shrink = 0.01


def swap(b, r):
    return 2 * (b // 2) + r % 2, 2 * (r // 2) + b % 2


def flat_pairs(n_batch, n_rows, move):
    pairs = []
    for b in range(n_batch):
        for r in range(n_rows):
            to = move(b, r)
            if to is not None:
                pairs.append((b * n_rows + r, to[0] * n_rows + to[1]))
    return pairs


def redeal(array, n_batch, n_rows):
    return lax.ppermute(array, ("batch", "rows"), flat_pairs(n_batch, n_rows, swap))


def peer_place(batch, block):
    two = jnp.int32(2)
    return (
        two * lax.div(batch, two) + lax.rem(block, two),
        two * lax.div(block, two) + lax.rem(batch, two),
    )


def my_place():
    return peer_place(lax.axis_index("batch"), lax.axis_index("rows"))


def order_kernel(wide, to_ref, from_ref, w_ref, key_out, w_out, col_out, lo_out, hi_out):
    to, frm = to_ref[...].astype(jnp.int32), from_ref[...].astype(jnp.int32)
    key = (((to >> 8) * wide + (frm >> 8)) << 16) | ((to & 255) << 8) | (frm & 255)
    shape3 = (16, 8, LANES)
    key = key.astype(f32).reshape(shape3)
    w = w_ref[...].reshape(shape3)
    sub = lax.broadcasted_iota(jnp.int32, shape3, 1)
    lane = lax.broadcasted_iota(jnp.int32, shape3, 2)
    vreg = lax.broadcasted_iota(jnp.int32, shape3, 0)
    place = vreg + 16 * sub + 128 * lane
    for phase in range(14):
        for bit in range(phase, -1, -1):
            down = ((place >> (phase + 1)) & 1) == 1
            if bit < 4:
                view = (16 >> (bit + 1), 2, 1 << bit, 8, LANES)
                kv, wv = key.reshape(view), w.reshape(view)
                dv = down.astype(jnp.int32).reshape(view)[:, 0] == 1
                a, b, wa, wb = kv[:, 0], kv[:, 1], wv[:, 0], wv[:, 1]
                turn = jnp.logical_xor(a > b, dv)
                key = jnp.stack([jnp.where(turn, b, a), jnp.where(turn, a, b)], 1).reshape(shape3)
                w = jnp.stack([jnp.where(turn, wb, wa), jnp.where(turn, wa, wb)], 1).reshape(shape3)
            else:
                if bit < 7:
                    axis, gap, size, pos = 1, 1 << (bit - 4), 8, sub
                else:
                    axis, gap, size, pos = 2, 1 << (bit - 7), LANES, lane
                low = (pos & gap) == 0
                kp = jnp.where(low, pltpu.roll(key, size - gap, axis), pltpu.roll(key, gap, axis))
                wp = jnp.where(low, pltpu.roll(w, size - gap, axis), pltpu.roll(w, gap, axis))
                smaller = jnp.logical_xor(low, down)
                take = jnp.where(smaller, kp, key) < jnp.where(smaller, key, kp)
                key = jnp.where(take, kp, key)
                w = jnp.where(take, wp, w)
    flat = key.reshape(LANES, LANES)
    key_out[...] = flat.T.astype(jnp.int32)
    w_out[...] = w.reshape(LANES, LANES).T
    start = (lax.broadcasted_iota(jnp.int32, (8, LANES), 1).astype(f32) * 65536.0)[None]
    below = jnp.zeros(shape3, f32)
    upto = jnp.zeros(shape3, f32)
    for c in range(LANES):
        wide_key = jnp.broadcast_to(flat[:, c : c + 1], (LANES, LANES))
        col_out[c] = (wide_key - jnp.floor(wide_key * (1.0 / 256.0)) * 256.0).astype(bf16)
        wide_key = wide_key.reshape(shape3)
        below = below + jnp.where(wide_key < start, 1.0, 0.0)
        upto = upto + jnp.where(wide_key < start + 65536.0, 1.0, 0.0)
    n_below = jnp.sum(below.reshape(LANES, LANES), axis=0, keepdims=True)
    n_upto = jnp.sum(upto.reshape(LANES, LANES), axis=0, keepdims=True)
    first = jnp.floor(n_below * (1.0 / 128.0))
    end = jnp.floor((n_upto + 127.0) * (1.0 / 128.0))
    lo_out[...] = first.astype(jnp.int32)
    hi_out[...] = jnp.where(n_upto > n_below, end, first).astype(jnp.int32)


def order_edges(to, frm, w, wide):
    vmem = pl.BlockSpec(memory_space=pltpu.VMEM)
    return pl.pallas_call(
        functools.partial(order_kernel, wide),
        out_shape=(
            jax.ShapeDtypeStruct((LANES, LANES), jnp.int32),
            jax.ShapeDtypeStruct((LANES, LANES), f32),
            jax.ShapeDtypeStruct((LANES, LANES, LANES), bf16),
            jax.ShapeDtypeStruct((1, LANES), jnp.int32),
            jax.ShapeDtypeStruct((1, LANES), jnp.int32),
        ),
        in_specs=[vmem] * 3,
        out_specs=(vmem,) * 5,
        compiler_params=pltpu.CompilerParams(vmem_limit_bytes=40 << 20),
        name="order_edges",
    )(to, frm, w)


def fill_kernel(wide, rim, chunk, parts, lo, hi, rims, key_ref, w_ref, col_ref, *refs):
    outs, sums, acc, rowacc = refs[:parts], refs[parts], refs[parts + 1], refs[parts + 2]
    i = pl.program_id(0)
    pack = 16
    shape = (TILE // pack, pack, LANES)
    rows = lax.broadcasted_iota(jnp.int32, shape, 0) * pack + lax.broadcasted_iota(jnp.int32, shape, 1)
    rows = rows.astype(f32).astype(bf16)
    lanes = lax.broadcasted_iota(jnp.int32, (LANES, LANES), 1).astype(f32)
    lanes0, lanes1 = lanes.astype(bf16), (lanes + 128.0).astype(bf16)
    one, zero = jnp.ones((), bf16), jnp.zeros((), bf16)

    def spread(row):
        return jnp.broadcast_to(row, (pack, LANES)).astype(bf16)[None]

    rowacc[...] = jnp.zeros_like(rowacc)

    def tile(j, _):
        b = i * wide + j
        first, end = lo[0, b], hi[0, b]
        end = jnp.where(jnp.logical_and(j < rim, rims[0] == 0), first, end)
        end = jnp.where(jnp.logical_and(j >= wide - rim, rims[1] == 0), first, end)
        slot = jnp.where(j < rim, wide - 2 * rim + j, jnp.where(j < wide - rim, j - rim, j))
        cols = pl.ds(pl.multiple_of(slot * TILE, TILE), TILE)

        @pl.when(end <= first)
        def _():
            for out in outs:
                out[:, cols] = jnp.zeros((TILE, TILE), bf16)

        @pl.when(end > first)
        def _():
            def part(base, c):
                row = jnp.minimum(base + c, LANES - 1)
                here = key_ref[pl.ds(row, 1), :] - (b << 16)
                if c:
                    here = jnp.where(base + c < end, here, -1)
                at = rows == spread((here >> 8).astype(f32))
                rest = w_ref[pl.ds(row, 1), :]
                left = []
                for q in range(parts):
                    piece = rest.astype(bf16).astype(f32)
                    rest = rest - piece
                    left.append(jnp.where(at, spread(piece), zero).reshape(TILE, LANES))
                col = col_ref[row]
                right = jnp.concatenate(
                    [jnp.where(col == lanes0, one, zero), jnp.where(col == lanes1, one, zero)], 1
                )
                return left, right

            def get(base):
                made = [part(base, c) for c in range(chunk)]
                lhs = jnp.concatenate([m[0][q] for q in range(parts) for m in made], 1)
                rhs = jnp.concatenate([m[1] for m in made] * parts, 0)
                return jnp.dot(lhs, rhs, preferred_element_type=f32)

            acc[...] = get(first)

            def more(t, _):
                acc[...] += get(first + t * chunk)
                return 0

            lax.fori_loop(1, lax.div(end - first + chunk - 1, chunk), more, 0)
            rest = acc[...]
            rowacc[...] += rest[:, :LANES] + rest[:, LANES:]
            for out in outs:
                piece = rest.astype(bf16)
                out[:, cols] = piece
                rest = rest - piece.astype(f32)

        return 0

    lax.fori_loop(0, wide, tile, 0)
    total = jnp.sum(rowacc[...], axis=1, keepdims=True)
    for half in range(TILE // LANES):
        column = jnp.broadcast_to(total[half * LANES : (half + 1) * LANES], (LANES, LANES))
        sums[0, half : half + 1] = column.T[0:1]


def fill(order, rims, tiles, wide, rim, parts, chunk=4):
    key, w, col, lo, hi = order
    cols = wide * TILE
    return pl.pallas_call(
        functools.partial(fill_kernel, wide, rim, chunk, parts),
        out_shape=tuple(jax.ShapeDtypeStruct((tiles * TILE, cols), bf16) for _ in range(parts))
        + (jax.ShapeDtypeStruct((tiles, TILE // LANES, LANES), f32),),
        grid_spec=pltpu.PrefetchScalarGridSpec(
            num_scalar_prefetch=3,
            grid=(tiles,),
            in_specs=[pl.BlockSpec((LANES, LANES), lambda i, *_: (0, 0))] * 2
            + [pl.BlockSpec((LANES, LANES, LANES), lambda i, *_: (0, 0, 0))],
            out_specs=tuple(pl.BlockSpec((TILE, cols), lambda i, *_: (i, 0)) for _ in range(parts))
            + (pl.BlockSpec((1, TILE // LANES, LANES), lambda i, *_: (i, 0, 0)),),
            scratch_shapes=[pltpu.VMEM((TILE, TILE), f32), pltpu.VMEM((TILE, LANES), f32)],
        ),
        compiler_params=pltpu.CompilerParams(vmem_limit_bytes=50 << 20),
        name="fill_tiles",
    )(lo, hi, rims, key, w, col)


def parts_of(x, count):
    found = []
    for q in range(count):
        piece = x.astype(bf16)
        found.append(piece)
        if q + 1 < count:
            x = x - piece.astype(f32)
    return found


def pair_list(count):
    return [(p, q) for p in range(count) for q in range(count) if p + q < count]


def dots(left, right, dims=((1,), (0,))):
    total = None
    for p, q in pair_list(len(left)):
        piece = lax.dot_general(left[p], right[q], (dims, ((), ())), preferred_element_type=f32)
        total = piece if total is None else total + piece
    return total


def remote(src, dst, send, recv, to):
    return pltpu.make_async_remote_copy(
        src_ref=src,
        dst_ref=dst,
        send_sem=send,
        recv_sem=recv,
        device_id=to,
        device_id_type=pl.DeviceIdType.MESH,
    )


def column_sums(x):
    return jnp.sum(x, axis=0, keepdims=True)


def folded(x):
    return jnp.sum(x.reshape(x.shape[0] // 8, 8, x.shape[1]), axis=0)


def plane_split(nb, n):
    cores = 2 if nb % 2 == 0 else 1
    across = 1
    while across * across * 4 <= n and n % (across * 2) == 0:
        across *= 2
    return cores, nb // cores, across, n // across


class Places:
    def __init__(self, n, nb):
        self.cores, ys, self.xs, self.zs = plane_split(nb, n)
        self.planes = ys * self.xs
        self.b, self.r = lax.axis_index("batch"), lax.axis_index("rows")
        self.core, y = lax.rem(self.b, self.cores), lax.div(self.b, self.cores)
        self.x, self.z = lax.rem(self.r, self.xs), lax.div(self.r, self.xs)
        self.spot = y * self.xs + self.x
        self.core_peer = (y * self.cores + lax.rem(self.core + 1, self.cores), self.r)
        self.peers = [self.plane_peer(k)[1] for k in range(1, self.planes)]
        self.peers += [self.column_peer(k)[1] for k in range(1, self.zs)]
        if self.cores == 2:
            self.peers.append(self.core_peer)

    def plane_peer(self, k):
        p = lax.rem(self.spot + k, self.planes)
        return p, (lax.div(p, self.xs) * self.cores + self.core, self.z * self.xs + lax.rem(p, self.xs))

    def column_peer(self, k):
        q = lax.rem(self.z + k, self.zs)
        return q, (self.b, q * self.xs + self.x)


TURNED = ((0,), (0,))
GATHERED = 3


def step_kernel(n, nb, layers, nodes, all_nodes, classes, rows_at, summed_rows, *refs):
    (x_ref, label_ref, sums_ref, bias_ref, norm_ref, head_bias_ref, pick_smem, pick_row, a1_hbm, a2_hbm) = refs[:10]
    own_in, own_conv, own_head, own_min, own_mconv, own_mhead = refs[10:16]
    pay, full_min, full_mconv, full_mhead = refs[16:20]
    (act, agg, a1, a2, p1, p2, g1, g2, gh, rim, out_rim, logit, sent, got, stat, held, w_in, w_conv, w_head,
     wt, a_sem, stat_send, stat_recv, rim_send, rim_recv, pair_send, pair_recv, w_send, w_recv, w_own, sum_send, sum_recv,
     ready, normed, keep) = refs[20:]
    rows, width = act.shape[1], act.shape[2]
    halo = rim.shape[2]
    a, ps, gs = (a1, a2), (p1, p2), (g1, g2)
    here_b, here_r = lax.axis_index("batch"), lax.axis_index("rows")
    batch, block = my_place()
    first, last = block == 0, block == n - 1
    not_first, not_last = jnp.logical_not(first), jnp.logical_not(last)

    barrier = pltpu.get_barrier_semaphore()
    for k in range(1, n):
        pl.semaphore_signal(
            barrier, inc=1, device_id=peer_place(batch, lax.rem(block + k, n)), device_id_type=pl.DeviceIdType.MESH
        )
    for k in range(1, nb):
        pl.semaphore_signal(
            barrier, inc=1, device_id=(lax.rem(here_b + k, nb), here_r), device_id_type=pl.DeviceIdType.MESH
        )
    places = Places(n, nb)
    for peer in places.peers:
        pl.semaphore_signal(barrier, inc=1, device_id=peer, device_id_type=pl.DeviceIdType.MESH)
    height = 512
    for s in range(rows // height):
        span = pl.ds(s * height, height)
        for q, (src, dst) in enumerate(zip((a1_hbm, a2_hbm), a)):
            pltpu.make_async_copy(src.at[span], dst.at[span], a_sem.at[2 * s + q]).start()
    pl.semaphore_wait(barrier, n - 1 + nb - 1 + len(places.peers))

    def gathers(item, src, dst):
        span = src.shape[-2]
        lead = (slice(None),) * (len(src.shape) - 2)
        mine = dst.at[lead + (pl.ds(pl.multiple_of(here_b * span, 8), span),)]
        copies = [pltpu.make_async_copy(src, mine, w_own.at[item])]
        for k in range(1, nb):
            copies.append(remote(src, mine, w_send.at[item, k], w_recv.at[item, k], (lax.rem(here_b + k, nb), here_r)))
        return copies

    def gather(item, src, dst):
        copies = gathers(item, src, dst)
        for copy in copies:
            copy.start()
        return copies

    def arrived(copies):
        for copy in copies:
            copy.wait()

    in_copies = gather(0, own_in, w_in)
    for q in range(layers):
        gather(2 + q, own_conv.at[q], w_conv.at[q])
    head_copies = gather(1, own_head, w_head)

    def stat_copies(e):
        return [
            remote(stat.at[e], held.at[e, k], stat_send.at[e, k], stat_recv.at[e, k], peer_place(batch, lax.rem(block + k, n)))
            for k in range(1, n)
        ]

    def stats_start(e):
        held[e, 0] = stat[e]
        for copy in stat_copies(e):
            copy.start()

    def stats_finish(e):
        arrived(stat_copies(e))
        total = held[e, lax.rem(block, n)]
        for q in range(1, n):
            total = total + held[e, lax.rem(block + n - q, n)]
        return total

    def rims_of(e, low_src, high_src):
        slot = lax.rem(e, 2)
        return (
            remote(low_src, rim.at[slot, 1], rim_send.at[e, 1], rim_recv.at[e, 1], peer_place(batch, lax.rem(block + n - 1, n))),
            remote(high_src, rim.at[slot, 0], rim_send.at[e, 0], rim_recv.at[e, 0], peer_place(batch, lax.rem(block + 1, n))),
        )

    def start_if(condition, copy):
        @pl.when(condition)
        def _():
            copy.start()

    def rims_sent(copies):
        @pl.when(not_first)
        def _():
            copies[0].wait_send()

        @pl.when(not_last)
        def _():
            copies[1].wait_send()

    tile = 256
    tiles = rows // tile

    def rows_of(s, size):
        return pl.ds(pl.multiple_of(s * size, size), size)

    zeros8 = jnp.zeros((8, width), f32)

    arrived(in_copies)
    turned_in = parts_of(w_in[...].T, 3)

    def project(s, _):
        span = rows_of(s, tile)
        act[0, span] = dots(parts_of(x_ref[span, :], 3), turned_in) + bias_ref[0]
        return 0

    lax.fori_loop(0, tiles, project, 0)
    stat[0] = jnp.zeros((2, width), f32)
    own_cols, rim_cols = pl.ds(0, rows), pl.ds(rows, 2 * halo)

    def set_norm(l, totals):
        mean = totals[0:1] * (1.0 / nodes)
        inverse = lax.rsqrt(totals[1:2] * (1.0 / nodes) - mean * mean + norm_epsilon)
        under = lax.max(l - 1, 0)
        scale = norm_ref[under, 0:1] * inverse
        offset = norm_ref[under, 1:2] - mean * scale
        plain = l == 0
        normed[l, 0:1] = jnp.where(plain, 0.0, mean)
        normed[l, 1:2] = jnp.where(plain, 1.0, inverse)
        normed[l, 2:3] = jnp.where(plain, 1.0, scale)
        normed[l, 3:4] = jnp.where(plain, 0.0, offset)

    def forward(l, _):
        copies = rims_of(l, act.at[l, pl.ds(0, halo)], act.at[l, pl.ds(rows - halo, halo)])
        start_if(not_first, copies[0])
        start_if(not_last, copies[1])
        stats_start(l)

        def split(s, _):
            span = rows_of(s, tile)
            for dst, piece in zip(ps, parts_of(act[l, span], 2)):
                dst[span, :] = piece
            return 0

        lax.fori_loop(0, tiles, split, 0)

        def own(s, _):
            span = rows_of(s, height)

            @pl.when(l == 0)
            def _():
                for q, (src, dst) in enumerate(zip((a1_hbm, a2_hbm), a)):
                    pltpu.make_async_copy(src.at[span], dst.at[span], a_sem.at[2 * s + q]).wait()

            agg[l, span] = dots([q[span, own_cols] for q in a], [q[own_cols, :] for q in ps])
            return 0

        lax.fori_loop(0, rows // height, own, 0)
        set_norm(l, stats_finish(l))
        slot = lax.rem(l, 2)
        for which, gone in ((0, first), (1, last)):
            @pl.when(gone)
            def _():
                rim[slot, which] = jnp.zeros((halo, width), f32)

            @pl.when(jnp.logical_not(gone))
            def _():
                remote(rim.at[slot, which], rim.at[slot, which], rim_send.at[l, which], rim_recv.at[l, which],
                       peer_place(batch, lax.rem(block + 1, n))).wait_recv()

            for dst, piece in zip(ps, parts_of(rim[slot, which], 2)):
                dst[pl.ds(rows + which * halo, halo), :] = piece

        def rims_in(s, _):
            span = rows_of(s, height)
            agg[l, span] += dots([q[span, rim_cols] for q in a], [q[rim_cols, :] for q in ps])
            return 0

        lax.fori_loop(0, rows // height, rims_in, 0)
        arrived(gathers(2 + l, own_conv.at[l], w_conv.at[l]))
        weights = parts_of(w_conv[l], 3)
        bias = bias_ref[l + 1]
        scale, offset = normed[l, 2:3], normed[l, 3:4]

        def finish(s, sums):
            span = rows_of(s, tile)
            row_sum = jnp.concatenate(
                [jnp.broadcast_to(sums_ref[s, i : i + 1], (LANES, LANES)).T for i in range(tile // LANES)], 0
            )
            found = agg[l, span] * scale + jnp.concatenate([row_sum] * (width // LANES), 1) * offset
            agg[l, span] = found
            h = act[l, span] * scale + offset
            pre = dots(parts_of(jnp.concatenate([h, found], 1), 3), weights) + bias
            active = jnp.maximum(pre, 0.0)
            act[l + 1, span] = active
            return sums[0] + folded(active), sums[1] + folded(active * active)

        sums = lax.fori_loop(0, tiles, finish, (zeros8, zeros8))
        stat[l + 1, 0:1] = column_sums(sums[0])
        stat[l + 1, 1:2] = column_sums(sums[1])
        rims_sent(copies)
        return 0

    lax.fori_loop(0, layers, forward, 0)

    stats_start(layers)
    base = 2 + layers
    late = [gather(base, own_min, full_min), gather(base + 1, own_mhead, full_mhead), gather(base + 2, own_mconv, full_mconv)]
    arrived(head_copies)
    head_parts = parts_of(w_head[...], 3)
    head_turned = parts_of(w_head[...].T, 2)
    set_norm(layers, stats_finish(layers))
    top_scale, top_offset = normed[layers, 2:3], normed[layers, 3:4]
    top_mean, top_inverse = normed[layers, 0:1], normed[layers, 1:2]

    def top(span):
        return act[layers, span] * top_scale + top_offset

    def classify(s, _):
        span = rows_of(s, tile)
        logit[span, :] = dots(parts_of(top(span), 3), head_parts) + head_bias_ref[...]
        return 0

    lax.fori_loop(0, tiles, classify, 0)
    per = pick_smem.shape[0] // n
    sent[...] = jnp.zeros_like(sent)
    for d in range(n):
        for k in range(per):
            sent[d, k : k + 1] = logit[pl.ds(pick_smem[d * per + k], 1), :]
    pair_copies = []
    for k in range(1, n):
        peer = lax.rem(block + k, n)
        copy = remote(sent.at[peer], got.at[k], pair_send.at[k], pair_recv.at[k], peer_place(batch, peer))
        copy.start()
        pair_copies.append(copy)
    got[0] = sent[block]
    lane = lax.broadcasted_iota(jnp.int32, (tile, LANES), 1)
    real = lane < classes

    def soften(s, loss):
        span = rows_of(s, tile)
        z = logit[span, :]
        top_z = jnp.max(jnp.where(real, z, -jnp.inf), axis=1, keepdims=True)
        e = jnp.where(real, jnp.exp(z - top_z), 0.0)
        total = jnp.sum(e, axis=1, keepdims=True)
        named = [
            jnp.broadcast_to(label_ref[pl.ds(s * (tile // LANES) + i, 1), :], (LANES, LANES)).T for i in range(tile // LANES)
        ]
        hot = jnp.logical_and(real, lane.astype(f32) == jnp.concatenate(named, 0))
        logit[span, :] = e / total - jnp.where(hot, 1.0, 0.0)
        part = jnp.where(lane == 0, top_z + jnp.log(total), 0.0) - jnp.where(hot, z, 0.0)
        return loss + folded(part)

    loss = lax.fori_loop(0, tiles, soften, jnp.zeros((8, LANES), f32))
    arrived(pair_copies)
    gaps = []
    for d in range(n):
        gaps.append(sent[d] - got[lax.rem(block + n - d, n)])
    gap = jnp.concatenate(gaps, 0)
    loss = loss + pair_weight * folded(gap * gap)
    spare = pick_row.shape[1] - gap.shape[0]
    if spare:
        gap = jnp.concatenate([gap, jnp.zeros((spare, LANES), f32)], 0)
    gap_parts = parts_of(gap * (4.0 * pair_weight), 3)
    at_head, at_small = rows_at[1], rows_at[2]
    small = layers + 1

    def finish_head(s, sums):
        span = rows_of(s, tile)
        spot = lax.broadcasted_iota(jnp.int32, (tile, pick_row.shape[1]), 0) + s * tile
        chosen = jnp.where(spot == pick_row[...], 1.0, 0.0).astype(bf16)
        add = None
        for piece in gap_parts:
            v = jnp.dot(chosen, piece, preferred_element_type=f32)
            add = v if add is None else add + v
        grad = (logit[span, :] + add) * (1.0 / all_nodes)
        grad_parts = parts_of(grad, 2)
        h = top(span)
        back = dots(grad_parts, head_turned)
        gh[span, :] = back
        ready_top = (act[layers, span] - top_mean) * top_inverse
        return (
            sums[0] + dots(parts_of(h, 2), grad_parts, TURNED),
            sums[1] + folded(grad),
            sums[2] + folded(back),
            sums[3] + folded(back * ready_top),
        )

    begin = (
        jnp.zeros((width, LANES), f32),
        jnp.zeros((8, LANES), f32),
        jnp.zeros((8, width), f32),
        jnp.zeros((8, width), f32),
    )
    sums = lax.fori_loop(0, tiles, finish_head, begin)
    half = width // 2
    pay[pl.ds(at_head, half), :] = jnp.concatenate([sums[0][:half], sums[0][half:]], 1)
    tail = pl.ds(at_small, summed_rows - at_small)
    pay[tail, :] = jnp.zeros((summed_rows - at_small, width), f32)
    at_norm = at_small + small
    at_last = at_norm + 2 * layers
    pay[at_last : at_last + 1, 0:LANES] = column_sums(sums[1])
    pay[at_last + 1 : at_last + 2, 0:LANES] = column_sums(loss)
    after = layers + 1
    stat[after, 0:1] = column_sums(sums[2])
    stat[after, 1:2] = column_sums(sums[3])
    stats_start(after)

    big = 2 * width

    def conv_rows(l):
        return pl.multiple_of(jnp.where(l == 0, 0, summed_rows + (l - 1) * big), 8)

    def told(which):
        for peer in places.peers:
            pl.semaphore_signal(ready.at[which], inc=1, device_id=peer, device_id_type=pl.DeviceIdType.MESH)

    cores, planes, zs = places.cores, places.planes, places.zs
    core, spot = places.core, places.spot
    piece_rows = big // cores
    block_rows = piece_rows // planes

    def part(ref, index, count):
        return ref.at[pl.ds(pl.multiple_of(index * count, 8), count)]

    class Sum:
        def __init__(self, l):
            self.which, room = l - 1, act.at[l + 1]
            self.local = pay.at[pl.ds(conv_rows(l), big)]
            self.whole = room.at[pl.ds(0, big)]
            spots = [piece_rows, piece_rows, piece_rows, block_rows, block_rows * zs]
            views, at = [], big
            for count in spots:
                views.append(room.at[pl.ds(at, count)])
                at += count
            self.got1, self.sum1, self.got2, self.sum2, self.got3 = views

        def copies(self, stage):
            found = []

            def add(i, src, dst, to):
                found.append(remote(src, dst, sum_send.at[self.which, i], sum_recv.at[self.which, i], to))

            if stage == 0 and cores == 2:
                add(0, part(self.local, 1 - core, piece_rows), self.got1, places.core_peer)
            if stage == 1:
                for k in range(1, planes):
                    p, to = places.plane_peer(k)
                    add(k, part(self.sum1, p, block_rows), part(self.got2, k, block_rows), to)
            if stage == 2:
                for k in range(1, zs):
                    add(planes + k, self.sum2, part(self.got3, k, block_rows), places.column_peer(k)[1])
            if stage == 3:
                mine = part(self.whole, core * planes + spot, block_rows)
                for k in range(1, planes):
                    add(planes + zs + k, mine, mine, places.plane_peer(k)[1])
            if stage == 4 and cores == 2:
                mine = part(self.whole, core, piece_rows)
                add(2 * planes + zs, mine, mine, places.core_peer)
            return found

        def go(self, stage):
            if stage == 0:
                pl.semaphore_wait(ready.at[self.which], len(places.peers))
            else:
                arrived(self.copies(stage - 1))
            if stage == 1:
                total = part(self.local, core, piece_rows)[...]
                if cores == 2:
                    total = total + self.got1[...]
                self.sum1[...] = total
            if stage == 2:
                total = part(self.sum1, spot, block_rows)[...]
                for k in range(1, planes):
                    total = total + part(self.got2, k, block_rows)[...]
                self.sum2[...] = total
                self.got3[pl.ds(0, block_rows), :] = total
            if stage == 3:
                total = part(self.got3, lax.rem(places.z, zs), block_rows)[...]
                for q in range(1, zs):
                    total = total + part(self.got3, lax.rem(places.z + zs - q, zs), block_rows)[...]
                part(self.whole, core * planes + spot, block_rows)[...] = total
            if stage == 5:
                self.local[...] = self.whole[...]
            for copy in self.copies(stage):
                copy.start()

    def backward(turn, _):
        l = layers - 1 - turn
        e = after + turn

        def advance(stage):
            @pl.when(turn > 0)
            def _():
                Sum(l + 1).go(stage)

        keep[l, 0:1] = stat[e, 1:2]
        keep[l, 1:2] = stat[e, 0:1]
        for q, piece in enumerate(parts_of(w_conv[l].T, 2)):
            wt[q] = piece
        gain = norm_ref[l, 0:1]
        totals = stats_finish(e) * gain * (1.0 / nodes)
        mean, inverse = normed[l + 1, 0:1], normed[l + 1, 1:2]

        def enter(s, total):
            span = rows_of(s, tile)
            active = act[l + 1, span]
            rated = (active - mean) * inverse
            grad = inverse * (gh[span, :] * gain - totals[0:1] - rated * totals[1:2])
            grad = jnp.where(active > 0.0, grad, 0.0)
            pieces = parts_of(grad, 2)
            for dst, piece in zip(gs, pieces):
                dst[span, :] = piece
            joined = dots(pieces, [wt[0], wt[1]])
            gh[span, :] = joined[:, :width]
            for dst, piece in zip(ps, parts_of(joined[:, width:], 2)):
                dst[span, :] = piece
            return total + folded(grad)

        total = lax.fori_loop(0, tiles, enter, zeros8)
        keep[l, 2:3] = column_sums(total)

        @pl.when(l > 0)
        def _():
            told(l - 1)

        advance(1)
        copies = rims_of(e, out_rim.at[0], out_rim.at[1])

        def rims_out(which, _):
            cols = pl.ds(pl.multiple_of(rows + which * halo, 128), halo)
            out_rim[which] = dots([q[:, cols] for q in a], [q[own_cols, :] for q in ps], TURNED)
            for at, go in ((0, not_first), (1, not_last)):
                start_if(jnp.logical_and(go, which == at), copies[at])
            return 0

        lax.fori_loop(0, 2, rims_out, 0)
        advance(2)

        def spread_back(s, _):
            span = rows_of(s, height)
            gh[span, :] += dots([q[:, span] for q in a], [q[own_cols, :] for q in ps], TURNED)
            return 0

        lax.fori_loop(0, rows // height, spread_back, 0)
        advance(3)
        slot = lax.rem(e, 2)
        for which, go, start in ((1, not_last, rows - halo), (0, not_first, 0)):
            @pl.when(go)
            def _():
                remote(rim.at[slot, which], rim.at[slot, which], rim_send.at[e, which], rim_recv.at[e, which],
                       peer_place(batch, lax.rem(block + 1, n))).wait_recv()
                gh[pl.ds(start, halo), :] += rim[slot, which]

        below_mean, below_inverse = normed[l, 0:1], normed[l, 1:2]

        def tail_sums(s, sums):
            span = rows_of(s, tile)
            grad = gh[span, :]
            return sums[0] + folded(grad), sums[1] + folded(grad * ((act[l, span] - below_mean) * below_inverse))

        sums = lax.fori_loop(0, tiles, tail_sums, (zeros8, zeros8))
        stat[e + 1, 0:1] = column_sums(sums[0])
        stat[e + 1, 1:2] = column_sums(sums[1])

        @pl.when(l > 0)
        def _():
            stats_start(e + 1)

        rims_sent(copies)
        advance(4)
        base = conv_rows(l)
        where = pl.ds(base, width)
        under = pl.ds(pl.multiple_of(base + width, 8), width)
        scale, offset = normed[l, 2:3], normed[l, 3:4]
        pay[pl.ds(base, big), :] = jnp.zeros((big, width), f32)

        def weigh(s, _):
            span = rows_of(s, height)
            h = act[l, span] * scale + offset
            grad = [q[span, :] for q in gs]
            pay[where, :] += dots(parts_of(h, 2), grad, TURNED)
            pay[under, :] += dots(parts_of(agg[l, span], 2), grad, TURNED)
            return 0

        lax.fori_loop(0, rows // height, weigh, 0)
        advance(5)

        @pl.when(l > 0)
        def _():
            Sum(l).go(0)

        return 0

    lax.fori_loop(0, layers, backward, 0)
    pay[at_small : at_small + 1, :] = stat[after + layers, 0:1]
    for l in range(layers):
        pay[at_norm + 2 * l : at_norm + 2 * l + 2, :] = keep[l, 0:2]
        pay[at_small + 1 + l : at_small + 2 + l, :] = keep[l, 2:3]
    feat = x_ref.shape[1]
    pay[pl.ds(rows_at[0], rows_at[1] - rows_at[0]), :] = jnp.zeros((rows_at[1] - rows_at[0], width), f32)

    def weigh_in(s, total):
        span = rows_of(s, height)
        return total + dots(parts_of(x_ref[span, :], 2), parts_of(gh[span, :], 2), TURNED)

    pay[pl.ds(rows_at[0], feat), :] = lax.fori_loop(0, rows // height, weigh_in, jnp.zeros((feat, width), f32))
    for copies in late:
        arrived(copies)


def step_call(n, nb, layers, nodes, all_nodes, classes, rows_at, summed_rows, x, labels, sums, biases, norms, head_bias,
              picks, pick_row, adjacency, shards):
    rows = x.shape[0]
    width = biases.shape[1]
    cols = adjacency[0].shape[1]
    halo = (cols - rows) // 2
    feat = x.shape[1]
    vmem = pl.BlockSpec(memory_space=pltpu.VMEM)
    smem = pl.BlockSpec(memory_space=pltpu.SMEM)
    hbm = pl.BlockSpec(memory_space=pl.ANY)
    dma = pltpu.SemaphoreType.DMA
    items = 2 + layers + 3
    exchanges = 2 * layers + 1
    _, ys, across, zs = plane_split(nb, n)
    hops = 2 * ys * across + zs + 1
    return pl.pallas_call(
        functools.partial(step_kernel, n, nb, layers, nodes, all_nodes, classes, rows_at, summed_rows),
        out_shape=(
            jax.ShapeDtypeStruct((summed_rows + (layers - 1) * 2 * width, width), f32),
            jax.ShapeDtypeStruct((width, feat), f32),
            jax.ShapeDtypeStruct((layers, 2 * width, width), f32),
            jax.ShapeDtypeStruct((width, LANES), f32),
        ),
        in_specs=[vmem] * 6 + [smem, vmem] + [hbm] * 8,
        out_specs=(vmem, hbm, hbm, hbm),
        scratch_shapes=[
            pltpu.VMEM((layers + 1, rows, width), f32),
            pltpu.VMEM((layers, rows, width), f32),
            pltpu.VMEM((rows, cols), bf16),
            pltpu.VMEM((rows, cols), bf16),
            pltpu.VMEM((cols, width), bf16),
            pltpu.VMEM((cols, width), bf16),
            pltpu.VMEM((rows, width), bf16),
            pltpu.VMEM((rows, width), bf16),
            pltpu.VMEM((rows, width), f32),
            pltpu.VMEM((2, 2, halo, width), f32),
            pltpu.VMEM((2, halo, width), f32),
            pltpu.VMEM((rows, LANES), f32),
            pltpu.VMEM((n, 8, LANES), f32),
            pltpu.VMEM((n, 8, LANES), f32),
            pltpu.VMEM((exchanges + 1, 2, width), f32),
            pltpu.VMEM((exchanges, n, 2, width), f32),
            pltpu.VMEM((width, feat), f32),
            pltpu.VMEM((layers, 2 * width, width), f32),
            pltpu.VMEM((width, LANES), f32),
            pltpu.VMEM((2, width, 2 * width), bf16),
            dma((2 * rows // 512,)),
            dma((exchanges, n)),
            dma((exchanges, n)),
            dma((exchanges, 2)),
            dma((exchanges, 2)),
            dma((n,)),
            dma((n,)),
            dma((items, nb)),
            dma((items, nb)),
            dma((items,)),
            dma((layers - 1, hops)),
            dma((layers - 1, hops)),
            pltpu.SemaphoreType.REGULAR((layers - 1,)),
            pltpu.VMEM((layers + 1, 4, width), f32),
            pltpu.VMEM((layers, 4, width), f32),
        ],
        compiler_params=pltpu.CompilerParams(collective_id=1, has_side_effects=True, vmem_limit_bytes=63 << 20),
        name="forward_backward",
    )(x, labels, sums, biases[:, None], norms, head_bias, picks, pick_row, *adjacency, *shards)


def update_kernel(n, nb, layers, all_nodes, rows_at, classes, ns_parts, scales, summed_rows, pay, mom_in, mom_conv, mom_head, w_in,
                  w_conv, w_head, biases, norms, head_bias, fb, fn, fh, sb, sn, sh, power, *refs):
    (loss_o, in_o, conv_o, head_o, min_o, mconv_o, mhead_o, b_o, n_o, h_o, fb_o, fn_o, fh_o, sb_o, sn_o, sh_o) = refs[:16]
    (got1, sum1, got2, sum2, got3, full, gram, poly, small_gram, small_poly, mconv, send, recv) = refs[16:]
    places = Places(n, nb)
    cores, planes, zs = places.cores, places.planes, places.zs
    core, spot, z = places.core, places.spot, places.z
    plane_peer, column_peer, core_peer = places.plane_peer, places.column_peer, places.core_peer
    here_b = places.b
    width = w_conv.shape[2]
    barrier = pltpu.get_barrier_semaphore()
    for peer in places.peers:
        pl.semaphore_signal(barrier, inc=1, device_id=peer, device_id_type=pl.DeviceIdType.MESH)

    def kdot(left, right, dims=((1,), (0,))):
        return dots(parts_of(left, ns_parts), parts_of(right, ns_parts), dims)

    def eye(k):
        return (lax.broadcasted_iota(jnp.int32, (k, k), 0) == lax.broadcasted_iota(jnp.int32, (k, k), 1)).astype(f32)

    def begin(moment, grams, i):
        size = jnp.sqrt(jnp.sum(moment * moment)) + 1e-07
        g = kdot(moment, moment, TURNED) / (size * size)
        grams[i] = g
        return size

    def step(grams, polys, which, early, late):
        k = grams.shape[1]
        count = len(which)
        a1 = [grams[i] for i in which]
        a2 = [kdot(v, v) for v in a1]
        p = [newton_a * eye(k) + newton_b * v + newton_c * u for v, u in zip(a1, a2)]
        if early:
            q = p
        else:
            q = [kdot(v, polys[i]) for i, v in zip(which, p)]
        if not late:
            pa = [kdot(v, u) for v, u in zip(p, a1)]
            nxt = [kdot(v, u) for v, u in zip(pa, p)]
        for j in range(count):
            polys[which[j]] = q[j]
            if not late:
                grams[which[j]] = nxt[j]

    sizes = {}
    ready = tuple(range(1, layers))

    def start_ready():
        for l in ready:
            mconv[l] = muon_decay * mom_conv[l] + pay[summed_rows + (l - 1) * 2 * width : summed_rows + l * 2 * width]
            sizes[l] = begin(mconv[l], gram, l)

    def middle(count, grams, polys, which):
        lax.fori_loop(0, count, lambda _, c: (step(grams, polys, which, False, False), c)[1], 0)

    pl.semaphore_wait(barrier, len(places.peers))
    used = [0]

    def go(src, dst, to):
        i = used[0]
        used[0] += 1
        copy = remote(src, dst, send.at[i], recv.at[i], to)
        copy.start()
        return copy

    def settle(copies):
        for copy in copies:
            copy.wait()

    half_rows = summed_rows // cores
    block_rows = half_rows // planes
    m = block_rows // zs

    def part(ref, index, count):
        return ref.at[pl.ds(pl.multiple_of(index * count, 8), count)]

    if cores == 2:
        copies = [go(part(pay, 1 - core, half_rows), got1, core_peer)]
        start_ready()
        settle(copies)
        sum1[...] = part(pay, core, half_rows)[...] + got1[...]
    else:
        start_ready()
        sum1[...] = pay[pl.ds(0, half_rows), :]
    copies = []
    for k in range(1, planes):
        p, to = plane_peer(k)
        copies.append(go(part(sum1, p, block_rows), got2.at[k], to))
    step(gram, poly, ready, True, False)
    middle(1, gram, poly, ready)
    settle(copies)
    total = part(sum1, spot, block_rows)[...]
    for k in range(1, planes):
        total = total + got2[k]
    sum2[...] = total
    copies = []
    for k in range(1, zs):
        q, to = column_peer(k)
        copies.append(go(part(sum2, q, m), got3.at[k], to))
    middle(1, gram, poly, ready)
    settle(copies)
    total = part(sum2, z, m)[...]
    for k in range(1, zs):
        total = total + got3[k]
    block = core * planes + spot
    mine = part(full, block * zs + z, m)
    mine[...] = total
    copies = [go(mine, mine, column_peer(k)[1]) for k in range(1, zs)]
    middle(1, gram, poly, ready)
    settle(copies)
    mine = part(full, block, block_rows)
    copies = [go(mine, mine, plane_peer(k)[1]) for k in range(1, planes)]
    step(gram, poly, ready, False, True)
    scale_in, scale_conv, scale_head = scales
    span = w_conv.shape[1]

    def turn_conv(l):
        own = mconv[l, pl.ds(pl.multiple_of(here_b * span, 8), span)]
        mconv_o[l] = own
        w = w_conv[l]
        turn = kdot(own, poly[l]) * (scale_conv / sizes[l])
        conv_o[l] = w - muon_rate * (turn + muon_shrink * w)

    for l in ready:
        turn_conv(l)
    settle(copies)
    if cores == 2:
        mine = part(full, core, half_rows)
        settle([go(mine, mine, core_peer)])
    summed = full[...]
    mconv[0] = muon_decay * mom_conv[0] + summed[: 2 * width]
    sizes[0] = begin(mconv[0], gram, 0)
    feat = w_in.shape[1]
    half = width // 2
    grad_in = summed[rows_at[0] : rows_at[0] + LANES].T
    grad_head = summed[rows_at[1] : rows_at[1] + half]
    moment_in = muon_decay * mom_in[...] + jnp.where(lax.broadcasted_iota(jnp.int32, (width, LANES), 1) < feat, grad_in, 0.0)
    moment_head = muon_decay * mom_head[...] + jnp.concatenate([grad_head[:, :LANES], grad_head[:, LANES:]], 0)
    sizes[layers] = begin(moment_in, small_gram, 0)
    sizes[layers + 1] = begin(moment_head, small_gram, 1)

    def both(early, late):
        step(gram, poly, (0,), early, late)
        step(small_gram, small_poly, (0, 1), early, late)

    both(True, False)
    lax.fori_loop(1, NS_STEPS - 1, lambda _, c: (both(False, False), c)[1], 0)
    both(False, True)
    turn_conv(0)
    span = w_in.shape[0]
    mconv[0, pl.ds(0, width), 0:LANES] = moment_in
    mconv[0, pl.ds(0, width), LANES : 2 * LANES] = moment_head
    own = mconv[0, pl.ds(pl.multiple_of(here_b * span, 8), span), 0:LANES]
    min_o[...] = own[:, :feat]
    w = w_in[...]
    turn = kdot(own, small_poly[0]) * (scale_in / sizes[layers])
    in_o[...] = w - muon_rate * (turn[:, :feat] + muon_shrink * w)
    span = w_head.shape[0]
    own = mconv[0, pl.ds(pl.multiple_of(here_b * span, 8), span), LANES : 2 * LANES]
    mhead_o[...] = own[:, :classes]
    w = w_head[...]
    turn = kdot(own, small_poly[1]) * (scale_head / sizes[layers + 1])
    head_o[...] = w - muon_rate * (turn[:, :classes] + muon_shrink * w)

    def adamw(param, grad, first, second, outs):
        first = adam_first_decay * first + (1.0 - adam_first_decay) * grad
        second = adam_second_decay * second + (1.0 - adam_second_decay) * grad * grad
        first_hat = first / power[0]
        second_hat = second / power[1]
        outs[0][...] = param - adam_rate * (first_hat / (jnp.sqrt(second_hat) + adam_epsilon) + adam_shrink * param)
        outs[1][...] = first
        outs[2][...] = second

    at = rows_at[2]
    adamw(biases[...], summed[at : at + layers + 1], fb[...], sb[...], (b_o, fb_o, sb_o))
    at = at + layers + 1
    adamw(norms[...], summed[at : at + 2 * layers], fn[...], sn[...], (n_o, fn_o, sn_o))
    at = at + 2 * layers
    adamw(head_bias[...], summed[at : at + 1, :classes], fh[...], sh[...], (h_o, fh_o, sh_o))
    loss_o[...] = jnp.sum(summed[at + 1 : at + 2], axis=1, keepdims=True) / all_nodes


def update_call(n, nb, layers, all_nodes, rows_at, classes, ns_parts, scales, summed_rows, pay, moments, shards, smalls, power):
    cores, ys, xs, zs = plane_split(nb, n)
    planes = ys * xs
    width = pay.shape[1]
    m = summed_rows // (n * nb)
    w_in, w_conv, w_head = shards
    vmem = pl.BlockSpec(memory_space=pltpu.VMEM)
    smem = pl.BlockSpec(memory_space=pltpu.SMEM)
    like = [jax.ShapeDtypeStruct(v.shape, f32) for v in (w_in, w_conv, w_head)]
    like_small = [jax.ShapeDtypeStruct(v.shape, f32) for v in smalls[:3]]
    copies = 2 * (planes + zs)
    return pl.pallas_call(
        functools.partial(update_kernel, n, nb, layers, all_nodes, rows_at, classes, ns_parts, scales, summed_rows),
        out_shape=tuple([jax.ShapeDtypeStruct((1, 1), f32)] + like + like + like_small * 3),
        in_specs=[vmem] * 16 + [smem],
        out_specs=(vmem,) * 16,
        scratch_shapes=[
            pltpu.VMEM((zs * planes * m, width), f32),
            pltpu.VMEM((zs * planes * m, width), f32),
            pltpu.VMEM((planes, zs * m, width), f32),
            pltpu.VMEM((zs * m, width), f32),
            pltpu.VMEM((zs, m, width), f32),
            pltpu.VMEM((summed_rows, width), f32),
            pltpu.VMEM((layers, width, width), f32),
            pltpu.VMEM((layers, width, width), f32),
            pltpu.VMEM((2, LANES, LANES), f32),
            pltpu.VMEM((2, LANES, LANES), f32),
            pltpu.VMEM((layers, 2 * width, width), f32),
            pltpu.SemaphoreType.DMA((copies,)),
            pltpu.SemaphoreType.DMA((copies,)),
        ],
        compiler_params=pltpu.CompilerParams(collective_id=2, has_side_effects=True, vmem_limit_bytes=48 << 20),
        name="sum_and_update",
    )(pay, *moments, *shards, *smalls, power)


NS_PARTS = 3


def per_device(
    n_batch,
    n_rows,
    features,
    edge_rows,
    edge_weight,
    halo_counts,
    labels,
    pair_rows,
    step,
    w_in,
    w_conv,
    w_head,
    biases,
    norm_params,
    head_bias,
    mom_in,
    mom_conv,
    mom_head,
    first_bias,
    first_norm,
    first_head,
    second_bias,
    second_norm,
    second_head,
):
    rows_dev = features.shape[1]
    halo_rows = rows_dev // 4
    edge_count = edge_rows.shape[3]
    layers, hid = w_conv.shape[0], w_conv.shape[2]
    feat, classes = w_in.shape[0], w_head.shape[1]
    pairs = pair_rows.shape[3]
    node_count = rows_dev * n_rows
    all_nodes = node_count * n_batch
    flat = [
        edge_rows.reshape(2 * edge_count).astype(f32),
        edge_weight.reshape(edge_count),
        labels.reshape(rows_dev).astype(f32),
        pair_rows.reshape(n_rows * pairs).astype(f32),
    ]
    flat = jnp.concatenate(flat)
    flat = jnp.pad(flat, (0, -flat.shape[0] % (8 * LANES))).reshape(-1, LANES)
    flat = redeal(flat, n_batch, n_rows)
    inputs = redeal(features, n_batch, n_rows)[0]
    e = edge_count // LANES
    block = my_place()[1]
    wide = (rows_dev + 2 * halo_rows) // TILE
    rims = jnp.stack([(block > 0).astype(jnp.int32), (block < n_rows - 1).astype(jnp.int32)])
    order = order_edges(flat[:e], flat[e : 2 * e], flat[2 * e : 3 * e], wide)
    *adjacency, row_sums = fill(order, rims, rows_dev // TILE, wide, halo_rows // TILE, 2)
    label_rows = rows_dev // LANES
    node_labels = flat[3 * e : 3 * e + label_rows]
    picks = flat[3 * e + label_rows :].reshape(-1)[: n_rows * pairs].astype(jnp.int32)
    spread = jnp.pad(picks.reshape(n_rows, pairs), ((0, 0), (0, 8 - pairs)), constant_values=-1).reshape(1, n_rows * 8)
    spread = jnp.pad(spread, ((0, 0), (0, -spread.shape[1] % LANES)), constant_values=-1)
    at_in = 2 * hid
    at_head = at_in + -(-feat // 8) * 8
    at_small = at_head + hid // 2
    used = at_small + layers + 1 + 2 * layers + 2
    unit = 8 * n_rows * n_batch
    pay_rows = -(-used // unit) * unit
    rows_at = (at_in, at_head, at_small)
    turned = [
        w_in.T,
        w_conv,
        jnp.pad(w_head, ((0, 0), (0, LANES - classes))),
        mom_in.T,
        mom_conv,
        jnp.pad(mom_head, ((0, 0), (0, LANES - classes))),
    ]
    pay, full_min, full_mconv, full_mhead = step_call(
        n_rows,
        n_batch,
        layers,
        node_count,
        all_nodes,
        classes,
        rows_at,
        pay_rows,
        inputs,
        node_labels,
        row_sums,
        biases,
        norm_params,
        jnp.pad(head_bias, (0, LANES - classes))[None],
        picks,
        spread,
        adjacency,
        turned,
    )
    count = step[0].astype(f32)
    power = jnp.stack([1.0 - jnp.power(adam_first_decay, count), 1.0 - jnp.power(adam_second_decay, count)])
    scales = (
        math.sqrt(max(1.0, hid / feat)),
        math.sqrt(max(1.0, hid / (2 * hid))),
        math.sqrt(max(1.0, classes / hid)),
    )
    norm_rows = (2 * layers, hid)
    smalls = (
        biases,
        norm_params.reshape(norm_rows),
        head_bias[None],
        first_bias,
        first_norm.reshape(norm_rows),
        first_head[None],
        second_bias,
        second_norm.reshape(norm_rows),
        second_head[None],
    )
    outs = update_call(
        n_rows,
        n_batch,
        layers,
        all_nodes,
        rows_at,
        classes,
        NS_PARTS,
        scales,
        pay_rows,
        pay,
        (jnp.pad(full_min, ((0, 0), (0, LANES - feat))), full_mconv, full_mhead),
        (turned[0], w_conv, w_head),
        smalls,
        power,
    )
    loss, new_in, new_conv, new_head, moment_in, moment_conv, moment_head = outs[:7]
    rest = []
    for i in range(0, 9, 3):
        rest += [outs[7 + i], outs[8 + i].reshape(layers, 2, hid), outs[9 + i][0]]
    return (loss[0, 0], new_in.T, new_conv, new_head, moment_in.T, moment_conv, moment_head, *rest)


def solution(mesh):
    in_specs = (
        P("batch", "rows", None),
        P("batch", "rows", None, None),
        P("batch", "rows", None),
        P("batch", "rows", None),
        P("batch", "rows"),
        P("batch", "rows", None, None),
        P(),
        P(None, "batch"),
        P(None, "batch", None),
        P("batch", None),
        P(),
        P(),
        P(),
        P(None, "batch"),
        P(None, "batch", None),
        P("batch", None),
        P(),
        P(),
        P(),
        P(),
        P(),
        P(),
    )
    out_specs = (
        P(),
        P(None, "batch"),
        P(None, "batch", None),
        P("batch", None),
        P(None, "batch"),
        P(None, "batch", None),
        P("batch", None),
        P(),
        P(),
        P(),
        P(),
        P(),
        P(),
        P(),
        P(),
        P(),
    )
    body = functools.partial(per_device, mesh.shape["batch"], mesh.shape["rows"])
    return jax.shard_map(body, mesh=mesh, in_specs=in_specs, out_specs=out_specs, check_vma=False)
```

```python
import functools
import math

import jax
import jax.numpy as jnp
from jax import lax
from jax.experimental import pallas as pl
from jax.experimental.pallas import tpu as pltpu
from jax.sharding import PartitionSpec as P

NS_STEPS = 5

f32 = jnp.float32
bf16 = jnp.bfloat16
LANES = 128
TILE = 256
highest = lax.Precision.HIGHEST
norm_epsilon = 1e-05
pair_weight = 0.05
newton_a = 3.4445
newton_b = -4.775
newton_c = 2.0315
muon_decay = 0.9
muon_rate = 0.5
muon_shrink = 0.01
adam_first_decay = 0.9
adam_second_decay = 0.999
adam_epsilon = 1e-08
adam_rate = 0.1
adam_shrink = 0.01


def swap(b, r):
    return 2 * (b // 2) + r % 2, 2 * (r // 2) + b % 2


def flat_pairs(n_batch, n_rows, move):
    pairs = []
    for b in range(n_batch):
        for r in range(n_rows):
            to = move(b, r)
            if to is not None:
                pairs.append((b * n_rows + r, to[0] * n_rows + to[1]))
    return pairs


def redeal(array, n_batch, n_rows):
    return lax.ppermute(array, ("batch", "rows"), flat_pairs(n_batch, n_rows, swap))


def peer_place(batch, block):
    two = jnp.int32(2)
    return (
        two * lax.div(batch, two) + lax.rem(block, two),
        two * lax.div(block, two) + lax.rem(batch, two),
    )


def my_place():
    return peer_place(lax.axis_index("batch"), lax.axis_index("rows"))


def put_in_order(wide, to_ref, from_ref, w_ref, key_out, w_out, col_out, range_out):
    to, frm = to_ref[...].astype(jnp.int32), from_ref[...].astype(jnp.int32)
    key = (((to >> 8) * wide + (frm >> 8)) << 16) | ((to & 255) << 8) | (frm & 255)
    shape3 = (16, 8, LANES)
    key = key.astype(f32).reshape(shape3)
    w = w_ref[...].reshape(shape3)
    sub = lax.broadcasted_iota(jnp.int32, shape3, 1)
    lane = lax.broadcasted_iota(jnp.int32, shape3, 2)
    vreg = lax.broadcasted_iota(jnp.int32, shape3, 0)
    place = vreg + 16 * sub + 128 * lane
    for phase in range(14):
        for bit in range(phase, -1, -1):
            down = ((place >> (phase + 1)) & 1) == 1
            if bit < 4:
                view = (16 >> (bit + 1), 2, 1 << bit, 8, LANES)
                kv, wv = key.reshape(view), w.reshape(view)
                dv = down.astype(jnp.int32).reshape(view)[:, 0] == 1
                a, b, wa, wb = kv[:, 0], kv[:, 1], wv[:, 0], wv[:, 1]
                turn = jnp.logical_xor(a > b, dv)
                key = jnp.stack([jnp.where(turn, b, a), jnp.where(turn, a, b)], 1).reshape(shape3)
                w = jnp.stack([jnp.where(turn, wb, wa), jnp.where(turn, wa, wb)], 1).reshape(shape3)
            else:
                if bit < 7:
                    axis, gap, size, pos = 1, 1 << (bit - 4), 8, sub
                else:
                    axis, gap, size, pos = 2, 1 << (bit - 7), LANES, lane
                low = (pos & gap) == 0
                kp = jnp.where(low, pltpu.roll(key, size - gap, axis), pltpu.roll(key, gap, axis))
                wp = jnp.where(low, pltpu.roll(w, size - gap, axis), pltpu.roll(w, gap, axis))
                smaller = jnp.logical_xor(low, down)
                take = jnp.where(smaller, kp, key) < jnp.where(smaller, key, kp)
                key = jnp.where(take, kp, key)
                w = jnp.where(take, wp, w)
    flat = key.reshape(LANES, LANES)
    key_out[...] = flat.T.astype(jnp.int32)
    w_out[...] = w.reshape(LANES, LANES).T
    start = (lax.broadcasted_iota(jnp.int32, (8, LANES), 1).astype(f32) * 65536.0)[None]
    below = jnp.zeros(shape3, f32)
    upto = jnp.zeros(shape3, f32)
    for c in range(LANES):
        wide_key = jnp.broadcast_to(flat[:, c : c + 1], (LANES, LANES))
        col_out[c] = (wide_key - jnp.floor(wide_key * (1.0 / 256.0)) * 256.0).astype(bf16)
        wide_key = wide_key.reshape(shape3)
        below = below + jnp.where(wide_key < start, 1.0, 0.0)
        upto = upto + jnp.where(wide_key < start + 65536.0, 1.0, 0.0)
    range_out[...] = jnp.zeros_like(range_out)
    n_below = jnp.sum(below.reshape(LANES, LANES), axis=0, keepdims=True)
    n_upto = jnp.sum(upto.reshape(LANES, LANES), axis=0, keepdims=True)
    first = jnp.floor(n_below * (1.0 / 128.0))
    end = jnp.floor((n_upto + 127.0) * (1.0 / 128.0))
    range_out[0:1] = first.astype(jnp.int32)
    range_out[1:2] = jnp.where(n_upto > n_below, end, first).astype(jnp.int32)


def fill_kernel(wide, rim, chunk, parts, rims, to_ref, from_ref, weight_ref, *refs):
    outs, sums = refs[:parts], refs[parts]
    acc, rowacc, key_ref, w_ref, col_ref, ranges, span_of, sem = refs[parts + 1 :]
    i = pl.program_id(0)

    @pl.when(i == 0)
    def _():
        put_in_order(wide, to_ref, from_ref, weight_ref, key_ref, w_ref, col_ref, ranges)
        copy = pltpu.make_async_copy(ranges, span_of, sem)
        copy.start()
        copy.wait()

    pack = 16
    shape = (TILE // pack, pack, LANES)
    rows = lax.broadcasted_iota(jnp.int32, shape, 0) * pack + lax.broadcasted_iota(jnp.int32, shape, 1)
    rows = rows.astype(f32).astype(bf16)
    lanes = lax.broadcasted_iota(jnp.int32, (LANES, LANES), 1).astype(f32)
    lanes0, lanes1 = lanes.astype(bf16), (lanes + 128.0).astype(bf16)
    one, zero = jnp.ones((), bf16), jnp.zeros((), bf16)

    def spread(row):
        return jnp.broadcast_to(row, (pack, LANES)).astype(bf16)[None]

    rowacc[...] = jnp.zeros_like(rowacc)

    def tile(j, _):
        b = i * wide + j
        first, end = span_of[0, b], span_of[1, b]
        end = jnp.where(jnp.logical_and(j < rim, rims[0] == 0), first, end)
        end = jnp.where(jnp.logical_and(j >= wide - rim, rims[1] == 0), first, end)
        slot = jnp.where(j < rim, wide - 2 * rim + j, jnp.where(j < wide - rim, j - rim, j))
        cols = pl.ds(pl.multiple_of(slot * TILE, TILE), TILE)

        @pl.when(end <= first)
        def _():
            for out in outs:
                out[:, cols] = jnp.zeros((TILE, TILE), bf16)

        @pl.when(end > first)
        def _():
            def part(base, c):
                row = jnp.minimum(base + c, LANES - 1)
                here = key_ref[pl.ds(row, 1), :] - (b << 16)
                if c:
                    here = jnp.where(base + c < end, here, -1)
                at = rows == spread((here >> 8).astype(f32))
                rest = w_ref[pl.ds(row, 1), :]
                left = []
                for q in range(parts):
                    piece = rest.astype(bf16).astype(f32)
                    rest = rest - piece
                    left.append(jnp.where(at, spread(piece), zero).reshape(TILE, LANES))
                col = col_ref[row]
                right = jnp.concatenate(
                    [jnp.where(col == lanes0, one, zero), jnp.where(col == lanes1, one, zero)], 1
                )
                return left, right

            def get(base):
                made = [part(base, c) for c in range(chunk)]
                lhs = jnp.concatenate([m[0][q] for q in range(parts) for m in made], 1)
                rhs = jnp.concatenate([m[1] for m in made] * parts, 0)
                return jnp.dot(lhs, rhs, preferred_element_type=f32)

            acc[...] = get(first)

            def more(t, _):
                acc[...] += get(first + t * chunk)
                return 0

            lax.fori_loop(1, lax.div(end - first + chunk - 1, chunk), more, 0)
            rest = acc[...]
            rowacc[...] += rest[:, :LANES] + rest[:, LANES:]
            for out in outs:
                piece = rest.astype(bf16)
                out[:, cols] = piece
                rest = rest - piece.astype(f32)

        return 0

    lax.fori_loop(0, wide, tile, 0)
    total = jnp.sum(rowacc[...], axis=1, keepdims=True)
    for half in range(TILE // LANES):
        column = jnp.broadcast_to(total[half * LANES : (half + 1) * LANES], (LANES, LANES))
        sums[0, half : half + 1] = column.T[0:1]


def fill(to, frm, weights, rims, tiles, wide, rim, parts, chunk=4):
    cols = wide * TILE
    return pl.pallas_call(
        functools.partial(fill_kernel, wide, rim, chunk, parts),
        out_shape=tuple(jax.ShapeDtypeStruct((tiles * TILE, cols), bf16) for _ in range(parts))
        + (jax.ShapeDtypeStruct((tiles, TILE // LANES, LANES), f32),),
        grid_spec=pltpu.PrefetchScalarGridSpec(
            num_scalar_prefetch=1,
            grid=(tiles,),
            in_specs=[pl.BlockSpec((LANES, LANES), lambda i, *_: (0, 0))] * 3,
            out_specs=tuple(pl.BlockSpec((TILE, cols), lambda i, *_: (i, 0)) for _ in range(parts))
            + (pl.BlockSpec((1, TILE // LANES, LANES), lambda i, *_: (i, 0, 0)),),
            scratch_shapes=[
                pltpu.VMEM((TILE, TILE), f32),
                pltpu.VMEM((TILE, LANES), f32),
                pltpu.VMEM((LANES, LANES), jnp.int32),
                pltpu.VMEM((LANES, LANES), f32),
                pltpu.VMEM((LANES, LANES, LANES), bf16),
                pltpu.VMEM((8, LANES), jnp.int32),
                pltpu.SMEM((8, LANES), jnp.int32),
                pltpu.SemaphoreType.DMA,
            ],
        ),
        compiler_params=pltpu.CompilerParams(vmem_limit_bytes=50 << 20),
        name="adjacency_tiles",
    )(rims, to, frm, weights)


def parts_of(x, count):
    found = []
    for q in range(count):
        piece = x.astype(bf16)
        found.append(piece)
        if q + 1 < count:
            x = x - piece.astype(f32)
    return found


def pair_list(count):
    return [(p, q) for p in range(count) for q in range(count) if p + q < count]


def dots(left, right, dims=((1,), (0,))):
    total = None
    for p, q in pair_list(len(left)):
        piece = lax.dot_general(left[p], right[q], (dims, ((), ())), preferred_element_type=f32)
        total = piece if total is None else total + piece
    return total


def remote(src, dst, send, recv, to):
    return pltpu.make_async_remote_copy(
        src_ref=src,
        dst_ref=dst,
        send_sem=send,
        recv_sem=recv,
        device_id=to,
        device_id_type=pl.DeviceIdType.MESH,
    )


def column_sums(x):
    return jnp.sum(x, axis=0, keepdims=True)


def folded(x):
    return jnp.sum(x.reshape(x.shape[0] // 8, 8, x.shape[1]), axis=0)


def plane_split(nb, n):
    cores = 2 if nb % 2 == 0 else 1
    across = 1
    while across * across * 4 <= n and n % (across * 2) == 0:
        across *= 2
    return cores, nb // cores, across, n // across


class Places:
    def __init__(self, n, nb):
        self.cores, ys, self.xs, self.zs = plane_split(nb, n)
        self.planes = ys * self.xs
        self.b, self.r = lax.axis_index("batch"), lax.axis_index("rows")
        self.core, y = lax.rem(self.b, self.cores), lax.div(self.b, self.cores)
        self.x, self.z = lax.rem(self.r, self.xs), lax.div(self.r, self.xs)
        self.spot = y * self.xs + self.x
        self.core_peer = (y * self.cores + lax.rem(self.core + 1, self.cores), self.r)
        self.peers = [self.plane_peer(k)[1] for k in range(1, self.planes)]
        self.peers += [self.column_peer(k)[1] for k in range(1, self.zs)]
        if self.cores == 2:
            self.peers.append(self.core_peer)

    def plane_peer(self, k):
        p = lax.rem(self.spot + k, self.planes)
        return p, (lax.div(p, self.xs) * self.cores + self.core, self.z * self.xs + lax.rem(p, self.xs))

    def column_peer(self, k):
        q = lax.rem(self.z + k, self.zs)
        return q, (self.b, q * self.xs + self.x)


TURNED = ((0,), (0,))
GATHERED = 3


def step_kernel(n, nb, layers, nodes, all_nodes, classes, rows_at, summed_rows, label_at, *refs):
    (x_ref, label_ref, sums_ref, bias_ref, norm_ref, head_bias_ref, pick_smem, pick_row, a1_hbm, a2_hbm) = refs[:10]
    own_in, own_conv, own_head, own_min, own_mconv, own_mhead = refs[10:16]
    pay, full_min, full_mconv, full_mhead = refs[16:20]
    (act, agg, a1, a2, p1, p2, g1, g2, gh, rim, out_rim, logit, sent, got, stat, held, w_in, w_conv, w_head,
     wt, a_sem, stat_send, stat_recv, rim_send, rim_recv, pair_send, pair_recv, w_send, w_recv, w_own, sum_send, sum_recv,
     ready, normed, keep, stood, laid_head, laid_mhead, wide_bias) = refs[20:]
    rows, width = act.shape[1], act.shape[2]
    halo = rim.shape[2]
    a, ps, gs = (a1, a2), (p1, p2), (g1, g2)
    here_b, here_r = lax.axis_index("batch"), lax.axis_index("rows")
    batch, block = my_place()
    first, last = block == 0, block == n - 1
    not_first, not_last = jnp.logical_not(first), jnp.logical_not(last)

    barrier = pltpu.get_barrier_semaphore()
    for k in range(1, n):
        pl.semaphore_signal(
            barrier, inc=1, device_id=peer_place(batch, lax.rem(block + k, n)), device_id_type=pl.DeviceIdType.MESH
        )
    for k in range(1, nb):
        pl.semaphore_signal(
            barrier, inc=1, device_id=(lax.rem(here_b + k, nb), here_r), device_id_type=pl.DeviceIdType.MESH
        )
    places = Places(n, nb)
    for peer in places.peers:
        pl.semaphore_signal(barrier, inc=1, device_id=peer, device_id_type=pl.DeviceIdType.MESH)
    height = 512
    for s in range(rows // height):
        span = pl.ds(s * height, height)
        for q, (src, dst) in enumerate(zip((a1_hbm, a2_hbm), a)):
            pltpu.make_async_copy(src.at[span], dst.at[span], a_sem.at[2 * s + q]).start()
    for src, dst in ((own_head, laid_head), (own_mhead, laid_mhead)):
        stood[...] = jnp.zeros_like(stood)
        stood[0:classes] = src[...]
        dst[...] = stood[...].T
    wide_bias[...] = jnp.zeros_like(wide_bias)
    wide_bias[0:1, 0:classes] = head_bias_ref[...]
    pl.semaphore_wait(barrier, n - 1 + nb - 1 + len(places.peers))

    def gathers(item, src, dst):
        span = src.shape[-2]
        lead = (slice(None),) * (len(src.shape) - 2)
        mine = dst.at[lead + (pl.ds(pl.multiple_of(here_b * span, 8), span),)]
        copies = [pltpu.make_async_copy(src, mine, w_own.at[item])]
        for k in range(1, nb):
            copies.append(remote(src, mine, w_send.at[item, k], w_recv.at[item, k], (lax.rem(here_b + k, nb), here_r)))
        return copies

    def gather(item, src, dst):
        copies = gathers(item, src, dst)
        for copy in copies:
            copy.start()
        return copies

    def arrived(copies):
        for copy in copies:
            copy.wait()

    in_copies = gather(0, own_in, w_in)
    for q in range(layers):
        gather(2 + q, own_conv.at[q], w_conv.at[q])
    head_copies = gather(1, laid_head, w_head)

    def stat_copies(e):
        return [
            remote(stat.at[e], held.at[e, k], stat_send.at[e, k], stat_recv.at[e, k], peer_place(batch, lax.rem(block + k, n)))
            for k in range(1, n)
        ]

    def stats_start(e):
        held[e, 0] = stat[e]
        for copy in stat_copies(e):
            copy.start()

    def stats_finish(e):
        arrived(stat_copies(e))
        total = held[e, lax.rem(block, n)]
        for q in range(1, n):
            total = total + held[e, lax.rem(block + n - q, n)]
        return total

    def rims_of(e, low_src, high_src):
        slot = lax.rem(e, 2)
        return (
            remote(low_src, rim.at[slot, 1], rim_send.at[e, 1], rim_recv.at[e, 1], peer_place(batch, lax.rem(block + n - 1, n))),
            remote(high_src, rim.at[slot, 0], rim_send.at[e, 0], rim_recv.at[e, 0], peer_place(batch, lax.rem(block + 1, n))),
        )

    def start_if(condition, copy):
        @pl.when(condition)
        def _():
            copy.start()

    def rims_sent(copies):
        @pl.when(not_first)
        def _():
            copies[0].wait_send()

        @pl.when(not_last)
        def _():
            copies[1].wait_send()

    tile = 256
    tiles = rows // tile

    def rows_of(s, size):
        return pl.ds(pl.multiple_of(s * size, size), size)

    zeros8 = jnp.zeros((8, width), f32)

    arrived(in_copies)
    turned_in = parts_of(w_in[...].T, 3)

    def project(s, _):
        span = rows_of(s, tile)
        act[0, span] = dots(parts_of(x_ref[span, :], 3), turned_in) + bias_ref[0:1]
        return 0

    lax.fori_loop(0, tiles, project, 0)
    stat[0] = jnp.zeros((2, width), f32)
    own_cols, rim_cols = pl.ds(0, rows), pl.ds(rows, 2 * halo)

    def set_norm(l, totals):
        mean = totals[0:1] * (1.0 / nodes)
        inverse = lax.rsqrt(totals[1:2] * (1.0 / nodes) - mean * mean + norm_epsilon)
        under = lax.max(l - 1, 0)
        scale = norm_ref[under, 0:1] * inverse
        offset = norm_ref[under, 1:2] - mean * scale
        plain = l == 0
        normed[l, 0:1] = jnp.where(plain, 0.0, mean)
        normed[l, 1:2] = jnp.where(plain, 1.0, inverse)
        normed[l, 2:3] = jnp.where(plain, 1.0, scale)
        normed[l, 3:4] = jnp.where(plain, 0.0, offset)

    bias_row = lax.broadcasted_iota(jnp.int32, bias_ref.shape, 0)

    def forward(l, _):
        copies = rims_of(l, act.at[l, pl.ds(0, halo)], act.at[l, pl.ds(rows - halo, halo)])
        start_if(not_first, copies[0])
        start_if(not_last, copies[1])
        stats_start(l)

        def split(s, _):
            span = rows_of(s, tile)
            for dst, piece in zip(ps, parts_of(act[l, span], 2)):
                dst[span, :] = piece
            return 0

        lax.fori_loop(0, tiles, split, 0)

        def own(s, _):
            span = rows_of(s, height)

            @pl.when(l == 0)
            def _():
                for q, (src, dst) in enumerate(zip((a1_hbm, a2_hbm), a)):
                    pltpu.make_async_copy(src.at[span], dst.at[span], a_sem.at[2 * s + q]).wait()

            agg[l, span] = dots([q[span, own_cols] for q in a], [q[own_cols, :] for q in ps])
            return 0

        lax.fori_loop(0, rows // height, own, 0)
        set_norm(l, stats_finish(l))
        slot = lax.rem(l, 2)
        for which, gone in ((0, first), (1, last)):
            @pl.when(gone)
            def _():
                rim[slot, which] = jnp.zeros((halo, width), f32)

            @pl.when(jnp.logical_not(gone))
            def _():
                remote(rim.at[slot, which], rim.at[slot, which], rim_send.at[l, which], rim_recv.at[l, which],
                       peer_place(batch, lax.rem(block + 1, n))).wait_recv()

            for dst, piece in zip(ps, parts_of(rim[slot, which], 2)):
                dst[pl.ds(rows + which * halo, halo), :] = piece

        def rims_in(s, _):
            span = rows_of(s, height)
            agg[l, span] += dots([q[span, rim_cols] for q in a], [q[rim_cols, :] for q in ps])
            return 0

        lax.fori_loop(0, rows // height, rims_in, 0)
        arrived(gathers(2 + l, own_conv.at[l], w_conv.at[l]))
        weights = parts_of(w_conv[l], 3)
        bias = column_sums(jnp.where(bias_row == l + 1, bias_ref[...], 0.0))
        scale, offset = normed[l, 2:3], normed[l, 3:4]

        def finish(s, sums):
            span = rows_of(s, tile)
            row_sum = jnp.concatenate(
                [jnp.broadcast_to(sums_ref[s, i : i + 1], (LANES, LANES)).T for i in range(tile // LANES)], 0
            )
            found = agg[l, span] * scale + jnp.concatenate([row_sum] * (width // LANES), 1) * offset
            agg[l, span] = found
            h = act[l, span] * scale + offset
            pre = dots(parts_of(jnp.concatenate([h, found], 1), 3), weights) + bias
            active = jnp.maximum(pre, 0.0)
            act[l + 1, span] = active
            return sums[0] + folded(active), sums[1] + folded(active * active)

        sums = lax.fori_loop(0, tiles, finish, (zeros8, zeros8))
        stat[l + 1, 0:1] = column_sums(sums[0])
        stat[l + 1, 1:2] = column_sums(sums[1])
        rims_sent(copies)
        return 0

    lax.fori_loop(0, layers, forward, 0)

    stats_start(layers)
    base = 2 + layers
    late = [gather(base, own_min, full_min), gather(base + 1, laid_mhead, full_mhead), gather(base + 2, own_mconv, full_mconv)]
    arrived(head_copies)
    head_parts = parts_of(w_head[...], 3)
    head_turned = parts_of(w_head[...].T, 2)
    set_norm(layers, stats_finish(layers))
    top_scale, top_offset = normed[layers, 2:3], normed[layers, 3:4]
    top_mean, top_inverse = normed[layers, 0:1], normed[layers, 1:2]

    def top(span):
        return act[layers, span] * top_scale + top_offset

    def classify(s, _):
        span = rows_of(s, tile)
        logit[span, :] = dots(parts_of(top(span), 3), head_parts) + wide_bias[0:1]
        return 0

    lax.fori_loop(0, tiles, classify, 0)
    per = pick_smem.shape[0] // n
    sent[...] = jnp.zeros_like(sent)
    for d in range(n):
        for k in range(per):
            sent[d, k : k + 1] = logit[pl.ds(pick_smem[d * per + k], 1), :]
    pair_copies = []
    for k in range(1, n):
        peer = lax.rem(block + k, n)
        copy = remote(sent.at[peer], got.at[k], pair_send.at[k], pair_recv.at[k], peer_place(batch, peer))
        copy.start()
        pair_copies.append(copy)
    got[0] = sent[block]
    lane = lax.broadcasted_iota(jnp.int32, (tile, LANES), 1)
    real = lane < classes

    def soften(s, loss):
        span = rows_of(s, tile)
        z = logit[span, :]
        top_z = jnp.max(jnp.where(real, z, -jnp.inf), axis=1, keepdims=True)
        e = jnp.where(real, jnp.exp(z - top_z), 0.0)
        total = jnp.sum(e, axis=1, keepdims=True)
        named = [
            jnp.broadcast_to(label_ref[pl.ds(label_at + s * (tile // LANES) + i, 1), :], (LANES, LANES)).T for i in range(tile // LANES)
        ]
        hot = jnp.logical_and(real, lane.astype(f32) == jnp.concatenate(named, 0))
        logit[span, :] = e / total - jnp.where(hot, 1.0, 0.0)
        part = jnp.where(lane == 0, top_z + jnp.log(total), 0.0) - jnp.where(hot, z, 0.0)
        return loss + folded(part)

    loss = lax.fori_loop(0, tiles, soften, jnp.zeros((8, LANES), f32))
    arrived(pair_copies)
    gaps = []
    for d in range(n):
        gaps.append(sent[d] - got[lax.rem(block + n - d, n)])
    gap = jnp.concatenate(gaps, 0)
    loss = loss + pair_weight * folded(gap * gap)
    spare = pick_row.shape[1] - gap.shape[0]
    if spare:
        gap = jnp.concatenate([gap, jnp.zeros((spare, LANES), f32)], 0)
    gap_parts = parts_of(gap * (4.0 * pair_weight), 3)
    at_head, at_small = rows_at[1], rows_at[2]
    small = layers + 1

    def finish_head(s, sums):
        span = rows_of(s, tile)
        spot = lax.broadcasted_iota(jnp.int32, (tile, pick_row.shape[1]), 0) + s * tile
        chosen = jnp.where(spot == pick_row[...], 1.0, 0.0).astype(bf16)
        add = None
        for piece in gap_parts:
            v = jnp.dot(chosen, piece, preferred_element_type=f32)
            add = v if add is None else add + v
        grad = (logit[span, :] + add) * (1.0 / all_nodes)
        grad_parts = parts_of(grad, 2)
        h = top(span)
        back = dots(grad_parts, head_turned)
        gh[span, :] = back
        ready_top = (act[layers, span] - top_mean) * top_inverse
        return (
            sums[0] + dots(parts_of(h, 2), grad_parts, TURNED),
            sums[1] + folded(grad),
            sums[2] + folded(back),
            sums[3] + folded(back * ready_top),
        )

    begin = (
        jnp.zeros((width, LANES), f32),
        jnp.zeros((8, LANES), f32),
        jnp.zeros((8, width), f32),
        jnp.zeros((8, width), f32),
    )
    sums = lax.fori_loop(0, tiles, finish_head, begin)
    half = width // 2
    pay[pl.ds(at_head, half), :] = jnp.concatenate([sums[0][:half], sums[0][half:]], 1)
    tail = pl.ds(at_small, summed_rows - at_small)
    pay[tail, :] = jnp.zeros((summed_rows - at_small, width), f32)
    at_norm = at_small + small
    at_last = at_norm + 2 * layers
    pay[at_last : at_last + 1, 0:LANES] = column_sums(sums[1])
    pay[at_last + 1 : at_last + 2, 0:LANES] = column_sums(loss)
    after = layers + 1
    stat[after, 0:1] = column_sums(sums[2])
    stat[after, 1:2] = column_sums(sums[3])
    stats_start(after)

    big = 2 * width

    def conv_rows(l):
        return pl.multiple_of(jnp.where(l == 0, 0, summed_rows + (l - 1) * big), 8)

    def told(which):
        for peer in places.peers:
            pl.semaphore_signal(ready.at[which], inc=1, device_id=peer, device_id_type=pl.DeviceIdType.MESH)

    cores, planes, zs = places.cores, places.planes, places.zs
    core, spot = places.core, places.spot
    piece_rows = big // cores
    block_rows = piece_rows // planes

    def part(ref, index, count):
        return ref.at[pl.ds(pl.multiple_of(index * count, 8), count)]

    class Sum:
        def __init__(self, l):
            self.which, room = l - 1, act.at[l + 1]
            self.local = pay.at[pl.ds(conv_rows(l), big)]
            self.whole = room.at[pl.ds(0, big)]
            spots = [piece_rows, piece_rows, piece_rows, block_rows, block_rows * zs]
            views, at = [], big
            for count in spots:
                views.append(room.at[pl.ds(at, count)])
                at += count
            self.got1, self.sum1, self.got2, self.sum2, self.got3 = views

        def copies(self, stage):
            found = []

            def add(i, src, dst, to):
                found.append(remote(src, dst, sum_send.at[self.which, i], sum_recv.at[self.which, i], to))

            if stage == 0 and cores == 2:
                add(0, part(self.local, 1 - core, piece_rows), self.got1, places.core_peer)
            if stage == 1:
                for k in range(1, planes):
                    p, to = places.plane_peer(k)
                    add(k, part(self.sum1, p, block_rows), part(self.got2, k, block_rows), to)
            if stage == 2:
                for k in range(1, zs):
                    add(planes + k, self.sum2, part(self.got3, k, block_rows), places.column_peer(k)[1])
            if stage == 3:
                mine = part(self.whole, core * planes + spot, block_rows)
                for k in range(1, planes):
                    add(planes + zs + k, mine, mine, places.plane_peer(k)[1])
            if stage == 4 and cores == 2:
                mine = part(self.whole, core, piece_rows)
                add(2 * planes + zs, mine, mine, places.core_peer)
            return found

        def go(self, stage):
            if stage == 0:
                pl.semaphore_wait(ready.at[self.which], len(places.peers))
            else:
                arrived(self.copies(stage - 1))
            if stage == 1:
                total = part(self.local, core, piece_rows)[...]
                if cores == 2:
                    total = total + self.got1[...]
                self.sum1[...] = total
            if stage == 2:
                total = part(self.sum1, spot, block_rows)[...]
                for k in range(1, planes):
                    total = total + part(self.got2, k, block_rows)[...]
                self.sum2[...] = total
                self.got3[pl.ds(0, block_rows), :] = total
            if stage == 3:
                total = part(self.got3, lax.rem(places.z, zs), block_rows)[...]
                for q in range(1, zs):
                    total = total + part(self.got3, lax.rem(places.z + zs - q, zs), block_rows)[...]
                part(self.whole, core * planes + spot, block_rows)[...] = total
            if stage == 5:
                self.local[...] = self.whole[...]
            for copy in self.copies(stage):
                copy.start()

    def backward(turn, _):
        l = layers - 1 - turn
        e = after + turn

        def advance(stage):
            @pl.when(turn > 0)
            def _():
                Sum(l + 1).go(stage)

        keep[l, 0:1] = stat[e, 1:2]
        keep[l, 1:2] = stat[e, 0:1]
        for q, piece in enumerate(parts_of(w_conv[l].T, 2)):
            wt[q] = piece
        gain = norm_ref[l, 0:1]
        totals = stats_finish(e) * gain * (1.0 / nodes)
        mean, inverse = normed[l + 1, 0:1], normed[l + 1, 1:2]

        def enter(s, total):
            span = rows_of(s, tile)
            active = act[l + 1, span]
            rated = (active - mean) * inverse
            grad = inverse * (gh[span, :] * gain - totals[0:1] - rated * totals[1:2])
            grad = jnp.where(active > 0.0, grad, 0.0)
            pieces = parts_of(grad, 2)
            for dst, piece in zip(gs, pieces):
                dst[span, :] = piece
            joined = dots(pieces, [wt[0], wt[1]])
            gh[span, :] = joined[:, :width]
            for dst, piece in zip(ps, parts_of(joined[:, width:], 2)):
                dst[span, :] = piece
            return total + folded(grad)

        total = lax.fori_loop(0, tiles, enter, zeros8)
        keep[l, 2:3] = column_sums(total)

        @pl.when(l > 0)
        def _():
            told(l - 1)

        advance(1)
        copies = rims_of(e, out_rim.at[0], out_rim.at[1])

        def rims_out(which, _):
            cols = pl.ds(pl.multiple_of(rows + which * halo, 128), halo)
            out_rim[which] = dots([q[:, cols] for q in a], [q[own_cols, :] for q in ps], TURNED)
            for at, go in ((0, not_first), (1, not_last)):
                start_if(jnp.logical_and(go, which == at), copies[at])
            return 0

        lax.fori_loop(0, 2, rims_out, 0)
        advance(2)

        def spread_back(s, _):
            span = rows_of(s, height)
            gh[span, :] += dots([q[:, span] for q in a], [q[own_cols, :] for q in ps], TURNED)
            return 0

        lax.fori_loop(0, rows // height, spread_back, 0)
        advance(3)
        slot = lax.rem(e, 2)
        for which, go, start in ((1, not_last, rows - halo), (0, not_first, 0)):
            @pl.when(go)
            def _():
                remote(rim.at[slot, which], rim.at[slot, which], rim_send.at[e, which], rim_recv.at[e, which],
                       peer_place(batch, lax.rem(block + 1, n))).wait_recv()
                gh[pl.ds(start, halo), :] += rim[slot, which]

        below_mean, below_inverse = normed[l, 0:1], normed[l, 1:2]

        def tail_sums(s, sums):
            span = rows_of(s, tile)
            grad = gh[span, :]
            return sums[0] + folded(grad), sums[1] + folded(grad * ((act[l, span] - below_mean) * below_inverse))

        sums = lax.fori_loop(0, tiles, tail_sums, (zeros8, zeros8))
        stat[e + 1, 0:1] = column_sums(sums[0])
        stat[e + 1, 1:2] = column_sums(sums[1])

        @pl.when(l > 0)
        def _():
            stats_start(e + 1)

        rims_sent(copies)
        advance(4)
        base = conv_rows(l)
        where = pl.ds(base, width)
        under = pl.ds(pl.multiple_of(base + width, 8), width)
        scale, offset = normed[l, 2:3], normed[l, 3:4]
        pay[pl.ds(base, big), :] = jnp.zeros((big, width), f32)

        def weigh(s, _):
            span = rows_of(s, height)
            h = act[l, span] * scale + offset
            grad = [q[span, :] for q in gs]
            pay[where, :] += dots(parts_of(h, 2), grad, TURNED)
            pay[under, :] += dots(parts_of(agg[l, span], 2), grad, TURNED)
            return 0

        lax.fori_loop(0, rows // height, weigh, 0)
        advance(5)

        @pl.when(l > 0)
        def _():
            Sum(l).go(0)

        return 0

    lax.fori_loop(0, layers, backward, 0)
    pay[at_small : at_small + 1, :] = stat[after + layers, 0:1]
    for l in range(layers):
        pay[at_norm + 2 * l : at_norm + 2 * l + 2, :] = keep[l, 0:2]
        pay[at_small + 1 + l : at_small + 2 + l, :] = keep[l, 2:3]
    feat = x_ref.shape[1]
    pay[pl.ds(rows_at[0], rows_at[1] - rows_at[0]), :] = jnp.zeros((rows_at[1] - rows_at[0], width), f32)

    def weigh_in(s, total):
        span = rows_of(s, height)
        return total + dots(parts_of(x_ref[span, :], 2), parts_of(gh[span, :], 2), TURNED)

    pay[pl.ds(rows_at[0], feat), :] = lax.fori_loop(0, rows // height, weigh_in, jnp.zeros((feat, width), f32))
    for copies in late:
        arrived(copies)


def step_call(n, nb, layers, nodes, all_nodes, classes, rows_at, summed_rows, label_at, x, labels, sums, biases, norms, head_bias,
              picks, pick_row, adjacency, shards):
    rows = x.shape[0]
    width = biases.shape[1]
    cols = adjacency[0].shape[1]
    halo = (cols - rows) // 2
    feat = x.shape[1]
    vmem = pl.BlockSpec(memory_space=pltpu.VMEM)
    smem = pl.BlockSpec(memory_space=pltpu.SMEM)
    hbm = pl.BlockSpec(memory_space=pl.ANY)
    dma = pltpu.SemaphoreType.DMA
    items = 2 + layers + 3
    exchanges = 2 * layers + 1
    _, ys, across, zs = plane_split(nb, n)
    hops = 2 * ys * across + zs + 1
    return pl.pallas_call(
        functools.partial(step_kernel, n, nb, layers, nodes, all_nodes, classes, rows_at, summed_rows, label_at),
        out_shape=(
            jax.ShapeDtypeStruct((summed_rows + (layers - 1) * 2 * width, width), f32),
            jax.ShapeDtypeStruct((width, feat), f32),
            jax.ShapeDtypeStruct((layers, 2 * width, width), f32),
            jax.ShapeDtypeStruct((width, LANES), f32),
        ),
        in_specs=[vmem] * 6 + [smem, vmem] + [hbm] * 4 + [vmem] + [hbm] * 2 + [vmem],
        out_specs=(vmem, hbm, hbm, hbm),
        scratch_shapes=[
            pltpu.VMEM((layers + 1, rows, width), f32),
            pltpu.VMEM((layers, rows, width), f32),
            pltpu.VMEM((rows, cols), bf16),
            pltpu.VMEM((rows, cols), bf16),
            pltpu.VMEM((cols, width), bf16),
            pltpu.VMEM((cols, width), bf16),
            pltpu.VMEM((rows, width), bf16),
            pltpu.VMEM((rows, width), bf16),
            pltpu.VMEM((rows, width), f32),
            pltpu.VMEM((2, 2, halo, width), f32),
            pltpu.VMEM((2, halo, width), f32),
            pltpu.VMEM((rows, LANES), f32),
            pltpu.VMEM((n, 8, LANES), f32),
            pltpu.VMEM((n, 8, LANES), f32),
            pltpu.VMEM((exchanges + 1, 2, width), f32),
            pltpu.VMEM((exchanges, n, 2, width), f32),
            pltpu.VMEM((width, feat), f32),
            pltpu.VMEM((layers, 2 * width, width), f32),
            pltpu.VMEM((width, LANES), f32),
            pltpu.VMEM((2, width, 2 * width), bf16),
            dma((2 * rows // 512,)),
            dma((exchanges, n)),
            dma((exchanges, n)),
            dma((exchanges, 2)),
            dma((exchanges, 2)),
            dma((n,)),
            dma((n,)),
            dma((items, nb)),
            dma((items, nb)),
            dma((items,)),
            dma((layers - 1, hops)),
            dma((layers - 1, hops)),
            pltpu.SemaphoreType.REGULAR((layers - 1,)),
            pltpu.VMEM((layers + 1, 4, width), f32),
            pltpu.VMEM((layers, 4, width), f32),
            pltpu.VMEM((LANES, width // nb), f32),
            pltpu.VMEM((width // nb, LANES), f32),
            pltpu.VMEM((width // nb, LANES), f32),
            pltpu.VMEM((8, LANES), f32),
        ],
        compiler_params=pltpu.CompilerParams(collective_id=1, has_side_effects=True, vmem_limit_bytes=63 << 20),
        name="forward_backward",
    )(x, labels, sums, biases, norms, head_bias, picks, pick_row, *adjacency, *shards)


def update_kernel(n, nb, layers, all_nodes, rows_at, classes, ns_parts, scales, summed_rows, pay, mom_in, mom_conv, mom_head, w_in,
                  w_conv, w_head, biases, norms, head_bias, fb, fn, fh, sb, sn, sh, power, *refs):
    (loss_o, in_o, conv_o, head_o, min_o, mconv_o, mhead_o, b_o, n_o, h_o, fb_o, fn_o, fh_o, sb_o, sn_o, sh_o) = refs[:16]
    (got1, sum1, got2, sum2, got3, full, gram, poly, small_gram, small_poly, mconv, send, recv, old_conv, old_sem, spread) = refs[16:]
    places = Places(n, nb)
    cores, planes, zs = places.cores, places.planes, places.zs
    core, spot, z = places.core, places.spot, places.z
    plane_peer, column_peer, core_peer = places.plane_peer, places.column_peer, places.core_peer
    here_b = places.b
    width = w_conv.shape[2]
    barrier = pltpu.get_barrier_semaphore()
    for peer in places.peers:
        pl.semaphore_signal(barrier, inc=1, device_id=peer, device_id_type=pl.DeviceIdType.MESH)

    def kdot(left, right, dims=((1,), (0,))):
        return dots(parts_of(left, ns_parts), parts_of(right, ns_parts), dims)

    def eye(k):
        return (lax.broadcasted_iota(jnp.int32, (k, k), 0) == lax.broadcasted_iota(jnp.int32, (k, k), 1)).astype(f32)

    def begin(moment, grams, i):
        size = jnp.sqrt(jnp.sum(moment * moment)) + 1e-07
        g = kdot(moment, moment, TURNED) / (size * size)
        grams[i] = g
        return size

    def step(grams, polys, which, early, late):
        k = grams.shape[1]
        count = len(which)
        a1 = [grams[i] for i in which]
        a2 = [kdot(v, v) for v in a1]
        p = [newton_a * eye(k) + newton_b * v + newton_c * u for v, u in zip(a1, a2)]
        if early:
            q = p
        else:
            q = [kdot(v, polys[i]) for i, v in zip(which, p)]
        if not late:
            pa = [kdot(v, u) for v, u in zip(p, a1)]
            nxt = [kdot(v, u) for v, u in zip(pa, p)]
        for j in range(count):
            polys[which[j]] = q[j]
            if not late:
                grams[which[j]] = nxt[j]

    fetch = pltpu.make_async_copy(mom_conv, old_conv, old_sem)
    fetch.start()
    sizes = {}
    ready = tuple(range(1, layers))

    def start_ready():
        fetch.wait()
        for l in ready:
            mconv[l] = muon_decay * old_conv[l] + pay[summed_rows + (l - 1) * 2 * width : summed_rows + l * 2 * width]
            sizes[l] = begin(mconv[l], gram, l)

    def middle(count, grams, polys, which):
        lax.fori_loop(0, count, lambda _, c: (step(grams, polys, which, False, False), c)[1], 0)

    pl.semaphore_wait(barrier, len(places.peers))
    used = [0]

    def go(src, dst, to):
        i = used[0]
        used[0] += 1
        copy = remote(src, dst, send.at[i], recv.at[i], to)
        copy.start()
        return copy

    def settle(copies):
        for copy in copies:
            copy.wait()

    half_rows = summed_rows // cores
    block_rows = half_rows // planes
    m = block_rows // zs

    def part(ref, index, count):
        return ref.at[pl.ds(pl.multiple_of(index * count, 8), count)]

    if cores == 2:
        copies = [go(part(pay, 1 - core, half_rows), got1, core_peer)]
        start_ready()
        settle(copies)
        sum1[...] = part(pay, core, half_rows)[...] + got1[...]
    else:
        start_ready()
        sum1[...] = pay[pl.ds(0, half_rows), :]
    copies = []
    for k in range(1, planes):
        p, to = plane_peer(k)
        copies.append(go(part(sum1, p, block_rows), got2.at[k], to))
    step(gram, poly, ready, True, False)
    middle(1, gram, poly, ready)
    settle(copies)
    total = part(sum1, spot, block_rows)[...]
    for k in range(1, planes):
        total = total + got2[k]
    sum2[...] = total
    copies = []
    for k in range(1, zs):
        q, to = column_peer(k)
        copies.append(go(part(sum2, q, m), got3.at[k], to))
    middle(1, gram, poly, ready)
    settle(copies)
    total = part(sum2, z, m)[...]
    for k in range(1, zs):
        total = total + got3[k]
    block = core * planes + spot
    mine = part(full, block * zs + z, m)
    mine[...] = total
    copies = [go(mine, mine, column_peer(k)[1]) for k in range(1, zs)]
    middle(1, gram, poly, ready)
    settle(copies)
    mine = part(full, block, block_rows)
    copies = [go(mine, mine, plane_peer(k)[1]) for k in range(1, planes)]
    step(gram, poly, ready, False, True)
    scale_in, scale_conv, scale_head = scales
    span = w_conv.shape[1]

    def turn_conv(l):
        own = mconv[l, pl.ds(pl.multiple_of(here_b * span, 8), span)]
        mconv_o[l] = own
        w = w_conv[l]
        turn = kdot(own, poly[l]) * (scale_conv / sizes[l])
        conv_o[l] = w - muon_rate * (turn + muon_shrink * w)

    for l in ready:
        turn_conv(l)
    settle(copies)
    if cores == 2:
        mine = part(full, core, half_rows)
        settle([go(mine, mine, core_peer)])
    summed = full[...]
    mconv[0] = muon_decay * old_conv[0] + summed[: 2 * width]
    sizes[0] = begin(mconv[0], gram, 0)
    feat = w_in.shape[1]
    half = width // 2
    grad_in = summed[rows_at[0] : rows_at[0] + LANES].T
    grad_head = summed[rows_at[1] : rows_at[1] + half]
    spread[...] = jnp.zeros_like(spread)
    spread[:, 0:feat] = mom_in[...]
    moment_in = muon_decay * spread[...] + jnp.where(lax.broadcasted_iota(jnp.int32, (width, LANES), 1) < feat, grad_in, 0.0)
    moment_head = muon_decay * mom_head[...] + jnp.concatenate([grad_head[:, :LANES], grad_head[:, LANES:]], 0)
    sizes[layers] = begin(moment_in, small_gram, 0)
    sizes[layers + 1] = begin(moment_head, small_gram, 1)

    def both(early, late):
        step(gram, poly, (0,), early, late)
        step(small_gram, small_poly, (0, 1), early, late)

    both(True, False)
    lax.fori_loop(1, NS_STEPS - 1, lambda _, c: (both(False, False), c)[1], 0)
    both(False, True)
    turn_conv(0)
    span = w_in.shape[0]
    mconv[0, pl.ds(0, width), 0:LANES] = moment_in
    mconv[0, pl.ds(0, width), LANES : 2 * LANES] = moment_head
    own = mconv[0, pl.ds(pl.multiple_of(here_b * span, 8), span), 0:LANES]
    min_o[...] = own[:, :feat]
    w = w_in[...]
    turn = kdot(own, small_poly[0]) * (scale_in / sizes[layers])
    in_o[...] = w - muon_rate * (turn[:, :feat] + muon_shrink * w)
    span = w_head.shape[1]
    own = mconv[0, pl.ds(pl.multiple_of(here_b * span, 8), span), LANES : 2 * LANES]
    mhead_o[...] = own.T[:classes]
    w = w_head[...]
    turn = kdot(own, small_poly[1]) * (scale_head / sizes[layers + 1])
    head_o[...] = w - muon_rate * (turn.T[:classes] + muon_shrink * w)

    def adamw(param, grad, first, second, outs):
        first = adam_first_decay * first + (1.0 - adam_first_decay) * grad
        second = adam_second_decay * second + (1.0 - adam_second_decay) * grad * grad
        first_hat = first / power[0]
        second_hat = second / power[1]
        outs[0][...] = param - adam_rate * (first_hat / (jnp.sqrt(second_hat) + adam_epsilon) + adam_shrink * param)
        outs[1][...] = first
        outs[2][...] = second

    at = rows_at[2]
    adamw(biases[...], summed[at : at + layers + 1], fb[...], sb[...], (b_o, fb_o, sb_o))
    at = at + layers + 1
    for l in range(layers):
        rows = summed[at + 2 * l : at + 2 * l + 2]
        adamw(norms[l], rows, fn[l], sn[l], (n_o.at[l], fn_o.at[l], sn_o.at[l]))
    at = at + 2 * layers
    adamw(head_bias[...], summed[at : at + 1, :classes], fh[...], sh[...], (h_o, fh_o, sh_o))
    loss_o[...] = jnp.sum(summed[at + 1 : at + 2], axis=1, keepdims=True) / all_nodes


def update_call(n, nb, layers, all_nodes, rows_at, classes, ns_parts, scales, summed_rows, pay, moments, shards, smalls, power):
    cores, ys, xs, zs = plane_split(nb, n)
    planes = ys * xs
    width = pay.shape[1]
    m = summed_rows // (n * nb)
    w_in, w_conv, w_head = shards
    vmem = pl.BlockSpec(memory_space=pltpu.VMEM)
    smem = pl.BlockSpec(memory_space=pltpu.SMEM)
    like = [jax.ShapeDtypeStruct(v.shape, f32) for v in (w_in, w_conv, w_head)]
    like_small = [jax.ShapeDtypeStruct(v.shape, f32) for v in smalls[:3]]
    copies = 2 * (planes + zs)
    return pl.pallas_call(
        functools.partial(update_kernel, n, nb, layers, all_nodes, rows_at, classes, ns_parts, scales, summed_rows),
        out_shape=tuple([jax.ShapeDtypeStruct((1, 1), f32)] + like + like + like_small * 3),
        in_specs=[vmem] * 2 + [pl.BlockSpec(memory_space=pl.ANY)] + [vmem] * 13 + [smem],
        out_specs=(vmem,) * 16,
        scratch_shapes=[
            pltpu.VMEM((zs * planes * m, width), f32),
            pltpu.VMEM((zs * planes * m, width), f32),
            pltpu.VMEM((planes, zs * m, width), f32),
            pltpu.VMEM((zs * m, width), f32),
            pltpu.VMEM((zs, m, width), f32),
            pltpu.VMEM((summed_rows, width), f32),
            pltpu.VMEM((layers, width, width), f32),
            pltpu.VMEM((layers, width, width), f32),
            pltpu.VMEM((2, LANES, LANES), f32),
            pltpu.VMEM((2, LANES, LANES), f32),
            pltpu.VMEM((layers, 2 * width, width), f32),
            pltpu.SemaphoreType.DMA((copies,)),
            pltpu.SemaphoreType.DMA((copies,)),
            pltpu.VMEM((layers, 2 * width, width), f32),
            pltpu.SemaphoreType.DMA,
            pltpu.VMEM((width, LANES), f32),
        ],
        compiler_params=pltpu.CompilerParams(collective_id=2, has_side_effects=True, vmem_limit_bytes=63 << 20),
        name="sum_and_update",
    )(pay, *moments, *shards, *smalls, power)


NS_PARTS = 3


def hand_over_kernel(*refs):
    half = len(refs) // 2
    for src, dst in zip(refs[:half], refs[half:]):
        dst[...] = src[...]


def hand_over(arrays):
    vmem = pl.BlockSpec(memory_space=pltpu.VMEM)
    return pl.pallas_call(
        hand_over_kernel,
        out_shape=tuple(jax.ShapeDtypeStruct(v.shape, v.dtype) for v in arrays),
        in_specs=[vmem] * len(arrays),
        out_specs=(vmem,) * len(arrays),
        name="hand_over",
    )(*arrays)


def per_device(
    n_batch,
    n_rows,
    features,
    edge_rows,
    edge_weight,
    halo_counts,
    labels,
    pair_rows,
    step,
    w_in,
    w_conv,
    w_head,
    biases,
    norm_params,
    head_bias,
    mom_in,
    mom_conv,
    mom_head,
    first_bias,
    first_norm,
    first_head,
    second_bias,
    second_norm,
    second_head,
):
    rows_dev = features.shape[1]
    halo_rows = rows_dev // 4
    edge_count = edge_rows.shape[3]
    layers, hid = w_conv.shape[0], w_conv.shape[2]
    feat, classes = w_in.shape[0], w_head.shape[1]
    pairs = pair_rows.shape[3]
    node_count = rows_dev * n_rows
    all_nodes = node_count * n_batch
    flat = [
        edge_rows.reshape(2 * edge_count).astype(f32),
        edge_weight.reshape(edge_count),
        labels.reshape(rows_dev).astype(f32),
        pair_rows.reshape(n_rows * pairs).astype(f32),
    ]
    flat = jnp.concatenate(flat)
    flat = jnp.pad(flat, (0, -flat.shape[0] % (8 * LANES))).reshape(-1, LANES)
    flat = redeal(flat, n_batch, n_rows)
    inputs = redeal(features, n_batch, n_rows)[0]
    e = edge_count // LANES
    block = my_place()[1]
    wide = (rows_dev + 2 * halo_rows) // TILE
    rims = jnp.stack([(block > 0).astype(jnp.int32), (block < n_rows - 1).astype(jnp.int32)])
    *adjacency, row_sums = fill(flat[:e], flat[e : 2 * e], flat[2 * e : 3 * e], rims, rows_dev // TILE, wide, halo_rows // TILE, 2)
    label_rows = rows_dev // LANES
    picks = flat[3 * e + label_rows :].reshape(-1)[: n_rows * pairs].astype(jnp.int32)
    spread = jnp.pad(picks.reshape(n_rows, pairs), ((0, 0), (0, 8 - pairs)), constant_values=-1).reshape(1, n_rows * 8)
    spread = jnp.pad(spread, ((0, 0), (0, -spread.shape[1] % LANES)), constant_values=-1)
    at_in = 2 * hid
    at_head = at_in + -(-feat // 8) * 8
    at_small = at_head + hid // 2
    used = at_small + layers + 1 + 2 * layers + 2
    unit = 8 * n_rows * n_batch
    pay_rows = -(-used // unit) * unit
    rows_at = (at_in, at_head, at_small)
    turned = [
        w_in.T,
        w_conv,
        w_head.T,
        mom_in.T,
        mom_conv,
        mom_head.T,
    ]
    pay, full_min, full_mconv, full_mhead = step_call(
        n_rows,
        n_batch,
        layers,
        node_count,
        all_nodes,
        classes,
        rows_at,
        pay_rows,
        3 * e,
        inputs,
        flat,
        row_sums,
        biases,
        norm_params,
        head_bias[None],
        picks,
        spread,
        adjacency,
        turned,
    )
    count = step[0].astype(f32)
    power = jnp.stack([1.0 - jnp.power(adam_first_decay, count), 1.0 - jnp.power(adam_second_decay, count)])
    scales = (
        math.sqrt(max(1.0, hid / feat)),
        math.sqrt(max(1.0, hid / (2 * hid))),
        math.sqrt(max(1.0, classes / hid)),
    )
    smalls = (
        biases,
        norm_params,
        head_bias[None],
        first_bias,
        first_norm,
        first_head[None],
        second_bias,
        second_norm,
        second_head[None],
    )
    outs = update_call(
        n_rows,
        n_batch,
        layers,
        all_nodes,
        rows_at,
        classes,
        NS_PARTS,
        scales,
        pay_rows,
        pay,
        (full_min, full_mconv, full_mhead),
        (turned[0], w_conv, turned[2]),
        smalls,
        power,
    )
    outs = hand_over(outs)
    loss, new_in, new_conv, new_head, moment_in, moment_conv, moment_head = outs[:7]
    rest = []
    for i in range(0, 9, 3):
        rest += [outs[7 + i], outs[8 + i], outs[9 + i][0]]
    return (loss[0, 0], new_in.T, new_conv, new_head.T, moment_in.T, moment_conv, moment_head.T, *rest)


def solution(mesh):
    in_specs = (
        P("batch", "rows", None),
        P("batch", "rows", None, None),
        P("batch", "rows", None),
        P("batch", "rows", None),
        P("batch", "rows"),
        P("batch", "rows", None, None),
        P(),
        P(None, "batch"),
        P(None, "batch", None),
        P("batch", None),
        P(),
        P(),
        P(),
        P(None, "batch"),
        P(None, "batch", None),
        P("batch", None),
        P(),
        P(),
        P(),
        P(),
        P(),
        P(),
    )
    out_specs = (
        P(),
        P(None, "batch"),
        P(None, "batch", None),
        P("batch", None),
        P(None, "batch"),
        P(None, "batch", None),
        P("batch", None),
        P(),
        P(),
        P(),
        P(),
        P(),
        P(),
        P(),
        P(),
        P(),
    )
    body = functools.partial(per_device, mesh.shape["batch"], mesh.shape["rows"])
    return jax.shard_map(body, mesh=mesh, in_specs=in_specs, out_specs=out_specs, check_vma=False)
```

```python
import functools
import math

import jax
import jax.numpy as jnp
from jax import lax
from jax.experimental import pallas as pl
from jax.experimental.pallas import tpu as pltpu
from jax.sharding import PartitionSpec as P

NS_STEPS = 5

f32 = jnp.float32
bf16 = jnp.bfloat16
LANES = 128
TILE = 256
highest = lax.Precision.HIGHEST
norm_epsilon = 1e-05
pair_weight = 0.05
newton_a = 3.4445
newton_b = -4.775
newton_c = 2.0315
muon_decay = 0.9
muon_rate = 0.5
muon_shrink = 0.01
adam_first_decay = 0.9
adam_second_decay = 0.999
adam_epsilon = 1e-08
adam_rate = 0.1
adam_shrink = 0.01


def swap(b, r):
    return 2 * (b // 2) + r % 2, 2 * (r // 2) + b % 2


def flat_pairs(n_batch, n_rows, move):
    pairs = []
    for b in range(n_batch):
        for r in range(n_rows):
            to = move(b, r)
            if to is not None:
                pairs.append((b * n_rows + r, to[0] * n_rows + to[1]))
    return pairs


def redeal(array, n_batch, n_rows):
    return lax.ppermute(array, ("batch", "rows"), flat_pairs(n_batch, n_rows, swap))


def peer_place(batch, block):
    two = jnp.int32(2)
    return (
        two * lax.div(batch, two) + lax.rem(block, two),
        two * lax.div(block, two) + lax.rem(batch, two),
    )


def my_place():
    return peer_place(lax.axis_index("batch"), lax.axis_index("rows"))


def put_in_order(wide, to_ref, from_ref, w_ref, key_out, w_out, col_out, range_out):
    to, frm = to_ref[...].astype(jnp.int32), from_ref[...].astype(jnp.int32)
    key = (((to >> 8) * wide + (frm >> 8)) << 16) | ((to & 255) << 8) | (frm & 255)
    shape3 = (16, 8, LANES)
    key = key.astype(f32).reshape(shape3)
    w = w_ref[...].reshape(shape3)
    sub = lax.broadcasted_iota(jnp.int32, shape3, 1)
    lane = lax.broadcasted_iota(jnp.int32, shape3, 2)
    vreg = lax.broadcasted_iota(jnp.int32, shape3, 0)
    place = vreg + 16 * sub + 128 * lane
    for phase in range(14):
        for bit in range(phase, -1, -1):
            down = ((place >> (phase + 1)) & 1) == 1
            if bit < 4:
                view = (16 >> (bit + 1), 2, 1 << bit, 8, LANES)
                kv, wv = key.reshape(view), w.reshape(view)
                dv = down.astype(jnp.int32).reshape(view)[:, 0] == 1
                a, b, wa, wb = kv[:, 0], kv[:, 1], wv[:, 0], wv[:, 1]
                turn = jnp.logical_xor(a > b, dv)
                key = jnp.stack([jnp.where(turn, b, a), jnp.where(turn, a, b)], 1).reshape(shape3)
                w = jnp.stack([jnp.where(turn, wb, wa), jnp.where(turn, wa, wb)], 1).reshape(shape3)
            else:
                if bit < 7:
                    axis, gap, size, pos = 1, 1 << (bit - 4), 8, sub
                else:
                    axis, gap, size, pos = 2, 1 << (bit - 7), LANES, lane
                low = (pos & gap) == 0
                kp = jnp.where(low, pltpu.roll(key, size - gap, axis), pltpu.roll(key, gap, axis))
                wp = jnp.where(low, pltpu.roll(w, size - gap, axis), pltpu.roll(w, gap, axis))
                smaller = jnp.logical_xor(low, down)
                take = jnp.where(smaller, kp, key) < jnp.where(smaller, key, kp)
                key = jnp.where(take, kp, key)
                w = jnp.where(take, wp, w)
    flat = key.reshape(LANES, LANES)
    key_out[...] = flat.T.astype(jnp.int32)
    w_out[...] = w.reshape(LANES, LANES).T
    start = (lax.broadcasted_iota(jnp.int32, (8, LANES), 1).astype(f32) * 65536.0)[None]
    below = jnp.zeros(shape3, f32)
    upto = jnp.zeros(shape3, f32)
    for c in range(LANES):
        wide_key = jnp.broadcast_to(flat[:, c : c + 1], (LANES, LANES))
        col_out[c] = (wide_key - jnp.floor(wide_key * (1.0 / 256.0)) * 256.0).astype(bf16)
        wide_key = wide_key.reshape(shape3)
        below = below + jnp.where(wide_key < start, 1.0, 0.0)
        upto = upto + jnp.where(wide_key < start + 65536.0, 1.0, 0.0)
    range_out[...] = jnp.zeros_like(range_out)
    n_below = jnp.sum(below.reshape(LANES, LANES), axis=0, keepdims=True)
    n_upto = jnp.sum(upto.reshape(LANES, LANES), axis=0, keepdims=True)
    first = jnp.floor(n_below * (1.0 / 128.0))
    end = jnp.floor((n_upto + 127.0) * (1.0 / 128.0))
    range_out[0:1] = first.astype(jnp.int32)
    range_out[1:2] = jnp.where(n_upto > n_below, end, first).astype(jnp.int32)


def fill_kernel(wide, rim, chunk, parts, rims, to_ref, from_ref, weight_ref, *refs):
    outs, sums = refs[:parts], refs[parts]
    acc, rowacc, key_ref, w_ref, col_ref, ranges, span_of, sem = refs[parts + 1 :]
    i = pl.program_id(0)

    @pl.when(i == 0)
    def _():
        put_in_order(wide, to_ref, from_ref, weight_ref, key_ref, w_ref, col_ref, ranges)
        copy = pltpu.make_async_copy(ranges, span_of, sem)
        copy.start()
        copy.wait()

    pack = 16
    shape = (TILE // pack, pack, LANES)
    rows = lax.broadcasted_iota(jnp.int32, shape, 0) * pack + lax.broadcasted_iota(jnp.int32, shape, 1)
    rows = rows.astype(f32).astype(bf16)
    lanes = lax.broadcasted_iota(jnp.int32, (LANES, LANES), 1).astype(f32)
    lanes0, lanes1 = lanes.astype(bf16), (lanes + 128.0).astype(bf16)
    one, zero = jnp.ones((), bf16), jnp.zeros((), bf16)

    def spread(row):
        return jnp.broadcast_to(row, (pack, LANES)).astype(bf16)[None]

    rowacc[...] = jnp.zeros_like(rowacc)

    def tile(j, _):
        b = i * wide + j
        first, end = span_of[0, b], span_of[1, b]
        end = jnp.where(jnp.logical_and(j < rim, rims[0] == 0), first, end)
        end = jnp.where(jnp.logical_and(j >= wide - rim, rims[1] == 0), first, end)
        slot = jnp.where(j < rim, wide - 2 * rim + j, jnp.where(j < wide - rim, j - rim, j))
        cols = pl.ds(pl.multiple_of(slot * TILE, TILE), TILE)

        @pl.when(end <= first)
        def _():
            for out in outs:
                out[:, cols] = jnp.zeros((TILE, TILE), bf16)

        @pl.when(end > first)
        def _():
            def part(base, c):
                row = jnp.minimum(base + c, LANES - 1)
                here = key_ref[pl.ds(row, 1), :] - (b << 16)
                if c:
                    here = jnp.where(base + c < end, here, -1)
                at = rows == spread((here >> 8).astype(f32))
                rest = w_ref[pl.ds(row, 1), :]
                left = []
                for q in range(parts):
                    piece = rest.astype(bf16).astype(f32)
                    rest = rest - piece
                    left.append(jnp.where(at, spread(piece), zero).reshape(TILE, LANES))
                col = col_ref[row]
                right = jnp.concatenate(
                    [jnp.where(col == lanes0, one, zero), jnp.where(col == lanes1, one, zero)], 1
                )
                return left, right

            def get(base):
                made = [part(base, c) for c in range(chunk)]
                lhs = jnp.concatenate([m[0][q] for q in range(parts) for m in made], 1)
                rhs = jnp.concatenate([m[1] for m in made] * parts, 0)
                return jnp.dot(lhs, rhs, preferred_element_type=f32)

            acc[...] = get(first)

            def more(t, _):
                acc[...] += get(first + t * chunk)
                return 0

            lax.fori_loop(1, lax.div(end - first + chunk - 1, chunk), more, 0)
            rest = acc[...]
            rowacc[...] += rest[:, :LANES] + rest[:, LANES:]
            for out in outs:
                piece = rest.astype(bf16)
                out[:, cols] = piece
                rest = rest - piece.astype(f32)

        return 0

    lax.fori_loop(0, wide, tile, 0)
    total = jnp.sum(rowacc[...], axis=1, keepdims=True)
    for half in range(TILE // LANES):
        column = jnp.broadcast_to(total[half * LANES : (half + 1) * LANES], (LANES, LANES))
        sums[0, half : half + 1] = column.T[0:1]


def fill(to, frm, weights, rims, tiles, wide, rim, parts, chunk=4):
    cols = wide * TILE
    return pl.pallas_call(
        functools.partial(fill_kernel, wide, rim, chunk, parts),
        out_shape=tuple(jax.ShapeDtypeStruct((tiles * TILE, cols), bf16) for _ in range(parts))
        + (jax.ShapeDtypeStruct((tiles, TILE // LANES, LANES), f32),),
        grid_spec=pltpu.PrefetchScalarGridSpec(
            num_scalar_prefetch=1,
            grid=(tiles,),
            in_specs=[pl.BlockSpec((LANES, LANES), lambda i, *_: (0, 0))] * 3,
            out_specs=tuple(pl.BlockSpec((TILE, cols), lambda i, *_: (i, 0)) for _ in range(parts))
            + (pl.BlockSpec((1, TILE // LANES, LANES), lambda i, *_: (i, 0, 0)),),
            scratch_shapes=[
                pltpu.VMEM((TILE, TILE), f32),
                pltpu.VMEM((TILE, LANES), f32),
                pltpu.VMEM((LANES, LANES), jnp.int32),
                pltpu.VMEM((LANES, LANES), f32),
                pltpu.VMEM((LANES, LANES, LANES), bf16),
                pltpu.VMEM((8, LANES), jnp.int32),
                pltpu.SMEM((8, LANES), jnp.int32),
                pltpu.SemaphoreType.DMA,
            ],
        ),
        compiler_params=pltpu.CompilerParams(vmem_limit_bytes=50 << 20),
        name="adjacency_tiles",
    )(rims, to, frm, weights)


def parts_of(x, count):
    found = []
    for q in range(count):
        piece = x.astype(bf16)
        found.append(piece)
        if q + 1 < count:
            x = x - piece.astype(f32)
    return found


def pair_list(count):
    return [(p, q) for p in range(count) for q in range(count) if p + q < count]


def dots(left, right, dims=((1,), (0,))):
    total = None
    for p, q in pair_list(len(left)):
        piece = lax.dot_general(left[p], right[q], (dims, ((), ())), preferred_element_type=f32)
        total = piece if total is None else total + piece
    return total


def remote(src, dst, send, recv, to):
    return pltpu.make_async_remote_copy(
        src_ref=src,
        dst_ref=dst,
        send_sem=send,
        recv_sem=recv,
        device_id=to,
        device_id_type=pl.DeviceIdType.MESH,
    )


def column_sums(x):
    return jnp.sum(x, axis=0, keepdims=True)


def folded(x):
    return jnp.sum(x.reshape(x.shape[0] // 8, 8, x.shape[1]), axis=0)


def plane_split(nb, n):
    cores = 2 if nb % 2 == 0 else 1
    across = 1
    while across * across * 4 <= n and n % (across * 2) == 0:
        across *= 2
    return cores, nb // cores, across, n // across


class Places:
    def __init__(self, n, nb):
        self.cores, ys, self.xs, self.zs = plane_split(nb, n)
        self.planes = ys * self.xs
        self.b, self.r = lax.axis_index("batch"), lax.axis_index("rows")
        self.core, y = lax.rem(self.b, self.cores), lax.div(self.b, self.cores)
        self.x, self.z = lax.rem(self.r, self.xs), lax.div(self.r, self.xs)
        self.spot = y * self.xs + self.x
        self.core_peer = (y * self.cores + lax.rem(self.core + 1, self.cores), self.r)
        self.peers = [self.plane_peer(k)[1] for k in range(1, self.planes)]
        self.peers += [self.column_peer(k)[1] for k in range(1, self.zs)]
        if self.cores == 2:
            self.peers.append(self.core_peer)

    def plane_peer(self, k):
        p = lax.rem(self.spot + k, self.planes)
        return p, (lax.div(p, self.xs) * self.cores + self.core, self.z * self.xs + lax.rem(p, self.xs))

    def column_peer(self, k):
        q = lax.rem(self.z + k, self.zs)
        return q, (self.b, q * self.xs + self.x)


TURNED = ((0,), (0,))
GATHERED = 3


def step_kernel(n, nb, layers, nodes, all_nodes, classes, rows_at, summed_rows, label_at, *refs):
    (x_ref, label_ref, sums_ref, bias_ref, norm_ref, head_bias_ref, pick_smem, pick_row, a1_hbm, a2_hbm) = refs[:10]
    own_in, own_conv, own_head, own_min, own_mconv, own_mhead = refs[10:16]
    pay, full_min, full_mconv, full_mhead = refs[16:20]
    (act, agg, a1, a2, p1, p2, g1, g2, gh, rim, out_rim, logit, sent, got, stat, held, w_in, w_conv, w_head,
     wt, a_sem, stat_send, stat_recv, rim_send, rim_recv, pair_send, pair_recv, w_send, w_recv, w_own, sum_send, sum_recv,
     ready, normed, keep, stood, laid_head, laid_mhead, wide_bias) = refs[20:]
    rows, width = act.shape[1], act.shape[2]
    halo = rim.shape[2]
    a, ps, gs = (a1, a2), (p1, p2), (g1, g2)
    here_b, here_r = lax.axis_index("batch"), lax.axis_index("rows")
    batch, block = my_place()
    first, last = block == 0, block == n - 1
    not_first, not_last = jnp.logical_not(first), jnp.logical_not(last)

    barrier = pltpu.get_barrier_semaphore()
    for k in range(1, n):
        pl.semaphore_signal(
            barrier, inc=1, device_id=peer_place(batch, lax.rem(block + k, n)), device_id_type=pl.DeviceIdType.MESH
        )
    for k in range(1, nb):
        pl.semaphore_signal(
            barrier, inc=1, device_id=(lax.rem(here_b + k, nb), here_r), device_id_type=pl.DeviceIdType.MESH
        )
    places = Places(n, nb)
    for peer in places.peers:
        pl.semaphore_signal(barrier, inc=1, device_id=peer, device_id_type=pl.DeviceIdType.MESH)
    height = 512
    for s in range(rows // height):
        span = pl.ds(s * height, height)
        for q, (src, dst) in enumerate(zip((a1_hbm, a2_hbm), a)):
            pltpu.make_async_copy(src.at[span], dst.at[span], a_sem.at[2 * s + q]).start()
    for src, dst in ((own_head, laid_head), (own_mhead, laid_mhead)):
        stood[...] = jnp.zeros_like(stood)
        stood[0:classes] = src[...]
        dst[...] = stood[...].T
    wide_bias[...] = jnp.zeros_like(wide_bias)
    wide_bias[0:1, 0:classes] = head_bias_ref[...]
    pl.semaphore_wait(barrier, n - 1 + nb - 1 + len(places.peers))

    def gathers(item, src, dst):
        span = src.shape[-2]
        lead = (slice(None),) * (len(src.shape) - 2)
        mine = dst.at[lead + (pl.ds(pl.multiple_of(here_b * span, 8), span),)]
        copies = [pltpu.make_async_copy(src, mine, w_own.at[item])]
        for k in range(1, nb):
            copies.append(remote(src, mine, w_send.at[item, k], w_recv.at[item, k], (lax.rem(here_b + k, nb), here_r)))
        return copies

    def gather(item, src, dst):
        copies = gathers(item, src, dst)
        for copy in copies:
            copy.start()
        return copies

    def arrived(copies):
        for copy in copies:
            copy.wait()

    in_copies = gather(0, own_in, w_in)
    for q in range(layers):
        gather(2 + q, own_conv.at[q], w_conv.at[q])
    head_copies = gather(1, laid_head, w_head)

    def stat_copies(e):
        return [
            remote(stat.at[e], held.at[e, k], stat_send.at[e, k], stat_recv.at[e, k], peer_place(batch, lax.rem(block + k, n)))
            for k in range(1, n)
        ]

    def stats_start(e):
        held[e, 0] = stat[e]
        for copy in stat_copies(e):
            copy.start()

    def stats_finish(e):
        arrived(stat_copies(e))
        total = held[e, lax.rem(block, n)]
        for q in range(1, n):
            total = total + held[e, lax.rem(block + n - q, n)]
        return total

    def rims_of(e, low_src, high_src):
        slot = lax.rem(e, 2)
        return (
            remote(low_src, rim.at[slot, 1], rim_send.at[e, 1], rim_recv.at[e, 1], peer_place(batch, lax.rem(block + n - 1, n))),
            remote(high_src, rim.at[slot, 0], rim_send.at[e, 0], rim_recv.at[e, 0], peer_place(batch, lax.rem(block + 1, n))),
        )

    def start_if(condition, copy):
        @pl.when(condition)
        def _():
            copy.start()

    def rims_sent(copies):
        @pl.when(not_first)
        def _():
            copies[0].wait_send()

        @pl.when(not_last)
        def _():
            copies[1].wait_send()

    tile = 256
    tiles = rows // tile

    def rows_of(s, size):
        return pl.ds(pl.multiple_of(s * size, size), size)

    zeros8 = jnp.zeros((8, width), f32)

    arrived(in_copies)
    turned_in = parts_of(w_in[...].T, 3)

    def project(s, _):
        span = rows_of(s, tile)
        h = dots(parts_of(x_ref[span, :], 3), turned_in) + bias_ref[0:1]
        act[0, span] = h
        for dst, piece in zip(ps, parts_of(h, 2)):
            dst[span, :] = piece
        return 0

    lax.fori_loop(0, tiles, project, 0)
    stat[0] = jnp.zeros((2, width), f32)
    own_cols, rim_cols = pl.ds(0, rows), pl.ds(rows, 2 * halo)

    def set_norm(l, totals):
        mean = totals[0:1] * (1.0 / nodes)
        inverse = lax.rsqrt(totals[1:2] * (1.0 / nodes) - mean * mean + norm_epsilon)
        under = lax.max(l - 1, 0)
        scale = norm_ref[under, 0:1] * inverse
        offset = norm_ref[under, 1:2] - mean * scale
        plain = l == 0
        normed[l, 0:1] = jnp.where(plain, 0.0, mean)
        normed[l, 1:2] = jnp.where(plain, 1.0, inverse)
        normed[l, 2:3] = jnp.where(plain, 1.0, scale)
        normed[l, 3:4] = jnp.where(plain, 0.0, offset)

    bias_row = lax.broadcasted_iota(jnp.int32, bias_ref.shape, 0)

    def forward(l, _):
        copies = rims_of(l, act.at[l, pl.ds(0, halo)], act.at[l, pl.ds(rows - halo, halo)])
        start_if(not_first, copies[0])
        start_if(not_last, copies[1])
        stats_start(l)

        def own(s, _):
            span = rows_of(s, height)

            @pl.when(l == 0)
            def _():
                for q, (src, dst) in enumerate(zip((a1_hbm, a2_hbm), a)):
                    pltpu.make_async_copy(src.at[span], dst.at[span], a_sem.at[2 * s + q]).wait()

            agg[l, span] = dots([q[span, own_cols] for q in a], [q[own_cols, :] for q in ps])
            return 0

        lax.fori_loop(0, rows // height, own, 0)
        set_norm(l, stats_finish(l))
        slot = lax.rem(l, 2)
        for which, gone in ((0, first), (1, last)):
            @pl.when(gone)
            def _():
                rim[slot, which] = jnp.zeros((halo, width), f32)

            @pl.when(jnp.logical_not(gone))
            def _():
                remote(rim.at[slot, which], rim.at[slot, which], rim_send.at[l, which], rim_recv.at[l, which],
                       peer_place(batch, lax.rem(block + 1, n))).wait_recv()

            for dst, piece in zip(ps, parts_of(rim[slot, which], 2)):
                dst[pl.ds(rows + which * halo, halo), :] = piece

        def rims_in(s, _):
            span = rows_of(s, height)
            agg[l, span] += dots([q[span, rim_cols] for q in a], [q[rim_cols, :] for q in ps])
            return 0

        lax.fori_loop(0, rows // height, rims_in, 0)
        arrived(gathers(2 + l, own_conv.at[l], w_conv.at[l]))
        weights = parts_of(w_conv[l], 3)
        bias = column_sums(jnp.where(bias_row == l + 1, bias_ref[...], 0.0))
        scale, offset = normed[l, 2:3], normed[l, 3:4]

        def finish(s, sums):
            span = rows_of(s, tile)
            row_sum = jnp.concatenate(
                [jnp.broadcast_to(sums_ref[s, i : i + 1], (LANES, LANES)).T for i in range(tile // LANES)], 0
            )
            found = agg[l, span] * scale + jnp.concatenate([row_sum] * (width // LANES), 1) * offset
            agg[l, span] = found
            h = act[l, span] * scale + offset
            pre = dots(parts_of(jnp.concatenate([h, found], 1), 3), weights) + bias
            active = jnp.maximum(pre, 0.0)
            act[l + 1, span] = active
            for dst, piece in zip(ps, parts_of(active, 2)):
                dst[span, :] = piece
            return sums[0] + folded(active), sums[1] + folded(active * active)

        sums = lax.fori_loop(0, tiles, finish, (zeros8, zeros8))
        stat[l + 1, 0:1] = column_sums(sums[0])
        stat[l + 1, 1:2] = column_sums(sums[1])
        rims_sent(copies)
        return 0

    lax.fori_loop(0, layers, forward, 0)

    stats_start(layers)
    base = 2 + layers
    late = [gather(base, own_min, full_min), gather(base + 1, laid_mhead, full_mhead), gather(base + 2, own_mconv, full_mconv)]
    arrived(head_copies)
    head_parts = parts_of(w_head[...], 3)
    head_turned = parts_of(w_head[...].T, 2)
    set_norm(layers, stats_finish(layers))
    top_scale, top_offset = normed[layers, 2:3], normed[layers, 3:4]
    top_mean, top_inverse = normed[layers, 0:1], normed[layers, 1:2]

    def top(span):
        return act[layers, span] * top_scale + top_offset

    def classify(s, _):
        span = rows_of(s, tile)
        logit[span, :] = dots(parts_of(top(span), 3), head_parts) + wide_bias[0:1]
        return 0

    lax.fori_loop(0, tiles, classify, 0)
    per = pick_smem.shape[0] // n
    sent[...] = jnp.zeros_like(sent)
    for d in range(n):
        for k in range(per):
            sent[d, k : k + 1] = logit[pl.ds(pick_smem[d * per + k], 1), :]
    pair_copies = []
    for k in range(1, n):
        peer = lax.rem(block + k, n)
        copy = remote(sent.at[peer], got.at[k], pair_send.at[k], pair_recv.at[k], peer_place(batch, peer))
        copy.start()
        pair_copies.append(copy)
    got[0] = sent[block]
    lane = lax.broadcasted_iota(jnp.int32, (tile, LANES), 1)
    real = lane < classes

    def soften(s, loss):
        span = rows_of(s, tile)
        z = logit[span, :]
        top_z = jnp.max(jnp.where(real, z, -jnp.inf), axis=1, keepdims=True)
        e = jnp.where(real, jnp.exp(z - top_z), 0.0)
        total = jnp.sum(e, axis=1, keepdims=True)
        named = [
            jnp.broadcast_to(label_ref[pl.ds(label_at + s * (tile // LANES) + i, 1), :], (LANES, LANES)).T for i in range(tile // LANES)
        ]
        hot = jnp.logical_and(real, lane.astype(f32) == jnp.concatenate(named, 0))
        logit[span, :] = e / total - jnp.where(hot, 1.0, 0.0)
        part = jnp.where(lane == 0, top_z + jnp.log(total), 0.0) - jnp.where(hot, z, 0.0)
        return loss + folded(part)

    loss = lax.fori_loop(0, tiles, soften, jnp.zeros((8, LANES), f32))
    arrived(pair_copies)
    gaps = []
    for d in range(n):
        gaps.append(sent[d] - got[lax.rem(block + n - d, n)])
    gap = jnp.concatenate(gaps, 0)
    loss = loss + pair_weight * folded(gap * gap)
    spare = pick_row.shape[1] - gap.shape[0]
    if spare:
        gap = jnp.concatenate([gap, jnp.zeros((spare, LANES), f32)], 0)
    gap_parts = parts_of(gap * (4.0 * pair_weight), 3)
    at_head, at_small = rows_at[1], rows_at[2]
    small = layers + 1

    def finish_head(s, sums):
        span = rows_of(s, tile)
        spot = lax.broadcasted_iota(jnp.int32, (tile, pick_row.shape[1]), 0) + s * tile
        chosen = jnp.where(spot == pick_row[...], 1.0, 0.0).astype(bf16)
        add = None
        for piece in gap_parts:
            v = jnp.dot(chosen, piece, preferred_element_type=f32)
            add = v if add is None else add + v
        grad = (logit[span, :] + add) * (1.0 / all_nodes)
        grad_parts = parts_of(grad, 2)
        h = top(span)
        back = dots(grad_parts, head_turned)
        gh[span, :] = back
        ready_top = (act[layers, span] - top_mean) * top_inverse
        return (
            sums[0] + dots(parts_of(h, 2), grad_parts, TURNED),
            sums[1] + folded(grad),
            sums[2] + folded(back),
            sums[3] + folded(back * ready_top),
        )

    begin = (
        jnp.zeros((width, LANES), f32),
        jnp.zeros((8, LANES), f32),
        jnp.zeros((8, width), f32),
        jnp.zeros((8, width), f32),
    )
    sums = lax.fori_loop(0, tiles, finish_head, begin)
    half = width // 2
    pay[pl.ds(at_head, half), :] = jnp.concatenate([sums[0][:half], sums[0][half:]], 1)
    tail = pl.ds(at_small, summed_rows - at_small)
    pay[tail, :] = jnp.zeros((summed_rows - at_small, width), f32)
    at_norm = at_small + small
    at_last = at_norm + 2 * layers
    pay[at_last : at_last + 1, 0:LANES] = column_sums(sums[1])
    pay[at_last + 1 : at_last + 2, 0:LANES] = column_sums(loss)
    after = layers + 1
    stat[after, 0:1] = column_sums(sums[2])
    stat[after, 1:2] = column_sums(sums[3])
    stats_start(after)

    big = 2 * width

    def conv_rows(l):
        return pl.multiple_of(jnp.where(l == 0, 0, summed_rows + (l - 1) * big), 8)

    def told(which):
        for peer in places.peers:
            pl.semaphore_signal(ready.at[which], inc=1, device_id=peer, device_id_type=pl.DeviceIdType.MESH)

    cores, planes, zs = places.cores, places.planes, places.zs
    core, spot = places.core, places.spot
    piece_rows = big // cores
    block_rows = piece_rows // planes
    cut = block_rows % (8 * zs) == 0
    slice_rows = block_rows // zs if cut else block_rows

    def part(ref, index, count):
        return ref.at[pl.ds(pl.multiple_of(index * count, 8), count)]

    class Sum:
        def __init__(self, l):
            self.which, room = l - 1, act.at[l + 1]
            self.local = pay.at[pl.ds(conv_rows(l), big)]
            self.whole = room.at[pl.ds(0, big)]
            spots = [piece_rows, piece_rows, piece_rows, block_rows, slice_rows * zs]
            views, at = [], big
            for count in spots:
                views.append(room.at[pl.ds(at, count)])
                at += count
            self.got1, self.sum1, self.got2, self.sum2, self.got3 = views

        def copies(self, stage):
            found = []

            def add(i, src, dst, to):
                found.append(remote(src, dst, sum_send.at[self.which, i], sum_recv.at[self.which, i], to))

            if stage == 0 and cores == 2:
                add(0, part(self.local, 1 - core, piece_rows), self.got1, places.core_peer)
            if stage == 1:
                for k in range(1, planes):
                    p, to = places.plane_peer(k)
                    add(k, part(self.sum1, p, block_rows), part(self.got2, k, block_rows), to)
            if stage == 2:
                for k in range(1, zs):
                    q, to = places.column_peer(k)
                    src = part(self.sum2, q, slice_rows) if cut else self.sum2
                    add(planes + k, src, part(self.got3, k, slice_rows), to)
            block = part(self.whole, core * planes + spot, block_rows)
            if stage == 3 and cut:
                mine = part(self.whole, (core * planes + spot) * zs + places.z, slice_rows)
                for k in range(1, zs):
                    add(planes + zs + k, mine, mine, places.column_peer(k)[1])
            if stage == 4:
                for k in range(1, planes):
                    add(planes + 2 * zs + k, block, block, places.plane_peer(k)[1])
            if stage == 5 and cores == 2:
                mine = part(self.whole, core, piece_rows)
                add(2 * planes + 2 * zs, mine, mine, places.core_peer)
            return found

        def go(self, stage):
            if stage == 0:
                pl.semaphore_wait(ready.at[self.which], len(places.peers))
            else:
                arrived(self.copies(stage - 1))
            if stage == 1:
                total = part(self.local, core, piece_rows)[...]
                if cores == 2:
                    total = total + self.got1[...]
                self.sum1[...] = total
            if stage == 2:
                total = part(self.sum1, spot, block_rows)[...]
                for k in range(1, planes):
                    total = total + part(self.got2, k, block_rows)[...]
                self.sum2[...] = total
                self.got3[pl.ds(0, slice_rows), :] = part(self.sum2, places.z, slice_rows)[...] if cut else total
            if stage == 3:
                total = part(self.got3, lax.rem(places.z, zs), slice_rows)[...]
                for q in range(1, zs):
                    total = total + part(self.got3, lax.rem(places.z + zs - q, zs), slice_rows)[...]
                if cut:
                    part(self.whole, (core * planes + spot) * zs + places.z, slice_rows)[...] = total
                else:
                    part(self.whole, core * planes + spot, block_rows)[...] = total
            if stage == 6:
                self.local[...] = self.whole[...]
            for copy in self.copies(stage):
                copy.start()

    def backward(turn, _):
        l = layers - 1 - turn
        e = after + turn

        def advance(stage):
            @pl.when(turn > 0)
            def _():
                Sum(l + 1).go(stage)

        keep[l, 0:1] = stat[e, 1:2]
        keep[l, 1:2] = stat[e, 0:1]
        for q, piece in enumerate(parts_of(w_conv[l].T, 2)):
            wt[q] = piece
        gain = norm_ref[l, 0:1]
        totals = stats_finish(e) * gain * (1.0 / nodes)
        mean, inverse = normed[l + 1, 0:1], normed[l + 1, 1:2]

        def enter(s, total):
            span = rows_of(s, tile)
            active = act[l + 1, span]
            rated = (active - mean) * inverse
            grad = inverse * (gh[span, :] * gain - totals[0:1] - rated * totals[1:2])
            grad = jnp.where(active > 0.0, grad, 0.0)
            pieces = parts_of(grad, 2)
            for dst, piece in zip(gs, pieces):
                dst[span, :] = piece
            joined = dots(pieces, [wt[0], wt[1]])
            gh[span, :] = joined[:, :width]
            for dst, piece in zip(ps, parts_of(joined[:, width:], 2)):
                dst[span, :] = piece
            return total + folded(grad)

        total = lax.fori_loop(0, tiles, enter, zeros8)
        keep[l, 2:3] = column_sums(total)

        @pl.when(l > 0)
        def _():
            told(l - 1)

        advance(1)

        @pl.when(turn > 1)
        def _():
            Sum(l + 2).go(6)

        copies = rims_of(e, out_rim.at[0], out_rim.at[1])

        def rims_out(which, _):
            cols = pl.ds(pl.multiple_of(rows + which * halo, 128), halo)
            out_rim[which] = dots([q[:, cols] for q in a], [q[own_cols, :] for q in ps], TURNED)
            for at, go in ((0, not_first), (1, not_last)):
                start_if(jnp.logical_and(go, which == at), copies[at])
            return 0

        lax.fori_loop(0, 2, rims_out, 0)
        advance(2)

        def spread_back(s, _):
            span = rows_of(s, height)
            gh[span, :] += dots([q[:, span] for q in a], [q[own_cols, :] for q in ps], TURNED)

            @pl.when(jnp.logical_and(turn > 0, s == rows // height // 2))
            def _():
                Sum(l + 1).go(3)

            return 0

        lax.fori_loop(0, rows // height, spread_back, 0)
        advance(4)
        slot = lax.rem(e, 2)
        for which, go, start in ((1, not_last, rows - halo), (0, not_first, 0)):
            @pl.when(go)
            def _():
                remote(rim.at[slot, which], rim.at[slot, which], rim_send.at[e, which], rim_recv.at[e, which],
                       peer_place(batch, lax.rem(block + 1, n))).wait_recv()
                gh[pl.ds(start, halo), :] += rim[slot, which]

        below_mean, below_inverse = normed[l, 0:1], normed[l, 1:2]

        def tail_sums(s, sums):
            span = rows_of(s, tile)
            grad = gh[span, :]
            return sums[0] + folded(grad), sums[1] + folded(grad * ((act[l, span] - below_mean) * below_inverse))

        sums = lax.fori_loop(0, tiles, tail_sums, (zeros8, zeros8))
        stat[e + 1, 0:1] = column_sums(sums[0])
        stat[e + 1, 1:2] = column_sums(sums[1])

        @pl.when(l > 0)
        def _():
            stats_start(e + 1)

        rims_sent(copies)
        base = conv_rows(l)
        where = pl.ds(base, width)
        under = pl.ds(pl.multiple_of(base + width, 8), width)
        scale, offset = normed[l, 2:3], normed[l, 3:4]
        pay[pl.ds(base, big), :] = jnp.zeros((big, width), f32)

        def weigh(s, _):
            span = rows_of(s, height)
            h = act[l, span] * scale + offset
            grad = [q[span, :] for q in gs]
            pay[where, :] += dots(parts_of(h, 2), grad, TURNED)
            pay[under, :] += dots(parts_of(agg[l, span], 2), grad, TURNED)
            return 0

        lax.fori_loop(0, rows // height, weigh, 0)
        advance(5)

        @pl.when(l > 0)
        def _():
            Sum(l).go(0)

        return 0

    lax.fori_loop(0, layers, backward, 0)
    pay[at_small : at_small + 1, :] = stat[after + layers, 0:1]
    for l in range(layers):
        pay[at_norm + 2 * l : at_norm + 2 * l + 2, :] = keep[l, 0:2]
        pay[at_small + 1 + l : at_small + 2 + l, :] = keep[l, 2:3]
    feat = x_ref.shape[1]
    pay[pl.ds(rows_at[0], rows_at[1] - rows_at[0]), :] = jnp.zeros((rows_at[1] - rows_at[0], width), f32)

    def weigh_in(s, total):
        span = rows_of(s, height)
        return total + dots(parts_of(x_ref[span, :], 2), parts_of(gh[span, :], 2), TURNED)

    pay[pl.ds(rows_at[0], feat), :] = lax.fori_loop(0, rows // height, weigh_in, jnp.zeros((feat, width), f32))
    for copies in late:
        arrived(copies)
    if layers > 1:
        Sum(1).go(6)


def step_call(n, nb, layers, nodes, all_nodes, classes, rows_at, summed_rows, label_at, x, labels, sums, biases, norms, head_bias,
              picks, pick_row, adjacency, shards):
    rows = x.shape[0]
    width = biases.shape[1]
    cols = adjacency[0].shape[1]
    halo = (cols - rows) // 2
    feat = x.shape[1]
    vmem = pl.BlockSpec(memory_space=pltpu.VMEM)
    smem = pl.BlockSpec(memory_space=pltpu.SMEM)
    hbm = pl.BlockSpec(memory_space=pl.ANY)
    dma = pltpu.SemaphoreType.DMA
    items = 2 + layers + 3
    exchanges = 2 * layers + 1
    _, ys, across, zs = plane_split(nb, n)
    hops = 2 * ys * across + 2 * zs + 1
    return pl.pallas_call(
        functools.partial(step_kernel, n, nb, layers, nodes, all_nodes, classes, rows_at, summed_rows, label_at),
        out_shape=(
            jax.ShapeDtypeStruct((summed_rows + (layers - 1) * 2 * width, width), f32),
            jax.ShapeDtypeStruct((width, feat), f32),
            jax.ShapeDtypeStruct((layers, 2 * width, width), f32),
            jax.ShapeDtypeStruct((width, LANES), f32),
        ),
        in_specs=[vmem] * 6 + [smem, vmem] + [hbm] * 4 + [vmem] + [hbm] * 2 + [vmem],
        out_specs=(vmem, hbm, hbm, hbm),
        scratch_shapes=[
            pltpu.VMEM((layers + 1, rows, width), f32),
            pltpu.VMEM((layers, rows, width), f32),
            pltpu.VMEM((rows, cols), bf16),
            pltpu.VMEM((rows, cols), bf16),
            pltpu.VMEM((cols, width), bf16),
            pltpu.VMEM((cols, width), bf16),
            pltpu.VMEM((rows, width), bf16),
            pltpu.VMEM((rows, width), bf16),
            pltpu.VMEM((rows, width), f32),
            pltpu.VMEM((2, 2, halo, width), f32),
            pltpu.VMEM((2, halo, width), f32),
            pltpu.VMEM((rows, LANES), f32),
            pltpu.VMEM((n, 8, LANES), f32),
            pltpu.VMEM((n, 8, LANES), f32),
            pltpu.VMEM((exchanges + 1, 2, width), f32),
            pltpu.VMEM((exchanges, n, 2, width), f32),
            pltpu.VMEM((width, feat), f32),
            pltpu.VMEM((layers, 2 * width, width), f32),
            pltpu.VMEM((width, LANES), f32),
            pltpu.VMEM((2, width, 2 * width), bf16),
            dma((2 * rows // 512,)),
            dma((exchanges, n)),
            dma((exchanges, n)),
            dma((exchanges, 2)),
            dma((exchanges, 2)),
            dma((n,)),
            dma((n,)),
            dma((items, nb)),
            dma((items, nb)),
            dma((items,)),
            dma((layers - 1, hops)),
            dma((layers - 1, hops)),
            pltpu.SemaphoreType.REGULAR((layers - 1,)),
            pltpu.VMEM((layers + 1, 4, width), f32),
            pltpu.VMEM((layers, 4, width), f32),
            pltpu.VMEM((LANES, width // nb), f32),
            pltpu.VMEM((width // nb, LANES), f32),
            pltpu.VMEM((width // nb, LANES), f32),
            pltpu.VMEM((8, LANES), f32),
        ],
        compiler_params=pltpu.CompilerParams(collective_id=1, has_side_effects=True, vmem_limit_bytes=63 << 20),
        name="forward_backward",
    )(x, labels, sums, biases, norms, head_bias, picks, pick_row, *adjacency, *shards)


def update_kernel(n, nb, layers, all_nodes, rows_at, classes, ns_parts, scales, summed_rows, pay, mom_in, mom_conv, mom_head, w_in,
                  w_conv, w_head, biases, norms, head_bias, fb, fn, fh, sb, sn, sh, power, *refs):
    (loss_o, in_o, conv_o, head_o, min_o, mconv_o, mhead_o, b_o, n_o, h_o, fb_o, fn_o, fh_o, sb_o, sn_o, sh_o) = refs[:16]
    (got1, sum1, got2, sum2, got3, full, gram, poly, small_gram, small_poly, mconv, send, recv, old_conv, old_sem, spread) = refs[16:]
    places = Places(n, nb)
    cores, planes, zs = places.cores, places.planes, places.zs
    core, spot, z = places.core, places.spot, places.z
    plane_peer, column_peer, core_peer = places.plane_peer, places.column_peer, places.core_peer
    here_b = places.b
    width = w_conv.shape[2]
    barrier = pltpu.get_barrier_semaphore()
    for peer in places.peers:
        pl.semaphore_signal(barrier, inc=1, device_id=peer, device_id_type=pl.DeviceIdType.MESH)

    def kdot(left, right, dims=((1,), (0,))):
        return dots(parts_of(left, ns_parts), parts_of(right, ns_parts), dims)

    def eye(k):
        return (lax.broadcasted_iota(jnp.int32, (k, k), 0) == lax.broadcasted_iota(jnp.int32, (k, k), 1)).astype(f32)

    def begin(moment, grams, i):
        size = jnp.sqrt(jnp.sum(moment * moment)) + 1e-07
        g = kdot(moment, moment, TURNED) / (size * size)
        grams[i] = g
        return size

    def step(grams, polys, which, early, late):
        k = grams.shape[1]
        count = len(which)
        a1 = [grams[i] for i in which]
        a2 = [kdot(v, v) for v in a1]
        p = [newton_a * eye(k) + newton_b * v + newton_c * u for v, u in zip(a1, a2)]
        if early:
            q = p
        else:
            q = [kdot(v, polys[i]) for i, v in zip(which, p)]
        if not late:
            pa = [kdot(v, u) for v, u in zip(p, a1)]
            nxt = [kdot(v, u) for v, u in zip(pa, p)]
        for j in range(count):
            polys[which[j]] = q[j]
            if not late:
                grams[which[j]] = nxt[j]

    fetch = pltpu.make_async_copy(mom_conv, old_conv, old_sem)
    fetch.start()
    sizes = {}
    ready = tuple(range(1, layers))

    def start_ready():
        fetch.wait()
        for l in ready:
            mconv[l] = muon_decay * old_conv[l] + pay[summed_rows + (l - 1) * 2 * width : summed_rows + l * 2 * width]
            sizes[l] = begin(mconv[l], gram, l)

    def middle(count, grams, polys, which):
        lax.fori_loop(0, count, lambda _, c: (step(grams, polys, which, False, False), c)[1], 0)

    pl.semaphore_wait(barrier, len(places.peers))
    used = [0]

    def go(src, dst, to):
        i = used[0]
        used[0] += 1
        copy = remote(src, dst, send.at[i], recv.at[i], to)
        copy.start()
        return copy

    def settle(copies):
        for copy in copies:
            copy.wait()

    half_rows = summed_rows // cores
    block_rows = half_rows // planes
    m = block_rows // zs

    def part(ref, index, count):
        return ref.at[pl.ds(pl.multiple_of(index * count, 8), count)]

    if cores == 2:
        copies = [go(part(pay, 1 - core, half_rows), got1, core_peer)]
        start_ready()
        settle(copies)
        sum1[...] = part(pay, core, half_rows)[...] + got1[...]
    else:
        start_ready()
        sum1[...] = pay[pl.ds(0, half_rows), :]
    copies = []
    for k in range(1, planes):
        p, to = plane_peer(k)
        copies.append(go(part(sum1, p, block_rows), got2.at[k], to))
    step(gram, poly, ready, True, False)
    middle(1, gram, poly, ready)
    settle(copies)
    total = part(sum1, spot, block_rows)[...]
    for k in range(1, planes):
        total = total + got2[k]
    sum2[...] = total
    copies = []
    for k in range(1, zs):
        q, to = column_peer(k)
        copies.append(go(part(sum2, q, m), got3.at[k], to))
    middle(1, gram, poly, ready)
    settle(copies)
    total = part(sum2, z, m)[...]
    for k in range(1, zs):
        total = total + got3[k]
    block = core * planes + spot
    mine = part(full, block * zs + z, m)
    mine[...] = total
    copies = [go(mine, mine, column_peer(k)[1]) for k in range(1, zs)]
    middle(1, gram, poly, ready)
    settle(copies)
    mine = part(full, block, block_rows)
    copies = [go(mine, mine, plane_peer(k)[1]) for k in range(1, planes)]
    step(gram, poly, ready, False, True)
    scale_in, scale_conv, scale_head = scales
    span = w_conv.shape[1]

    def turn_conv(l):
        own = mconv[l, pl.ds(pl.multiple_of(here_b * span, 8), span)]
        mconv_o[l] = own
        w = w_conv[l]
        turn = kdot(own, poly[l]) * (scale_conv / sizes[l])
        conv_o[l] = w - muon_rate * (turn + muon_shrink * w)

    for l in ready:
        turn_conv(l)
    settle(copies)
    if cores == 2:
        mine = part(full, core, half_rows)
        settle([go(mine, mine, core_peer)])
    summed = full[...]
    mconv[0] = muon_decay * old_conv[0] + summed[: 2 * width]
    sizes[0] = begin(mconv[0], gram, 0)
    feat = w_in.shape[1]
    half = width // 2
    grad_in = summed[rows_at[0] : rows_at[0] + LANES].T
    grad_head = summed[rows_at[1] : rows_at[1] + half]
    spread[...] = jnp.zeros_like(spread)
    spread[:, 0:feat] = mom_in[...]
    moment_in = muon_decay * spread[...] + jnp.where(lax.broadcasted_iota(jnp.int32, (width, LANES), 1) < feat, grad_in, 0.0)
    moment_head = muon_decay * mom_head[...] + jnp.concatenate([grad_head[:, :LANES], grad_head[:, LANES:]], 0)
    sizes[layers] = begin(moment_in, small_gram, 0)
    sizes[layers + 1] = begin(moment_head, small_gram, 1)

    def both(early, late):
        step(gram, poly, (0,), early, late)
        step(small_gram, small_poly, (0, 1), early, late)

    both(True, False)
    lax.fori_loop(1, NS_STEPS - 1, lambda _, c: (both(False, False), c)[1], 0)
    both(False, True)
    turn_conv(0)
    span = w_in.shape[0]
    mconv[0, pl.ds(0, width), 0:LANES] = moment_in
    mconv[0, pl.ds(0, width), LANES : 2 * LANES] = moment_head
    own = mconv[0, pl.ds(pl.multiple_of(here_b * span, 8), span), 0:LANES]
    min_o[...] = own[:, :feat]
    w = w_in[...]
    turn = kdot(own, small_poly[0]) * (scale_in / sizes[layers])
    in_o[...] = w - muon_rate * (turn[:, :feat] + muon_shrink * w)
    span = w_head.shape[1]
    own = mconv[0, pl.ds(pl.multiple_of(here_b * span, 8), span), LANES : 2 * LANES]
    mhead_o[...] = own.T[:classes]
    w = w_head[...]
    turn = kdot(own, small_poly[1]) * (scale_head / sizes[layers + 1])
    head_o[...] = w - muon_rate * (turn.T[:classes] + muon_shrink * w)

    def adamw(param, grad, first, second, outs):
        first = adam_first_decay * first + (1.0 - adam_first_decay) * grad
        second = adam_second_decay * second + (1.0 - adam_second_decay) * grad * grad
        first_hat = first / power[0]
        second_hat = second / power[1]
        outs[0][...] = param - adam_rate * (first_hat / (jnp.sqrt(second_hat) + adam_epsilon) + adam_shrink * param)
        outs[1][...] = first
        outs[2][...] = second

    at = rows_at[2]
    adamw(biases[...], summed[at : at + layers + 1], fb[...], sb[...], (b_o, fb_o, sb_o))
    at = at + layers + 1
    for l in range(layers):
        rows = summed[at + 2 * l : at + 2 * l + 2]
        adamw(norms[l], rows, fn[l], sn[l], (n_o.at[l], fn_o.at[l], sn_o.at[l]))
    at = at + 2 * layers
    adamw(head_bias[...], summed[at : at + 1, :classes], fh[...], sh[...], (h_o, fh_o, sh_o))
    loss_o[...] = jnp.sum(summed[at + 1 : at + 2], axis=1, keepdims=True) / all_nodes


def update_call(n, nb, layers, all_nodes, rows_at, classes, ns_parts, scales, summed_rows, pay, moments, shards, smalls, power):
    cores, ys, xs, zs = plane_split(nb, n)
    planes = ys * xs
    width = pay.shape[1]
    m = summed_rows // (n * nb)
    w_in, w_conv, w_head = shards
    vmem = pl.BlockSpec(memory_space=pltpu.VMEM)
    smem = pl.BlockSpec(memory_space=pltpu.SMEM)
    like = [jax.ShapeDtypeStruct(v.shape, f32) for v in (w_in, w_conv, w_head)]
    like_small = [jax.ShapeDtypeStruct(v.shape, f32) for v in smalls[:3]]
    copies = 2 * (planes + zs)
    return pl.pallas_call(
        functools.partial(update_kernel, n, nb, layers, all_nodes, rows_at, classes, ns_parts, scales, summed_rows),
        out_shape=tuple([jax.ShapeDtypeStruct((1, 1), f32)] + like + like + like_small * 3),
        in_specs=[vmem] * 2 + [pl.BlockSpec(memory_space=pl.ANY)] + [vmem] * 13 + [smem],
        out_specs=(vmem,) * 16,
        scratch_shapes=[
            pltpu.VMEM((zs * planes * m, width), f32),
            pltpu.VMEM((zs * planes * m, width), f32),
            pltpu.VMEM((planes, zs * m, width), f32),
            pltpu.VMEM((zs * m, width), f32),
            pltpu.VMEM((zs, m, width), f32),
            pltpu.VMEM((summed_rows, width), f32),
            pltpu.VMEM((layers, width, width), f32),
            pltpu.VMEM((layers, width, width), f32),
            pltpu.VMEM((2, LANES, LANES), f32),
            pltpu.VMEM((2, LANES, LANES), f32),
            pltpu.VMEM((layers, 2 * width, width), f32),
            pltpu.SemaphoreType.DMA((copies,)),
            pltpu.SemaphoreType.DMA((copies,)),
            pltpu.VMEM((layers, 2 * width, width), f32),
            pltpu.SemaphoreType.DMA,
            pltpu.VMEM((width, LANES), f32),
        ],
        compiler_params=pltpu.CompilerParams(collective_id=2, has_side_effects=True, vmem_limit_bytes=63 << 20),
        name="sum_and_update",
    )(pay, *moments, *shards, *smalls, power)


NS_PARTS = 3


def hand_over_kernel(*refs):
    half = len(refs) // 2
    for src, dst in zip(refs[:half], refs[half:]):
        dst[...] = src[...]


def hand_over(arrays):
    vmem = pl.BlockSpec(memory_space=pltpu.VMEM)
    return pl.pallas_call(
        hand_over_kernel,
        out_shape=tuple(jax.ShapeDtypeStruct(v.shape, v.dtype) for v in arrays),
        in_specs=[vmem] * len(arrays),
        out_specs=(vmem,) * len(arrays),
        name="hand_over",
    )(*arrays)


def per_device(
    n_batch,
    n_rows,
    features,
    edge_rows,
    edge_weight,
    halo_counts,
    labels,
    pair_rows,
    step,
    w_in,
    w_conv,
    w_head,
    biases,
    norm_params,
    head_bias,
    mom_in,
    mom_conv,
    mom_head,
    first_bias,
    first_norm,
    first_head,
    second_bias,
    second_norm,
    second_head,
):
    rows_dev = features.shape[1]
    halo_rows = rows_dev // 4
    edge_count = edge_rows.shape[3]
    layers, hid = w_conv.shape[0], w_conv.shape[2]
    feat, classes = w_in.shape[0], w_head.shape[1]
    pairs = pair_rows.shape[3]
    node_count = rows_dev * n_rows
    all_nodes = node_count * n_batch
    flat = [
        edge_rows.reshape(2 * edge_count).astype(f32),
        edge_weight.reshape(edge_count),
        labels.reshape(rows_dev).astype(f32),
        pair_rows.reshape(n_rows * pairs).astype(f32),
    ]
    flat = jnp.concatenate(flat)
    flat = jnp.pad(flat, (0, -flat.shape[0] % (8 * LANES))).reshape(-1, LANES)
    flat = redeal(flat, n_batch, n_rows)
    inputs = redeal(features, n_batch, n_rows)[0]
    e = edge_count // LANES
    block = my_place()[1]
    wide = (rows_dev + 2 * halo_rows) // TILE
    rims = jnp.stack([(block > 0).astype(jnp.int32), (block < n_rows - 1).astype(jnp.int32)])
    *adjacency, row_sums = fill(flat[:e], flat[e : 2 * e], flat[2 * e : 3 * e], rims, rows_dev // TILE, wide, halo_rows // TILE, 2)
    label_rows = rows_dev // LANES
    picks = flat[3 * e + label_rows :].reshape(-1)[: n_rows * pairs].astype(jnp.int32)
    spread = jnp.pad(picks.reshape(n_rows, pairs), ((0, 0), (0, 8 - pairs)), constant_values=-1).reshape(1, n_rows * 8)
    spread = jnp.pad(spread, ((0, 0), (0, -spread.shape[1] % LANES)), constant_values=-1)
    at_in = 2 * hid
    at_head = at_in + -(-feat // 8) * 8
    at_small = at_head + hid // 2
    used = at_small + layers + 1 + 2 * layers + 2
    unit = 8 * n_rows * n_batch
    pay_rows = -(-used // unit) * unit
    rows_at = (at_in, at_head, at_small)
    turned = [
        w_in.T,
        w_conv,
        w_head.T,
        mom_in.T,
        mom_conv,
        mom_head.T,
    ]
    pay, full_min, full_mconv, full_mhead = step_call(
        n_rows,
        n_batch,
        layers,
        node_count,
        all_nodes,
        classes,
        rows_at,
        pay_rows,
        3 * e,
        inputs,
        flat,
        row_sums,
        biases,
        norm_params,
        head_bias[None],
        picks,
        spread,
        adjacency,
        turned,
    )
    count = step[0].astype(f32)
    power = jnp.stack([1.0 - jnp.power(adam_first_decay, count), 1.0 - jnp.power(adam_second_decay, count)])
    scales = (
        math.sqrt(max(1.0, hid / feat)),
        math.sqrt(max(1.0, hid / (2 * hid))),
        math.sqrt(max(1.0, classes / hid)),
    )
    smalls = (
        biases,
        norm_params,
        head_bias[None],
        first_bias,
        first_norm,
        first_head[None],
        second_bias,
        second_norm,
        second_head[None],
    )
    outs = update_call(
        n_rows,
        n_batch,
        layers,
        all_nodes,
        rows_at,
        classes,
        NS_PARTS,
        scales,
        pay_rows,
        pay,
        (full_min, full_mconv, full_mhead),
        (turned[0], w_conv, turned[2]),
        smalls,
        power,
    )
    outs = hand_over(outs)
    loss, new_in, new_conv, new_head, moment_in, moment_conv, moment_head = outs[:7]
    rest = []
    for i in range(0, 9, 3):
        rest += [outs[7 + i], outs[8 + i], outs[9 + i][0]]
    return (loss[0, 0], new_in.T, new_conv, new_head.T, moment_in.T, moment_conv, moment_head.T, *rest)


def solution(mesh):
    in_specs = (
        P("batch", "rows", None),
        P("batch", "rows", None, None),
        P("batch", "rows", None),
        P("batch", "rows", None),
        P("batch", "rows"),
        P("batch", "rows", None, None),
        P(),
        P(None, "batch"),
        P(None, "batch", None),
        P("batch", None),
        P(),
        P(),
        P(),
        P(None, "batch"),
        P(None, "batch", None),
        P("batch", None),
        P(),
        P(),
        P(),
        P(),
        P(),
        P(),
    )
    out_specs = (
        P(),
        P(None, "batch"),
        P(None, "batch", None),
        P("batch", None),
        P(None, "batch"),
        P(None, "batch", None),
        P("batch", None),
        P(),
        P(),
        P(),
        P(),
        P(),
        P(),
        P(),
        P(),
        P(),
    )
    body = functools.partial(per_device, mesh.shape["batch"], mesh.shape["rows"])
    return jax.shard_map(body, mesh=mesh, in_specs=in_specs, out_specs=out_specs, check_vma=False)
```

```python
import functools
import math

import jax
import jax.numpy as jnp
from jax import lax
from jax.experimental import pallas as pl
from jax.experimental.pallas import tpu as pltpu
from jax.sharding import PartitionSpec as P

NS_STEPS = 5

f32 = jnp.float32
bf16 = jnp.bfloat16
LANES = 128
TILE = 256
highest = lax.Precision.HIGHEST
norm_epsilon = 1e-05
pair_weight = 0.05
newton_a = 3.4445
newton_b = -4.775
newton_c = 2.0315
muon_decay = 0.9
muon_rate = 0.5
muon_shrink = 0.01
adam_first_decay = 0.9
adam_second_decay = 0.999
adam_epsilon = 1e-08
adam_rate = 0.1
adam_shrink = 0.01


def swap(b, r):
    return 2 * (b // 2) + r % 2, 2 * (r // 2) + b % 2


def flat_pairs(n_batch, n_rows, move):
    pairs = []
    for b in range(n_batch):
        for r in range(n_rows):
            to = move(b, r)
            if to is not None:
                pairs.append((b * n_rows + r, to[0] * n_rows + to[1]))
    return pairs


def redeal(array, n_batch, n_rows):
    return lax.ppermute(array, ("batch", "rows"), flat_pairs(n_batch, n_rows, swap))


def peer_place(batch, block):
    two = jnp.int32(2)
    return (
        two * lax.div(batch, two) + lax.rem(block, two),
        two * lax.div(block, two) + lax.rem(batch, two),
    )


def my_place():
    return peer_place(lax.axis_index("batch"), lax.axis_index("rows"))


def put_in_order(wide, to_ref, from_ref, w_ref, key_out, w_out, col_out, range_out):
    to, frm = to_ref[...].astype(jnp.int32), from_ref[...].astype(jnp.int32)
    key = (((to >> 8) * wide + (frm >> 8)) << 16) | ((to & 255) << 8) | (frm & 255)
    shape3 = (16, 8, LANES)
    key = key.astype(f32).reshape(shape3)
    w = w_ref[...].reshape(shape3)
    sub = lax.broadcasted_iota(jnp.int32, shape3, 1)
    lane = lax.broadcasted_iota(jnp.int32, shape3, 2)
    vreg = lax.broadcasted_iota(jnp.int32, shape3, 0)
    place = vreg + 16 * sub + 128 * lane
    for phase in range(14):
        for bit in range(phase, -1, -1):
            down = ((place >> (phase + 1)) & 1) == 1
            if bit < 4:
                view = (16 >> (bit + 1), 2, 1 << bit, 8, LANES)
                kv, wv = key.reshape(view), w.reshape(view)
                dv = down.astype(jnp.int32).reshape(view)[:, 0] == 1
                a, b, wa, wb = kv[:, 0], kv[:, 1], wv[:, 0], wv[:, 1]
                turn = jnp.logical_xor(a > b, dv)
                key = jnp.stack([jnp.where(turn, b, a), jnp.where(turn, a, b)], 1).reshape(shape3)
                w = jnp.stack([jnp.where(turn, wb, wa), jnp.where(turn, wa, wb)], 1).reshape(shape3)
            else:
                if bit < 7:
                    axis, gap, size, pos = 1, 1 << (bit - 4), 8, sub
                else:
                    axis, gap, size, pos = 2, 1 << (bit - 7), LANES, lane
                low = (pos & gap) == 0
                kp = jnp.where(low, pltpu.roll(key, size - gap, axis), pltpu.roll(key, gap, axis))
                wp = jnp.where(low, pltpu.roll(w, size - gap, axis), pltpu.roll(w, gap, axis))
                smaller = jnp.logical_xor(low, down)
                take = jnp.where(smaller, kp, key) < jnp.where(smaller, key, kp)
                key = jnp.where(take, kp, key)
                w = jnp.where(take, wp, w)
    flat = key.reshape(LANES, LANES)
    key_out[...] = flat.T.astype(jnp.int32)
    w_out[...] = w.reshape(LANES, LANES).T
    start = (lax.broadcasted_iota(jnp.int32, (8, LANES), 1).astype(f32) * 65536.0)[None]
    below = jnp.zeros(shape3, f32)
    upto = jnp.zeros(shape3, f32)
    for c in range(LANES):
        wide_key = jnp.broadcast_to(flat[:, c : c + 1], (LANES, LANES))
        col_out[c] = (wide_key - jnp.floor(wide_key * (1.0 / 256.0)) * 256.0).astype(bf16)
        wide_key = wide_key.reshape(shape3)
        below = below + jnp.where(wide_key < start, 1.0, 0.0)
        upto = upto + jnp.where(wide_key < start + 65536.0, 1.0, 0.0)
    range_out[...] = jnp.zeros_like(range_out)
    n_below = jnp.sum(below.reshape(LANES, LANES), axis=0, keepdims=True)
    n_upto = jnp.sum(upto.reshape(LANES, LANES), axis=0, keepdims=True)
    first = jnp.floor(n_below * (1.0 / 128.0))
    end = jnp.floor((n_upto + 127.0) * (1.0 / 128.0))
    range_out[0:1] = first.astype(jnp.int32)
    range_out[1:2] = jnp.where(n_upto > n_below, end, first).astype(jnp.int32)


def fill_kernel(wide, rim, chunk, parts, rims, to_ref, from_ref, weight_ref, *refs):
    outs, sums = refs[:parts], refs[parts]
    acc, rowacc, key_ref, w_ref, col_ref, ranges, span_of, sem = refs[parts + 1 :]
    i = pl.program_id(0)

    @pl.when(i == 0)
    def _():
        put_in_order(wide, to_ref, from_ref, weight_ref, key_ref, w_ref, col_ref, ranges)
        copy = pltpu.make_async_copy(ranges, span_of, sem)
        copy.start()
        copy.wait()

    pack = 16
    shape = (TILE // pack, pack, LANES)
    rows = lax.broadcasted_iota(jnp.int32, shape, 0) * pack + lax.broadcasted_iota(jnp.int32, shape, 1)
    rows = rows.astype(f32).astype(bf16)
    lanes = lax.broadcasted_iota(jnp.int32, (LANES, LANES), 1).astype(f32)
    lanes0, lanes1 = lanes.astype(bf16), (lanes + 128.0).astype(bf16)
    one, zero = jnp.ones((), bf16), jnp.zeros((), bf16)

    def spread(row):
        return jnp.broadcast_to(row, (pack, LANES)).astype(bf16)[None]

    rowacc[...] = jnp.zeros_like(rowacc)

    def tile(j, _):
        b = i * wide + j
        first, end = span_of[0, b], span_of[1, b]
        end = jnp.where(jnp.logical_and(j < rim, rims[0] == 0), first, end)
        end = jnp.where(jnp.logical_and(j >= wide - rim, rims[1] == 0), first, end)
        slot = jnp.where(j < rim, wide - 2 * rim + j, jnp.where(j < wide - rim, j - rim, j))
        cols = pl.ds(pl.multiple_of(slot * TILE, TILE), TILE)

        @pl.when(end <= first)
        def _():
            for out in outs:
                out[:, cols] = jnp.zeros((TILE, TILE), bf16)

        @pl.when(end > first)
        def _():
            def part(base, c):
                row = jnp.minimum(base + c, LANES - 1)
                here = key_ref[pl.ds(row, 1), :] - (b << 16)
                if c:
                    here = jnp.where(base + c < end, here, -1)
                at = rows == spread((here >> 8).astype(f32))
                rest = w_ref[pl.ds(row, 1), :]
                left = []
                for q in range(parts):
                    piece = rest.astype(bf16).astype(f32)
                    rest = rest - piece
                    left.append(jnp.where(at, spread(piece), zero).reshape(TILE, LANES))
                col = col_ref[row]
                right = jnp.concatenate(
                    [jnp.where(col == lanes0, one, zero), jnp.where(col == lanes1, one, zero)], 1
                )
                return left, right

            def get(base):
                made = [part(base, c) for c in range(chunk)]
                lhs = jnp.concatenate([m[0][q] for q in range(parts) for m in made], 1)
                rhs = jnp.concatenate([m[1] for m in made] * parts, 0)
                return jnp.dot(lhs, rhs, preferred_element_type=f32)

            acc[...] = get(first)

            def more(t, _):
                acc[...] += get(first + t * chunk)
                return 0

            lax.fori_loop(1, lax.div(end - first + chunk - 1, chunk), more, 0)
            rest = acc[...]
            rowacc[...] += rest[:, :LANES] + rest[:, LANES:]
            for out in outs:
                piece = rest.astype(bf16)
                out[:, cols] = piece
                rest = rest - piece.astype(f32)

        return 0

    lax.fori_loop(0, wide, tile, 0)
    total = jnp.sum(rowacc[...], axis=1, keepdims=True)
    for half in range(TILE // LANES):
        column = jnp.broadcast_to(total[half * LANES : (half + 1) * LANES], (LANES, LANES))
        sums[0, half : half + 1] = column.T[0:1]


def fill(to, frm, weights, rims, tiles, wide, rim, parts, chunk=5):
    cols = wide * TILE
    return pl.pallas_call(
        functools.partial(fill_kernel, wide, rim, chunk, parts),
        out_shape=tuple(jax.ShapeDtypeStruct((tiles * TILE, cols), bf16) for _ in range(parts))
        + (jax.ShapeDtypeStruct((tiles, TILE // LANES, LANES), f32),),
        grid_spec=pltpu.PrefetchScalarGridSpec(
            num_scalar_prefetch=1,
            grid=(tiles,),
            in_specs=[pl.BlockSpec((LANES, LANES), lambda i, *_: (0, 0))] * 3,
            out_specs=tuple(pl.BlockSpec((TILE, cols), lambda i, *_: (i, 0)) for _ in range(parts))
            + (pl.BlockSpec((1, TILE // LANES, LANES), lambda i, *_: (i, 0, 0)),),
            scratch_shapes=[
                pltpu.VMEM((TILE, TILE), f32),
                pltpu.VMEM((TILE, LANES), f32),
                pltpu.VMEM((LANES, LANES), jnp.int32),
                pltpu.VMEM((LANES, LANES), f32),
                pltpu.VMEM((LANES, LANES, LANES), bf16),
                pltpu.VMEM((8, LANES), jnp.int32),
                pltpu.SMEM((8, LANES), jnp.int32),
                pltpu.SemaphoreType.DMA,
            ],
        ),
        compiler_params=pltpu.CompilerParams(vmem_limit_bytes=50 << 20),
        name="adjacency_tiles",
    )(rims, to, frm, weights)


def parts_of(x, count):
    found = []
    for q in range(count):
        piece = x.astype(bf16)
        found.append(piece)
        if q + 1 < count:
            x = x - piece.astype(f32)
    return found


def pair_list(count):
    return [(p, q) for p in range(count) for q in range(count) if p + q < count]


def dots(left, right, dims=((1,), (0,))):
    total = None
    for p, q in pair_list(len(left)):
        piece = lax.dot_general(left[p], right[q], (dims, ((), ())), preferred_element_type=f32)
        total = piece if total is None else total + piece
    return total


def remote(src, dst, send, recv, to):
    return pltpu.make_async_remote_copy(
        src_ref=src,
        dst_ref=dst,
        send_sem=send,
        recv_sem=recv,
        device_id=to,
        device_id_type=pl.DeviceIdType.MESH,
    )


def column_sums(x):
    return jnp.sum(x, axis=0, keepdims=True)


def folded(x):
    return jnp.sum(x.reshape(x.shape[0] // 8, 8, x.shape[1]), axis=0)


def plane_split(nb, n):
    cores = 2 if nb % 2 == 0 else 1
    across = 1
    while across * across * 4 <= n and n % (across * 2) == 0:
        across *= 2
    return cores, nb // cores, across, n // across


class Places:
    def __init__(self, n, nb):
        self.cores, ys, self.xs, self.zs = plane_split(nb, n)
        self.planes = ys * self.xs
        self.b, self.r = lax.axis_index("batch"), lax.axis_index("rows")
        self.core, y = lax.rem(self.b, self.cores), lax.div(self.b, self.cores)
        self.x, self.z = lax.rem(self.r, self.xs), lax.div(self.r, self.xs)
        self.spot = y * self.xs + self.x
        self.core_peer = (y * self.cores + lax.rem(self.core + 1, self.cores), self.r)
        self.peers = [self.plane_peer(k)[1] for k in range(1, self.planes)]
        self.peers += [self.column_peer(k)[1] for k in range(1, self.zs)]
        if self.cores == 2:
            self.peers.append(self.core_peer)

    def plane_peer(self, k):
        p = lax.rem(self.spot + k, self.planes)
        return p, (lax.div(p, self.xs) * self.cores + self.core, self.z * self.xs + lax.rem(p, self.xs))

    def column_peer(self, k):
        q = lax.rem(self.z + k, self.zs)
        return q, (self.b, q * self.xs + self.x)


TURNED = ((0,), (0,))
GATHERED = 3


def step_kernel(n, nb, layers, nodes, all_nodes, classes, rows_at, summed_rows, label_at, *refs):
    (x_ref, label_ref, sums_ref, bias_ref, norm_ref, head_bias_ref, pick_smem, pick_row, a1_hbm, a2_hbm) = refs[:10]
    own_in, own_conv, own_head, own_min, own_mconv, own_mhead = refs[10:16]
    pay, full_min, full_mconv, full_mhead = refs[16:20]
    (act, agg, a1, a2, p1, p2, g1, g2, gh, rim, out_rim, logit, sent, got, stat, held, w_in, w_conv, w_head,
     wt, a_sem, stat_send, stat_recv, rim_send, rim_recv, pair_send, pair_recv, w_send, w_recv, w_own, sum_send, sum_recv,
     ready, normed, keep, stood, laid_head, laid_mhead, wide_bias) = refs[20:]
    rows, width = act.shape[1], act.shape[2]
    halo = rim.shape[2]
    a, ps, gs = (a1, a2), (p1, p2), (g1, g2)
    here_b, here_r = lax.axis_index("batch"), lax.axis_index("rows")
    batch, block = my_place()
    first, last = block == 0, block == n - 1
    not_first, not_last = jnp.logical_not(first), jnp.logical_not(last)

    barrier = pltpu.get_barrier_semaphore()
    for k in range(1, n):
        pl.semaphore_signal(
            barrier, inc=1, device_id=peer_place(batch, lax.rem(block + k, n)), device_id_type=pl.DeviceIdType.MESH
        )
    for k in range(1, nb):
        pl.semaphore_signal(
            barrier, inc=1, device_id=(lax.rem(here_b + k, nb), here_r), device_id_type=pl.DeviceIdType.MESH
        )
    places = Places(n, nb)
    for peer in places.peers:
        pl.semaphore_signal(barrier, inc=1, device_id=peer, device_id_type=pl.DeviceIdType.MESH)
    height = 512
    steps = rows // height
    own_cols, rim_cols = pl.ds(0, rows), pl.ds(rows, 2 * halo)

    def load(s, cols, which):
        span = pl.ds(pl.multiple_of(s * height, height), height)
        return [
            pltpu.make_async_copy(src.at[span, cols], dst.at[span, cols], a_sem.at[2 * (steps * which + s) + q])
            for q, (src, dst) in enumerate(zip((a1_hbm, a2_hbm), a))
        ]

    for s in range(steps):
        for copy in load(s, own_cols, 0):
            copy.start()
    for src, dst in ((own_head, laid_head), (own_mhead, laid_mhead)):
        stood[...] = jnp.zeros_like(stood)
        stood[0:classes] = src[...]
        dst[...] = stood[...].T
    wide_bias[...] = jnp.zeros_like(wide_bias)
    wide_bias[0:1, 0:classes] = head_bias_ref[...]
    pl.semaphore_wait(barrier, n - 1 + nb - 1 + len(places.peers))

    def gathers(item, src, dst):
        span = src.shape[-2]
        lead = (slice(None),) * (len(src.shape) - 2)
        mine = dst.at[lead + (pl.ds(pl.multiple_of(here_b * span, 8), span),)]
        copies = [pltpu.make_async_copy(src, mine, w_own.at[item])]
        for k in range(1, nb):
            copies.append(remote(src, mine, w_send.at[item, k], w_recv.at[item, k], (lax.rem(here_b + k, nb), here_r)))
        return copies

    def gather(item, src, dst):
        copies = gathers(item, src, dst)
        for copy in copies:
            copy.start()
        return copies

    def arrived(copies):
        for copy in copies:
            copy.wait()

    in_copies = gather(0, own_in, w_in)
    for q in range(layers):
        gather(2 + q, own_conv.at[q], w_conv.at[q])
    head_copies = gather(1, laid_head, w_head)

    def stat_copies(e):
        return [
            remote(stat.at[e], held.at[e, k], stat_send.at[e, k], stat_recv.at[e, k], peer_place(batch, lax.rem(block + k, n)))
            for k in range(1, n)
        ]

    def stats_start(e):
        held[e, 0] = stat[e]
        for copy in stat_copies(e):
            copy.start()

    def stats_finish(e):
        arrived(stat_copies(e))
        total = held[e, lax.rem(block, n)]
        for q in range(1, n):
            total = total + held[e, lax.rem(block + n - q, n)]
        return total

    def rims_of(e, low_src, high_src):
        slot = lax.rem(e, 2)
        return (
            remote(low_src, rim.at[slot, 1], rim_send.at[e, 1], rim_recv.at[e, 1], peer_place(batch, lax.rem(block + n - 1, n))),
            remote(high_src, rim.at[slot, 0], rim_send.at[e, 0], rim_recv.at[e, 0], peer_place(batch, lax.rem(block + 1, n))),
        )

    def start_if(condition, copy):
        @pl.when(condition)
        def _():
            copy.start()

    def rims_sent(copies):
        @pl.when(not_first)
        def _():
            copies[0].wait_send()

        @pl.when(not_last)
        def _():
            copies[1].wait_send()

    tile = 256
    tiles = rows // tile

    def rows_of(s, size):
        return pl.ds(pl.multiple_of(s * size, size), size)

    zeros8 = jnp.zeros((8, width), f32)

    arrived(in_copies)
    turned_in = parts_of(w_in[...].T, 3)

    def project(s, _):
        span = rows_of(s, tile)
        h = dots(parts_of(x_ref[span, :], 3), turned_in) + bias_ref[0:1]
        act[0, span] = h
        for dst, piece in zip(ps, parts_of(h, 2)):
            dst[span, :] = piece
        return 0

    lax.fori_loop(0, tiles, project, 0)
    stat[0] = jnp.zeros((2, width), f32)
    def set_norm(l, totals):
        mean = totals[0:1] * (1.0 / nodes)
        inverse = lax.rsqrt(totals[1:2] * (1.0 / nodes) - mean * mean + norm_epsilon)
        under = lax.max(l - 1, 0)
        scale = norm_ref[under, 0:1] * inverse
        offset = norm_ref[under, 1:2] - mean * scale
        plain = l == 0
        normed[l, 0:1] = jnp.where(plain, 0.0, mean)
        normed[l, 1:2] = jnp.where(plain, 1.0, inverse)
        normed[l, 2:3] = jnp.where(plain, 1.0, scale)
        normed[l, 3:4] = jnp.where(plain, 0.0, offset)

    bias_row = lax.broadcasted_iota(jnp.int32, bias_ref.shape, 0)

    def forward(l, _):
        copies = rims_of(l, act.at[l, pl.ds(0, halo)], act.at[l, pl.ds(rows - halo, halo)])
        start_if(not_first, copies[0])
        start_if(not_last, copies[1])
        stats_start(l)

        def own(s, _):
            span = rows_of(s, height)

            @pl.when(l == 0)
            def _():
                for copy in load(s, own_cols, 0):
                    copy.wait()
                for copy in load(s, rim_cols, 1):
                    copy.start()

            agg[l, span] = dots([q[span, own_cols] for q in a], [q[own_cols, :] for q in ps])
            return 0

        lax.fori_loop(0, rows // height, own, 0)
        set_norm(l, stats_finish(l))
        slot = lax.rem(l, 2)
        for which, gone in ((0, first), (1, last)):
            @pl.when(gone)
            def _():
                rim[slot, which] = jnp.zeros((halo, width), f32)

            @pl.when(jnp.logical_not(gone))
            def _():
                remote(rim.at[slot, which], rim.at[slot, which], rim_send.at[l, which], rim_recv.at[l, which],
                       peer_place(batch, lax.rem(block + 1, n))).wait_recv()

            for dst, piece in zip(ps, parts_of(rim[slot, which], 2)):
                dst[pl.ds(rows + which * halo, halo), :] = piece

        def rims_in(s, _):
            span = rows_of(s, height)

            @pl.when(l == 0)
            def _():
                for copy in load(s, rim_cols, 1):
                    copy.wait()

            agg[l, span] += dots([q[span, rim_cols] for q in a], [q[rim_cols, :] for q in ps])
            return 0

        lax.fori_loop(0, rows // height, rims_in, 0)
        arrived(gathers(2 + l, own_conv.at[l], w_conv.at[l]))
        weights = parts_of(w_conv[l], 3)
        bias = column_sums(jnp.where(bias_row == l + 1, bias_ref[...], 0.0))
        scale, offset = normed[l, 2:3], normed[l, 3:4]

        def finish(s, sums):
            span = rows_of(s, tile)
            row_sum = jnp.concatenate(
                [jnp.broadcast_to(sums_ref[s, i : i + 1], (LANES, LANES)).T for i in range(tile // LANES)], 0
            )
            found = agg[l, span] * scale + jnp.concatenate([row_sum] * (width // LANES), 1) * offset
            agg[l, span] = found
            h = act[l, span] * scale + offset
            pre = dots(parts_of(jnp.concatenate([h, found], 1), 3), weights) + bias
            active = jnp.maximum(pre, 0.0)
            act[l + 1, span] = active
            for dst, piece in zip(ps, parts_of(active, 2)):
                dst[span, :] = piece
            return sums[0] + folded(active), sums[1] + folded(active * active)

        sums = lax.fori_loop(0, tiles, finish, (zeros8, zeros8))
        stat[l + 1, 0:1] = column_sums(sums[0])
        stat[l + 1, 1:2] = column_sums(sums[1])
        rims_sent(copies)
        return 0

    lax.fori_loop(0, layers, forward, 0)

    stats_start(layers)
    base = 2 + layers
    late = [gather(base, own_min, full_min), gather(base + 1, laid_mhead, full_mhead), gather(base + 2, own_mconv, full_mconv)]
    arrived(head_copies)
    head_parts = parts_of(w_head[...], 3)
    head_turned = parts_of(w_head[...].T, 2)
    set_norm(layers, stats_finish(layers))
    top_scale, top_offset = normed[layers, 2:3], normed[layers, 3:4]
    top_mean, top_inverse = normed[layers, 0:1], normed[layers, 1:2]

    def top(span):
        return act[layers, span] * top_scale + top_offset

    def classify(s, _):
        span = rows_of(s, tile)
        logit[span, :] = dots(parts_of(top(span), 3), head_parts) + wide_bias[0:1]
        return 0

    lax.fori_loop(0, tiles, classify, 0)
    per = pick_smem.shape[0] // n
    sent[...] = jnp.zeros_like(sent)
    for d in range(n):
        for k in range(per):
            sent[d, k : k + 1] = logit[pl.ds(pick_smem[d * per + k], 1), :]
    pair_copies = []
    for k in range(1, n):
        peer = lax.rem(block + k, n)
        copy = remote(sent.at[peer], got.at[k], pair_send.at[k], pair_recv.at[k], peer_place(batch, peer))
        copy.start()
        pair_copies.append(copy)
    got[0] = sent[block]
    lane = lax.broadcasted_iota(jnp.int32, (tile, LANES), 1)
    real = lane < classes

    def soften(s, loss):
        span = rows_of(s, tile)
        z = logit[span, :]
        top_z = jnp.max(jnp.where(real, z, -jnp.inf), axis=1, keepdims=True)
        e = jnp.where(real, jnp.exp(z - top_z), 0.0)
        total = jnp.sum(e, axis=1, keepdims=True)
        named = [
            jnp.broadcast_to(label_ref[pl.ds(label_at + s * (tile // LANES) + i, 1), :], (LANES, LANES)).T for i in range(tile // LANES)
        ]
        hot = jnp.logical_and(real, lane.astype(f32) == jnp.concatenate(named, 0))
        logit[span, :] = e / total - jnp.where(hot, 1.0, 0.0)
        part = jnp.where(lane == 0, top_z + jnp.log(total), 0.0) - jnp.where(hot, z, 0.0)
        return loss + folded(part)

    loss = lax.fori_loop(0, tiles, soften, jnp.zeros((8, LANES), f32))
    arrived(pair_copies)
    gaps = []
    for d in range(n):
        gaps.append(sent[d] - got[lax.rem(block + n - d, n)])
    gap = jnp.concatenate(gaps, 0)
    loss = loss + pair_weight * folded(gap * gap)
    spare = pick_row.shape[1] - gap.shape[0]
    if spare:
        gap = jnp.concatenate([gap, jnp.zeros((spare, LANES), f32)], 0)
    gap_parts = parts_of(gap * (4.0 * pair_weight), 3)
    at_head, at_small = rows_at[1], rows_at[2]
    small = layers + 1

    def finish_head(s, sums):
        span = rows_of(s, tile)
        spot = lax.broadcasted_iota(jnp.int32, (tile, pick_row.shape[1]), 0) + s * tile
        chosen = jnp.where(spot == pick_row[...], 1.0, 0.0).astype(bf16)
        add = None
        for piece in gap_parts:
            v = jnp.dot(chosen, piece, preferred_element_type=f32)
            add = v if add is None else add + v
        grad = (logit[span, :] + add) * (1.0 / all_nodes)
        grad_parts = parts_of(grad, 2)
        h = top(span)
        back = dots(grad_parts, head_turned)
        gh[span, :] = back
        ready_top = (act[layers, span] - top_mean) * top_inverse
        return (
            sums[0] + dots(parts_of(h, 2), grad_parts, TURNED),
            sums[1] + folded(grad),
            sums[2] + folded(back),
            sums[3] + folded(back * ready_top),
        )

    begin = (
        jnp.zeros((width, LANES), f32),
        jnp.zeros((8, LANES), f32),
        jnp.zeros((8, width), f32),
        jnp.zeros((8, width), f32),
    )
    sums = lax.fori_loop(0, tiles, finish_head, begin)
    half = width // 2
    pay[pl.ds(at_head, half), :] = jnp.concatenate([sums[0][:half], sums[0][half:]], 1)
    tail = pl.ds(at_small, summed_rows - at_small)
    pay[tail, :] = jnp.zeros((summed_rows - at_small, width), f32)
    at_norm = at_small + small
    at_last = at_norm + 2 * layers
    pay[at_last : at_last + 1, 0:LANES] = column_sums(sums[1])
    pay[at_last + 1 : at_last + 2, 0:LANES] = column_sums(loss)
    after = layers + 1
    stat[after, 0:1] = column_sums(sums[2])
    stat[after, 1:2] = column_sums(sums[3])
    stats_start(after)

    big = 2 * width

    def conv_rows(l):
        return pl.multiple_of(jnp.where(l == 0, 0, summed_rows + (l - 1) * big), 8)

    def told(which):
        for peer in places.peers:
            pl.semaphore_signal(ready.at[which], inc=1, device_id=peer, device_id_type=pl.DeviceIdType.MESH)

    cores, planes, zs = places.cores, places.planes, places.zs
    core, spot = places.core, places.spot
    piece_rows = big // cores
    block_rows = piece_rows // planes
    cut = block_rows % (8 * zs) == 0
    slice_rows = block_rows // zs if cut else block_rows

    def part(ref, index, count):
        return ref.at[pl.ds(pl.multiple_of(index * count, 8), count)]

    class Sum:
        def __init__(self, l):
            self.which, room = l - 1, act.at[l + 1]
            self.local = pay.at[pl.ds(conv_rows(l), big)]
            self.whole = room.at[pl.ds(0, big)]
            spots = [piece_rows, piece_rows, piece_rows, block_rows, slice_rows * zs]
            views, at = [], big
            for count in spots:
                views.append(room.at[pl.ds(at, count)])
                at += count
            self.got1, self.sum1, self.got2, self.sum2, self.got3 = views

        def copies(self, stage):
            found = []

            def add(i, src, dst, to):
                found.append(remote(src, dst, sum_send.at[self.which, i], sum_recv.at[self.which, i], to))

            if stage == 0 and cores == 2:
                add(0, part(self.local, 1 - core, piece_rows), self.got1, places.core_peer)
            if stage == 1:
                for k in range(1, planes):
                    p, to = places.plane_peer(k)
                    add(k, part(self.sum1, p, block_rows), part(self.got2, k, block_rows), to)
            if stage == 2:
                for k in range(1, zs):
                    q, to = places.column_peer(k)
                    src = part(self.sum2, q, slice_rows) if cut else self.sum2
                    add(planes + k, src, part(self.got3, k, slice_rows), to)
            block = part(self.whole, core * planes + spot, block_rows)
            if stage == 3 and cut:
                mine = part(self.whole, (core * planes + spot) * zs + places.z, slice_rows)
                for k in range(1, zs):
                    add(planes + zs + k, mine, mine, places.column_peer(k)[1])
            if stage == 4:
                for k in range(1, planes):
                    add(planes + 2 * zs + k, block, block, places.plane_peer(k)[1])
            if stage == 5 and cores == 2:
                mine = part(self.whole, core, piece_rows)
                add(2 * planes + 2 * zs, mine, mine, places.core_peer)
            return found

        def go(self, stage):
            if stage == 0:
                pl.semaphore_wait(ready.at[self.which], len(places.peers))
            else:
                arrived(self.copies(stage - 1))
            if stage == 1:
                total = part(self.local, core, piece_rows)[...]
                if cores == 2:
                    total = total + self.got1[...]
                self.sum1[...] = total
            if stage == 2:
                total = part(self.sum1, spot, block_rows)[...]
                for k in range(1, planes):
                    total = total + part(self.got2, k, block_rows)[...]
                self.sum2[...] = total
                self.got3[pl.ds(0, slice_rows), :] = part(self.sum2, places.z, slice_rows)[...] if cut else total
            if stage == 3:
                total = part(self.got3, lax.rem(places.z, zs), slice_rows)[...]
                for q in range(1, zs):
                    total = total + part(self.got3, lax.rem(places.z + zs - q, zs), slice_rows)[...]
                if cut:
                    part(self.whole, (core * planes + spot) * zs + places.z, slice_rows)[...] = total
                else:
                    part(self.whole, core * planes + spot, block_rows)[...] = total
            if stage == 6:
                self.local[...] = self.whole[...]
            for copy in self.copies(stage):
                copy.start()

    def backward(turn, _):
        l = layers - 1 - turn
        e = after + turn

        def advance(stage):
            @pl.when(turn > 0)
            def _():
                Sum(l + 1).go(stage)

        keep[l, 0:1] = stat[e, 1:2]
        keep[l, 1:2] = stat[e, 0:1]
        for q, piece in enumerate(parts_of(w_conv[l].T, 2)):
            wt[q] = piece
        gain = norm_ref[l, 0:1]
        totals = stats_finish(e) * gain * (1.0 / nodes)
        mean, inverse = normed[l + 1, 0:1], normed[l + 1, 1:2]

        def enter(s, total):
            span = rows_of(s, tile)
            active = act[l + 1, span]
            rated = (active - mean) * inverse
            grad = inverse * (gh[span, :] * gain - totals[0:1] - rated * totals[1:2])
            grad = jnp.where(active > 0.0, grad, 0.0)
            pieces = parts_of(grad, 2)
            for dst, piece in zip(gs, pieces):
                dst[span, :] = piece
            joined = dots(pieces, [wt[0], wt[1]])
            gh[span, :] = joined[:, :width]
            for dst, piece in zip(ps, parts_of(joined[:, width:], 2)):
                dst[span, :] = piece
            return total + folded(grad)

        total = lax.fori_loop(0, tiles, enter, zeros8)
        keep[l, 2:3] = column_sums(total)

        @pl.when(l > 0)
        def _():
            told(l - 1)

        advance(1)

        @pl.when(turn > 1)
        def _():
            Sum(l + 2).go(5)

        copies = rims_of(e, out_rim.at[0], out_rim.at[1])

        def rims_out(which, _):
            cols = pl.ds(pl.multiple_of(rows + which * halo, 128), halo)
            out_rim[which] = dots([q[:, cols] for q in a], [q[own_cols, :] for q in ps], TURNED)
            for at, go in ((0, not_first), (1, not_last)):
                start_if(jnp.logical_and(go, which == at), copies[at])
            return 0

        lax.fori_loop(0, 2, rims_out, 0)
        advance(2)

        @pl.when(turn > 1)
        def _():
            Sum(l + 2).go(6)

        def spread_back(s, _):
            span = rows_of(s, height)
            gh[span, :] += dots([q[:, span] for q in a], [q[own_cols, :] for q in ps], TURNED)
            return 0

        lax.fori_loop(0, rows // height, spread_back, 0)
        advance(3)
        slot = lax.rem(e, 2)
        for which, go, start in ((1, not_last, rows - halo), (0, not_first, 0)):
            @pl.when(go)
            def _():
                remote(rim.at[slot, which], rim.at[slot, which], rim_send.at[e, which], rim_recv.at[e, which],
                       peer_place(batch, lax.rem(block + 1, n))).wait_recv()
                gh[pl.ds(start, halo), :] += rim[slot, which]

        below_mean, below_inverse = normed[l, 0:1], normed[l, 1:2]

        def tail_sums(s, sums):
            span = rows_of(s, tile)
            grad = gh[span, :]
            return sums[0] + folded(grad), sums[1] + folded(grad * ((act[l, span] - below_mean) * below_inverse))

        sums = lax.fori_loop(0, tiles, tail_sums, (zeros8, zeros8))
        stat[e + 1, 0:1] = column_sums(sums[0])
        stat[e + 1, 1:2] = column_sums(sums[1])

        @pl.when(l > 0)
        def _():
            stats_start(e + 1)

        rims_sent(copies)
        advance(4)
        base = conv_rows(l)
        where = pl.ds(base, width)
        under = pl.ds(pl.multiple_of(base + width, 8), width)
        scale, offset = normed[l, 2:3], normed[l, 3:4]
        pay[pl.ds(base, big), :] = jnp.zeros((big, width), f32)

        def weigh(s, _):
            span = rows_of(s, height)
            h = act[l, span] * scale + offset
            grad = [q[span, :] for q in gs]
            pay[where, :] += dots(parts_of(h, 2), grad, TURNED)
            pay[under, :] += dots(parts_of(agg[l, span], 2), grad, TURNED)
            return 0

        lax.fori_loop(0, rows // height, weigh, 0)

        @pl.when(l > 0)
        def _():
            Sum(l).go(0)

        return 0

    lax.fori_loop(0, layers, backward, 0)
    pay[at_small : at_small + 1, :] = stat[after + layers, 0:1]
    for l in range(layers):
        pay[at_norm + 2 * l : at_norm + 2 * l + 2, :] = keep[l, 0:2]
        pay[at_small + 1 + l : at_small + 2 + l, :] = keep[l, 2:3]
    feat = x_ref.shape[1]
    pay[pl.ds(rows_at[0], rows_at[1] - rows_at[0]), :] = jnp.zeros((rows_at[1] - rows_at[0], width), f32)

    def weigh_in(s, total):
        span = rows_of(s, height)
        return total + dots(parts_of(x_ref[span, :], 2), parts_of(gh[span, :], 2), TURNED)

    pay[pl.ds(rows_at[0], feat), :] = lax.fori_loop(0, rows // height, weigh_in, jnp.zeros((feat, width), f32))
    if layers > 1:
        Sum(1).go(5)
    for copies in late:
        arrived(copies)
    if layers > 1:
        Sum(1).go(6)


def step_call(n, nb, layers, nodes, all_nodes, classes, rows_at, summed_rows, label_at, x, labels, sums, biases, norms, head_bias,
              picks, pick_row, adjacency, shards):
    rows = x.shape[0]
    width = biases.shape[1]
    cols = adjacency[0].shape[1]
    halo = (cols - rows) // 2
    feat = x.shape[1]
    vmem = pl.BlockSpec(memory_space=pltpu.VMEM)
    smem = pl.BlockSpec(memory_space=pltpu.SMEM)
    hbm = pl.BlockSpec(memory_space=pl.ANY)
    dma = pltpu.SemaphoreType.DMA
    items = 2 + layers + 3
    exchanges = 2 * layers + 1
    _, ys, across, zs = plane_split(nb, n)
    hops = 2 * ys * across + 2 * zs + 1
    return pl.pallas_call(
        functools.partial(step_kernel, n, nb, layers, nodes, all_nodes, classes, rows_at, summed_rows, label_at),
        out_shape=(
            jax.ShapeDtypeStruct((summed_rows + (layers - 1) * 2 * width, width), f32),
            jax.ShapeDtypeStruct((width, feat), f32),
            jax.ShapeDtypeStruct((layers, 2 * width, width), f32),
            jax.ShapeDtypeStruct((width, LANES), f32),
        ),
        in_specs=[vmem] * 6 + [smem, vmem] + [hbm] * 4 + [vmem] + [hbm] * 2 + [vmem],
        out_specs=(vmem, hbm, hbm, hbm),
        scratch_shapes=[
            pltpu.VMEM((layers + 1, rows, width), f32),
            pltpu.VMEM((layers, rows, width), f32),
            pltpu.VMEM((rows, cols), bf16),
            pltpu.VMEM((rows, cols), bf16),
            pltpu.VMEM((cols, width), bf16),
            pltpu.VMEM((cols, width), bf16),
            pltpu.VMEM((rows, width), bf16),
            pltpu.VMEM((rows, width), bf16),
            pltpu.VMEM((rows, width), f32),
            pltpu.VMEM((2, 2, halo, width), f32),
            pltpu.VMEM((2, halo, width), f32),
            pltpu.VMEM((rows, LANES), f32),
            pltpu.VMEM((n, 8, LANES), f32),
            pltpu.VMEM((n, 8, LANES), f32),
            pltpu.VMEM((exchanges + 1, 2, width), f32),
            pltpu.VMEM((exchanges, n, 2, width), f32),
            pltpu.VMEM((width, feat), f32),
            pltpu.VMEM((layers, 2 * width, width), f32),
            pltpu.VMEM((width, LANES), f32),
            pltpu.VMEM((2, width, 2 * width), bf16),
            dma((4 * rows // 512,)),
            dma((exchanges, n)),
            dma((exchanges, n)),
            dma((exchanges, 2)),
            dma((exchanges, 2)),
            dma((n,)),
            dma((n,)),
            dma((items, nb)),
            dma((items, nb)),
            dma((items,)),
            dma((layers - 1, hops)),
            dma((layers - 1, hops)),
            pltpu.SemaphoreType.REGULAR((layers - 1,)),
            pltpu.VMEM((layers + 1, 4, width), f32),
            pltpu.VMEM((layers, 4, width), f32),
            pltpu.VMEM((LANES, width // nb), f32),
            pltpu.VMEM((width // nb, LANES), f32),
            pltpu.VMEM((width // nb, LANES), f32),
            pltpu.VMEM((8, LANES), f32),
        ],
        compiler_params=pltpu.CompilerParams(collective_id=1, has_side_effects=True, vmem_limit_bytes=63 << 20),
        name="forward_backward",
    )(x, labels, sums, biases, norms, head_bias, picks, pick_row, *adjacency, *shards)


def update_kernel(n, nb, layers, all_nodes, rows_at, classes, ns_parts, scales, summed_rows, pay, mom_in, mom_conv, mom_head, w_in,
                  w_conv, w_head, biases, norms, head_bias, fb, fn, fh, sb, sn, sh, power, *refs):
    (loss_o, in_o, conv_o, head_o, min_o, mconv_o, mhead_o, b_o, n_o, h_o, fb_o, fn_o, fh_o, sb_o, sn_o, sh_o) = refs[:16]
    (got1, sum1, got2, sum2, got3, full, gram, poly, small_gram, small_poly, mconv, send, recv, old_conv, old_sem, spread) = refs[16:]
    places = Places(n, nb)
    cores, planes, zs = places.cores, places.planes, places.zs
    core, spot, z = places.core, places.spot, places.z
    plane_peer, column_peer, core_peer = places.plane_peer, places.column_peer, places.core_peer
    here_b = places.b
    width = w_conv.shape[2]
    barrier = pltpu.get_barrier_semaphore()
    for peer in places.peers:
        pl.semaphore_signal(barrier, inc=1, device_id=peer, device_id_type=pl.DeviceIdType.MESH)

    def kdot(left, right, dims=((1,), (0,))):
        return dots(parts_of(left, ns_parts), parts_of(right, ns_parts), dims)

    def eye(k):
        return (lax.broadcasted_iota(jnp.int32, (k, k), 0) == lax.broadcasted_iota(jnp.int32, (k, k), 1)).astype(f32)

    def begin(moment, grams, i):
        size = jnp.sqrt(jnp.sum(moment * moment)) + 1e-07
        g = kdot(moment, moment, TURNED) / (size * size)
        grams[i] = g
        return size

    def step(grams, polys, which, early, late):
        k = grams.shape[1]
        count = len(which)
        def split(values):
            return [parts_of(v, ns_parts) for v in values]

        a1 = [grams[i] for i in which]
        a1_parts = split(a1)
        a2 = [dots(v, v) for v in a1_parts]
        p = [newton_a * eye(k) + newton_b * v + newton_c * u for v, u in zip(a1, a2)]
        p_parts = split(p)
        if not late:
            pa = [dots(v, u) for v, u in zip(p_parts, a1_parts)]
        if early:
            q = p
        else:
            q = [dots(v, parts_of(polys[i], ns_parts)) for i, v in zip(which, p_parts)]
        if not late:
            nxt = [dots(v, u) for v, u in zip(split(pa), p_parts)]
        for j in range(count):
            polys[which[j]] = q[j]
            if not late:
                grams[which[j]] = nxt[j]

    fetch = pltpu.make_async_copy(mom_conv, old_conv, old_sem)
    fetch.start()
    sizes = {}
    ready = tuple(range(1, layers))

    def start_ready():
        fetch.wait()
        for l in ready:
            mconv[l] = muon_decay * old_conv[l] + pay[summed_rows + (l - 1) * 2 * width : summed_rows + l * 2 * width]
            sizes[l] = begin(mconv[l], gram, l)

    def middle(count, grams, polys, which):
        lax.fori_loop(0, count, lambda _, c: (step(grams, polys, which, False, False), c)[1], 0)

    pl.semaphore_wait(barrier, len(places.peers))
    used = [0]

    def go(src, dst, to):
        i = used[0]
        used[0] += 1
        copy = remote(src, dst, send.at[i], recv.at[i], to)
        copy.start()
        return copy

    def settle(copies):
        for copy in copies:
            copy.wait()

    half_rows = summed_rows // cores
    block_rows = half_rows // planes
    m = block_rows // zs

    def part(ref, index, count):
        return ref.at[pl.ds(pl.multiple_of(index * count, 8), count)]

    if cores == 2:
        copies = [go(part(pay, 1 - core, half_rows), got1, core_peer)]
        start_ready()
        settle(copies)
        sum1[...] = part(pay, core, half_rows)[...] + got1[...]
    else:
        start_ready()
        sum1[...] = pay[pl.ds(0, half_rows), :]
    copies = []
    for k in range(1, planes):
        p, to = plane_peer(k)
        copies.append(go(part(sum1, p, block_rows), got2.at[k], to))
    step(gram, poly, ready, True, False)
    middle(1, gram, poly, ready)
    settle(copies)
    total = part(sum1, spot, block_rows)[...]
    for k in range(1, planes):
        total = total + got2[k]
    sum2[...] = total
    copies = []
    for k in range(1, zs):
        q, to = column_peer(k)
        copies.append(go(part(sum2, q, m), got3.at[k], to))
    middle(1, gram, poly, ready)
    settle(copies)
    total = part(sum2, z, m)[...]
    for k in range(1, zs):
        total = total + got3[k]
    block = core * planes + spot
    mine = part(full, block * zs + z, m)
    mine[...] = total
    copies = [go(mine, mine, column_peer(k)[1]) for k in range(1, zs)]
    middle(1, gram, poly, ready)
    settle(copies)
    mine = part(full, block, block_rows)
    copies = [go(mine, mine, plane_peer(k)[1]) for k in range(1, planes)]
    step(gram, poly, ready, False, True)
    scale_in, scale_conv, scale_head = scales
    span = w_conv.shape[1]

    def turn_conv(l):
        own = mconv[l, pl.ds(pl.multiple_of(here_b * span, 8), span)]
        mconv_o[l] = own
        w = w_conv[l]
        turn = kdot(own, poly[l]) * (scale_conv / sizes[l])
        conv_o[l] = w - muon_rate * (turn + muon_shrink * w)

    for l in ready:
        turn_conv(l)
    settle(copies)
    if cores == 2:
        mine = part(full, core, half_rows)
        settle([go(mine, mine, core_peer)])
    summed = full[...]
    mconv[0] = muon_decay * old_conv[0] + summed[: 2 * width]
    sizes[0] = begin(mconv[0], gram, 0)
    feat = w_in.shape[1]
    half = width // 2
    grad_in = summed[rows_at[0] : rows_at[0] + LANES].T
    grad_head = summed[rows_at[1] : rows_at[1] + half]
    spread[...] = jnp.zeros_like(spread)
    spread[:, 0:feat] = mom_in[...]
    moment_in = muon_decay * spread[...] + jnp.where(lax.broadcasted_iota(jnp.int32, (width, LANES), 1) < feat, grad_in, 0.0)
    moment_head = muon_decay * mom_head[...] + jnp.concatenate([grad_head[:, :LANES], grad_head[:, LANES:]], 0)
    sizes[layers] = begin(moment_in, small_gram, 0)
    sizes[layers + 1] = begin(moment_head, small_gram, 1)

    def both(early, late):
        step(gram, poly, (0,), early, late)
        step(small_gram, small_poly, (0, 1), early, late)

    both(True, False)
    lax.fori_loop(1, NS_STEPS - 1, lambda _, c: (both(False, False), c)[1], 0)
    both(False, True)
    turn_conv(0)
    span = w_in.shape[0]
    mconv[0, pl.ds(0, width), 0:LANES] = moment_in
    mconv[0, pl.ds(0, width), LANES : 2 * LANES] = moment_head
    own = mconv[0, pl.ds(pl.multiple_of(here_b * span, 8), span), 0:LANES]
    min_o[...] = own[:, :feat]
    w = w_in[...]
    turn = kdot(own, small_poly[0]) * (scale_in / sizes[layers])
    in_o[...] = w - muon_rate * (turn[:, :feat] + muon_shrink * w)
    span = w_head.shape[1]
    own = mconv[0, pl.ds(pl.multiple_of(here_b * span, 8), span), LANES : 2 * LANES]
    mhead_o[...] = own.T[:classes]
    w = w_head[...]
    turn = kdot(own, small_poly[1]) * (scale_head / sizes[layers + 1])
    head_o[...] = w - muon_rate * (turn.T[:classes] + muon_shrink * w)

    def adamw(param, grad, first, second, outs):
        first = adam_first_decay * first + (1.0 - adam_first_decay) * grad
        second = adam_second_decay * second + (1.0 - adam_second_decay) * grad * grad
        first_hat = first / power[0]
        second_hat = second / power[1]
        outs[0][...] = param - adam_rate * (first_hat / (jnp.sqrt(second_hat) + adam_epsilon) + adam_shrink * param)
        outs[1][...] = first
        outs[2][...] = second

    at = rows_at[2]
    adamw(biases[...], summed[at : at + layers + 1], fb[...], sb[...], (b_o, fb_o, sb_o))
    at = at + layers + 1
    for l in range(layers):
        rows = summed[at + 2 * l : at + 2 * l + 2]
        adamw(norms[l], rows, fn[l], sn[l], (n_o.at[l], fn_o.at[l], sn_o.at[l]))
    at = at + 2 * layers
    adamw(head_bias[...], summed[at : at + 1, :classes], fh[...], sh[...], (h_o, fh_o, sh_o))
    loss_o[...] = jnp.sum(summed[at + 1 : at + 2], axis=1, keepdims=True) / all_nodes


def update_call(n, nb, layers, all_nodes, rows_at, classes, ns_parts, scales, summed_rows, pay, moments, shards, smalls, power):
    cores, ys, xs, zs = plane_split(nb, n)
    planes = ys * xs
    width = pay.shape[1]
    m = summed_rows // (n * nb)
    w_in, w_conv, w_head = shards
    vmem = pl.BlockSpec(memory_space=pltpu.VMEM)
    smem = pl.BlockSpec(memory_space=pltpu.SMEM)
    like = [jax.ShapeDtypeStruct(v.shape, f32) for v in (w_in, w_conv, w_head)]
    like_small = [jax.ShapeDtypeStruct(v.shape, f32) for v in smalls[:3]]
    copies = 2 * (planes + zs)
    return pl.pallas_call(
        functools.partial(update_kernel, n, nb, layers, all_nodes, rows_at, classes, ns_parts, scales, summed_rows),
        out_shape=tuple([jax.ShapeDtypeStruct((1, 1), f32)] + like + like + like_small * 3),
        in_specs=[vmem] * 2 + [pl.BlockSpec(memory_space=pl.ANY)] + [vmem] * 13 + [smem],
        out_specs=(vmem,) * 16,
        scratch_shapes=[
            pltpu.VMEM((zs * planes * m, width), f32),
            pltpu.VMEM((zs * planes * m, width), f32),
            pltpu.VMEM((planes, zs * m, width), f32),
            pltpu.VMEM((zs * m, width), f32),
            pltpu.VMEM((zs, m, width), f32),
            pltpu.VMEM((summed_rows, width), f32),
            pltpu.VMEM((layers, width, width), f32),
            pltpu.VMEM((layers, width, width), f32),
            pltpu.VMEM((2, LANES, LANES), f32),
            pltpu.VMEM((2, LANES, LANES), f32),
            pltpu.VMEM((layers, 2 * width, width), f32),
            pltpu.SemaphoreType.DMA((copies,)),
            pltpu.SemaphoreType.DMA((copies,)),
            pltpu.VMEM((layers, 2 * width, width), f32),
            pltpu.SemaphoreType.DMA,
            pltpu.VMEM((width, LANES), f32),
        ],
        compiler_params=pltpu.CompilerParams(collective_id=2, has_side_effects=True, vmem_limit_bytes=63 << 20),
        name="sum_and_update",
    )(pay, *moments, *shards, *smalls, power)


NS_PARTS = 3


def hand_over_kernel(*refs):
    half = len(refs) // 2
    for src, dst in zip(refs[:half], refs[half:]):
        dst[...] = src[...]


def hand_over(arrays):
    vmem = pl.BlockSpec(memory_space=pltpu.VMEM)
    return pl.pallas_call(
        hand_over_kernel,
        out_shape=tuple(jax.ShapeDtypeStruct(v.shape, v.dtype) for v in arrays),
        in_specs=[vmem] * len(arrays),
        out_specs=(vmem,) * len(arrays),
        name="hand_over",
    )(*arrays)


def per_device(
    n_batch,
    n_rows,
    features,
    edge_rows,
    edge_weight,
    halo_counts,
    labels,
    pair_rows,
    step,
    w_in,
    w_conv,
    w_head,
    biases,
    norm_params,
    head_bias,
    mom_in,
    mom_conv,
    mom_head,
    first_bias,
    first_norm,
    first_head,
    second_bias,
    second_norm,
    second_head,
):
    rows_dev = features.shape[1]
    halo_rows = rows_dev // 4
    edge_count = edge_rows.shape[3]
    layers, hid = w_conv.shape[0], w_conv.shape[2]
    feat, classes = w_in.shape[0], w_head.shape[1]
    pairs = pair_rows.shape[3]
    node_count = rows_dev * n_rows
    all_nodes = node_count * n_batch
    flat = [
        edge_rows.reshape(2 * edge_count).astype(f32),
        edge_weight.reshape(edge_count),
        labels.reshape(rows_dev).astype(f32),
        pair_rows.reshape(n_rows * pairs).astype(f32),
    ]
    flat = jnp.concatenate(flat)
    flat = jnp.pad(flat, (0, -flat.shape[0] % (8 * LANES))).reshape(-1, LANES)
    flat = redeal(flat, n_batch, n_rows)
    inputs = redeal(features, n_batch, n_rows)[0]
    e = edge_count // LANES
    block = my_place()[1]
    wide = (rows_dev + 2 * halo_rows) // TILE
    rims = jnp.stack([(block > 0).astype(jnp.int32), (block < n_rows - 1).astype(jnp.int32)])
    *adjacency, row_sums = fill(flat[:e], flat[e : 2 * e], flat[2 * e : 3 * e], rims, rows_dev // TILE, wide, halo_rows // TILE, 2)
    label_rows = rows_dev // LANES
    picks = flat[3 * e + label_rows :].reshape(-1)[: n_rows * pairs].astype(jnp.int32)
    spread = jnp.pad(picks.reshape(n_rows, pairs), ((0, 0), (0, 8 - pairs)), constant_values=-1).reshape(1, n_rows * 8)
    spread = jnp.pad(spread, ((0, 0), (0, -spread.shape[1] % LANES)), constant_values=-1)
    at_in = 2 * hid
    at_head = at_in + -(-feat // 8) * 8
    at_small = at_head + hid // 2
    used = at_small + layers + 1 + 2 * layers + 2
    unit = 8 * n_rows * n_batch
    pay_rows = -(-used // unit) * unit
    rows_at = (at_in, at_head, at_small)
    turned = [
        w_in.T,
        w_conv,
        w_head.T,
        mom_in.T,
        mom_conv,
        mom_head.T,
    ]
    pay, full_min, full_mconv, full_mhead = step_call(
        n_rows,
        n_batch,
        layers,
        node_count,
        all_nodes,
        classes,
        rows_at,
        pay_rows,
        3 * e,
        inputs,
        flat,
        row_sums,
        biases,
        norm_params,
        head_bias[None],
        picks,
        spread,
        adjacency,
        turned,
    )
    count = step[0].astype(f32)
    power = jnp.stack([1.0 - jnp.power(adam_first_decay, count), 1.0 - jnp.power(adam_second_decay, count)])
    scales = (
        math.sqrt(max(1.0, hid / feat)),
        math.sqrt(max(1.0, hid / (2 * hid))),
        math.sqrt(max(1.0, classes / hid)),
    )
    smalls = (
        biases,
        norm_params,
        head_bias[None],
        first_bias,
        first_norm,
        first_head[None],
        second_bias,
        second_norm,
        second_head[None],
    )
    outs = update_call(
        n_rows,
        n_batch,
        layers,
        all_nodes,
        rows_at,
        classes,
        NS_PARTS,
        scales,
        pay_rows,
        pay,
        (full_min, full_mconv, full_mhead),
        (turned[0], w_conv, turned[2]),
        smalls,
        power,
    )
    outs = hand_over(outs)
    loss, new_in, new_conv, new_head, moment_in, moment_conv, moment_head = outs[:7]
    rest = []
    for i in range(0, 9, 3):
        rest += [outs[7 + i], outs[8 + i], outs[9 + i][0]]
    return (loss[0, 0], new_in.T, new_conv, new_head.T, moment_in.T, moment_conv, moment_head.T, *rest)


def solution(mesh):
    in_specs = (
        P("batch", "rows", None),
        P("batch", "rows", None, None),
        P("batch", "rows", None),
        P("batch", "rows", None),
        P("batch", "rows"),
        P("batch", "rows", None, None),
        P(),
        P(None, "batch"),
        P(None, "batch", None),
        P("batch", None),
        P(),
        P(),
        P(),
        P(None, "batch"),
        P(None, "batch", None),
        P("batch", None),
        P(),
        P(),
        P(),
        P(),
        P(),
        P(),
    )
    out_specs = (
        P(),
        P(None, "batch"),
        P(None, "batch", None),
        P("batch", None),
        P(None, "batch"),
        P(None, "batch", None),
        P("batch", None),
        P(),
        P(),
        P(),
        P(),
        P(),
        P(),
        P(),
        P(),
        P(),
    )
    body = functools.partial(per_device, mesh.shape["batch"], mesh.shape["rows"])
    return jax.shard_map(body, mesh=mesh, in_specs=in_specs, out_specs=out_specs, check_vma=False)
```

```python
import functools
import math

import jax
import jax.numpy as jnp
from jax import lax
from jax.experimental import pallas as pl
from jax.experimental.pallas import tpu as pltpu
from jax.sharding import PartitionSpec as P

NS_STEPS = 5

f32 = jnp.float32
bf16 = jnp.bfloat16
LANES = 128
TILE = 256
highest = lax.Precision.HIGHEST
norm_epsilon = 1e-05
pair_weight = 0.05
newton_a = 3.4445
newton_b = -4.775
newton_c = 2.0315
muon_decay = 0.9
muon_rate = 0.5
muon_shrink = 0.01
adam_first_decay = 0.9
adam_second_decay = 0.999
adam_epsilon = 1e-08
adam_rate = 0.1
adam_shrink = 0.01


def swap(b, r):
    return 2 * (b // 2) + r % 2, 2 * (r // 2) + b % 2


def flat_pairs(n_batch, n_rows, move):
    pairs = []
    for b in range(n_batch):
        for r in range(n_rows):
            to = move(b, r)
            if to is not None:
                pairs.append((b * n_rows + r, to[0] * n_rows + to[1]))
    return pairs


def redeal(array, n_batch, n_rows):
    return lax.ppermute(array, ("batch", "rows"), flat_pairs(n_batch, n_rows, swap))


def peer_place(batch, block):
    two = jnp.int32(2)
    return (
        two * lax.div(batch, two) + lax.rem(block, two),
        two * lax.div(block, two) + lax.rem(batch, two),
    )


def my_place():
    return peer_place(lax.axis_index("batch"), lax.axis_index("rows"))


def put_in_order(wide, to_ref, from_ref, w_ref, key_out, w_out, col_out, range_out):
    to, frm = to_ref[...].astype(jnp.int32), from_ref[...].astype(jnp.int32)
    key = (((to >> 8) * wide + (frm >> 8)) << 16) | ((to & 255) << 8) | (frm & 255)
    shape3 = (16, 8, LANES)
    key = key.astype(f32).reshape(shape3)
    w = w_ref[...].reshape(shape3)
    sub = lax.broadcasted_iota(jnp.int32, shape3, 1)
    lane = lax.broadcasted_iota(jnp.int32, shape3, 2)
    vreg = lax.broadcasted_iota(jnp.int32, shape3, 0)
    place = vreg + 16 * sub + 128 * lane
    for phase in range(14):
        for bit in range(phase, -1, -1):
            down = ((place >> (phase + 1)) & 1) == 1
            if bit < 4:
                view = (16 >> (bit + 1), 2, 1 << bit, 8, LANES)
                kv, wv = key.reshape(view), w.reshape(view)
                dv = down.astype(jnp.int32).reshape(view)[:, 0] == 1
                a, b, wa, wb = kv[:, 0], kv[:, 1], wv[:, 0], wv[:, 1]
                turn = jnp.logical_xor(a > b, dv)
                key = jnp.stack([jnp.where(turn, b, a), jnp.where(turn, a, b)], 1).reshape(shape3)
                w = jnp.stack([jnp.where(turn, wb, wa), jnp.where(turn, wa, wb)], 1).reshape(shape3)
            else:
                if bit < 7:
                    axis, gap, size, pos = 1, 1 << (bit - 4), 8, sub
                else:
                    axis, gap, size, pos = 2, 1 << (bit - 7), LANES, lane
                low = (pos & gap) == 0
                kp = jnp.where(low, pltpu.roll(key, size - gap, axis), pltpu.roll(key, gap, axis))
                wp = jnp.where(low, pltpu.roll(w, size - gap, axis), pltpu.roll(w, gap, axis))
                smaller = jnp.logical_xor(low, down)
                take = jnp.where(smaller, kp, key) < jnp.where(smaller, key, kp)
                key = jnp.where(take, kp, key)
                w = jnp.where(take, wp, w)
    flat = key.reshape(LANES, LANES)
    key_out[...] = flat.T.astype(jnp.int32)
    w_out[...] = w.reshape(LANES, LANES).T
    start = (lax.broadcasted_iota(jnp.int32, (8, LANES), 1).astype(f32) * 65536.0)[None]
    below = jnp.zeros(shape3, f32)
    upto = jnp.zeros(shape3, f32)
    for c in range(LANES):
        wide_key = jnp.broadcast_to(flat[:, c : c + 1], (LANES, LANES))
        col_out[c] = (wide_key - jnp.floor(wide_key * (1.0 / 256.0)) * 256.0).astype(bf16)
        wide_key = wide_key.reshape(shape3)
        below = below + jnp.where(wide_key < start, 1.0, 0.0)
        upto = upto + jnp.where(wide_key < start + 65536.0, 1.0, 0.0)
    range_out[...] = jnp.zeros_like(range_out)
    n_below = jnp.sum(below.reshape(LANES, LANES), axis=0, keepdims=True)
    n_upto = jnp.sum(upto.reshape(LANES, LANES), axis=0, keepdims=True)
    first = jnp.floor(n_below * (1.0 / 128.0))
    end = jnp.floor((n_upto + 127.0) * (1.0 / 128.0))
    range_out[0:1] = first.astype(jnp.int32)
    range_out[1:2] = jnp.where(n_upto > n_below, end, first).astype(jnp.int32)


def fill_kernel(wide, rim, chunk, parts, rims, to_ref, from_ref, weight_ref, *refs):
    outs, sums = refs[:parts], refs[parts]
    acc, rowacc, key_ref, w_ref, col_ref, ranges, span_of, sem = refs[parts + 1 :]
    i = pl.program_id(0)

    @pl.when(i == 0)
    def _():
        put_in_order(wide, to_ref, from_ref, weight_ref, key_ref, w_ref, col_ref, ranges)
        copy = pltpu.make_async_copy(ranges, span_of, sem)
        copy.start()
        copy.wait()

    pack = 16
    shape = (TILE // pack, pack, LANES)
    rows = lax.broadcasted_iota(jnp.int32, shape, 0) * pack + lax.broadcasted_iota(jnp.int32, shape, 1)
    rows = rows.astype(f32).astype(bf16)
    lanes = lax.broadcasted_iota(jnp.int32, (LANES, LANES), 1).astype(f32)
    lanes0, lanes1 = lanes.astype(bf16), (lanes + 128.0).astype(bf16)
    one, zero = jnp.ones((), bf16), jnp.zeros((), bf16)

    def spread(row):
        return jnp.broadcast_to(row, (pack, LANES)).astype(bf16)[None]

    rowacc[...] = jnp.zeros_like(rowacc)

    def tile(j, _):
        b = i * wide + j
        first, end = span_of[0, b], span_of[1, b]
        end = jnp.where(jnp.logical_and(j < rim, rims[0] == 0), first, end)
        end = jnp.where(jnp.logical_and(j >= wide - rim, rims[1] == 0), first, end)
        slot = jnp.where(j < rim, wide - 2 * rim + j, jnp.where(j < wide - rim, j - rim, j))
        cols = pl.ds(pl.multiple_of(slot * TILE, TILE), TILE)

        @pl.when(end <= first)
        def _():
            for out in outs:
                out[:, cols] = jnp.zeros((TILE, TILE), bf16)

        @pl.when(end > first)
        def _():
            def part(base, c):
                row = jnp.minimum(base + c, LANES - 1)
                here = key_ref[pl.ds(row, 1), :] - (b << 16)
                if c:
                    here = jnp.where(base + c < end, here, -1)
                at = rows == spread((here >> 8).astype(f32))
                rest = w_ref[pl.ds(row, 1), :]
                left = []
                for q in range(parts):
                    piece = rest.astype(bf16).astype(f32)
                    rest = rest - piece
                    left.append(jnp.where(at, spread(piece), zero).reshape(TILE, LANES))
                col = col_ref[row]
                right = jnp.concatenate(
                    [jnp.where(col == lanes0, one, zero), jnp.where(col == lanes1, one, zero)], 1
                )
                return left, right

            def get(base):
                made = [part(base, c) for c in range(chunk)]
                lhs = jnp.concatenate([m[0][q] for q in range(parts) for m in made], 1)
                rhs = jnp.concatenate([m[1] for m in made] * parts, 0)
                return jnp.dot(lhs, rhs, preferred_element_type=f32)

            acc[...] = get(first)

            def more(t, _):
                acc[...] += get(first + t * chunk)
                return 0

            lax.fori_loop(1, lax.div(end - first + chunk - 1, chunk), more, 0)
            rest = acc[...]
            rowacc[...] += rest[:, :LANES] + rest[:, LANES:]
            for out in outs:
                piece = rest.astype(bf16)
                out[:, cols] = piece
                rest = rest - piece.astype(f32)

        return 0

    lax.fori_loop(0, wide, tile, 0)
    total = jnp.sum(rowacc[...], axis=1, keepdims=True)
    for half in range(TILE // LANES):
        column = jnp.broadcast_to(total[half * LANES : (half + 1) * LANES], (LANES, LANES))
        sums[0, half : half + 1] = column.T[0:1]


def fill(to, frm, weights, rims, tiles, wide, rim, parts, chunk=5):
    cols = wide * TILE
    return pl.pallas_call(
        functools.partial(fill_kernel, wide, rim, chunk, parts),
        out_shape=tuple(jax.ShapeDtypeStruct((tiles * TILE, cols), bf16) for _ in range(parts))
        + (jax.ShapeDtypeStruct((tiles, TILE // LANES, LANES), f32),),
        grid_spec=pltpu.PrefetchScalarGridSpec(
            num_scalar_prefetch=1,
            grid=(tiles,),
            in_specs=[pl.BlockSpec((LANES, LANES), lambda i, *_: (0, 0))] * 3,
            out_specs=tuple(pl.BlockSpec((TILE, cols), lambda i, *_: (i, 0)) for _ in range(parts))
            + (pl.BlockSpec((1, TILE // LANES, LANES), lambda i, *_: (i, 0, 0)),),
            scratch_shapes=[
                pltpu.VMEM((TILE, TILE), f32),
                pltpu.VMEM((TILE, LANES), f32),
                pltpu.VMEM((LANES, LANES), jnp.int32),
                pltpu.VMEM((LANES, LANES), f32),
                pltpu.VMEM((LANES, LANES, LANES), bf16),
                pltpu.VMEM((8, LANES), jnp.int32),
                pltpu.SMEM((8, LANES), jnp.int32),
                pltpu.SemaphoreType.DMA,
            ],
        ),
        compiler_params=pltpu.CompilerParams(vmem_limit_bytes=50 << 20),
        name="adjacency_tiles",
    )(rims, to, frm, weights)


def parts_of(x, count):
    found = []
    for q in range(count):
        piece = x.astype(bf16)
        found.append(piece)
        if q + 1 < count:
            x = x - piece.astype(f32)
    return found


def pair_list(count):
    return [(p, q) for p in range(count) for q in range(count) if p + q < count]


def dots(left, right, dims=((1,), (0,))):
    total = None
    for p, q in pair_list(len(left)):
        piece = lax.dot_general(left[p], right[q], (dims, ((), ())), preferred_element_type=f32)
        total = piece if total is None else total + piece
    return total


def remote(src, dst, send, recv, to):
    return pltpu.make_async_remote_copy(
        src_ref=src,
        dst_ref=dst,
        send_sem=send,
        recv_sem=recv,
        device_id=to,
        device_id_type=pl.DeviceIdType.MESH,
    )


def column_sums(x):
    return jnp.sum(x, axis=0, keepdims=True)


def folded(x):
    return jnp.sum(x.reshape(x.shape[0] // 8, 8, x.shape[1]), axis=0)


def plane_split(nb, n):
    cores = 2 if nb % 2 == 0 else 1
    across = 1
    while across * across * 4 <= n and n % (across * 2) == 0:
        across *= 2
    return cores, nb // cores, across, n // across


class Places:
    def __init__(self, n, nb):
        self.cores, ys, self.xs, self.zs = plane_split(nb, n)
        self.planes = ys * self.xs
        self.b, self.r = lax.axis_index("batch"), lax.axis_index("rows")
        self.core, y = lax.rem(self.b, self.cores), lax.div(self.b, self.cores)
        self.x, self.z = lax.rem(self.r, self.xs), lax.div(self.r, self.xs)
        self.spot = y * self.xs + self.x
        self.core_peer = (y * self.cores + lax.rem(self.core + 1, self.cores), self.r)
        self.peers = [self.plane_peer(k)[1] for k in range(1, self.planes)]
        self.peers += [self.column_peer(k)[1] for k in range(1, self.zs)]
        if self.cores == 2:
            self.peers.append(self.core_peer)

    def plane_peer(self, k):
        p = lax.rem(self.spot + k, self.planes)
        return p, (lax.div(p, self.xs) * self.cores + self.core, self.z * self.xs + lax.rem(p, self.xs))

    def column_peer(self, k):
        q = lax.rem(self.z + k, self.zs)
        return q, (self.b, q * self.xs + self.x)


TURNED = ((0,), (0,))
GATHERED = 3


def step_kernel(n, nb, layers, nodes, all_nodes, classes, rows_at, summed_rows, label_at, *refs):
    (x_ref, label_ref, sums_ref, bias_ref, norm_ref, head_bias_ref, pick_smem, pick_row, a1_hbm, a2_hbm) = refs[:10]
    own_in, own_conv, own_head, own_min, own_mconv, own_mhead = refs[10:16]
    pay, full_min, full_mconv, full_mhead = refs[16:20]
    (act, agg, a1, a2, p1, p2, g1, g2, gh, rim, out_rim, logit, sent, got, stat, held, w_in, w_conv, w_head,
     wt, a_sem, stat_send, stat_recv, rim_send, rim_recv, pair_send, pair_recv, w_send, w_recv, w_own, sum_send, sum_recv,
     ready, normed, keep, stood, laid_head, laid_mhead, wide_bias) = refs[20:]
    rows, width = act.shape[1], act.shape[2]
    halo = rim.shape[2]
    a, ps, gs = (a1, a2), (p1, p2), (g1, g2)
    here_b, here_r = lax.axis_index("batch"), lax.axis_index("rows")
    batch, block = my_place()
    first, last = block == 0, block == n - 1
    not_first, not_last = jnp.logical_not(first), jnp.logical_not(last)

    barrier = pltpu.get_barrier_semaphore()
    for k in range(1, n):
        pl.semaphore_signal(
            barrier, inc=1, device_id=peer_place(batch, lax.rem(block + k, n)), device_id_type=pl.DeviceIdType.MESH
        )
    for k in range(1, nb):
        pl.semaphore_signal(
            barrier, inc=1, device_id=(lax.rem(here_b + k, nb), here_r), device_id_type=pl.DeviceIdType.MESH
        )
    places = Places(n, nb)
    for peer in places.peers:
        pl.semaphore_signal(barrier, inc=1, device_id=peer, device_id_type=pl.DeviceIdType.MESH)
    height = 512
    steps = rows // height
    own_cols, rim_cols = pl.ds(0, rows), pl.ds(rows, 2 * halo)

    def load(s, cols, which):
        span = pl.ds(pl.multiple_of(s * height, height), height)
        return [
            pltpu.make_async_copy(src.at[span, cols], dst.at[span, cols], a_sem.at[2 * (steps * which + s) + q])
            for q, (src, dst) in enumerate(zip((a1_hbm, a2_hbm), a))
        ]

    for s in range(steps):
        for copy in load(s, own_cols, 0):
            copy.start()
    for src, dst in ((own_head, laid_head), (own_mhead, laid_mhead)):
        stood[...] = jnp.zeros_like(stood)
        stood[0:classes] = src[...]
        dst[...] = stood[...].T
    wide_bias[...] = jnp.zeros_like(wide_bias)
    wide_bias[0:1, 0:classes] = head_bias_ref[...]
    pl.semaphore_wait(barrier, n - 1 + nb - 1 + len(places.peers))

    def gathers(item, src, dst):
        span = src.shape[-2]
        lead = (slice(None),) * (len(src.shape) - 2)
        mine = dst.at[lead + (pl.ds(pl.multiple_of(here_b * span, 8), span),)]
        copies = [pltpu.make_async_copy(src, mine, w_own.at[item])]
        for k in range(1, nb):
            copies.append(remote(src, mine, w_send.at[item, k], w_recv.at[item, k], (lax.rem(here_b + k, nb), here_r)))
        return copies

    def gather(item, src, dst):
        copies = gathers(item, src, dst)
        for copy in copies:
            copy.start()
        return copies

    def arrived(copies):
        for copy in copies:
            copy.wait()

    in_copies = gather(0, own_in, w_in)
    for q in range(layers):
        gather(2 + q, own_conv.at[q], w_conv.at[q])
    head_copies = gather(1, laid_head, w_head)

    def stat_copies(e):
        return [
            remote(stat.at[e], held.at[e, k], stat_send.at[e, k], stat_recv.at[e, k], peer_place(batch, lax.rem(block + k, n)))
            for k in range(1, n)
        ]

    def stats_start(e):
        held[e, 0] = stat[e]
        for copy in stat_copies(e):
            copy.start()

    def stats_finish(e):
        arrived(stat_copies(e))
        total = held[e, lax.rem(block, n)]
        for q in range(1, n):
            total = total + held[e, lax.rem(block + n - q, n)]
        return total

    def rims_of(e, low_src, high_src):
        slot = lax.rem(e, 2)
        return (
            remote(low_src, rim.at[slot, 1], rim_send.at[e, 1], rim_recv.at[e, 1], peer_place(batch, lax.rem(block + n - 1, n))),
            remote(high_src, rim.at[slot, 0], rim_send.at[e, 0], rim_recv.at[e, 0], peer_place(batch, lax.rem(block + 1, n))),
        )

    def start_if(condition, copy):
        @pl.when(condition)
        def _():
            copy.start()

    def rims_sent(copies):
        @pl.when(not_first)
        def _():
            copies[0].wait_send()

        @pl.when(not_last)
        def _():
            copies[1].wait_send()

    tile = 256
    tiles = rows // tile

    def rows_of(s, size):
        return pl.ds(pl.multiple_of(s * size, size), size)

    zeros8 = jnp.zeros((8, width), f32)

    arrived(in_copies)
    turned_in = parts_of(w_in[...].T, 3)

    def project(s, _):
        span = rows_of(s, tile)
        h = dots(parts_of(x_ref[span, :], 3), turned_in) + bias_ref[0:1]
        act[0, span] = h
        for dst, piece in zip(ps, parts_of(h, 2)):
            dst[span, :] = piece
        return 0

    lax.fori_loop(0, tiles, project, 0)
    stat[0] = jnp.zeros((2, width), f32)
    def set_norm(l, totals):
        mean = totals[0:1] * (1.0 / nodes)
        inverse = lax.rsqrt(totals[1:2] * (1.0 / nodes) - mean * mean + norm_epsilon)
        under = lax.max(l - 1, 0)
        scale = norm_ref[under, 0:1] * inverse
        offset = norm_ref[under, 1:2] - mean * scale
        plain = l == 0
        normed[l, 0:1] = jnp.where(plain, 0.0, mean)
        normed[l, 1:2] = jnp.where(plain, 1.0, inverse)
        normed[l, 2:3] = jnp.where(plain, 1.0, scale)
        normed[l, 3:4] = jnp.where(plain, 0.0, offset)

    bias_row = lax.broadcasted_iota(jnp.int32, bias_ref.shape, 0)

    def forward(l, _):
        copies = rims_of(l, act.at[l, pl.ds(0, halo)], act.at[l, pl.ds(rows - halo, halo)])
        start_if(not_first, copies[0])
        start_if(not_last, copies[1])
        stats_start(l)

        def own(s, _):
            span = rows_of(s, height)

            @pl.when(l == 0)
            def _():
                for copy in load(s, own_cols, 0):
                    copy.wait()
                for copy in load(s, rim_cols, 1):
                    copy.start()

            agg[l, span] = dots([q[span, own_cols] for q in a], [q[own_cols, :] for q in ps])
            return 0

        lax.fori_loop(0, rows // height, own, 0)
        set_norm(l, stats_finish(l))
        slot = lax.rem(l, 2)
        for which, gone in ((0, first), (1, last)):
            @pl.when(gone)
            def _():
                rim[slot, which] = jnp.zeros((halo, width), f32)

            @pl.when(jnp.logical_not(gone))
            def _():
                remote(rim.at[slot, which], rim.at[slot, which], rim_send.at[l, which], rim_recv.at[l, which],
                       peer_place(batch, lax.rem(block + 1, n))).wait_recv()

            for dst, piece in zip(ps, parts_of(rim[slot, which], 2)):
                dst[pl.ds(rows + which * halo, halo), :] = piece

        def rims_in(s, _):
            span = rows_of(s, height)

            @pl.when(l == 0)
            def _():
                for copy in load(s, rim_cols, 1):
                    copy.wait()

            agg[l, span] += dots([q[span, rim_cols] for q in a], [q[rim_cols, :] for q in ps])
            return 0

        lax.fori_loop(0, rows // height, rims_in, 0)
        arrived(gathers(2 + l, own_conv.at[l], w_conv.at[l]))
        weights = parts_of(w_conv[l], 3)
        bias = column_sums(jnp.where(bias_row == l + 1, bias_ref[...], 0.0))
        scale, offset = normed[l, 2:3], normed[l, 3:4]

        def finish(s, sums):
            span = rows_of(s, tile)
            row_sum = jnp.concatenate(
                [jnp.broadcast_to(sums_ref[s, i : i + 1], (LANES, LANES)).T for i in range(tile // LANES)], 0
            )
            found = agg[l, span] * scale + jnp.concatenate([row_sum] * (width // LANES), 1) * offset
            agg[l, span] = found
            h = act[l, span] * scale + offset
            pre = dots(parts_of(jnp.concatenate([h, found], 1), 3), weights) + bias
            active = jnp.maximum(pre, 0.0)
            act[l + 1, span] = active
            for dst, piece in zip(ps, parts_of(active, 2)):
                dst[span, :] = piece
            return sums[0] + folded(active), sums[1] + folded(active * active)

        sums = lax.fori_loop(0, tiles, finish, (zeros8, zeros8))
        stat[l + 1, 0:1] = column_sums(sums[0])
        stat[l + 1, 1:2] = column_sums(sums[1])
        rims_sent(copies)
        return 0

    lax.fori_loop(0, layers, forward, 0)

    stats_start(layers)
    base = 2 + layers
    late = [gather(base, own_min, full_min), gather(base + 1, laid_mhead, full_mhead), gather(base + 2, own_mconv, full_mconv)]
    arrived(head_copies)
    head_parts = parts_of(w_head[...], 3)
    head_turned = parts_of(w_head[...].T, 2)
    set_norm(layers, stats_finish(layers))
    top_scale, top_offset = normed[layers, 2:3], normed[layers, 3:4]
    top_mean, top_inverse = normed[layers, 0:1], normed[layers, 1:2]

    def top(span):
        return act[layers, span] * top_scale + top_offset

    def classify(s, _):
        span = rows_of(s, tile)
        logit[span, :] = dots(parts_of(top(span), 3), head_parts) + wide_bias[0:1]
        return 0

    lax.fori_loop(0, tiles, classify, 0)
    per = pick_smem.shape[0] // n
    sent[...] = jnp.zeros_like(sent)
    for d in range(n):
        for k in range(per):
            sent[d, k : k + 1] = logit[pl.ds(pick_smem[d * per + k], 1), :]
    pair_copies = []
    for k in range(1, n):
        peer = lax.rem(block + k, n)
        copy = remote(sent.at[peer], got.at[k], pair_send.at[k], pair_recv.at[k], peer_place(batch, peer))
        copy.start()
        pair_copies.append(copy)
    got[0] = sent[block]
    lane = lax.broadcasted_iota(jnp.int32, (tile, LANES), 1)
    real = lane < classes

    def soften(s, loss):
        span = rows_of(s, tile)
        z = logit[span, :]
        top_z = jnp.max(jnp.where(real, z, -jnp.inf), axis=1, keepdims=True)
        e = jnp.where(real, jnp.exp(z - top_z), 0.0)
        total = jnp.sum(e, axis=1, keepdims=True)
        named = [
            jnp.broadcast_to(label_ref[pl.ds(label_at + s * (tile // LANES) + i, 1), :], (LANES, LANES)).T for i in range(tile // LANES)
        ]
        hot = jnp.logical_and(real, lane.astype(f32) == jnp.concatenate(named, 0))
        logit[span, :] = e / total - jnp.where(hot, 1.0, 0.0)
        part = jnp.where(lane == 0, top_z + jnp.log(total), 0.0) - jnp.where(hot, z, 0.0)
        return loss + folded(part)

    loss = lax.fori_loop(0, tiles, soften, jnp.zeros((8, LANES), f32))
    arrived(pair_copies)
    gaps = []
    for d in range(n):
        gaps.append(sent[d] - got[lax.rem(block + n - d, n)])
    gap = jnp.concatenate(gaps, 0)
    loss = loss + pair_weight * folded(gap * gap)
    spare = pick_row.shape[1] - gap.shape[0]
    if spare:
        gap = jnp.concatenate([gap, jnp.zeros((spare, LANES), f32)], 0)
    gap_parts = parts_of(gap * (4.0 * pair_weight), 3)
    at_head, at_small = rows_at[1], rows_at[2]
    small = layers + 1

    def finish_head(s, sums):
        span = rows_of(s, tile)
        spot = lax.broadcasted_iota(jnp.int32, (tile, pick_row.shape[1]), 0) + s * tile
        chosen = jnp.where(spot == pick_row[...], 1.0, 0.0).astype(bf16)
        add = None
        for piece in gap_parts:
            v = jnp.dot(chosen, piece, preferred_element_type=f32)
            add = v if add is None else add + v
        grad = (logit[span, :] + add) * (1.0 / all_nodes)
        grad_parts = parts_of(grad, 2)
        h = top(span)
        back = dots(grad_parts, head_turned)
        gh[span, :] = back
        ready_top = (act[layers, span] - top_mean) * top_inverse
        return (
            sums[0] + dots(parts_of(h, 2), grad_parts, TURNED),
            sums[1] + folded(grad),
            sums[2] + folded(back),
            sums[3] + folded(back * ready_top),
        )

    begin = (
        jnp.zeros((width, LANES), f32),
        jnp.zeros((8, LANES), f32),
        jnp.zeros((8, width), f32),
        jnp.zeros((8, width), f32),
    )
    sums = lax.fori_loop(0, tiles, finish_head, begin)
    half = width // 2
    pay[pl.ds(at_head, half), :] = jnp.concatenate([sums[0][:half], sums[0][half:]], 1)
    tail = pl.ds(at_small, summed_rows - at_small)
    pay[tail, :] = jnp.zeros((summed_rows - at_small, width), f32)
    at_norm = at_small + small
    at_last = at_norm + 2 * layers
    pay[at_last : at_last + 1, 0:LANES] = column_sums(sums[1])
    pay[at_last + 1 : at_last + 2, 0:LANES] = column_sums(loss)
    after = layers + 1
    stat[after, 0:1] = column_sums(sums[2])
    stat[after, 1:2] = column_sums(sums[3])
    stats_start(after)

    big = 2 * width

    def conv_rows(l):
        return pl.multiple_of(jnp.where(l == 0, 0, summed_rows + (l - 1) * big), 8)

    def told(which):
        for peer in places.peers:
            pl.semaphore_signal(ready.at[which], inc=1, device_id=peer, device_id_type=pl.DeviceIdType.MESH)

    cores, planes, zs = places.cores, places.planes, places.zs
    core, spot = places.core, places.spot
    piece_rows = big // cores
    block_rows = piece_rows // planes
    cut = block_rows % (8 * zs) == 0
    slice_rows = block_rows // zs if cut else block_rows

    def part(ref, index, count):
        return ref.at[pl.ds(pl.multiple_of(index * count, 8), count)]

    class Sum:
        def __init__(self, l):
            self.which, room = l - 1, act.at[l + 1]
            self.local = pay.at[pl.ds(conv_rows(l), big)]
            self.whole = room.at[pl.ds(0, big)]
            spots = [piece_rows, piece_rows, piece_rows, block_rows, slice_rows * zs]
            views, at = [], big
            for count in spots:
                views.append(room.at[pl.ds(at, count)])
                at += count
            self.got1, self.sum1, self.got2, self.sum2, self.got3 = views

        def copies(self, stage):
            found = []

            def add(i, src, dst, to):
                found.append(remote(src, dst, sum_send.at[self.which, i], sum_recv.at[self.which, i], to))

            if stage == 0 and cores == 2:
                add(0, part(self.local, 1 - core, piece_rows), self.got1, places.core_peer)
            if stage == 1:
                for k in range(1, planes):
                    p, to = places.plane_peer(k)
                    add(k, part(self.sum1, p, block_rows), part(self.got2, k, block_rows), to)
            if stage == 2:
                for k in range(1, zs):
                    q, to = places.column_peer(k)
                    src = part(self.sum2, q, slice_rows) if cut else self.sum2
                    add(planes + k, src, part(self.got3, k, slice_rows), to)
            block = part(self.whole, core * planes + spot, block_rows)
            if stage == 3 and cut:
                mine = part(self.whole, (core * planes + spot) * zs + places.z, slice_rows)
                for k in range(1, zs):
                    add(planes + zs + k, mine, mine, places.column_peer(k)[1])
            if stage == 4:
                for k in range(1, planes):
                    add(planes + 2 * zs + k, block, block, places.plane_peer(k)[1])
            if stage == 5 and cores == 2:
                mine = part(self.whole, core, piece_rows)
                add(2 * planes + 2 * zs, mine, mine, places.core_peer)
            return found

        def go(self, stage):
            if stage == 0:
                pl.semaphore_wait(ready.at[self.which], len(places.peers))
            else:
                arrived(self.copies(stage - 1))
            if stage == 1:
                total = part(self.local, core, piece_rows)[...]
                if cores == 2:
                    total = total + self.got1[...]
                self.sum1[...] = total
            if stage == 2:
                total = part(self.sum1, spot, block_rows)[...]
                for k in range(1, planes):
                    total = total + part(self.got2, k, block_rows)[...]
                self.sum2[...] = total
                self.got3[pl.ds(0, slice_rows), :] = part(self.sum2, places.z, slice_rows)[...] if cut else total
            if stage == 3:
                total = part(self.got3, lax.rem(places.z, zs), slice_rows)[...]
                for q in range(1, zs):
                    total = total + part(self.got3, lax.rem(places.z + zs - q, zs), slice_rows)[...]
                if cut:
                    part(self.whole, (core * planes + spot) * zs + places.z, slice_rows)[...] = total
                else:
                    part(self.whole, core * planes + spot, block_rows)[...] = total
            if stage == 6:
                self.local[...] = self.whole[...]
            for copy in self.copies(stage):
                copy.start()

    def backward(turn, _):
        l = layers - 1 - turn
        e = after + turn

        def advance(stage):
            @pl.when(turn > 0)
            def _():
                Sum(l + 1).go(stage)

        keep[l, 0:1] = stat[e, 1:2]
        keep[l, 1:2] = stat[e, 0:1]
        for q, piece in enumerate(parts_of(w_conv[l].T, 2)):
            wt[q] = piece
        gain = norm_ref[l, 0:1]
        totals = stats_finish(e) * gain * (1.0 / nodes)
        mean, inverse = normed[l + 1, 0:1], normed[l + 1, 1:2]

        def enter(s, total):
            span = rows_of(s, tile)
            active = act[l + 1, span]
            rated = (active - mean) * inverse
            grad = inverse * (gh[span, :] * gain - totals[0:1] - rated * totals[1:2])
            grad = jnp.where(active > 0.0, grad, 0.0)
            pieces = parts_of(grad, 2)
            for dst, piece in zip(gs, pieces):
                dst[span, :] = piece
            joined = dots(pieces, [wt[0], wt[1]])
            gh[span, :] = joined[:, :width]
            for dst, piece in zip(ps, parts_of(joined[:, width:], 2)):
                dst[span, :] = piece
            return total + folded(grad)

        total = lax.fori_loop(0, tiles, enter, zeros8)
        keep[l, 2:3] = column_sums(total)

        @pl.when(l > 0)
        def _():
            told(l - 1)

        advance(1)

        @pl.when(turn > 1)
        def _():
            Sum(l + 2).go(5)

        copies = rims_of(e, out_rim.at[0], out_rim.at[1])

        def rims_out(which, _):
            cols = pl.ds(pl.multiple_of(rows + which * halo, 128), halo)
            out_rim[which] = dots([q[:, cols] for q in a], [q[own_cols, :] for q in ps], TURNED)
            for at, go in ((0, not_first), (1, not_last)):
                start_if(jnp.logical_and(go, which == at), copies[at])
            return 0

        lax.fori_loop(0, 2, rims_out, 0)
        advance(2)

        @pl.when(turn > 1)
        def _():
            Sum(l + 2).go(6)

        def spread_back(s, _):
            span = rows_of(s, height)
            gh[span, :] += dots([q[:, span] for q in a], [q[own_cols, :] for q in ps], TURNED)
            return 0

        lax.fori_loop(0, rows // height, spread_back, 0)
        advance(3)
        slot = lax.rem(e, 2)
        for which, go, start in ((1, not_last, rows - halo), (0, not_first, 0)):
            @pl.when(go)
            def _():
                remote(rim.at[slot, which], rim.at[slot, which], rim_send.at[e, which], rim_recv.at[e, which],
                       peer_place(batch, lax.rem(block + 1, n))).wait_recv()
                gh[pl.ds(start, halo), :] += rim[slot, which]

        below_mean, below_inverse = normed[l, 0:1], normed[l, 1:2]

        def tail_sums(s, sums):
            span = rows_of(s, tile)
            grad = gh[span, :]
            return sums[0] + folded(grad), sums[1] + folded(grad * ((act[l, span] - below_mean) * below_inverse))

        sums = lax.fori_loop(0, tiles, tail_sums, (zeros8, zeros8))
        stat[e + 1, 0:1] = column_sums(sums[0])
        stat[e + 1, 1:2] = column_sums(sums[1])

        @pl.when(l > 0)
        def _():
            stats_start(e + 1)

        rims_sent(copies)
        advance(4)
        base = conv_rows(l)
        where = pl.ds(base, width)
        under = pl.ds(pl.multiple_of(base + width, 8), width)
        scale, offset = normed[l, 2:3], normed[l, 3:4]
        pay[pl.ds(base, big), :] = jnp.zeros((big, width), f32)

        def weigh(s, _):
            span = rows_of(s, height)
            h = act[l, span] * scale + offset
            grad = [q[span, :] for q in gs]
            pay[where, :] += dots(parts_of(h, 2), grad, TURNED)
            pay[under, :] += dots(parts_of(agg[l, span], 2), grad, TURNED)
            return 0

        lax.fori_loop(0, rows // height, weigh, 0)

        @pl.when(l > 0)
        def _():
            Sum(l).go(0)

        return 0

    lax.fori_loop(0, layers, backward, 0)
    pay[at_small : at_small + 1, :] = stat[after + layers, 0:1]
    for l in range(layers):
        pay[at_norm + 2 * l : at_norm + 2 * l + 2, :] = keep[l, 0:2]
        pay[at_small + 1 + l : at_small + 2 + l, :] = keep[l, 2:3]
    feat = x_ref.shape[1]
    pay[pl.ds(rows_at[0], rows_at[1] - rows_at[0]), :] = jnp.zeros((rows_at[1] - rows_at[0], width), f32)

    def weigh_in(s, total):
        span = rows_of(s, height)
        return total + dots(parts_of(x_ref[span, :], 2), parts_of(gh[span, :], 2), TURNED)

    pay[pl.ds(rows_at[0], feat), :] = lax.fori_loop(0, rows // height, weigh_in, jnp.zeros((feat, width), f32))
    if layers > 1:
        Sum(1).go(5)
    for copies in late:
        arrived(copies)
    if layers > 1:
        Sum(1).go(6)


def step_call(n, nb, layers, nodes, all_nodes, classes, rows_at, summed_rows, label_at, x, labels, sums, biases, norms, head_bias,
              picks, pick_row, adjacency, shards):
    rows = x.shape[0]
    width = biases.shape[1]
    cols = adjacency[0].shape[1]
    halo = (cols - rows) // 2
    feat = x.shape[1]
    vmem = pl.BlockSpec(memory_space=pltpu.VMEM)
    smem = pl.BlockSpec(memory_space=pltpu.SMEM)
    hbm = pl.BlockSpec(memory_space=pl.ANY)
    dma = pltpu.SemaphoreType.DMA
    items = 2 + layers + 3
    exchanges = 2 * layers + 1
    _, ys, across, zs = plane_split(nb, n)
    hops = 2 * ys * across + 2 * zs + 1
    return pl.pallas_call(
        functools.partial(step_kernel, n, nb, layers, nodes, all_nodes, classes, rows_at, summed_rows, label_at),
        out_shape=(
            jax.ShapeDtypeStruct((summed_rows + (layers - 1) * 2 * width, width), f32),
            jax.ShapeDtypeStruct((width, feat), f32),
            jax.ShapeDtypeStruct((layers, 2 * width, width), f32),
            jax.ShapeDtypeStruct((width, LANES), f32),
        ),
        in_specs=[vmem] * 6 + [smem, vmem] + [hbm] * 4 + [vmem] + [hbm] * 2 + [vmem],
        out_specs=(vmem, hbm, hbm, hbm),
        scratch_shapes=[
            pltpu.VMEM((layers + 1, rows, width), f32),
            pltpu.VMEM((layers, rows, width), f32),
            pltpu.VMEM((rows, cols), bf16),
            pltpu.VMEM((rows, cols), bf16),
            pltpu.VMEM((cols, width), bf16),
            pltpu.VMEM((cols, width), bf16),
            pltpu.VMEM((rows, width), bf16),
            pltpu.VMEM((rows, width), bf16),
            pltpu.VMEM((rows, width), f32),
            pltpu.VMEM((2, 2, halo, width), f32),
            pltpu.VMEM((2, halo, width), f32),
            pltpu.VMEM((rows, LANES), f32),
            pltpu.VMEM((n, 8, LANES), f32),
            pltpu.VMEM((n, 8, LANES), f32),
            pltpu.VMEM((exchanges + 1, 2, width), f32),
            pltpu.VMEM((exchanges, n, 2, width), f32),
            pltpu.VMEM((width, feat), f32),
            pltpu.VMEM((layers, 2 * width, width), f32),
            pltpu.VMEM((width, LANES), f32),
            pltpu.VMEM((2, width, 2 * width), bf16),
            dma((4 * rows // 512,)),
            dma((exchanges, n)),
            dma((exchanges, n)),
            dma((exchanges, 2)),
            dma((exchanges, 2)),
            dma((n,)),
            dma((n,)),
            dma((items, nb)),
            dma((items, nb)),
            dma((items,)),
            dma((layers - 1, hops)),
            dma((layers - 1, hops)),
            pltpu.SemaphoreType.REGULAR((layers - 1,)),
            pltpu.VMEM((layers + 1, 4, width), f32),
            pltpu.VMEM((layers, 4, width), f32),
            pltpu.VMEM((LANES, width // nb), f32),
            pltpu.VMEM((width // nb, LANES), f32),
            pltpu.VMEM((width // nb, LANES), f32),
            pltpu.VMEM((8, LANES), f32),
        ],
        compiler_params=pltpu.CompilerParams(collective_id=1, has_side_effects=True, vmem_limit_bytes=63 << 20),
        name="forward_backward",
    )(x, labels, sums, biases, norms, head_bias, picks, pick_row, *adjacency, *shards)


def update_kernel(n, nb, layers, all_nodes, rows_at, classes, ns_parts, scales, summed_rows, pay, mom_in, mom_conv, mom_head, w_in,
                  w_conv, w_head, biases, norms, head_bias, fb, fn, fh, sb, sn, sh, power, *refs):
    (loss_o, in_o, conv_o, head_o, min_o, mconv_o, mhead_o, b_o, n_o, h_o, fb_o, fn_o, fh_o, sb_o, sn_o, sh_o) = refs[:16]
    (got1, sum1, got2, sum2, got3, full, gram, poly, small_gram, small_poly, mconv, send, recv, old_conv, old_sem, spread) = refs[16:]
    places = Places(n, nb)
    cores, planes, zs = places.cores, places.planes, places.zs
    core, spot, z = places.core, places.spot, places.z
    plane_peer, column_peer, core_peer = places.plane_peer, places.column_peer, places.core_peer
    here_b = places.b
    width = w_conv.shape[2]
    barrier = pltpu.get_barrier_semaphore()
    for peer in places.peers:
        pl.semaphore_signal(barrier, inc=1, device_id=peer, device_id_type=pl.DeviceIdType.MESH)

    def kdot(left, right, dims=((1,), (0,))):
        return dots(parts_of(left, ns_parts), parts_of(right, ns_parts), dims)

    def eye(k):
        return (lax.broadcasted_iota(jnp.int32, (k, k), 0) == lax.broadcasted_iota(jnp.int32, (k, k), 1)).astype(f32)

    def begin(moment, grams, i):
        size = jnp.sqrt(jnp.sum(moment * moment)) + 1e-07
        g = kdot(moment, moment, TURNED) / (size * size)
        grams[i] = g
        return size

    def step(grams, polys, which, early, late):
        k = grams.shape[1]
        count = len(which)
        def split(values):
            return [parts_of(v, ns_parts) for v in values]

        a1 = [grams[i] for i in which]
        a1_parts = split(a1)
        a2 = [dots(v, v) for v in a1_parts]
        p = [newton_a * eye(k) + newton_b * v + newton_c * u for v, u in zip(a1, a2)]
        p_parts = split(p)
        if not late:
            pa = [dots(v, u) for v, u in zip(p_parts, a1_parts)]
        if early:
            q = p
        else:
            q = [dots(v, parts_of(polys[i], ns_parts)) for i, v in zip(which, p_parts)]
        if not late:
            nxt = [dots(v, u) for v, u in zip(split(pa), p_parts)]
        for j in range(count):
            polys[which[j]] = q[j]
            if not late:
                grams[which[j]] = nxt[j]

    fetch = pltpu.make_async_copy(mom_conv, old_conv, old_sem)
    fetch.start()
    sizes = {}
    ready = tuple(range(1, layers))

    def start_ready():
        fetch.wait()
        for l in ready:
            mconv[l] = muon_decay * old_conv[l] + pay[summed_rows + (l - 1) * 2 * width : summed_rows + l * 2 * width]
            sizes[l] = begin(mconv[l], gram, l)

    def middle(count, grams, polys, which):
        lax.fori_loop(0, count, lambda _, c: (step(grams, polys, which, False, False), c)[1], 0)

    pl.semaphore_wait(barrier, len(places.peers))
    used = [0]

    def go(src, dst, to):
        i = used[0]
        used[0] += 1
        copy = remote(src, dst, send.at[i], recv.at[i], to)
        copy.start()
        return copy

    def settle(copies):
        for copy in copies:
            copy.wait()

    half_rows = summed_rows // cores
    block_rows = half_rows // planes
    m = block_rows // zs

    def part(ref, index, count):
        return ref.at[pl.ds(pl.multiple_of(index * count, 8), count)]

    if cores == 2:
        copies = [go(part(pay, 1 - core, half_rows), got1, core_peer)]
        start_ready()
        settle(copies)
        sum1[...] = part(pay, core, half_rows)[...] + got1[...]
    else:
        start_ready()
        sum1[...] = pay[pl.ds(0, half_rows), :]
    copies = []
    for k in range(1, planes):
        p, to = plane_peer(k)
        copies.append(go(part(sum1, p, block_rows), got2.at[k], to))
    step(gram, poly, ready, True, False)
    middle(1, gram, poly, ready)
    settle(copies)
    total = part(sum1, spot, block_rows)[...]
    for k in range(1, planes):
        total = total + got2[k]
    sum2[...] = total
    copies = []
    for k in range(1, zs):
        q, to = column_peer(k)
        copies.append(go(part(sum2, q, m), got3.at[k], to))
    middle(1, gram, poly, ready)
    settle(copies)
    total = part(sum2, z, m)[...]
    for k in range(1, zs):
        total = total + got3[k]
    block = core * planes + spot
    mine = part(full, block * zs + z, m)
    mine[...] = total
    copies = [go(mine, mine, column_peer(k)[1]) for k in range(1, zs)]
    middle(1, gram, poly, ready)
    settle(copies)
    mine = part(full, block, block_rows)
    copies = [go(mine, mine, plane_peer(k)[1]) for k in range(1, planes)]
    step(gram, poly, ready, False, True)
    scale_in, scale_conv, scale_head = scales
    span = w_conv.shape[1]

    def turn_conv(l):
        own = mconv[l, pl.ds(pl.multiple_of(here_b * span, 8), span)]
        mconv_o[l] = own
        w = w_conv[l]
        turn = kdot(own, poly[l]) * (scale_conv / sizes[l])
        conv_o[l] = w - muon_rate * (turn + muon_shrink * w)

    for l in ready:
        turn_conv(l)
    settle(copies)
    if cores == 2:
        mine = part(full, core, half_rows)
        settle([go(mine, mine, core_peer)])
    summed = full[...]
    mconv[0] = muon_decay * old_conv[0] + summed[: 2 * width]
    sizes[0] = begin(mconv[0], gram, 0)
    feat = w_in.shape[1]
    half = width // 2
    grad_in = summed[rows_at[0] : rows_at[0] + LANES].T
    grad_head = summed[rows_at[1] : rows_at[1] + half]
    spread[...] = jnp.zeros_like(spread)
    spread[:, 0:feat] = mom_in[...]
    moment_in = muon_decay * spread[...] + jnp.where(lax.broadcasted_iota(jnp.int32, (width, LANES), 1) < feat, grad_in, 0.0)
    moment_head = muon_decay * mom_head[...] + jnp.concatenate([grad_head[:, :LANES], grad_head[:, LANES:]], 0)
    sizes[layers] = begin(moment_in, small_gram, 0)
    sizes[layers + 1] = begin(moment_head, small_gram, 1)

    def both(early, late):
        step(gram, poly, (0,), early, late)
        step(small_gram, small_poly, (0, 1), early, late)

    both(True, False)
    lax.fori_loop(1, NS_STEPS - 1, lambda _, c: (both(False, False), c)[1], 0)
    both(False, True)
    turn_conv(0)
    span = w_in.shape[0]
    mconv[0, pl.ds(0, width), 0:LANES] = moment_in
    mconv[0, pl.ds(0, width), LANES : 2 * LANES] = moment_head
    own = mconv[0, pl.ds(pl.multiple_of(here_b * span, 8), span), 0:LANES]
    min_o[...] = own[:, :feat]
    w = w_in[...]
    turn = kdot(own, small_poly[0]) * (scale_in / sizes[layers])
    in_o[...] = w - muon_rate * (turn[:, :feat] + muon_shrink * w)
    span = w_head.shape[1]
    own = mconv[0, pl.ds(pl.multiple_of(here_b * span, 8), span), LANES : 2 * LANES]
    mhead_o[...] = own.T[:classes]
    w = w_head[...]
    turn = kdot(own, small_poly[1]) * (scale_head / sizes[layers + 1])
    head_o[...] = w - muon_rate * (turn.T[:classes] + muon_shrink * w)

    def adamw(param, grad, first, second, outs):
        first = adam_first_decay * first + (1.0 - adam_first_decay) * grad
        second = adam_second_decay * second + (1.0 - adam_second_decay) * grad * grad
        first_hat = first / power[0]
        second_hat = second / power[1]
        outs[0][...] = param - adam_rate * (first_hat / (jnp.sqrt(second_hat) + adam_epsilon) + adam_shrink * param)
        outs[1][...] = first
        outs[2][...] = second

    at = rows_at[2]
    adamw(biases[...], summed[at : at + layers + 1], fb[...], sb[...], (b_o, fb_o, sb_o))
    at = at + layers + 1
    for l in range(layers):
        rows = summed[at + 2 * l : at + 2 * l + 2]
        adamw(norms[l], rows, fn[l], sn[l], (n_o.at[l], fn_o.at[l], sn_o.at[l]))
    at = at + 2 * layers
    adamw(head_bias[...], summed[at : at + 1, :classes], fh[...], sh[...], (h_o, fh_o, sh_o))
    loss_o[...] = jnp.sum(summed[at + 1 : at + 2], axis=1, keepdims=True) / all_nodes


def update_call(n, nb, layers, all_nodes, rows_at, classes, ns_parts, scales, summed_rows, pay, moments, shards, smalls, power):
    cores, ys, xs, zs = plane_split(nb, n)
    planes = ys * xs
    width = pay.shape[1]
    m = summed_rows // (n * nb)
    w_in, w_conv, w_head = shards
    vmem = pl.BlockSpec(memory_space=pltpu.VMEM)
    smem = pl.BlockSpec(memory_space=pltpu.SMEM)
    like = [jax.ShapeDtypeStruct(v.shape, f32) for v in (w_in, w_conv, w_head)]
    like_small = [jax.ShapeDtypeStruct(v.shape, f32) for v in smalls[:3]]
    copies = 2 * (planes + zs)
    return pl.pallas_call(
        functools.partial(update_kernel, n, nb, layers, all_nodes, rows_at, classes, ns_parts, scales, summed_rows),
        out_shape=tuple([jax.ShapeDtypeStruct((1, 1), f32)] + like + like + like_small * 3),
        in_specs=[vmem] * 2 + [pl.BlockSpec(memory_space=pl.ANY)] + [vmem] * 13 + [smem],
        out_specs=(vmem,) * 16,
        scratch_shapes=[
            pltpu.VMEM((zs * planes * m, width), f32),
            pltpu.VMEM((zs * planes * m, width), f32),
            pltpu.VMEM((planes, zs * m, width), f32),
            pltpu.VMEM((zs * m, width), f32),
            pltpu.VMEM((zs, m, width), f32),
            pltpu.VMEM((summed_rows, width), f32),
            pltpu.VMEM((layers, width, width), f32),
            pltpu.VMEM((layers, width, width), f32),
            pltpu.VMEM((2, LANES, LANES), f32),
            pltpu.VMEM((2, LANES, LANES), f32),
            pltpu.VMEM((layers, 2 * width, width), f32),
            pltpu.SemaphoreType.DMA((copies,)),
            pltpu.SemaphoreType.DMA((copies,)),
            pltpu.VMEM((layers, 2 * width, width), f32),
            pltpu.SemaphoreType.DMA,
            pltpu.VMEM((width, LANES), f32),
        ],
        compiler_params=pltpu.CompilerParams(collective_id=2, has_side_effects=True, vmem_limit_bytes=63 << 20),
        name="sum_and_update",
    )(pay, *moments, *shards, *smalls, power)


NS_PARTS = 3


def hand_over_kernel(*refs):
    half = len(refs) // 2
    for src, dst in zip(refs[:half], refs[half:]):
        dst[...] = src[...]


def hand_over(arrays):
    vmem = pl.BlockSpec(memory_space=pltpu.VMEM)
    return pl.pallas_call(
        hand_over_kernel,
        out_shape=tuple(jax.ShapeDtypeStruct(v.shape, v.dtype) for v in arrays),
        in_specs=[vmem] * len(arrays),
        out_specs=(vmem,) * len(arrays),
        name="hand_over",
    )(*arrays)


def per_device(
    n_batch,
    n_rows,
    features,
    edge_rows,
    edge_weight,
    halo_counts,
    labels,
    pair_rows,
    step,
    w_in,
    w_conv,
    w_head,
    biases,
    norm_params,
    head_bias,
    mom_in,
    mom_conv,
    mom_head,
    first_bias,
    first_norm,
    first_head,
    second_bias,
    second_norm,
    second_head,
):
    rows_dev = features.shape[1]
    halo_rows = rows_dev // 4
    edge_count = edge_rows.shape[3]
    layers, hid = w_conv.shape[0], w_conv.shape[2]
    feat, classes = w_in.shape[0], w_head.shape[1]
    pairs = pair_rows.shape[3]
    node_count = rows_dev * n_rows
    all_nodes = node_count * n_batch
    flat = [
        edge_rows.reshape(2 * edge_count).astype(f32),
        edge_weight.reshape(edge_count),
        labels.reshape(rows_dev).astype(f32),
        pair_rows.reshape(n_rows * pairs).astype(f32),
    ]
    flat = jnp.concatenate(flat)
    flat = jnp.pad(flat, (0, -flat.shape[0] % (8 * LANES))).reshape(-1, LANES)
    flat = redeal(flat, n_batch, n_rows)
    inputs = redeal(features, n_batch, n_rows)[0]
    e = edge_count // LANES
    block = my_place()[1]
    wide = (rows_dev + 2 * halo_rows) // TILE
    rims = jnp.stack([(block > 0).astype(jnp.int32), (block < n_rows - 1).astype(jnp.int32)])
    *adjacency, row_sums = fill(flat[:e], flat[e : 2 * e], flat[2 * e : 3 * e], rims, rows_dev // TILE, wide, halo_rows // TILE, 2)
    label_rows = rows_dev // LANES
    picks = flat[3 * e + label_rows :].reshape(-1)[: n_rows * pairs].astype(jnp.int32)
    spread = jnp.pad(picks.reshape(n_rows, pairs), ((0, 0), (0, 8 - pairs)), constant_values=-1).reshape(1, n_rows * 8)
    at_in = 2 * hid
    at_head = at_in + -(-feat // 8) * 8
    at_small = at_head + hid // 2
    used = at_small + layers + 1 + 2 * layers + 2
    unit = 8 * n_rows * n_batch
    pay_rows = -(-used // unit) * unit
    rows_at = (at_in, at_head, at_small)
    turned = [
        w_in.T,
        w_conv,
        w_head.T,
        mom_in.T,
        mom_conv,
        mom_head.T,
    ]
    pay, full_min, full_mconv, full_mhead = step_call(
        n_rows,
        n_batch,
        layers,
        node_count,
        all_nodes,
        classes,
        rows_at,
        pay_rows,
        3 * e,
        inputs,
        flat,
        row_sums,
        biases,
        norm_params,
        head_bias[None],
        picks,
        spread,
        adjacency,
        turned,
    )
    count = step[0].astype(f32)
    power = jnp.stack([1.0 - jnp.power(adam_first_decay, count), 1.0 - jnp.power(adam_second_decay, count)])
    scales = (
        math.sqrt(max(1.0, hid / feat)),
        math.sqrt(max(1.0, hid / (2 * hid))),
        math.sqrt(max(1.0, classes / hid)),
    )
    smalls = (
        biases,
        norm_params,
        head_bias[None],
        first_bias,
        first_norm,
        first_head[None],
        second_bias,
        second_norm,
        second_head[None],
    )
    outs = update_call(
        n_rows,
        n_batch,
        layers,
        all_nodes,
        rows_at,
        classes,
        NS_PARTS,
        scales,
        pay_rows,
        pay,
        (full_min, full_mconv, full_mhead),
        (turned[0], w_conv, turned[2]),
        smalls,
        power,
    )
    outs = hand_over(outs)
    loss, new_in, new_conv, new_head, moment_in, moment_conv, moment_head = outs[:7]
    rest = []
    for i in range(0, 9, 3):
        rest += [outs[7 + i], outs[8 + i], outs[9 + i][0]]
    return (loss[0, 0], new_in.T, new_conv, new_head.T, moment_in.T, moment_conv, moment_head.T, *rest)


def solution(mesh):
    in_specs = (
        P("batch", "rows", None),
        P("batch", "rows", None, None),
        P("batch", "rows", None),
        P("batch", "rows", None),
        P("batch", "rows"),
        P("batch", "rows", None, None),
        P(),
        P(None, "batch"),
        P(None, "batch", None),
        P("batch", None),
        P(),
        P(),
        P(),
        P(None, "batch"),
        P(None, "batch", None),
        P("batch", None),
        P(),
        P(),
        P(),
        P(),
        P(),
        P(),
    )
    out_specs = (
        P(),
        P(None, "batch"),
        P(None, "batch", None),
        P("batch", None),
        P(None, "batch"),
        P(None, "batch", None),
        P("batch", None),
        P(),
        P(),
        P(),
        P(),
        P(),
        P(),
        P(),
        P(),
        P(),
    )
    body = functools.partial(per_device, mesh.shape["batch"], mesh.shape["rows"])
    return jax.shard_map(body, mesh=mesh, in_specs=in_specs, out_specs=out_specs, check_vma=False)
```
